32 devices in a mesh: dp: 16 (over z, y, x), mp: 2 (over core).
Axes of the slice: x: 2, y: 2, z: 4, core: 2. Of those that a mesh axis runs over, the one named last changes fastest.
Arguments:
- context: bfloat16 [16384, 4096], P('dp'), may hold values from -6 to 6
- counts: int32 [16, 2], P('dp'), may hold values from 256 to 768, as said below
- routes: int32 [2048, 1], P('dp'), may hold values from 0 to 15; in each aligned block of 128 rows (0 to 127, 128 to 255, ...) at most 16 rows name the same one
- w_query: bfloat16 [4096, 1536], P(None, 'mp'), may hold values from -0.09375 to 0.09375
- w_key: bfloat16 [4096, 384], P(None, 'mp'), may hold values from -0.09375 to 0.09375
- w_value: bfloat16 [4096, 384], P(None, 'mp'), may hold values from -0.09375 to 0.09375
- w_out: bfloat16 [1536, 4096], P('mp'), may hold values from -2 to 2
- latents: bfloat16 [64, 4096], replicated, may hold values from -9 to 9
- gain_ctx: float32 [4096], replicated, may hold values from 0.25 to 1.75
- gain_lat: float32 [4096], replicated, may hold values from 0.25 to 1.75
- gain_out: float32 [4096], replicated, may hold values from 0.25 to 1.75
- cotangent: bfloat16 [4096, 4096], P('dp', 'mp'), may hold values from -9 to 9
Outputs:
- routed: bfloat16 [4096, 4096], P('dp', 'mp')
- ctx_grad: bfloat16 [16384, 4096], P('dp', 'mp')
- grad_w_query: float32 [4096, 1536], P('dp', 'mp')
- grad_w_key: float32 [4096, 384], P('dp', 'mp')
- grad_w_value: float32 [4096, 384], P('dp', 'mp')
- grad_w_out: float32 [1536, 4096], P('mp', 'dp')
- grad_latents: float32 [64, 4096], P(None, ('dp', 'mp'))
- grad_gain_ctx: float32 [4096], P(('dp', 'mp'))
- grad_gain_lat: float32 [4096], P(('dp', 'mp'))
- grad_gain_out: float32 [4096], P(('dp', 'mp'))
The draws below stay inside these ranges and needn't reach their ends.
Inputs may be any that keep to these rules, and one draw needn't show every extreme that they name: `counts`: in every block the 2 images hold together at most 1024 patches, exactly 1024 in at least two blocks; each image has 256 or more patches and one has 768. `routes`: within the rows of one dp index no decoder shard is named by more than 16 rows.
All inputs are finite; a program needn't handle non-finite values.
Results may differ from the reference program's by a relative error of at most 0.01.
Values may be sent and summed in bfloat16 or wider, within the bound.
No kernel may reach another device: no remote copies, remote signals or barrier semaphores. Data moves between devices by JAX's collectives and lax.ppermute only.
A program may use at most 192 MiB of HBM per device.

```python
import math
import jax
import jax.numpy as jnp
import numpy as np
from jax import lax

D = 4096
HEADS = 16
KVH = 4
HD = 96
LATENTS = 64
CAP = 1024
MINLEN = 256
IMG_DEV = 2
QW = 1536
KW = 384
SLOT = 16
PATCHES = 16384
ROWS = 2048
RECV = 4096
N_DP = 16


def draw_counts(key, part):
    first_key, second_key, pick_key, other_key = jax.random.split(jax.random.fold_in(key, 17), 4)
    first = jax.random.randint(first_key, (N_DP,), MINLEN, CAP - MINLEN + 1)
    room = CAP - first - MINLEN + 1
    second = MINLEN + jax.random.randint(second_key, (N_DP,), 0, room)
    full_one = jax.random.randint(pick_key, (), 0, N_DP)
    full_two = (full_one + 1 + jax.random.randint(other_key, (), 0, N_DP - 1)) % N_DP
    index = jnp.arange(N_DP)
    second = jnp.where(index == full_one, CAP - first, second)
    first = jnp.where(index == full_two, CAP - MINLEN, first)
    second = jnp.where(index == full_two, MINLEN, second)
    return jnp.stack([first, second], axis=1).astype(jnp.int32)


def feature_profile(key):
    signs = jnp.where(jax.random.bernoulli(jax.random.fold_in(key, 5), 0.5, (D,)), 1.0, -1.0)
    ramp = jnp.arange(D, dtype=jnp.float32) / (D - 1)
    amplitude = 0.5 * jnp.exp(ramp * 1.0986123)
    return (signs * amplitude).astype(jnp.float32)


def draw_latents(key, part):
    noise = jnp.clip(jax.random.normal(jax.random.fold_in(key, 6), (LATENTS, D), jnp.float32), -6.0, 6.0)
    return (noise + feature_profile(key)[None, :]).astype(jnp.bfloat16)


def draw_cotangent(key, part):
    noise = jnp.clip(jax.random.normal(jax.random.fold_in(key, 7), (RECV, D), jnp.float32), -6.0, 6.0)
    return (noise + feature_profile(key)[None, :]).astype(jnp.bfloat16)


def steps_of(own_key, dims, cuts, smallest, high):
    def one(dim, shards_of):
        draws = jax.random.uniform(jax.random.fold_in(jax.random.fold_in(own_key, 6), dim), (shards_of,), jnp.float32, smallest / len(cuts), high / len(cuts))
        return jnp.repeat(jnp.exp(draws), dims[dim] // shards_of).reshape((-1,) + (1,) * (len(dims) - dim - 1))

    level = one(*cuts[0])
    for cut in cuts[1:]:
        level = level * one(*cut)
    return level


def routed_block(stream_key, own, number, rows, amount, top, bound, lean):
    ranking = jax.random.permutation(stream_key, amount)
    crowded, usual = load_shares(amount, rows * top, bound, lean, True), load_shares(amount, rows * top, bound, lean, False)
    places = jnp.arange(amount)

    def named(sizes, turn):
        used = int((sizes > 0).sum())
        fixed = max(1, used // 4)
        shifted = fixed + (places - fixed + turn * (used - fixed)) % max(1, amount - fixed)
        return jnp.zeros((amount,), jnp.int32).at[ranking[jnp.where(places < fixed, places, shifted)]].set(jnp.asarray(sizes, jnp.int32))

    sizes = jnp.where(number % 4 == 0, named(crowded, number // 4), named(usual, number - number // 4 - 1))
    mixed = jax.random.permutation(jax.random.fold_in(own, 3), amount)
    donor, taker = mixed[0:amount // 2 * 2:2], mixed[1:amount // 2 * 2:2]
    slack = jnp.minimum(sizes[donor] - 1, bound - sizes[taker]) // 2
    slack = jnp.where((donor == ranking[0]) | (taker == ranking[0]) | (sizes[taker] == 0), 0, jnp.maximum(slack, 0))
    shifted = jax.random.randint(jax.random.fold_in(own, 4), (amount // 2,), 0, 1 << 20) % (slack + 1)
    sizes = sizes.at[donor].add(-shifted).at[taker].add(shifted)
    members = jnp.searchsorted(jnp.cumsum(sizes), jnp.arange(rows * top), side="right").astype(jnp.int32)
    listing = members.reshape(top, rows).T
    listing = listing[jax.random.permutation(jax.random.fold_in(own, 1), rows)]
    turn = jax.random.randint(jax.random.fold_in(own, 2), (rows, 1), 0, top)
    return jnp.take_along_axis(listing, (jnp.arange(top)[None, :] + turn) % top, axis=1)


def load_shares(amount, total, most, slope, full):
    weights = [(1 << 20) // math.isqrt(grade ** slope) + 1 for grade in range(1, amount + 1)]
    largest = most if full else min(most, max(-(-total // amount), total * weights[0] // sum(weights)))
    least = 1 if total - largest >= amount - 1 else 0
    given, surplus = [largest] + [least] * (amount - 1), total - largest - least * (amount - 1)
    while surplus > 0:
        free = [i for i in range(1, amount) if given[i] < largest] or [i for i in range(1, amount) if given[i] < most]
        pool, remaining = sum([weights[i] for i in free]), surplus
        for i in free:
            addition = min(most - given[i], max(1, remaining * weights[i] // pool), surplus)
            given[i] = given[i] + addition
            surplus = surplus - addition
    return np.array(given)


def normal_values(rng, dims, deviation, bound, shards=(), held_as=jnp.bfloat16):
    result = deviation * jax.random.normal(rng, dims, jnp.float32)
    if shards:
        result = result * steps_of(rng, dims, shards, -0.22, 0.18)
    return jnp.clip(result, -bound, bound).astype(held_as)


def setup_inputs(seed: int = 0) -> dict:
    seeds = jax.random.split(jax.random.key(seed), 13)
    context = normal_values(seeds[0], (PATCHES, D), 1.0, 6.0, ((0, 16),))
    counts = draw_counts(jax.random.fold_in(seeds[12], 71), 0)
    routes_keys = jax.random.split(jax.random.fold_in(seeds[2], 1), ROWS // (IMG_DEV * LATENTS))
    routes_turns = jax.random.permutation(jax.random.fold_in(seeds[2], 3), ROWS // (IMG_DEV * LATENTS))
    routes = jax.vmap(lambda own, number: routed_block(jax.random.fold_in(seeds[2], 2), own, number, IMG_DEV * LATENTS, N_DP, 1, SLOT, 2))(routes_keys, routes_turns).reshape((ROWS, 1))
    w_query = normal_values(seeds[3], (D, QW), D ** -0.5, 0.09375, ((1, 2),))
    w_key = normal_values(seeds[4], (D, KW), D ** -0.5, 0.09375, ((1, 2),))
    w_value = normal_values(seeds[5], (D, KW), D ** -0.5, 0.09375, ((1, 2),))
    w_out = normal_values(seeds[6], (QW, D), 8 ** -0.5, 2.0, ((0, 2),))
    latents = draw_latents(jax.random.fold_in(seeds[12], 71), 0)
    gain_ctx = jnp.clip(1.0 + 0.15 * jax.random.normal(seeds[8], (D,), jnp.float32), 0.25, 1.75)
    gain_lat = jnp.clip(1.0 + 0.15 * jax.random.normal(seeds[9], (D,), jnp.float32), 0.25, 1.75)
    gain_out = jnp.clip(1.0 + 0.15 * jax.random.normal(seeds[10], (D,), jnp.float32), 0.25, 1.75)
    cotangent = draw_cotangent(jax.random.fold_in(seeds[12], 71), 0)
    return {"context": context, "counts": counts, "routes": routes, "w_query": w_query, "w_key": w_key, "w_value": w_value, "w_out": w_out, "latents": latents, "gain_ctx": gain_ctx, "gain_lat": gain_lat, "gain_out": gain_out, "cotangent": cotangent}


@jax.custom_vjp
def low(v):
    return lax.optimization_barrier(v.astype(jnp.bfloat16)).astype(jnp.float32)

@jax.custom_vjp
def low_back(v):
    return v

def low_keep(v):
    return (low(v), None)

def low_pass(kept, grad):
    return (grad,)

def back_keep(v):
    return (v, None)

def back_low(kept, grad):
    return (low(grad),)
low.defvjp(low_keep, low_pass)
low_back.defvjp(back_keep, back_low)
EPSILON = 1e-06
NEGATIVE = -1e+30
HIGHEST = lax.Precision.HIGHEST

def norm_rows(values_in, gain):
    inverse = lax.rsqrt(lax.optimization_barrier(jnp.mean(values_in * values_in, axis=-1, keepdims=True)) + EPSILON)
    return values_in * inverse * gain

def device_rows(patch_block, image_count, w_query, w_key, w_value, w_out, latents, gain_ctx, gain_lat, gain_out):
    group = HEADS // KVH
    normed_ctx = low(norm_rows(patch_block, gain_ctx))
    key_rows = low_back(low(jnp.dot(normed_ctx, w_key, precision=HIGHEST)))
    value_rows = low_back(low(jnp.dot(normed_ctx, w_value, precision=HIGHEST)))
    normed_lat = low(norm_rows(latents, gain_lat))
    lat_keys = low_back(low(jnp.dot(normed_lat, w_key, precision=HIGHEST)))
    lat_values = low_back(low(jnp.dot(normed_lat, w_value, precision=HIGHEST)))
    query_rows = low_back(low(jnp.dot(normed_lat, w_query, precision=HIGHEST) * HD ** (-0.5)))
    query_heads = query_rows.reshape(LATENTS, KVH, group, HD)
    key_heads = key_rows.reshape(CAP, KVH, HD)
    value_heads = value_rows.reshape(CAP, KVH, HD)
    lat_key_heads = lat_keys.reshape(LATENTS, KVH, HD)
    lat_value_heads = lat_values.reshape(LATENTS, KVH, HD)
    scores = low_back(jnp.einsum('rkgd,tkd->kgrt', query_heads, key_heads, precision=HIGHEST))
    lat_scores = low_back(jnp.einsum('rkgd,skd->kgrs', query_heads, lat_key_heads, precision=HIGHEST))
    position = jnp.arange(CAP, dtype=jnp.int32)
    image_start = jnp.cumsum(image_count) - image_count
    member = (position[None, :] >= image_start[:, None]) & (position[None, :] < (image_start + image_count)[:, None])
    member_wide = member[:, None, None, None, :]
    masked = jnp.where(member_wide, scores[None], NEGATIVE)
    row_max = jnp.maximum(lax.optimization_barrier(jnp.max(masked, axis=-1, keepdims=True)), lax.optimization_barrier(jnp.max(lat_scores, axis=-1, keepdims=True))[None])
    exponent = jnp.where(member_wide, jnp.exp(masked - row_max), 0.0)
    lat_exponent = jnp.exp(lat_scores[None] - row_max)
    total = lax.optimization_barrier(jnp.sum(exponent, axis=-1, keepdims=True)) + lax.optimization_barrier(jnp.sum(lat_exponent, axis=-1, keepdims=True))
    attention = low(exponent / total)
    lat_attention = low(lat_exponent / total)
    mixed = jnp.einsum('ikgrt,tkd->irkgd', attention, value_heads, precision=HIGHEST)
    mixed = mixed + jnp.einsum('ikgrs,skd->irkgd', lat_attention, lat_value_heads, precision=HIGHEST)
    attn_rows = low_back(low(mixed.reshape(IMG_DEV * LATENTS, HEADS * HD)))
    branch = low_back(jnp.dot(attn_rows, w_out, precision=HIGHEST))
    resid = jnp.tile(latents, (IMG_DEV, 1)) + branch
    return low(norm_rows(resid, gain_out))

def reference(context, counts, routes, w_query, w_key, w_value, w_out, latents, gain_ctx, gain_lat, gain_out, cotangent):
    patch_blocks = context.astype(jnp.float32).reshape(N_DP, CAP, D)
    shard_of = routes.reshape(N_DP, IMG_DEV * LATENTS)
    shard_hot = (shard_of[:, :, None] == jnp.arange(N_DP, dtype=jnp.int32)[None, None, :]).astype(jnp.int32)
    rank = lax.optimization_barrier(jnp.sum((jnp.cumsum(shard_hot, axis=1) - shard_hot) * shard_hot, axis=2))
    source = jnp.arange(N_DP, dtype=jnp.int32)[:, None]
    target = (shard_of * (N_DP * SLOT) + source * SLOT + rank).reshape(-1).astype(jnp.int32)

    def forward(blocks_in, query_w, key_w, value_w, out_w, latent_w, ctx_gain, lat_gain, out_gain):

        def one_device(item):
            return device_rows(item[0], item[1], query_w, key_w, value_w, out_w, latent_w, ctx_gain, lat_gain, out_gain)
        rows_all = lax.map(jax.checkpoint(one_device), (blocks_in, counts))
        empty = jnp.zeros((RECV, D), jnp.float32)
        return empty.at[target].set(rows_all.reshape(ROWS, D))
    routed, pullback = jax.vjp(forward, patch_blocks, w_query.astype(jnp.float32), w_key.astype(jnp.float32), w_value.astype(jnp.float32), w_out.astype(jnp.float32), latents.astype(jnp.float32), gain_ctx, gain_lat, gain_out)
    grads = pullback(cotangent.astype(jnp.float32))
    return (routed.astype(jnp.bfloat16), grads[0].reshape(PATCHES, D).astype(jnp.bfloat16), grads[1], grads[2], grads[3], grads[4], grads[5], grads[6], grads[7], grads[8])
```

```python
import jax
import jax.numpy as jnp
from jax import lax
from jax.sharding import PartitionSpec as P

HD = 96
EPSILON = 1e-06
NEGATIVE = -1e30
BF16 = jnp.bfloat16
F32 = jnp.float32


def dot_general(left, right, left_dim, right_dim):
    return lax.dot_general(
        left, right, (((left_dim,), (right_dim,)), ((), ())), preferred_element_type=F32
    )


def norm_parts(values_in):
    inverse = lax.rsqrt(jnp.mean(values_in * values_in, axis=-1, keepdims=True) + EPSILON)
    return (values_in * inverse, inverse)


def swap_cores(array):
    return lax.ppermute(array, "mp", [(0, 1), (1, 0)])


def swap_bit(array, bit, dp_count):
    return lax.ppermute(array, "dp", [(i, i ^ (1 << bit)) for i in range(dp_count)])


def halve(array, axis, bit, dp_count):
    mine = (lax.axis_index("dp") >> bit) & 1
    going = lax.dynamic_index_in_dim(array, 1 - mine, axis, keepdims=False)
    kept = lax.dynamic_index_in_dim(array, mine, axis, keepdims=False)
    return kept.astype(F32) + swap_bit(going.astype(BF16), bit, dp_count).astype(F32)


def scatter_sum(array, bits, dp_count):
    rows, owners, columns = array.shape
    left = sorted(bits, reverse=True)
    array = array.reshape((rows,) + (2,) * len(left) + (columns,))
    for bit in bits:
        axis = left.index(bit)
        array = halve(array, 1 + axis, bit, dp_count)
        left.pop(axis)
    return array


def local(
    context,
    counts,
    routes,
    w_query,
    w_key,
    w_value,
    w_out,
    latents,
    gain_ctx,
    gain_lat,
    gain_out,
    cotangent,
):
    dp_count = lax.axis_size("dp")
    mp_count = lax.axis_size("mp")
    mp_index = lax.axis_index("mp")
    dp_index = lax.axis_index("dp")
    bits = dp_count.bit_length() - 1
    gather_bits = [bits - 1, bits - 2]
    scatter_bits = list(range(bits - 2))
    order_one = list(range(bits))
    order_two = [1, 0] + order_one[2:]
    patch_rows, width = context.shape
    half_width = width // mp_count
    own_width = width // dp_count
    head_local = w_query.shape[1] // HD
    group_local = w_key.shape[1] // HD
    per_group = head_local // group_local
    latent_rows = latents.shape[0]
    image_slots = counts.shape[1]
    out_rows = image_slots * latent_rows
    slot_count = cotangent.shape[0] // dp_count
    key_width = w_key.shape[1]
    query_width = w_query.shape[1]
    scaling = HD ** (-0.5)

    returned = lax.all_to_all(
        cotangent.reshape(dp_count, slot_count, half_width),
        "dp",
        split_axis=0,
        concat_axis=0,
        tiled=True,
    ).reshape(dp_count * slot_count, half_width)
    returned_other = swap_cores(returned)
    w_out_other = swap_cores(w_out)
    w_pair = jnp.concatenate([w_key, w_value], axis=1)
    w_pair_half = lax.dynamic_slice_in_dim(w_pair, mp_index * half_width, half_width, 0)
    w_pair_other = swap_cores(
        lax.dynamic_slice_in_dim(w_pair, (1 - mp_index) * half_width, half_width, 0)
    )

    patch_hat, patch_inv = norm_parts(context.astype(F32))
    normed_ctx = (patch_hat * gain_ctx).astype(BF16)
    key_f32 = jnp.dot(normed_ctx, w_key, preferred_element_type=F32)
    value_f32 = jnp.dot(normed_ctx, w_value, preferred_element_type=F32)
    key_rows = key_f32.astype(BF16)
    value_rows = value_f32.astype(BF16)
    lat_float = latents.astype(F32)
    lat_hat, lat_inv = norm_parts(lat_float)
    normed_lat = (lat_hat * gain_lat).astype(BF16)
    lat_key_f32 = jnp.dot(normed_lat, w_key, preferred_element_type=F32)
    lat_value_f32 = jnp.dot(normed_lat, w_value, preferred_element_type=F32)
    lat_keys = lat_key_f32.astype(BF16)
    lat_values = lat_value_f32.astype(BF16)
    query_f32 = jnp.dot(normed_lat, w_query, preferred_element_type=F32) * scaling
    query_rows = query_f32.astype(BF16)
    query_heads = query_rows.reshape(latent_rows, group_local, per_group, HD)
    key_heads = key_rows.reshape(patch_rows, group_local, HD)
    value_heads = value_rows.reshape(patch_rows, group_local, HD)
    lat_key_heads = lat_keys.reshape(latent_rows, group_local, HD)
    lat_value_heads = lat_values.reshape(latent_rows, group_local, HD)
    scores = jnp.einsum(
        "rkgd,tkd->kgrt", query_heads, key_heads, preferred_element_type=jnp.float32
    )
    lat_scores = jnp.einsum(
        "rkgd,skd->kgrs", query_heads, lat_key_heads, preferred_element_type=jnp.float32
    )
    position = jnp.arange(patch_rows, dtype=jnp.int32)
    image_count = counts[0]
    image_start = jnp.cumsum(image_count) - image_count
    member = (position[None, :] >= image_start[:, None]) & (
        position[None, :] < (image_start + image_count)[:, None]
    )
    member_wide = member[:, None, None, None, :]
    masked = jnp.where(member_wide, scores[None], NEGATIVE)
    row_max = jnp.maximum(
        jnp.max(masked, axis=-1, keepdims=True), jnp.max(lat_scores, axis=-1, keepdims=True)[None]
    )
    exponent = jnp.where(member_wide, jnp.exp(masked - row_max), 0.0)
    lat_exponent = jnp.exp(lat_scores[None] - row_max)
    total = jnp.sum(exponent, axis=-1, keepdims=True) + jnp.sum(
        lat_exponent, axis=-1, keepdims=True
    )
    attention = exponent / total
    lat_attention = lat_exponent / total
    attention_low = attention.astype(BF16)
    lat_attention_low = lat_attention.astype(BF16)
    mixed = jnp.einsum(
        "ikgrt,tkd->irkgd", attention_low, value_heads, preferred_element_type=jnp.float32
    )
    mixed = mixed + jnp.einsum(
        "ikgrs,skd->irkgd", lat_attention_low, lat_value_heads, preferred_element_type=jnp.float32
    )
    attn_rows = mixed.reshape(out_rows, query_width).astype(BF16)
    attn_other = swap_cores(attn_rows)
    branch = jnp.dot(attn_rows, w_out, preferred_element_type=F32) + jnp.dot(
        attn_other, w_out_other, preferred_element_type=F32
    )
    resid = jnp.tile(lat_float, (image_slots, 1)) + branch
    out_hat, out_inv = norm_parts(resid)
    final_rows = (out_hat * gain_out).astype(BF16)
    shard_of = routes[:, 0]
    shard_hot = (shard_of[:, None] == jnp.arange(dp_count, dtype=jnp.int32)[None, :]).astype(
        jnp.int32
    )
    rank = jnp.sum((jnp.cumsum(shard_hot, axis=0) - shard_hot) * shard_hot, axis=1)
    place = shard_of * slot_count + rank
    scatter_table = (
        jnp.arange(dp_count * slot_count, dtype=jnp.int32)[:, None] == place[None, :]
    ).astype(BF16)
    final_half = lax.dynamic_slice_in_dim(final_rows, mp_index * half_width, half_width, 1)
    outgoing = jnp.dot(scatter_table, final_half, preferred_element_type=F32).astype(BF16)
    routed = lax.all_to_all(
        outgoing.reshape(dp_count, slot_count, half_width),
        "dp",
        split_axis=0,
        concat_axis=0,
        tiled=True,
    ).reshape(dp_count * slot_count, half_width)

    attn_line = attn_rows
    for bit in gather_bits:
        attn_line = jnp.concatenate([attn_line, swap_bit(attn_line, bit, dp_count)], axis=0)

    first = jnp.where(mp_index == 0, returned, returned_other)
    second = jnp.where(mp_index == 0, returned_other, returned)
    d_final = jnp.concatenate(
        [dot_general(scatter_table, first, 0, 0), dot_general(scatter_table, second, 0, 0)], axis=1
    )
    d_hat = d_final * gain_out
    d_resid = out_inv * (d_hat - out_hat * jnp.mean(d_hat * out_hat, axis=1, keepdims=True))
    gain_out_term = jnp.sum(d_final * out_hat, axis=0)
    d_branch = d_resid.astype(BF16)
    d_attn = dot_general(d_branch, w_out, 1, 1).astype(BF16)

    d_attn_heads = d_attn.reshape(image_slots, latent_rows, group_local, per_group, HD)
    d_probs = jnp.einsum(
        "irkgd,tkd->ikgrt", d_attn_heads, value_heads, preferred_element_type=jnp.float32
    )
    d_lat_probs = jnp.einsum(
        "irkgd,skd->ikgrs", d_attn_heads, lat_value_heads, preferred_element_type=jnp.float32
    )
    row_delta = jnp.sum(attention * d_probs, axis=-1, keepdims=True) + jnp.sum(
        lat_attention * d_lat_probs, axis=-1, keepdims=True
    )
    d_scores = jnp.sum(attention * (d_probs - row_delta), axis=0).astype(BF16)
    d_lat_scores = jnp.sum(lat_attention * (d_lat_probs - row_delta), axis=0).astype(BF16)
    d_query = jnp.einsum("kgrt,tkd->rkgd", d_scores, key_heads, preferred_element_type=jnp.float32)
    d_query = d_query + jnp.einsum(
        "kgrs,skd->rkgd", d_lat_scores, lat_key_heads, preferred_element_type=jnp.float32
    )
    d_query = d_query.reshape(latent_rows, query_width).astype(BF16)
    d_keys = jnp.einsum("kgrt,rkgd->tkd", d_scores, query_heads, preferred_element_type=jnp.float32)
    d_keys = d_keys.reshape(patch_rows, key_width).astype(BF16)
    d_values = jnp.einsum(
        "ikgrt,irkgd->tkd", attention_low, d_attn_heads, preferred_element_type=jnp.float32
    )
    d_values = d_values.reshape(patch_rows, key_width).astype(BF16)
    d_lat_keys = jnp.einsum(
        "kgrs,rkgd->skd", d_lat_scores, query_heads, preferred_element_type=jnp.float32
    )
    d_lat_keys = d_lat_keys.reshape(latent_rows, key_width).astype(BF16)
    d_lat_values = jnp.einsum(
        "ikgrs,irkgd->skd", lat_attention_low, d_attn_heads, preferred_element_type=jnp.float32
    )
    d_lat_values = d_lat_values.reshape(latent_rows, key_width).astype(BF16)
    d_pair = jnp.concatenate([d_keys, d_values], axis=1)

    value_grad = dot_general(d_values, normed_ctx, 0, 0).reshape(key_width, dp_count, own_width)
    key_grad = dot_general(d_keys, normed_ctx, 0, 0).reshape(key_width, dp_count, own_width)
    value_block = scatter_sum(value_grad, order_one, dp_count)
    key_block = scatter_sum(key_grad, order_two, dp_count)

    row_dot = jnp.sum(d_keys.astype(F32) * key_f32, axis=1) + jnp.sum(
        d_values.astype(F32) * value_f32, axis=1
    )
    row_dot = (row_dot + swap_cores(row_dot)) / width
    d_pair_other = swap_cores(d_pair)
    d_ctx_in = dot_general(d_pair, w_pair_half, 1, 1) + dot_general(
        d_pair_other, w_pair_other, 1, 1
    )
    gain_ctx_half = lax.dynamic_slice_in_dim(gain_ctx, mp_index * half_width, half_width, 0)
    hat_half = lax.dynamic_slice_in_dim(patch_hat, mp_index * half_width, half_width, 1)
    ctx_grad = (patch_inv * (d_ctx_in * gain_ctx_half - hat_half * row_dot[:, None])).astype(BF16)

    high = gain_out_term.astype(BF16)
    low = (gain_out_term - high.astype(F32)).astype(BF16)
    lat_sum = jnp.concatenate(
        [
            d_query,
            d_lat_keys,
            d_lat_values,
            high.reshape(latent_rows, width // latent_rows),
            low.reshape(latent_rows, width // latent_rows),
        ],
        axis=1,
    ).astype(F32)
    for bit in gather_bits + scatter_bits:
        lat_sum = lat_sum + swap_bit(lat_sum.astype(BF16), bit, dp_count).astype(F32)
    pair_sum = lat_sum[:, query_width : query_width + 2 * key_width]
    query_sum = lat_sum[:, :query_width]
    gains_at = query_width + 2 * key_width
    gain_step = width // latent_rows
    gain_out_full = (
        lat_sum[:, gains_at : gains_at + gain_step]
        + lat_sum[:, gains_at + gain_step : gains_at + 2 * gain_step]
    ).reshape(width)

    plane = dp_count // 4
    row_half = out_rows // mp_count
    d_block = lax.dynamic_slice_in_dim(d_branch, mp_index * row_half, row_half, 0)
    d_line = d_block.reshape(1, row_half, 2, 2, plane * own_width)
    for step, bit in enumerate(gather_bits):
        mine = (dp_index >> bit) & 1
        going = lax.dynamic_index_in_dim(d_line, 1 - mine, 2, keepdims=False)
        kept = lax.dynamic_index_in_dim(d_line, mine, 2, keepdims=False)
        d_line = jnp.concatenate([kept, swap_bit(going, bit, dp_count)], axis=0)
    d_line_other = swap_cores(d_line)
    d_line = jnp.concatenate(
        [
            jnp.where(mp_index == 0, d_line, d_line_other),
            jnp.where(mp_index == 0, d_line_other, d_line),
        ],
        axis=1,
    )
    out_part = dot_general(attn_line, d_line.reshape(4 * out_rows, plane * own_width), 0, 0)
    resid_part = jnp.sum(
        d_line.astype(F32).reshape(4 * image_slots, latent_rows, plane * own_width), axis=0
    )
    resid_part = lax.dynamic_index_in_dim(
        resid_part.reshape(2, latent_rows // 2, plane, mp_count, own_width // mp_count),
        mp_index,
        3,
        keepdims=False,
    )
    resid_part = jnp.transpose(resid_part, (1, 2, 0, 3)).reshape(
        latent_rows // 2, plane, own_width
    )
    out_part = jnp.concatenate([out_part.reshape(query_width, plane, own_width), resid_part], axis=0)
    cut = out_part.shape[0] // 2
    out_block = jnp.concatenate(
        [
            scatter_sum(out_part[:cut], scatter_bits, dp_count),
            scatter_sum(out_part[cut:], [1, 0] + scatter_bits[2:], dp_count),
        ],
        axis=0,
    )
    grad_w_out = out_block[:query_width]
    resid_sum = (
        out_block[query_width:]
        .reshape(latent_rows // 2, 2, own_width // mp_count)
        .transpose(1, 0, 2)
        .reshape(latent_rows, own_width // mp_count)
    )

    def own(array, axis):
        return lax.dynamic_slice_in_dim(array, dp_index * own_width, own_width, axis)

    lat_own = own(normed_lat, 1)
    pair_ctx = jnp.concatenate([key_block, value_block], axis=0).T
    query_grad = dot_general(lat_own, query_sum.astype(BF16), 0, 0) * scaling
    pair_lat = dot_general(lat_own, pair_sum.astype(BF16), 0, 0)
    pair_all = pair_ctx + pair_lat
    wq_own = own(w_query, 0)
    pair_own = own(w_pair, 0)
    gain_ctx_part = jnp.sum(pair_own.astype(F32) * pair_ctx, axis=1) / own(gain_ctx, 0)
    gain_lat_part = (
        jnp.sum(wq_own.astype(F32) * query_grad, axis=1)
        + jnp.sum(pair_own.astype(F32) * pair_lat, axis=1)
    ) / own(gain_lat, 0)
    d_lat_part = dot_general(
        (query_sum * scaling).astype(BF16), wq_own, 1, 1
    ) + dot_general(pair_sum.astype(BF16), pair_own, 1, 1)
    lat_dot_part = (
        jnp.sum(query_sum * query_f32, axis=1)
        + jnp.sum(pair_sum[:, :key_width] * lat_key_f32, axis=1)
        + jnp.sum(pair_sum[:, key_width:] * lat_value_f32, axis=1)
    )
    small = jnp.concatenate(
        [
            d_lat_part,
            jnp.broadcast_to(lat_dot_part[:, None], (latent_rows, own_width)),
            jnp.broadcast_to(gain_ctx_part[None, :], (8, own_width)),
            jnp.broadcast_to(gain_lat_part[None, :], (8, own_width)),
        ],
        axis=0,
    )
    small = small + swap_cores(small)
    share = own_width // mp_count
    small = lax.dynamic_slice_in_dim(small, mp_index * share, share, 1)
    d_lat_in = small[:latent_rows]
    lat_dot = small[latent_rows : 2 * latent_rows] / width

    def mine_of(array, axis):
        return lax.dynamic_slice_in_dim(
            array, dp_index * own_width + mp_index * share, share, axis
        )

    grad_latents = resid_sum + lat_inv * (
        mine_of(gain_lat, 0) * d_lat_in - mine_of(lat_hat, 1) * lat_dot
    )
    return (
        routed,
        ctx_grad,
        query_grad,
        pair_all[:, :key_width],
        pair_all[:, key_width:],
        grad_w_out,
        grad_latents,
        small[2 * latent_rows],
        small[2 * latent_rows + 8],
        mine_of(gain_out_full, 0),
    )


def solution(mesh):
    placed = (
        P("dp", None),
        P("dp", None),
        P("dp", None),
        P(None, "mp"),
        P(None, "mp"),
        P(None, "mp"),
        P("mp", None),
        P(),
        P(),
        P(),
        P(),
        P("dp", "mp"),
    )
    return jax.shard_map(
        local,
        mesh=mesh,
        in_specs=placed,
        out_specs=(
            P("dp", "mp"),
            P("dp", "mp"),
            P("dp", "mp"),
            P("dp", "mp"),
            P("dp", "mp"),
            P("mp", "dp"),
            P(None, ("dp", "mp")),
            P(("dp", "mp")),
            P(("dp", "mp")),
            P(("dp", "mp")),
        ),
        check_vma=False,
    )
```

```python
import functools

import jax
import jax.numpy as jnp
from jax import lax
from jax.experimental import pallas as pl
from jax.experimental.pallas import tpu as pltpu
from jax.sharding import PartitionSpec as P

HD = 96
EPSILON = 1e-06
NEGATIVE = -1e30
BF16 = jnp.bfloat16
F32 = jnp.float32
VMEM_LIMIT = 63 << 20


def dot_general(left, right, left_dim, right_dim):
    return lax.dot_general(
        left, right, (((left_dim,), (right_dim,)), ((), ())), preferred_element_type=F32
    )


def norm_parts(values_in):
    inverse = lax.rsqrt(jnp.mean(values_in * values_in, axis=-1, keepdims=True) + EPSILON)
    return (values_in * inverse, inverse)


def swap_cores(array):
    return lax.ppermute(array, "mp", [(0, 1), (1, 0)])


def swap_bit(array, bit, dp_count):
    return lax.ppermute(array, "dp", [(i, i ^ (1 << bit)) for i in range(dp_count)])


def halve(array, axis, bit, dp_count):
    mine = (lax.axis_index("dp") >> bit) & 1
    going = lax.dynamic_index_in_dim(array, 1 - mine, axis, keepdims=False)
    kept = lax.dynamic_index_in_dim(array, mine, axis, keepdims=False)
    return kept.astype(F32) + swap_bit(going.astype(BF16), bit, dp_count).astype(F32)


def scatter_sum(array, bits, dp_count):
    rows, owners, columns = array.shape
    left = sorted(bits, reverse=True)
    array = array.reshape((rows,) + (2,) * len(left) + (columns,))
    for bit in bits:
        axis = left.index(bit)
        array = halve(array, 1 + axis, bit, dp_count)
        left.pop(axis)
    return array


def forward_kernel(
    counts_ref,
    x_ref,
    wk_ref,
    wv_ref,
    wq_ref,
    lat_ref,
    gain_ctx_ref,
    gain_lat_ref,
    attn_ref,
    k_ref,
    v_ref,
    inv_row_ref,
    q_ref,
    lk_ref,
    lv_ref,
    lat_proj_ref,
    p_ref,
    pl_ref,
    lat_normed_ref,
    query_acc,
    gained_ref,
):
    step = pl.program_id(0)
    steps = pl.num_programs(0)
    rows, width = x_ref.shape
    slab = wq_ref.shape[0]
    groups, patch_rows, _ = k_ref.shape
    latent_rows = lat_ref.shape[0]
    key_width = wk_ref.shape[0]
    query_width = wq_ref.shape[1]
    per_group = query_width // key_width

    @pl.when(step == 0)
    def _():
        lat = lat_ref[...].astype(F32)
        inverse = lax.rsqrt(jnp.mean(lat * lat, axis=-1, keepdims=True) + EPSILON)
        lat_normed_ref[...] = (lat * inverse * gain_lat_ref[...]).astype(BF16)
        for i, ref in enumerate((wk_ref, wv_ref)):
            projected = dot_general(lat_normed_ref[...], ref[...], 1, 1)
            at = query_width + i * key_width
            lat_proj_ref[:, at : at + key_width] = projected
            for g in range(groups):
                (lk_ref, lv_ref)[i][g] = projected[:, g * HD : (g + 1) * HD].astype(BF16)
            gained_ref[i * key_width : (i + 1) * key_width, :] = (
                ref[...].astype(F32) * gain_ctx_ref[...]
            ).astype(BF16)
        query_acc[...] = jnp.zeros_like(query_acc)

    squares = jnp.zeros((rows, 128), F32)
    for c in range(width // 128):
        part = x_ref[:, c * 128 : (c + 1) * 128].astype(F32)
        squares = squares + part * part
    inverse = lax.rsqrt(jnp.sum(squares, axis=-1, keepdims=True) / width + EPSILON)
    pair = (dot_general(x_ref[...], gained_ref[...], 1, 1) * inverse).astype(BF16)
    at = pl.ds(pl.multiple_of(step * rows, rows), rows)
    inv_row_ref[:, at] = jnp.transpose(jnp.broadcast_to(inverse, (rows, 128)))[:8]
    for g in range(groups):
        k_ref[g, at, :] = pair[:, g * HD : (g + 1) * HD]
        v_ref[g, at, :] = pair[:, key_width + g * HD : key_width + (g + 1) * HD]
    query_acc[...] += jnp.dot(
        lat_normed_ref[:, pl.ds(pl.multiple_of(step * slab, slab), slab)],
        wq_ref[...],
        preferred_element_type=F32,
    )

    @pl.when(step == steps - 1)
    def _():
        query = query_acc[...] * HD ** (-0.5)
        lat_proj_ref[:, :query_width] = query
        stacked = per_group * latent_rows
        first_count = counts_ref[0, 0]
        both_count = first_count + counts_ref[0, 1]
        position = lax.broadcasted_iota(jnp.int32, (1, patch_rows), 1)
        in_first = position < first_count
        in_second = jnp.logical_and(position >= first_count, position < both_count)
        rows_at = lax.broadcasted_iota(jnp.int32, (patch_rows, HD), 0)
        row_first = rows_at < first_count
        row_second = jnp.logical_and(rows_at >= first_count, rows_at < both_count)
        for g in range(groups):
            for h in range(per_group):
                head = g * per_group + h
                q_ref[g, h * latent_rows : (h + 1) * latent_rows, :] = query[
                    :, head * HD : (head + 1) * HD
                ].astype(BF16)
            q = q_ref[g]
            scores = dot_general(q, k_ref[g], 1, 1)
            lat_scores = dot_general(q, lk_ref[g], 1, 1)
            lat_max = jnp.max(lat_scores, axis=-1, keepdims=True)
            max_first = jnp.maximum(
                jnp.max(jnp.where(in_first, scores, NEGATIVE), axis=-1, keepdims=True), lat_max
            )
            max_second = jnp.maximum(
                jnp.max(jnp.where(in_second, scores, NEGATIVE), axis=-1, keepdims=True), lat_max
            )
            masked = jnp.where(
                in_first, scores - max_first, jnp.where(in_second, scores - max_second, NEGATIVE)
            )
            exponent = jnp.exp(masked)
            lat_first = jnp.exp(lat_scores - max_first)
            lat_second = jnp.exp(lat_scores - max_second)
            sum_first = jnp.sum(
                jnp.where(in_first, exponent, 0.0), axis=-1, keepdims=True
            ) + jnp.sum(lat_first, axis=-1, keepdims=True)
            sum_second = jnp.sum(
                jnp.where(in_second, exponent, 0.0), axis=-1, keepdims=True
            ) + jnp.sum(lat_second, axis=-1, keepdims=True)
            per_first = 1.0 / sum_first
            per_second = 1.0 / sum_second
            p = (exponent * jnp.where(in_first, per_first, per_second)).astype(BF16)
            p_ref[g] = p
            lat_p_first = (lat_first * per_first).astype(BF16)
            lat_p_second = (lat_second * per_second).astype(BF16)
            pl_ref[g, 0] = lat_p_first
            pl_ref[g, 1] = lat_p_second
            v = v_ref[g]
            zero = jnp.zeros_like(v)
            lv = lv_ref[g]
            for j, (row_mask, lat_p) in enumerate(
                ((row_first, lat_p_first), (row_second, lat_p_second))
            ):
                mixed = jnp.dot(
                    p, jnp.where(row_mask, v, zero), preferred_element_type=F32
                ) + jnp.dot(lat_p, lv, preferred_element_type=F32)
                mixed = mixed.astype(BF16)
                for h in range(per_group):
                    head = g * per_group + h
                    attn_ref[
                        j * latent_rows : (j + 1) * latent_rows, head * HD : (head + 1) * HD
                    ] = mixed[h * latent_rows : (h + 1) * latent_rows]


def whole(shape):
    return pl.BlockSpec(shape, lambda *_: (0,) * len(shape))


def held(shape):
    return pl.BlockSpec(shape, lambda *_: (0,) * len(shape), pipeline_mode=pl.Buffered(1))


def forward_call(context, counts, w_query, w_key, w_value, latents, gain_ctx, gain_lat):
    patch_rows, width = context.shape
    steps = 4
    rows = patch_rows // steps
    slab = width // steps
    key_width = w_key.shape[0]
    query_width = w_query.shape[1]
    groups = key_width // HD
    latent_rows = latents.shape[0]
    stacked = query_width // key_width * latent_rows
    out = [
        ((2 * latent_rows, query_width), BF16),
        ((groups, patch_rows, HD), BF16),
        ((groups, patch_rows, HD), BF16),
        ((8, patch_rows), F32),
        ((groups, stacked, HD), BF16),
        ((groups, latent_rows, HD), BF16),
        ((groups, latent_rows, HD), BF16),
        ((latent_rows, query_width + 2 * key_width), F32),
        ((groups, stacked, patch_rows), BF16),
        ((groups, 2, stacked, latent_rows), BF16),
    ]
    return pl.pallas_call(
        forward_kernel,
        name="forward_attention",
        grid=(steps,),
        in_specs=[
            pl.BlockSpec(memory_space=pltpu.SMEM),
            pl.BlockSpec((rows, width), lambda i: (i, 0)),
            held(w_key.shape),
            held(w_value.shape),
            pl.BlockSpec((slab, query_width), lambda i: (i, 0)),
            held(latents.shape),
            held((1, width)),
            held((1, width)),
        ],
        out_specs=[held(shape) for shape, _ in out],
        out_shape=[jax.ShapeDtypeStruct(shape, dtype) for shape, dtype in out],
        scratch_shapes=[
            pltpu.VMEM((latent_rows, width), BF16),
            pltpu.VMEM((latent_rows, query_width), F32),
            pltpu.VMEM((2 * key_width, width), BF16),
        ],
        cost_estimate=pl.CostEstimate(
            flops=5_000_000_000, bytes_accessed=24_000_000, transcendentals=600_000
        ),
        compiler_params=pltpu.CompilerParams(vmem_limit_bytes=VMEM_LIMIT),
    )(
        counts,
        context,
        w_key,
        w_value,
        w_query,
        latents,
        gain_ctx.reshape(1, width),
        gain_lat.reshape(1, width),
    )


def slots_of(routes_ref, slot_count, as_row):
    rows = routes_ref.shape[1]
    turned = jnp.broadcast_to(routes_ref[...].astype(F32), (rows, rows))
    shard = jnp.transpose(turned)
    down = lax.broadcasted_iota(jnp.int32, (rows, rows), 0)
    across = lax.broadcasted_iota(jnp.int32, (rows, rows), 1)
    same = shard == turned
    if as_row:
        rank = jnp.sum(jnp.where(same & (down < across), 1.0, 0.0), axis=0, keepdims=True)
        return (turned[:1] * slot_count + rank).astype(jnp.int32)
    rank = jnp.sum(jnp.where(same & (across < down), 1.0, 0.0), axis=1, keepdims=True)
    return (shard[:, :1] * slot_count + rank).astype(jnp.int32)


def branch_kernel(
    slot_count,
    mp_ref,
    own_ref,
    other_ref,
    w_own_ref,
    w_other_ref,
    lat_ref,
    gain_ref,
    routes_ref,
    hat_ref,
    inv_ref,
    out_ref,
    square_acc,
):
    step = pl.program_id(0)
    steps = pl.num_programs(0)
    columns = w_own_ref.shape[1]
    half = out_ref.shape[1]
    slots = out_ref.shape[0]
    rows = own_ref.shape[0]

    @pl.when(step == 0)
    def _():
        square_acc[...] = jnp.zeros_like(square_acc)

    lat = lat_ref[...].astype(F32)
    resid = (
        jnp.concatenate([lat, lat], axis=0)
        + jnp.dot(own_ref[...], w_own_ref[...], preferred_element_type=F32)
        + jnp.dot(other_ref[...], w_other_ref[...], preferred_element_type=F32)
    )
    hat_ref[:, pl.ds(pl.multiple_of(step * columns, columns), columns)] = resid
    square_acc[...] += jnp.sum(resid * resid, axis=-1, keepdims=True)

    @pl.when(step == steps - 1)
    def _():
        width = hat_ref.shape[1]
        inverse = lax.rsqrt(square_acc[...] / width + EPSILON)
        inv_ref[...] = inverse
        hat_ref[...] = hat_ref[...] * inverse
        place = slots_of(routes_ref, slot_count, True)
        table = jnp.where(
            lax.broadcasted_iota(jnp.int32, (slots, rows), 0) == place, 1.0, 0.0
        ).astype(BF16)
        at = pl.ds(pl.multiple_of(mp_ref[0] * half, half), half)
        final = (hat_ref[:, at] * gain_ref[:, at]).astype(BF16)
        out_ref[...] = jnp.dot(table, final, preferred_element_type=F32).astype(BF16)


def branch_call(mp_index, own, other, w_own, w_other, latents, gain_out, routes, slots, slot_count):
    width = w_own.shape[1]
    rows, heads = own.shape
    steps = 8
    columns = width // steps
    half = width // 2
    return pl.pallas_call(
        functools.partial(branch_kernel, slot_count),
        name="branch_norm",
        grid_spec=pltpu.PrefetchScalarGridSpec(
            num_scalar_prefetch=1,
            grid=(steps,),
            in_specs=[
                held((rows, heads)),
                held((rows, heads)),
                pl.BlockSpec((heads, columns), lambda i, *_: (0, i)),
                pl.BlockSpec((heads, columns), lambda i, *_: (0, i)),
                pl.BlockSpec((latents.shape[0], columns), lambda i, *_: (0, i)),
                held((1, width)),
                held((1, rows)),
            ],
            out_specs=[held((rows, width)), held((rows, 1)), held((slots, half))],
            scratch_shapes=[pltpu.VMEM((rows, 1), F32)],
        ),
        out_shape=[
            jax.ShapeDtypeStruct((rows, width), F32),
            jax.ShapeDtypeStruct((rows, 1), F32),
            jax.ShapeDtypeStruct((slots, half), BF16),
        ],
        cost_estimate=pl.CostEstimate(
            flops=2 * 2 * rows * heads * width, bytes_accessed=16_000_000, transcendentals=0
        ),
        compiler_params=pltpu.CompilerParams(vmem_limit_bytes=VMEM_LIMIT),
    )(mp_index, own, other, w_own, w_other, latents, gain_out.reshape(1, width), routes)


def attention_backward(
    counts_ref,
    d_attn,
    k_ref,
    v_ref,
    q_ref,
    lk_ref,
    lv_ref,
    p_ref,
    pl_ref,
    inv_row_ref,
    pair_ref,
    scaled_ref,
    lat_ref,
):
    groups, patch_rows, _ = k_ref.shape
    latent_rows = lk_ref.shape[1]
    stacked = q_ref.shape[1]
    per_group = stacked // latent_rows
    key_width = groups * HD
    query_width = groups * per_group * HD
    first_count = counts_ref[0, 0]
    both_count = first_count + counts_ref[0, 1]
    position = lax.broadcasted_iota(jnp.int32, (1, patch_rows), 1)
    in_first = position < first_count
    rows_at = lax.broadcasted_iota(jnp.int32, (patch_rows, HD), 0)
    row_first = rows_at < first_count
    row_second = jnp.logical_and(rows_at >= first_count, rows_at < both_count)
    scale_row = inv_row_ref[:1]
    row_dot = jnp.zeros((1, patch_rows), F32)
    for g in range(groups):
        d_first = jnp.concatenate(
            [
                d_attn[:latent_rows, head * HD : (head + 1) * HD]
                for head in range(g * per_group, (g + 1) * per_group)
            ],
            axis=0,
        )
        d_second = jnp.concatenate(
            [
                d_attn[latent_rows:, head * HD : (head + 1) * HD]
                for head in range(g * per_group, (g + 1) * per_group)
            ],
            axis=0,
        )
        q = q_ref[g]
        k = k_ref[g]
        v = v_ref[g]
        lk = lk_ref[g]
        lv = lv_ref[g]
        p_low = p_ref[g]
        p = p_low.astype(F32)
        zero = jnp.zeros_like(v)
        d_p = dot_general(d_first, jnp.where(row_first, v, zero), 1, 1) + dot_general(
            d_second, jnp.where(row_second, v, zero), 1, 1
        )
        product = p * d_p
        lat_first = pl_ref[g, 0]
        lat_second = pl_ref[g, 1]
        d_lat_first = dot_general(d_first, lv, 1, 1)
        d_lat_second = dot_general(d_second, lv, 1, 1)
        lat_product_first = lat_first.astype(F32) * d_lat_first
        lat_product_second = lat_second.astype(F32) * d_lat_second
        whole_sum = jnp.sum(product, axis=-1, keepdims=True)
        first_sum = jnp.sum(jnp.where(in_first, product, 0.0), axis=-1, keepdims=True)
        delta_first = first_sum + jnp.sum(lat_product_first, axis=-1, keepdims=True)
        delta_second = (whole_sum - first_sum) + jnp.sum(
            lat_product_second, axis=-1, keepdims=True
        )
        ds = product - p * jnp.where(in_first, delta_first, delta_second)
        ds_low = ds.astype(BF16)
        dsl = (
            lat_product_first
            - lat_first.astype(F32) * delta_first
            + lat_product_second
            - lat_second.astype(F32) * delta_second
        ).astype(BF16)
        scores = dot_general(q, k, 1, 1)
        row_dot = row_dot + jnp.sum(ds * scores + product, axis=0, keepdims=True)
        d_q = (
            jnp.dot(ds_low, k, preferred_element_type=F32)
            + jnp.dot(dsl, lk, preferred_element_type=F32)
        ).astype(BF16)
        for h in range(per_group):
            head = g * per_group + h
            lat_ref[:latent_rows, head * HD : (head + 1) * HD] = d_q[
                h * latent_rows : (h + 1) * latent_rows
            ]
        d_k = dot_general(q, ds_low, 0, 0)
        nothing = jnp.zeros_like(p_low)
        d_v = dot_general(d_first, jnp.where(in_first, p_low, nothing), 0, 0) + dot_general(
            d_second, jnp.where(in_first, nothing, p_low), 0, 0
        )
        k_at = slice(g * HD, (g + 1) * HD)
        v_at = slice(key_width + g * HD, key_width + (g + 1) * HD)
        pair_ref[k_at, :] = d_k.astype(BF16)
        pair_ref[v_at, :] = d_v.astype(BF16)
        scaled_ref[k_at, :] = (d_k * scale_row).astype(BF16)
        scaled_ref[v_at, :] = (d_v * scale_row).astype(BF16)
        d_lk = dot_general(dsl, q, 0, 0)
        d_lv = dot_general(lat_first, d_first, 0, 0) + dot_general(lat_second, d_second, 0, 0)
        lat_ref[:latent_rows, query_width + g * HD : query_width + (g + 1) * HD] = d_lk.astype(BF16)
        at = query_width + key_width + g * HD
        lat_ref[:latent_rows, at : at + HD] = d_lv.astype(BF16)
    high = row_dot.astype(BF16)
    low = (row_dot - high.astype(F32)).astype(BF16)
    rest = pair_ref.shape[0] - 2 * key_width - 2
    pair_ref[2 * key_width :, :] = jnp.concatenate(
        [high.astype(F32), low.astype(F32), jnp.zeros((rest, patch_rows), F32)], axis=0
    ).astype(BF16)


def backward_kernel(
    slot_count,
    where_ref,
    counts_ref,
    got_own_ref,
    got_other_ref,
    hat_ref,
    inv_out_ref,
    gain_ref,
    routes_ref,
    w_out_ref,
    k_ref,
    v_ref,
    q_ref,
    lk_ref,
    lv_ref,
    p_ref,
    pl_ref,
    inv_row_ref,
    x_ref,
    line_own_ref,
    line_low_ref,
    line_high_ref,
    line_both_ref,
    pair_ref,
    lat_ref,
    value_going_ref,
    value_kept_ref,
    key_going_ref,
    key_kept_ref,
    d_final_ref,
    branch_ref,
    attn_acc,
    scaled_ref,
):
    step = pl.program_id(0)
    steps = pl.num_programs(0) // 2
    rows, width = hat_ref.shape
    half = width // 2
    columns = w_out_ref.shape[1]
    slots = got_own_ref.shape[0]
    latent_rows = lk_ref.shape[1]
    key_width = value_going_ref.shape[1]

    @pl.when(step == 0)
    def _():
        place = slots_of(routes_ref, slot_count, False)
        table = jnp.where(
            lax.broadcasted_iota(jnp.int32, (rows, slots), 1) == place, 1.0, 0.0
        ).astype(BF16)
        total = jnp.zeros((rows, 1), F32)
        chunk = 512
        for got_ref, which in ((got_own_ref, where_ref[1]), (got_other_ref, 1 - where_ref[1])):
            for c in range(half // chunk):
                at = pl.ds(pl.multiple_of(which * half + c * chunk, chunk), chunk)
                d_final = jnp.dot(
                    table, got_ref[:, c * chunk : (c + 1) * chunk], preferred_element_type=F32
                )
                product = d_final * hat_ref[:, at]
                total = total + jnp.sum(product * gain_ref[:, at], axis=-1, keepdims=True)
                d_final_ref[:, at] = d_final
        total = total / width
        lat_ref[latent_rows:, :] = jnp.zeros_like(lat_ref[latent_rows:, :])
        highs, lows = [], []
        part = width // 4
        for c in range(width // chunk):
            at = slice(c * chunk, (c + 1) * chunk)
            d_final = d_final_ref[:, at]
            hat = hat_ref[:, at]
            term = jnp.sum(d_final * hat, axis=0, keepdims=True)
            high = term.astype(BF16).astype(F32)
            highs.append(high)
            lows.append(term - high)
            branch_ref[:, at] = (
                inv_out_ref[...] * (d_final * gain_ref[:, at] - hat * total)
            ).astype(BF16)
        per_row = part // chunk
        lines = [
            jnp.concatenate(group[i * per_row : (i + 1) * per_row], axis=1)
            for group in (highs, lows)
            for i in range(4)
        ]
        lat_ref[latent_rows : latent_rows + 16, :part] = jnp.concatenate(
            lines + [jnp.zeros((8, part), F32)], axis=0
        ).astype(BF16)
        attn_acc[...] = jnp.zeros_like(attn_acc)
        z = where_ref[0] >> 2
        some = pl.ds(pl.multiple_of(where_ref[1] * (rows // 2), rows // 2), rows // 2)
        line_own_ref[...] = branch_ref[:, pl.ds(pl.multiple_of(z * part, part), part)]
        for turn, ref in ((1, line_low_ref), (2, line_high_ref), (3, line_both_ref)):
            ref[...] = branch_ref[some, pl.ds(pl.multiple_of((z ^ turn) * part, part), part)]

    @pl.when(step < steps)
    def _():
        at = pl.ds(pl.multiple_of(step * columns, columns), columns)
        attn_acc[...] += dot_general(branch_ref[:, at], w_out_ref[...], 1, 1)

    @pl.when(step == steps - 1)
    def _():
        attention_backward(
            counts_ref,
            attn_acc[...].astype(BF16),
            k_ref,
            v_ref,
            q_ref,
            lk_ref,
            lv_ref,
            p_ref,
            pl_ref,
            inv_row_ref,
            pair_ref,
            scaled_ref,
            lat_ref,
        )

    @pl.when(step >= steps)
    def _():
        own = x_ref.shape[1] // 2
        odd = where_ref[0] & 1
        far = x_ref[:, pl.ds(pl.multiple_of((1 - odd) * own, own), own)]
        near = x_ref[:, pl.ds(pl.multiple_of(odd * own, own), own)]
        far_grad = jnp.dot(scaled_ref[...], far, preferred_element_type=F32).astype(BF16)
        near_grad = jnp.dot(scaled_ref[...], near, preferred_element_type=F32).astype(BF16)
        value_going_ref[0] = far_grad[key_width:]
        value_kept_ref[0] = near_grad[key_width:]

        @pl.when(step < steps + steps // 2)
        def _():
            key_going_ref[0, 0] = far_grad[:key_width]
            key_going_ref[1, 0] = near_grad[:key_width]

        @pl.when(step >= steps + steps // 2)
        def _():
            key_kept_ref[0, 0] = far_grad[:key_width]
            key_kept_ref[1, 0] = near_grad[:key_width]


def backward_call(
    where, counts, got_own, got_other, hat, inv_out, gain_out, routes, w_out, kept, context, slot_count
):
    k, v, q, lk, lv, p, lat_p, inv_row = kept
    rows, width = hat.shape
    patch_rows = context.shape[0]
    heads = w_out.shape[0]
    groups = k.shape[0]
    key_width = groups * HD
    latent_rows = lk.shape[1]
    steps = 8
    columns = width // steps
    own = width // 16

    def x_block(i, where_ref):
        j = jnp.maximum(i - steps, 0)
        me = where_ref[0]
        y = ((me >> 1) & 1) ^ (1 - (j >> 2))
        low = 1 - ((j >> 1) & 1)
        high = 1 - (j & 1)
        z = (me >> 2) ^ (low + 2 * high)
        return (0, 2 * z + y)

    def turn(i):
        return jnp.maximum(i - steps, 0)

    lat_width = heads + 2 * key_width
    return pl.pallas_call(
        functools.partial(backward_kernel, slot_count),
        name="attention_backward",
        grid_spec=pltpu.PrefetchScalarGridSpec(
            num_scalar_prefetch=1,
            grid=(2 * steps,),
            in_specs=[
                pl.BlockSpec(memory_space=pltpu.SMEM),
                held(got_own.shape),
                held(got_other.shape),
                held(hat.shape),
                held(inv_out.shape),
                held((1, width)),
                held(routes.shape),
                pl.BlockSpec((heads, columns), lambda i, *_: (0, jnp.minimum(i, steps - 1))),
                held(k.shape),
                held(v.shape),
                held(q.shape),
                held(lk.shape),
                held(lv.shape),
                held(p.shape),
                held(lat_p.shape),
                held(inv_row.shape),
                pl.BlockSpec((patch_rows, 2 * own), x_block),
            ],
            out_specs=[
                held((rows, width // 4)),
                held((rows // 2, width // 4)),
                held((rows // 2, width // 4)),
                held((rows // 2, width // 4)),
                held((2 * key_width + 16, patch_rows)),
                held((latent_rows + 16, lat_width)),
                pl.BlockSpec((1, key_width, own), lambda i, *_: (turn(i), 0, 0)),
                pl.BlockSpec((1, key_width, own), lambda i, *_: (turn(i), 0, 0)),
                pl.BlockSpec(
                    (2, 1, key_width, own), lambda i, *_: (0, jnp.minimum(turn(i), 3), 0, 0)
                ),
                pl.BlockSpec(
                    (2, 1, key_width, own), lambda i, *_: (0, jnp.maximum(turn(i) - 4, 0), 0, 0)
                ),
            ],
            scratch_shapes=[
                pltpu.VMEM((rows, width), F32),
                pltpu.VMEM((rows, width), BF16),
                pltpu.VMEM((rows, heads), F32),
                pltpu.VMEM((2 * key_width, patch_rows), BF16),
            ],
        ),
        out_shape=[
            jax.ShapeDtypeStruct((rows, width // 4), BF16),
            jax.ShapeDtypeStruct((rows // 2, width // 4), BF16),
            jax.ShapeDtypeStruct((rows // 2, width // 4), BF16),
            jax.ShapeDtypeStruct((rows // 2, width // 4), BF16),
            jax.ShapeDtypeStruct((2 * key_width + 16, patch_rows), BF16),
            jax.ShapeDtypeStruct((latent_rows + 16, lat_width), BF16),
            jax.ShapeDtypeStruct((8, key_width, own), BF16),
            jax.ShapeDtypeStruct((8, key_width, own), BF16),
            jax.ShapeDtypeStruct((2, 4, key_width, own), BF16),
            jax.ShapeDtypeStruct((2, 4, key_width, own), BF16),
        ],
        cost_estimate=pl.CostEstimate(
            flops=5_000_000_000, bytes_accessed=26_000_000, transcendentals=0
        ),
        compiler_params=pltpu.CompilerParams(vmem_limit_bytes=VMEM_LIMIT),
    )(
        where,
        counts,
        got_own,
        got_other,
        hat,
        inv_out,
        gain_out.reshape(1, width),
        routes,
        w_out,
        k,
        v,
        q,
        lk,
        lv,
        p,
        lat_p,
        inv_row,
        context,
    )


def patch_kernel(
    width,
    mp_ref,
    own_ref,
    other_ref,
    wk_ref,
    wv_ref,
    wk_other_ref,
    wv_other_ref,
    x_ref,
    inv_row_ref,
    gain_ref,
    out_ref,
    turned_ref,
    inv_ref,
    dot_ref,
    w_ref,
):
    step = pl.program_id(0)
    key_width = wk_ref.shape[0]
    patch_rows = turned_ref.shape[0]
    pair = 2 * key_width

    @pl.when(step == 0)
    def _():
        row_dot = jnp.zeros((patch_rows, 1), F32)
        for i, ref in enumerate((own_ref, other_ref)):
            turned = jnp.transpose(ref[...])
            turned_ref[:, i * pair : (i + 1) * pair] = turned[:, :pair]
            row_dot = row_dot + turned[:, pair : pair + 1].astype(F32)
            row_dot = row_dot + turned[:, pair + 1 : pair + 2].astype(F32)
        inverse = jnp.transpose(jnp.broadcast_to(inv_row_ref[:1], (128, patch_rows)))[:, :1]
        inv_ref[...] = inverse
        dot_ref[...] = row_dot * (inverse * inverse / width)
        for i, ref in enumerate((wk_ref, wv_ref, wk_other_ref, wv_other_ref)):
            w_ref[i * key_width : (i + 1) * key_width, :] = ref[...]

    rows = x_ref.shape[0]
    at = pl.ds(pl.multiple_of(step * rows, rows), rows)
    d_in = jnp.dot(turned_ref[at, :], w_ref[...], preferred_element_type=F32)
    out_ref[...] = (
        d_in * gain_ref[...] * inv_ref[at, :] - x_ref[...].astype(F32) * dot_ref[at, :]
    ).astype(BF16)


def patch_call(mp_index, own, other, wk, wv, wk_other, wv_other, context, inv_row, gain_ctx):
    patch_rows, width = context.shape
    half = width // 2
    steps = 4
    rows = patch_rows // steps
    key_width = wk.shape[0]
    once = pl.Buffered(1)
    w_spec = pl.BlockSpec((key_width, half), lambda i, mp: (0, mp[0]), pipeline_mode=once)
    return pl.pallas_call(
        functools.partial(patch_kernel, width),
        name="patch_gradient",
        grid_spec=pltpu.PrefetchScalarGridSpec(
            num_scalar_prefetch=1,
            grid=(steps,),
            in_specs=[
                held(own.shape),
                held(other.shape),
                w_spec,
                w_spec,
                w_spec,
                w_spec,
                pl.BlockSpec((rows, half), lambda i, mp: (i, mp[0])),
                held(inv_row.shape),
                pl.BlockSpec((1, half), lambda i, mp: (0, mp[0])),
            ],
            out_specs=pl.BlockSpec((rows, half), lambda i, mp: (i, 0)),
            scratch_shapes=[
                pltpu.VMEM((patch_rows, 4 * key_width), BF16),
                pltpu.VMEM((patch_rows, 1), F32),
                pltpu.VMEM((patch_rows, 1), F32),
                pltpu.VMEM((4 * key_width, half), BF16),
            ],
        ),
        out_shape=jax.ShapeDtypeStruct((patch_rows, half), BF16),
        cost_estimate=pl.CostEstimate(
            flops=3_300_000_000, bytes_accessed=14_000_000, transcendentals=0
        ),
        compiler_params=pltpu.CompilerParams(vmem_limit_bytes=VMEM_LIMIT),
    )(mp_index, own, other, wk, wv, wk_other, wv_other, context, inv_row, gain_ctx.reshape(1, width))


def out_kernel(
    where_ref,
    a0_ref,
    a1_ref,
    a2_ref,
    a3_ref,
    d0_ref,
    d1_ref,
    d2_ref,
    d3_ref,
    e1_ref,
    e2_ref,
    e3_ref,
    first_going_ref,
    first_kept_ref,
    second_going_ref,
    second_kept_ref,
    attn_ref,
    line_ref,
    resid_ref,
):
    rows, heads = a0_ref.shape
    columns = line_ref.shape[1]
    own = columns // 4
    latent_rows = rows // 2
    mine = where_ref[1]
    for i, ref in enumerate((a0_ref, a1_ref, a2_ref, a3_ref)):
        attn_ref[i * rows : (i + 1) * rows, :] = ref[...]
    line_ref[:rows, :] = d0_ref[...]
    half = rows // 2
    for i, (ref, other) in enumerate(((d1_ref, e1_ref), (d2_ref, e2_ref), (d3_ref, e3_ref))):
        at = (i + 1) * rows
        line_ref[pl.ds(pl.multiple_of(at + mine * half, half), half), :] = ref[...]
        line_ref[pl.ds(pl.multiple_of(at + (1 - mine) * half, half), half), :] = other[...]
    resid = jnp.zeros((latent_rows, columns), F32)
    for i in range(8):
        resid = resid + line_ref[i * latent_rows : (i + 1) * latent_rows, :].astype(F32)
    resid_ref[...] = resid
    odd = where_ref[0] & 1
    upper = (where_ref[0] >> 1) & 1
    cut = heads // 2
    share = own // 2
    for turn in range(4):
        x_differs, y_differs = 1 - (turn & 1), 1 - (turn >> 1)
        owner = 2 * (upper ^ y_differs) + (odd ^ x_differs)
        at = pl.ds(pl.multiple_of(owner * own, own), own)
        grad = dot_general(attn_ref[...], line_ref[:, at], 0, 0).astype(BF16)
        mine_at = pl.ds(pl.multiple_of(owner * own + mine * share, share), share)
        part = resid_ref[:, mine_at]
        part = jnp.concatenate([part[: latent_rows // 2], part[latent_rows // 2 :]], axis=1)
        ref = first_going_ref if x_differs else first_kept_ref
        ref[1 - y_differs, :cut, :] = grad[:cut]
        ref[1 - y_differs, cut:, :] = part.astype(BF16)
        ref = second_going_ref if y_differs else second_kept_ref
        ref[1 - x_differs] = grad[cut:]


def out_call(where, attn, line, line_other):
    rows, heads = attn[0].shape
    columns = line[0].shape[1]
    own = columns // 4
    first = (2, heads // 2 + rows // 4, own)
    second = (2, heads // 2, own)
    shapes = [first, first, second, second]
    return pl.pallas_call(
        out_kernel,
        name="output_projection_gradient",
        grid_spec=pltpu.PrefetchScalarGridSpec(
            num_scalar_prefetch=1,
            grid=(1,),
            in_specs=[held(a.shape) for a in (*attn, *line, *line_other)],
            out_specs=[held(shape) for shape in shapes],
            scratch_shapes=[
                pltpu.VMEM((4 * rows, heads), BF16),
                pltpu.VMEM((4 * rows, columns), BF16),
                pltpu.VMEM((rows // 2, columns), F32),
            ],
        ),
        out_shape=[jax.ShapeDtypeStruct(shape, BF16) for shape in shapes],
        cost_estimate=pl.CostEstimate(
            flops=8 * rows * heads * columns, bytes_accessed=4_000_000, transcendentals=0
        ),
        compiler_params=pltpu.CompilerParams(vmem_limit_bytes=VMEM_LIMIT),
    )(where, *attn, *line, *line_other)


def latent_kernel(
    where_ref,
    sum_ref,
    got_ref,
    proj_ref,
    lat_ref,
    gain_ref,
    wq_ref,
    wk_ref,
    wv_ref,
    query_ref,
    pair_ref,
    message_ref,
    gain_out_ref,
    total_ref,
):
    latent_rows, width = lat_ref.shape
    own, query_width = wq_ref.shape
    key_width = wk_ref.shape[0]
    scaling = HD ** (-0.5)
    total_ref[...] = sum_ref[...] + got_ref[...].astype(F32)
    total = total_ref[:latent_rows, :]
    low = total.astype(BF16)
    at = pl.ds(pl.multiple_of(where_ref[0] * own, own), own)
    lat = lat_ref[...].astype(F32)
    inverse = lax.rsqrt(jnp.mean(lat * lat, axis=-1, keepdims=True) + EPSILON)
    gain = gain_ref[:, at]
    normed = (lat_ref[:, at].astype(F32) * inverse * gain).astype(BF16)
    query = dot_general(normed, low[:, :query_width], 0, 0) * scaling
    query_ref[...] = query
    pair = dot_general(low[:, query_width:], normed, 0, 0)
    pair_ref[...] = pair
    wq = wq_ref[...]
    wk = wk_ref[...]
    wv = wv_ref[...]
    gain_term = jnp.transpose(
        jnp.broadcast_to(jnp.sum(wq.astype(F32) * query, axis=1, keepdims=True), (own, 128))
    )[:1]
    gain_term = gain_term + jnp.sum(wk.astype(F32) * pair[:key_width], axis=0, keepdims=True)
    gain_term = gain_term + jnp.sum(wv.astype(F32) * pair[key_width:], axis=0, keepdims=True)
    scaled = (total[:, :query_width] * scaling).astype(BF16)
    d_lat = dot_general(scaled, wq, 1, 1)
    d_lat = d_lat + jnp.dot(
        low[:, query_width : query_width + key_width], wk, preferred_element_type=F32
    )
    d_lat = d_lat + jnp.dot(low[:, query_width + key_width :], wv, preferred_element_type=F32)
    message_ref[:latent_rows, :own] = d_lat
    message_ref[:latent_rows, own:] = jnp.broadcast_to(
        jnp.sum(total * proj_ref[...], axis=-1, keepdims=True), (latent_rows, 128)
    )
    message_ref[latent_rows:, :own] = jnp.broadcast_to(gain_term / gain, (8, own))
    message_ref[latent_rows:, own:] = jnp.zeros((8, 128), F32)
    part = width // 4
    share = own // 2
    first = where_ref[0] * own + where_ref[1] * share
    line = first // part
    mine = pl.ds(pl.multiple_of(first % part, share), share)
    gain_out_ref[...] = jnp.sum(
        jnp.where(
            lax.broadcasted_iota(jnp.int32, (8, share), 0) % 4 == line,
            total_ref[latent_rows : latent_rows + 8, mine],
            0.0,
        ),
        axis=0,
        keepdims=True,
    )


def latent_call(where, sums, got, proj, latents, gain_lat, w_query, wk, wv, own):
    latent_rows, width = latents.shape
    query_width = w_query.shape[1]
    key_width = wk.shape[0]
    return pl.pallas_call(
        latent_kernel,
        name="latent_gradients",
        grid_spec=pltpu.PrefetchScalarGridSpec(
            num_scalar_prefetch=1,
            grid=(1,),
            in_specs=[
                held(sums.shape),
                held(got.shape),
                held(proj.shape),
                held(latents.shape),
                held((1, width)),
                pl.BlockSpec((own, query_width), lambda i, w: (w[0], 0)),
                pl.BlockSpec((key_width, own), lambda i, w: (0, w[0])),
                pl.BlockSpec((key_width, own), lambda i, w: (0, w[0])),
            ],
            out_specs=[
                held((own, query_width)),
                held((2 * key_width, own)),
                held((latent_rows + 8, own + 128)),
                held((1, own // 2)),
            ],
            scratch_shapes=[pltpu.VMEM(sums.shape, F32)],
        ),
        out_shape=[
            jax.ShapeDtypeStruct((own, query_width), F32),
            jax.ShapeDtypeStruct((2 * key_width, own), F32),
            jax.ShapeDtypeStruct((latent_rows + 8, own + 128), F32),
            jax.ShapeDtypeStruct((1, own // 2), F32),
        ],
        cost_estimate=pl.CostEstimate(
            flops=100_000_000, bytes_accessed=3_000_000, transcendentals=0
        ),
        compiler_params=pltpu.CompilerParams(vmem_limit_bytes=VMEM_LIMIT),
    )(where, sums, got, proj, latents, gain_lat.reshape(1, width), w_query, wk, wv)


def plane_kernel(
    value_ref,
    value_got_ref,
    key_ref,
    key_got_ref,
    both_ref,
    low_ref,
    high_ref,
    kept_ref,
):
    key_width = value_ref.shape[1]
    for i, ref in enumerate((both_ref, low_ref, high_ref, kept_ref)):
        ref[:key_width, :] = (key_ref[i] + key_got_ref[i].astype(F32)).astype(ref.dtype)
        ref[key_width:, :] = (value_ref[i] + value_got_ref[i].astype(F32)).astype(ref.dtype)


def plane_call(value, value_got, key, key_got):
    _, key_width, own = value.shape
    shape = (2 * key_width, own)
    return pl.pallas_call(
        plane_kernel,
        name="plane_sum",
        out_shape=[jax.ShapeDtypeStruct(shape, BF16)] * 3 + [jax.ShapeDtypeStruct(shape, F32)],
        cost_estimate=pl.CostEstimate(flops=1_000_000, bytes_accessed=5_000_000, transcendentals=0),
        compiler_params=pltpu.CompilerParams(vmem_limit_bytes=VMEM_LIMIT),
    )(value, value_got, key, key_got)


def halve_kernel(kept_ref, got_ref, going_ref, rest_ref):
    half = going_ref.shape[0]
    going_ref[...] = (kept_ref[:half].astype(F32) + got_ref[:half].astype(F32)).astype(BF16)
    rest_ref[...] = kept_ref[half:].astype(F32) + got_ref[half:].astype(F32)


def halve_call(kept, got):
    shape = (kept.shape[0] // 2,) + kept.shape[1:]
    return pl.pallas_call(
        halve_kernel,
        name="halve_sum",
        out_shape=[jax.ShapeDtypeStruct(shape, BF16), jax.ShapeDtypeStruct(shape, F32)],
        cost_estimate=pl.CostEstimate(flops=1_000_000, bytes_accessed=4_000_000, transcendentals=0),
        compiler_params=pltpu.CompilerParams(vmem_limit_bytes=VMEM_LIMIT),
    )(kept, got)


def final_kernel(
    where_ref,
    kept_ref,
    both_ref,
    low_ref,
    high_ref,
    gain_ref,
    pair_ref,
    wk_ref,
    wv_ref,
    key_grad_ref,
    value_grad_ref,
    gain_term_ref,
):
    key_width = wk_ref.shape[0]
    total = (
        kept_ref[...]
        + both_ref[...].astype(F32)
        + low_ref[...].astype(F32)
        + high_ref[...].astype(F32)
    )
    term = jnp.sum(wk_ref[...].astype(F32) * total[:key_width], axis=0, keepdims=True)
    term = term + jnp.sum(wv_ref[...].astype(F32) * total[key_width:], axis=0, keepdims=True)
    gain_term_ref[...] = jnp.broadcast_to(term, gain_term_ref.shape)
    total = total * gain_ref[...] + pair_ref[...]
    key_grad_ref[...] = total[:key_width]
    value_grad_ref[...] = total[key_width:]


def final_call(where, kept, both, low, high, gain_ctx, pair, wk, wv):
    rows, own = kept.shape
    width = gain_ctx.shape[0]
    key_width = rows // 2
    w_spec = pl.BlockSpec((key_width, own), lambda i, w: (0, w[0]))
    return pl.pallas_call(
        final_kernel,
        name="key_value_gradients",
        grid_spec=pltpu.PrefetchScalarGridSpec(
            num_scalar_prefetch=1,
            grid=(1,),
            in_specs=[held(kept.shape)] * 4
            + [pl.BlockSpec((1, own), lambda i, w: (0, w[0])), held(pair.shape), w_spec, w_spec],
            out_specs=[held((key_width, own)), held((key_width, own)), held((8, own))],
        ),
        out_shape=[
            jax.ShapeDtypeStruct((key_width, own), F32),
            jax.ShapeDtypeStruct((key_width, own), F32),
            jax.ShapeDtypeStruct((8, own), F32),
        ],
        cost_estimate=pl.CostEstimate(flops=1_000_000, bytes_accessed=3_000_000, transcendentals=0),
        compiler_params=pltpu.CompilerParams(vmem_limit_bytes=VMEM_LIMIT),
    )(where, kept, both, low, high, gain_ctx.reshape(1, width), pair, wk, wv)


def local(
    context,
    counts,
    routes,
    w_query,
    w_key,
    w_value,
    w_out,
    latents,
    gain_ctx,
    gain_lat,
    gain_out,
    cotangent,
):
    dp_count = lax.axis_size("dp")
    mp_index = lax.axis_index("mp")
    dp_index = lax.axis_index("dp")
    patch_rows, width = context.shape
    half_width = width // 2
    own_width = width // dp_count
    latent_rows = latents.shape[0]
    slot_count = cotangent.shape[0] // dp_count
    slots = dp_count * slot_count
    query_width = w_query.shape[1]

    def swap(array, turn):
        return lax.ppermute(array, "dp", [(i, i ^ turn) for i in range(dp_count)])

    def exchange(array):
        blocks = array.reshape(dp_count, slot_count, half_width)
        return lax.all_to_all(blocks, "dp", split_axis=0, concat_axis=0, tiled=True).reshape(
            slots, half_width
        )

    wk = w_key.T
    wv = w_value.T
    turned_routes = routes.reshape(1, -1)
    mp_scalar = mp_index.reshape(1)
    where = jnp.stack([dp_index, mp_index])

    returned = exchange(cotangent)
    w_out_other = swap_cores(w_out)
    wk_other = swap_cores(wk)
    wv_other = swap_cores(wv)

    (attn_rows, k, v, inv_row, q, lat_k, lat_v, lat_proj, p, lat_p) = forward_call(
        context, counts, w_query, wk, wv, latents, gain_ctx, gain_lat
    )
    attn_other = swap_cores(attn_rows)
    attn_high = swap(attn_rows, 8)
    attn_low = swap(attn_rows, 4)
    attn_both = swap(attn_high, 4)
    out_hat, out_inv, outgoing = branch_call(
        mp_scalar,
        attn_rows,
        attn_other,
        w_out,
        w_out_other,
        latents,
        gain_out,
        turned_routes,
        slots,
        slot_count,
    )
    routed = exchange(outgoing)

    returned, out_inv = lax.optimization_barrier((returned, out_inv))
    returned_other = swap_cores(returned)
    (
        line_own,
        line_low,
        line_high,
        line_both,
        pair,
        lat_terms,
        value_going,
        value_kept,
        key_going,
        key_kept,
    ) = backward_call(
        where,
        counts,
        returned,
        returned_other,
        out_hat,
        out_inv,
        gain_out,
        turned_routes,
        w_out,
        (k, v, q, lat_k, lat_v, p, lat_p, inv_row),
        context,
        slot_count,
    )

    value_got = swap(value_going, 1)
    key_got = swap(key_going, 2)

    pair_other = swap_cores(pair)
    ctx_grad = patch_call(
        mp_scalar, pair, pair_other, wk, wv, wk_other, wv_other, context, inv_row, gain_ctx
    )

    got_low = swap(line_low, 4)
    got_high = swap(line_high, 8)
    got_both = swap(line_both, 12)

    lat_sum = lat_terms.astype(F32)
    for turn in (4, 8, 1):
        lat_sum = lat_sum + swap(lat_sum.astype(BF16), turn).astype(F32)
    lat_got = swap(lat_sum.astype(BF16), 2)

    value_going, value_kept = halve_call(value_kept, value_got)
    value_got = swap(value_going, 2)
    key_going, key_kept = halve_call(
        key_kept.reshape((8,) + key_kept.shape[2:]), key_got.reshape((8,) + key_got.shape[2:])
    )
    key_got = swap(key_going, 1)

    first_going, first_kept, second_going, second_kept = out_call(
        where,
        (attn_rows, attn_low, attn_high, attn_both),
        (line_own, got_low, got_high, got_both),
        (swap_cores(got_low), swap_cores(got_high), swap_cores(got_both)),
    )

    both, low, high, kept = plane_call(value_kept, value_got, key_kept, key_got)
    both = swap(both, 12)
    low = swap(low, 4)
    high = swap(high, 8)

    first_going, first_kept = halve_call(first_kept, swap(first_going, 1))
    second_going, second_kept = halve_call(second_kept, swap(second_going, 2))
    first = first_kept[0] + swap(first_going[0], 2).astype(F32)
    second = second_kept[0] + swap(second_going[0], 1).astype(F32)
    cut = query_width // 2
    grad_w_out = jnp.concatenate([first[:cut], second], axis=0)
    share = own_width // 2
    resid_sum = jnp.concatenate([first[cut:, :share], first[cut:, share:]], axis=0)

    grad_w_query, pair_lat, message, grad_gain_out = latent_call(
        where, lat_sum, lat_got, lat_proj, latents, gain_lat, w_query, wk, wv, own_width
    )
    message = message + swap_cores(message)

    grad_key, grad_value, gain_term = final_call(
        where, kept, both, low, high, gain_ctx, pair_lat, wk, wv
    )
    gain_term = gain_term + swap_cores(gain_term)

    def mine_of(array, axis):
        return lax.dynamic_slice_in_dim(
            array, dp_index * own_width + mp_index * share, share, axis
        )

    lat_hat, lat_inv = norm_parts(latents.astype(F32))
    mine = lax.dynamic_slice_in_dim(message, mp_index * share, share, 1)
    lat_dot = message[:latent_rows, own_width : own_width + 1] / width
    grad_latents = resid_sum + lat_inv * (
        mine_of(gain_lat, 0) * mine[:latent_rows] - mine_of(lat_hat, 1) * lat_dot
    )
    return (
        routed,
        ctx_grad,
        grad_w_query,
        grad_key.T,
        grad_value.T,
        grad_w_out,
        grad_latents,
        lax.dynamic_slice_in_dim(gain_term, mp_index * share, share, 1)[0],
        mine[latent_rows],
        grad_gain_out[0],
    )


def local_general(
    context,
    counts,
    routes,
    w_query,
    w_key,
    w_value,
    w_out,
    latents,
    gain_ctx,
    gain_lat,
    gain_out,
    cotangent,
):
    dp_count = lax.axis_size("dp")
    mp_count = lax.axis_size("mp")
    mp_index = lax.axis_index("mp")
    dp_index = lax.axis_index("dp")
    bits = dp_count.bit_length() - 1
    gather_bits = [bits - 1, bits - 2]
    scatter_bits = list(range(bits - 2))
    order_one = list(range(bits))
    order_two = [1, 0] + order_one[2:]
    patch_rows, width = context.shape
    half_width = width // mp_count
    own_width = width // dp_count
    head_local = w_query.shape[1] // HD
    group_local = w_key.shape[1] // HD
    per_group = head_local // group_local
    latent_rows = latents.shape[0]
    image_slots = counts.shape[1]
    out_rows = image_slots * latent_rows
    slot_count = cotangent.shape[0] // dp_count
    key_width = w_key.shape[1]
    query_width = w_query.shape[1]
    scaling = HD ** (-0.5)

    returned = lax.all_to_all(
        cotangent.reshape(dp_count, slot_count, half_width),
        "dp",
        split_axis=0,
        concat_axis=0,
        tiled=True,
    ).reshape(dp_count * slot_count, half_width)
    returned_other = swap_cores(returned)
    w_out_other = swap_cores(w_out)
    w_pair = jnp.concatenate([w_key, w_value], axis=1)
    w_pair_half = lax.dynamic_slice_in_dim(w_pair, mp_index * half_width, half_width, 0)
    w_pair_other = swap_cores(
        lax.dynamic_slice_in_dim(w_pair, (1 - mp_index) * half_width, half_width, 0)
    )

    patch_hat, patch_inv = norm_parts(context.astype(F32))
    normed_ctx = (patch_hat * gain_ctx).astype(BF16)
    key_f32 = jnp.dot(normed_ctx, w_key, preferred_element_type=F32)
    value_f32 = jnp.dot(normed_ctx, w_value, preferred_element_type=F32)
    key_rows = key_f32.astype(BF16)
    value_rows = value_f32.astype(BF16)
    lat_float = latents.astype(F32)
    lat_hat, lat_inv = norm_parts(lat_float)
    normed_lat = (lat_hat * gain_lat).astype(BF16)
    lat_key_f32 = jnp.dot(normed_lat, w_key, preferred_element_type=F32)
    lat_value_f32 = jnp.dot(normed_lat, w_value, preferred_element_type=F32)
    lat_keys = lat_key_f32.astype(BF16)
    lat_values = lat_value_f32.astype(BF16)
    query_f32 = jnp.dot(normed_lat, w_query, preferred_element_type=F32) * scaling
    query_rows = query_f32.astype(BF16)
    query_heads = query_rows.reshape(latent_rows, group_local, per_group, HD)
    key_heads = key_rows.reshape(patch_rows, group_local, HD)
    value_heads = value_rows.reshape(patch_rows, group_local, HD)
    lat_key_heads = lat_keys.reshape(latent_rows, group_local, HD)
    lat_value_heads = lat_values.reshape(latent_rows, group_local, HD)
    scores = jnp.einsum(
        "rkgd,tkd->kgrt", query_heads, key_heads, preferred_element_type=jnp.float32
    )
    lat_scores = jnp.einsum(
        "rkgd,skd->kgrs", query_heads, lat_key_heads, preferred_element_type=jnp.float32
    )
    position = jnp.arange(patch_rows, dtype=jnp.int32)
    image_count = counts[0]
    image_start = jnp.cumsum(image_count) - image_count
    member = (position[None, :] >= image_start[:, None]) & (
        position[None, :] < (image_start + image_count)[:, None]
    )
    member_wide = member[:, None, None, None, :]
    masked = jnp.where(member_wide, scores[None], NEGATIVE)
    row_max = jnp.maximum(
        jnp.max(masked, axis=-1, keepdims=True), jnp.max(lat_scores, axis=-1, keepdims=True)[None]
    )
    exponent = jnp.where(member_wide, jnp.exp(masked - row_max), 0.0)
    lat_exponent = jnp.exp(lat_scores[None] - row_max)
    total = jnp.sum(exponent, axis=-1, keepdims=True) + jnp.sum(
        lat_exponent, axis=-1, keepdims=True
    )
    attention = exponent / total
    lat_attention = lat_exponent / total
    attention_low = attention.astype(BF16)
    lat_attention_low = lat_attention.astype(BF16)
    mixed = jnp.einsum(
        "ikgrt,tkd->irkgd", attention_low, value_heads, preferred_element_type=jnp.float32
    )
    mixed = mixed + jnp.einsum(
        "ikgrs,skd->irkgd", lat_attention_low, lat_value_heads, preferred_element_type=jnp.float32
    )
    attn_rows = mixed.reshape(out_rows, query_width).astype(BF16)
    attn_other = swap_cores(attn_rows)
    branch = jnp.dot(attn_rows, w_out, preferred_element_type=F32) + jnp.dot(
        attn_other, w_out_other, preferred_element_type=F32
    )
    resid = jnp.tile(lat_float, (image_slots, 1)) + branch
    out_hat, out_inv = norm_parts(resid)
    final_rows = (out_hat * gain_out).astype(BF16)
    shard_of = routes[:, 0]
    shard_hot = (shard_of[:, None] == jnp.arange(dp_count, dtype=jnp.int32)[None, :]).astype(
        jnp.int32
    )
    rank = jnp.sum((jnp.cumsum(shard_hot, axis=0) - shard_hot) * shard_hot, axis=1)
    place = shard_of * slot_count + rank
    scatter_table = (
        jnp.arange(dp_count * slot_count, dtype=jnp.int32)[:, None] == place[None, :]
    ).astype(BF16)
    final_half = lax.dynamic_slice_in_dim(final_rows, mp_index * half_width, half_width, 1)
    outgoing = jnp.dot(scatter_table, final_half, preferred_element_type=F32).astype(BF16)
    routed = lax.all_to_all(
        outgoing.reshape(dp_count, slot_count, half_width),
        "dp",
        split_axis=0,
        concat_axis=0,
        tiled=True,
    ).reshape(dp_count * slot_count, half_width)

    attn_line = attn_rows
    for bit in gather_bits:
        attn_line = jnp.concatenate([attn_line, swap_bit(attn_line, bit, dp_count)], axis=0)

    first = jnp.where(mp_index == 0, returned, returned_other)
    second = jnp.where(mp_index == 0, returned_other, returned)
    d_final = jnp.concatenate(
        [dot_general(scatter_table, first, 0, 0), dot_general(scatter_table, second, 0, 0)], axis=1
    )
    d_hat = d_final * gain_out
    d_resid = out_inv * (d_hat - out_hat * jnp.mean(d_hat * out_hat, axis=1, keepdims=True))
    gain_out_term = jnp.sum(d_final * out_hat, axis=0)
    d_branch = d_resid.astype(BF16)
    d_attn = dot_general(d_branch, w_out, 1, 1).astype(BF16)

    d_attn_heads = d_attn.reshape(image_slots, latent_rows, group_local, per_group, HD)
    d_probs = jnp.einsum(
        "irkgd,tkd->ikgrt", d_attn_heads, value_heads, preferred_element_type=jnp.float32
    )
    d_lat_probs = jnp.einsum(
        "irkgd,skd->ikgrs", d_attn_heads, lat_value_heads, preferred_element_type=jnp.float32
    )
    row_delta = jnp.sum(attention * d_probs, axis=-1, keepdims=True) + jnp.sum(
        lat_attention * d_lat_probs, axis=-1, keepdims=True
    )
    d_scores = jnp.sum(attention * (d_probs - row_delta), axis=0).astype(BF16)
    d_lat_scores = jnp.sum(lat_attention * (d_lat_probs - row_delta), axis=0).astype(BF16)
    d_query = jnp.einsum("kgrt,tkd->rkgd", d_scores, key_heads, preferred_element_type=jnp.float32)
    d_query = d_query + jnp.einsum(
        "kgrs,skd->rkgd", d_lat_scores, lat_key_heads, preferred_element_type=jnp.float32
    )
    d_query = d_query.reshape(latent_rows, query_width).astype(BF16)
    d_keys = jnp.einsum("kgrt,rkgd->tkd", d_scores, query_heads, preferred_element_type=jnp.float32)
    d_keys = d_keys.reshape(patch_rows, key_width).astype(BF16)
    d_values = jnp.einsum(
        "ikgrt,irkgd->tkd", attention_low, d_attn_heads, preferred_element_type=jnp.float32
    )
    d_values = d_values.reshape(patch_rows, key_width).astype(BF16)
    d_lat_keys = jnp.einsum(
        "kgrs,rkgd->skd", d_lat_scores, query_heads, preferred_element_type=jnp.float32
    )
    d_lat_keys = d_lat_keys.reshape(latent_rows, key_width).astype(BF16)
    d_lat_values = jnp.einsum(
        "ikgrs,irkgd->skd", lat_attention_low, d_attn_heads, preferred_element_type=jnp.float32
    )
    d_lat_values = d_lat_values.reshape(latent_rows, key_width).astype(BF16)
    d_pair = jnp.concatenate([d_keys, d_values], axis=1)

    value_grad = dot_general(d_values, normed_ctx, 0, 0).reshape(key_width, dp_count, own_width)
    key_grad = dot_general(d_keys, normed_ctx, 0, 0).reshape(key_width, dp_count, own_width)
    value_block = scatter_sum(value_grad, order_one, dp_count)
    key_block = scatter_sum(key_grad, order_two, dp_count)

    row_dot = jnp.sum(d_keys.astype(F32) * key_f32, axis=1) + jnp.sum(
        d_values.astype(F32) * value_f32, axis=1
    )
    row_dot = (row_dot + swap_cores(row_dot)) / width
    d_pair_other = swap_cores(d_pair)
    d_ctx_in = dot_general(d_pair, w_pair_half, 1, 1) + dot_general(
        d_pair_other, w_pair_other, 1, 1
    )
    gain_ctx_half = lax.dynamic_slice_in_dim(gain_ctx, mp_index * half_width, half_width, 0)
    hat_half = lax.dynamic_slice_in_dim(patch_hat, mp_index * half_width, half_width, 1)
    ctx_grad = (patch_inv * (d_ctx_in * gain_ctx_half - hat_half * row_dot[:, None])).astype(BF16)

    high = gain_out_term.astype(BF16)
    low = (gain_out_term - high.astype(F32)).astype(BF16)
    lat_sum = jnp.concatenate(
        [
            d_query,
            d_lat_keys,
            d_lat_values,
            high.reshape(latent_rows, width // latent_rows),
            low.reshape(latent_rows, width // latent_rows),
        ],
        axis=1,
    ).astype(F32)
    for bit in gather_bits + scatter_bits:
        lat_sum = lat_sum + swap_bit(lat_sum.astype(BF16), bit, dp_count).astype(F32)
    pair_sum = lat_sum[:, query_width : query_width + 2 * key_width]
    query_sum = lat_sum[:, :query_width]
    gains_at = query_width + 2 * key_width
    gain_step = width // latent_rows
    gain_out_full = (
        lat_sum[:, gains_at : gains_at + gain_step]
        + lat_sum[:, gains_at + gain_step : gains_at + 2 * gain_step]
    ).reshape(width)

    plane = dp_count // 4
    row_half = out_rows // mp_count
    d_block = lax.dynamic_slice_in_dim(d_branch, mp_index * row_half, row_half, 0)
    d_line = d_block.reshape(1, row_half, 2, 2, plane * own_width)
    for step, bit in enumerate(gather_bits):
        mine = (dp_index >> bit) & 1
        going = lax.dynamic_index_in_dim(d_line, 1 - mine, 2, keepdims=False)
        kept = lax.dynamic_index_in_dim(d_line, mine, 2, keepdims=False)
        d_line = jnp.concatenate([kept, swap_bit(going, bit, dp_count)], axis=0)
    d_line_other = swap_cores(d_line)
    d_line = jnp.concatenate(
        [
            jnp.where(mp_index == 0, d_line, d_line_other),
            jnp.where(mp_index == 0, d_line_other, d_line),
        ],
        axis=1,
    )
    out_part = dot_general(attn_line, d_line.reshape(4 * out_rows, plane * own_width), 0, 0)
    resid_part = jnp.sum(
        d_line.astype(F32).reshape(4 * image_slots, latent_rows, plane * own_width), axis=0
    )
    resid_part = lax.dynamic_index_in_dim(
        resid_part.reshape(2, latent_rows // 2, plane, mp_count, own_width // mp_count),
        mp_index,
        3,
        keepdims=False,
    )
    resid_part = jnp.transpose(resid_part, (1, 2, 0, 3)).reshape(
        latent_rows // 2, plane, own_width
    )
    out_part = jnp.concatenate([out_part.reshape(query_width, plane, own_width), resid_part], axis=0)
    cut = out_part.shape[0] // 2
    out_block = jnp.concatenate(
        [
            scatter_sum(out_part[:cut], scatter_bits, dp_count),
            scatter_sum(out_part[cut:], [1, 0] + scatter_bits[2:], dp_count),
        ],
        axis=0,
    )
    grad_w_out = out_block[:query_width]
    resid_sum = (
        out_block[query_width:]
        .reshape(latent_rows // 2, 2, own_width // mp_count)
        .transpose(1, 0, 2)
        .reshape(latent_rows, own_width // mp_count)
    )

    def own(array, axis):
        return lax.dynamic_slice_in_dim(array, dp_index * own_width, own_width, axis)

    lat_own = own(normed_lat, 1)
    pair_ctx = jnp.concatenate([key_block, value_block], axis=0).T
    query_grad = dot_general(lat_own, query_sum.astype(BF16), 0, 0) * scaling
    pair_lat = dot_general(lat_own, pair_sum.astype(BF16), 0, 0)
    pair_all = pair_ctx + pair_lat
    wq_own = own(w_query, 0)
    pair_own = own(w_pair, 0)
    gain_ctx_part = jnp.sum(pair_own.astype(F32) * pair_ctx, axis=1) / own(gain_ctx, 0)
    gain_lat_part = (
        jnp.sum(wq_own.astype(F32) * query_grad, axis=1)
        + jnp.sum(pair_own.astype(F32) * pair_lat, axis=1)
    ) / own(gain_lat, 0)
    d_lat_part = dot_general(
        (query_sum * scaling).astype(BF16), wq_own, 1, 1
    ) + dot_general(pair_sum.astype(BF16), pair_own, 1, 1)
    lat_dot_part = (
        jnp.sum(query_sum * query_f32, axis=1)
        + jnp.sum(pair_sum[:, :key_width] * lat_key_f32, axis=1)
        + jnp.sum(pair_sum[:, key_width:] * lat_value_f32, axis=1)
    )
    small = jnp.concatenate(
        [
            d_lat_part,
            jnp.broadcast_to(lat_dot_part[:, None], (latent_rows, own_width)),
            jnp.broadcast_to(gain_ctx_part[None, :], (8, own_width)),
            jnp.broadcast_to(gain_lat_part[None, :], (8, own_width)),
        ],
        axis=0,
    )
    small = small + swap_cores(small)
    share = own_width // mp_count
    small = lax.dynamic_slice_in_dim(small, mp_index * share, share, 1)
    d_lat_in = small[:latent_rows]
    lat_dot = small[latent_rows : 2 * latent_rows] / width

    def mine_of(array, axis):
        return lax.dynamic_slice_in_dim(
            array, dp_index * own_width + mp_index * share, share, axis
        )

    grad_latents = resid_sum + lat_inv * (
        mine_of(gain_lat, 0) * d_lat_in - mine_of(lat_hat, 1) * lat_dot
    )
    return (
        routed,
        ctx_grad,
        query_grad,
        pair_all[:, :key_width],
        pair_all[:, key_width:],
        grad_w_out,
        grad_latents,
        small[2 * latent_rows],
        small[2 * latent_rows + 8],
        mine_of(gain_out_full, 0),
    )


def solution(mesh):
    placed = (
        P("dp", None),
        P("dp", None),
        P("dp", None),
        P(None, "mp"),
        P(None, "mp"),
        P(None, "mp"),
        P("mp", None),
        P(),
        P(),
        P(),
        P(),
        P("dp", "mp"),
    )
    return jax.shard_map(
        local if mesh.shape["dp"] == 16 else local_general,
        mesh=mesh,
        in_specs=placed,
        out_specs=(
            P("dp", "mp"),
            P("dp", "mp"),
            P("dp", "mp"),
            P("dp", "mp"),
            P("dp", "mp"),
            P("mp", "dp"),
            P(None, ("dp", "mp")),
            P(("dp", "mp")),
            P(("dp", "mp")),
            P(("dp", "mp")),
        ),
        check_vma=False,
    )
```

```python
import functools

import jax
import jax.numpy as jnp
from jax import lax
from jax.experimental import pallas as pl
from jax.experimental.pallas import tpu as pltpu
from jax.sharding import PartitionSpec as P

HD = 96
EPSILON = 1e-06
NEGATIVE = -1e30
BF16 = jnp.bfloat16
F32 = jnp.float32
VMEM_LIMIT = 63 << 20


def dot_general(left, right, left_dim, right_dim):
    return lax.dot_general(
        left, right, (((left_dim,), (right_dim,)), ((), ())), preferred_element_type=F32
    )


def norm_parts(values_in):
    inverse = lax.rsqrt(jnp.mean(values_in * values_in, axis=-1, keepdims=True) + EPSILON)
    return (values_in * inverse, inverse)


def swap_cores(array):
    return lax.ppermute(array, "mp", [(0, 1), (1, 0)])


def swap_bit(array, bit, dp_count):
    return lax.ppermute(array, "dp", [(i, i ^ (1 << bit)) for i in range(dp_count)])


def halve(array, axis, bit, dp_count):
    mine = (lax.axis_index("dp") >> bit) & 1
    going = lax.dynamic_index_in_dim(array, 1 - mine, axis, keepdims=False)
    kept = lax.dynamic_index_in_dim(array, mine, axis, keepdims=False)
    return kept.astype(F32) + swap_bit(going.astype(BF16), bit, dp_count).astype(F32)


def scatter_sum(array, bits, dp_count):
    rows, owners, columns = array.shape
    left = sorted(bits, reverse=True)
    array = array.reshape((rows,) + (2,) * len(left) + (columns,))
    for bit in bits:
        axis = left.index(bit)
        array = halve(array, 1 + axis, bit, dp_count)
        left.pop(axis)
    return array


def forward_kernel(
    counts_ref,
    gain_ctx_ref,
    gain_lat_ref,
    lat_hbm,
    wk_hbm,
    wv_hbm,
    x_hbm,
    wq_hbm,
    attn_hbm,
    k_hbm,
    v_hbm,
    inv_row_hbm,
    q_hbm,
    lk_hbm,
    lv_hbm,
    lat_proj_hbm,
    p_hbm,
    pl_hbm,
    lat_ref,
    wk_ref,
    wv_ref,
    x_ref,
    wq_ref,
    attn_ref,
    k_ref,
    v_ref,
    inv_row_ref,
    q_ref,
    lk_ref,
    lv_ref,
    lat_proj_ref,
    p_ref,
    pl_ref,
    lat_normed_ref,
    last_ref,
    gained_ref,
    sems,
    out_sems,
):
    patch_rows, width = x_ref.shape
    chunks = sems.shape[0] - 4
    rows = patch_rows // chunks
    groups = k_ref.shape[0]
    latent_rows = lat_ref.shape[0]
    key_width = wk_ref.shape[0]
    query_width = wq_ref.shape[1]
    per_group = query_width // key_width

    def fetch(source, target, i):
        return pltpu.make_async_copy(source, target, sems.at[i])

    def fetch_rows(i):
        at = pl.ds(i * rows, rows)
        return fetch(x_hbm.at[at], x_ref.at[at], i)

    weights = [
        fetch(source, target, chunks + i)
        for i, (source, target) in enumerate(
            ((lat_hbm, lat_ref), (wk_hbm, wk_ref), (wv_hbm, wv_ref), (wq_hbm, wq_ref))
        )
    ]
    for copy in weights[:3]:
        copy.start()
    blocks = [fetch_rows(i) for i in range(chunks)]
    for copy in blocks + weights[3:]:
        copy.start()
    results = {}
    for i, (name, source, target) in enumerate(
        (
            ("attn", attn_ref, attn_hbm),
            ("k", k_ref, k_hbm),
            ("v", v_ref, v_hbm),
            ("inv_row", inv_row_ref, inv_row_hbm),
            ("q", q_ref, q_hbm),
            ("lk", lk_ref, lk_hbm),
            ("lv", lv_ref, lv_hbm),
            ("lat_proj", lat_proj_ref, lat_proj_hbm),
            ("p0", p_ref.at[0], p_hbm.at[0]),
            ("p1", p_ref.at[1], p_hbm.at[1]),
            ("pl", pl_ref, pl_hbm),
        )
    ):
        results[name] = pltpu.make_async_copy(source, target, out_sems.at[i])

    weights[0].wait()
    lat = lat_ref[...].astype(F32)
    lat_inverse = lax.rsqrt(jnp.mean(lat * lat, axis=-1, keepdims=True) + EPSILON)
    lat_normed = lat * lat_inverse * gain_lat_ref[...]
    lat_normed_ref[...] = lat_normed.astype(BF16)
    last_ref[rows:, :] = (lat_normed / gain_ctx_ref[...]).astype(BF16)
    for i, ref in enumerate((wk_ref, wv_ref)):
        weights[1 + i].wait()
        gained_ref[i * key_width : (i + 1) * key_width, :] = (
            ref[...].astype(F32) * gain_ctx_ref[...]
        ).astype(BF16)
    for i in range(chunks):
        blocks[i].wait()
        at = slice(i * rows, (i + 1) * rows)
        squares = jnp.zeros((rows, 128), F32)
        for c in range(width // 128):
            part = x_ref[at, c * 128 : (c + 1) * 128].astype(F32)
            squares = squares + part * part
        inverse = lax.rsqrt(jnp.sum(squares, axis=-1, keepdims=True) / width + EPSILON)
        if i < chunks - 1:
            pair = dot_general(x_ref[at, :], gained_ref[...], 1, 1)
        else:
            last_ref[:rows, :] = x_ref[at, :]
            pair = dot_general(last_ref[...], gained_ref[...], 1, 1)
            projected = pair[rows:]
        pair = (pair[:rows] * inverse).astype(BF16)
        inv_row_ref[:, at] = jnp.transpose(jnp.broadcast_to(inverse, (rows, 128)))[:8]
        for g in range(groups):
            k_ref[g, at, :HD] = pair[:, g * HD : (g + 1) * HD]
            v_ref[g, at, :HD] = pair[:, key_width + g * HD : key_width + (g + 1) * HD]
    lat_proj_ref[:, query_width:] = projected
    for i, ref in enumerate((lk_ref, lv_ref)):
        for g in range(groups):
            at = i * key_width + g * HD
            ref[g, :, :HD] = projected[:, at : at + HD].astype(BF16)
    for name in ("k", "v", "inv_row", "lk", "lv"):
        results[name].start()
    weights[3].wait()
    query = jnp.dot(lat_normed_ref[...], wq_ref[...], preferred_element_type=F32) * HD ** (-0.5)
    lat_proj_ref[:, :query_width] = query
    first_count = counts_ref[0, 0]
    both_count = first_count + counts_ref[0, 1]
    position = lax.broadcasted_iota(jnp.int32, (1, patch_rows), 1)
    in_first = position < first_count
    in_second = jnp.logical_and(position >= first_count, position < both_count)
    rows_at = lax.broadcasted_iota(jnp.int32, (patch_rows, HD), 0)
    row_first = rows_at < first_count
    row_second = jnp.logical_and(rows_at >= first_count, rows_at < both_count)
    for g in range(groups):
        for h in range(per_group):
            head = g * per_group + h
            q_ref[g, h * latent_rows : (h + 1) * latent_rows, :HD] = query[
                :, head * HD : (head + 1) * HD
            ].astype(BF16)
    results["lat_proj"].start()
    results["q"].start()
    for g in range(groups):
        q = q_ref[g, :, :HD]
        scores = dot_general(q, k_ref[g, :, :HD], 1, 1)
        lat_scores = dot_general(q, lk_ref[g, :, :HD], 1, 1)
        lat_max = jnp.max(lat_scores, axis=-1, keepdims=True)
        max_first = jnp.maximum(
            jnp.max(jnp.where(in_first, scores, NEGATIVE), axis=-1, keepdims=True), lat_max
        )
        max_second = jnp.maximum(
            jnp.max(jnp.where(in_second, scores, NEGATIVE), axis=-1, keepdims=True), lat_max
        )
        masked = jnp.where(
            in_first, scores - max_first, jnp.where(in_second, scores - max_second, NEGATIVE)
        )
        exponent = jnp.exp(masked)
        lat_first = jnp.exp(lat_scores - max_first)
        lat_second = jnp.exp(lat_scores - max_second)
        sum_first = jnp.sum(
            jnp.where(in_first, exponent, 0.0), axis=-1, keepdims=True
        ) + jnp.sum(lat_first, axis=-1, keepdims=True)
        sum_second = jnp.sum(
            jnp.where(in_second, exponent, 0.0), axis=-1, keepdims=True
        ) + jnp.sum(lat_second, axis=-1, keepdims=True)
        per_first = 1.0 / sum_first
        per_second = 1.0 / sum_second
        p = (exponent * jnp.where(in_first, per_first, per_second)).astype(BF16)
        p_ref[g] = p
        results[f"p{g}"].start()
        lat_p_first = (lat_first * per_first).astype(BF16)
        lat_p_second = (lat_second * per_second).astype(BF16)
        pl_ref[g, :, :latent_rows] = lat_p_first
        pl_ref[g, :, latent_rows:] = lat_p_second
        v = v_ref[g, :, :HD]
        zero = jnp.zeros_like(v)
        lv = lv_ref[g, :, :HD]
        for j, (row_mask, lat_p) in enumerate(
            ((row_first, lat_p_first), (row_second, lat_p_second))
        ):
            mixed = jnp.dot(
                p, jnp.where(row_mask, v, zero), preferred_element_type=F32
            ) + jnp.dot(lat_p, lv, preferred_element_type=F32)
            mixed = mixed.astype(BF16)
            for h in range(per_group):
                head = g * per_group + h
                attn_ref[
                    j * latent_rows : (j + 1) * latent_rows, head * HD : (head + 1) * HD
                ] = mixed[h * latent_rows : (h + 1) * latent_rows]
    for name in ("attn", "pl"):
        results[name].start()
    for copy in results.values():
        copy.wait()


def whole(shape):
    return pl.BlockSpec(shape, lambda *_: (0,) * len(shape))


def held(shape):
    return pl.BlockSpec(shape, lambda *_: (0,) * len(shape), pipeline_mode=pl.Buffered(1))


def forward_call(context, counts, w_query, w_key, w_value, latents, gain_ctx, gain_lat):
    patch_rows, width = context.shape
    chunks = 4
    key_width = w_key.shape[0]
    query_width = w_query.shape[1]
    groups = key_width // HD
    latent_rows = latents.shape[0]
    stacked = query_width // key_width * latent_rows
    large = (latents, w_key, w_value, context, w_query)
    out = [
        ((2 * latent_rows, query_width), BF16),
        ((groups, patch_rows, 128), BF16),
        ((groups, patch_rows, 128), BF16),
        ((8, patch_rows), F32),
        ((groups, stacked, 128), BF16),
        ((groups, latent_rows, 128), BF16),
        ((groups, latent_rows, 128), BF16),
        ((latent_rows, query_width + 2 * key_width), F32),
        ((groups, stacked, patch_rows), BF16),
        ((groups, stacked, 2 * latent_rows), BF16),
    ]
    return pl.pallas_call(
        forward_kernel,
        name="forward_attention",
        in_specs=[
            pl.BlockSpec(memory_space=pltpu.SMEM),
            pl.BlockSpec(memory_space=pltpu.VMEM),
            pl.BlockSpec(memory_space=pltpu.VMEM),
        ]
        + [pl.BlockSpec(memory_space=pl.ANY)] * len(large),
        out_specs=[pl.BlockSpec(memory_space=pl.ANY)] * len(out),
        out_shape=[jax.ShapeDtypeStruct(shape, dtype) for shape, dtype in out],
        scratch_shapes=[pltpu.VMEM(a.shape, a.dtype) for a in large]
        + [pltpu.VMEM(shape, dtype) for shape, dtype in out]
        + [
            pltpu.VMEM((latent_rows, width), BF16),
            pltpu.VMEM((patch_rows // chunks + latent_rows, width), BF16),
            pltpu.VMEM((2 * key_width, width), BF16),
            pltpu.SemaphoreType.DMA((chunks + 4,)),
            pltpu.SemaphoreType.DMA((len(out) + 1,)),
        ],
        cost_estimate=pl.CostEstimate(
            flops=5_000_000_000, bytes_accessed=24_000_000, transcendentals=600_000
        ),
        compiler_params=pltpu.CompilerParams(vmem_limit_bytes=VMEM_LIMIT),
    )(counts, gain_ctx.reshape(1, width), gain_lat.reshape(1, width), *large)


def slots_of(routes_ref, slot_count, as_row):
    rows = routes_ref.shape[1]
    turned = jnp.broadcast_to(routes_ref[...].astype(F32), (rows, rows))
    shard = jnp.transpose(turned)
    down = lax.broadcasted_iota(jnp.int32, (rows, rows), 0)
    across = lax.broadcasted_iota(jnp.int32, (rows, rows), 1)
    same = shard == turned
    if as_row:
        rank = jnp.sum(jnp.where(same & (down < across), 1.0, 0.0), axis=0, keepdims=True)
        return (turned[:1] * slot_count + rank).astype(jnp.int32)
    rank = jnp.sum(jnp.where(same & (across < down), 1.0, 0.0), axis=1, keepdims=True)
    return (shard[:, :1] * slot_count + rank).astype(jnp.int32)


def branch_kernel(
    slot_count,
    mp_ref,
    own_ref,
    other_ref,
    lat_ref,
    gain_ref,
    routes_ref,
    w_own_hbm,
    w_other_hbm,
    hat_hbm,
    inv_ref,
    out_ref,
    w_own_ref,
    w_other_ref,
    hat_ref,
    sems,
    hat_sem,
):
    rows, width = hat_ref.shape
    slots, half = out_ref.shape
    parts = sems.shape[1]
    size = width // parts
    copies = []
    for part in range(parts):
        at = pl.ds(part * size, size)
        for i, (source, target) in enumerate(
            ((w_own_hbm, w_own_ref), (w_other_hbm, w_other_ref))
        ):
            copies.append(
                pltpu.make_async_copy(source.at[:, at], target.at[:, at], sems.at[i, part])
            )
    for copy in copies:
        copy.start()
    place = slots_of(routes_ref, slot_count, True)
    table = jnp.where(
        lax.broadcasted_iota(jnp.int32, (slots, rows), 0) == place, 1.0, 0.0
    ).astype(BF16)
    squares = jnp.zeros((rows, 128), F32)
    for part in range(parts):
        at = slice(part * size, (part + 1) * size)
        copies[2 * part].wait()
        copies[2 * part + 1].wait()
        lat = lat_ref[:, at].astype(F32)
        resid = (
            jnp.concatenate([lat, lat], axis=0)
            + jnp.dot(own_ref[...], w_own_ref[:, at], preferred_element_type=F32)
            + jnp.dot(other_ref[...], w_other_ref[:, at], preferred_element_type=F32)
        )
        hat_ref[:, at] = resid
        for c in range(size // 128):
            piece = resid[:, c * 128 : (c + 1) * 128]
            squares = squares + piece * piece
    inverse = lax.rsqrt(jnp.sum(squares, axis=-1, keepdims=True) / width + EPSILON)
    inv_ref[...] = inverse
    hat_ref[...] = hat_ref[...] * inverse
    hat_copy = pltpu.make_async_copy(hat_ref, hat_hbm, hat_sem)
    hat_copy.start()
    at = pl.ds(pl.multiple_of(mp_ref[0] * half, half), half)
    final = (hat_ref[:, at] * gain_ref[:, at]).astype(BF16)
    out_ref[...] = jnp.dot(table, final, preferred_element_type=F32).astype(BF16)
    hat_copy.wait()


def branch_call(mp_index, own, other, w_own, w_other, latents, gain_out, routes, slots, slot_count):
    width = w_own.shape[1]
    rows, heads = own.shape
    parts = 4
    return pl.pallas_call(
        functools.partial(branch_kernel, slot_count),
        name="branch_norm",
        grid_spec=pltpu.PrefetchScalarGridSpec(
            num_scalar_prefetch=1,
            grid=(1,),
            in_specs=[
                held((rows, heads)),
                held((rows, heads)),
                held(latents.shape),
                held((1, width)),
                held((1, rows)),
                pl.BlockSpec(memory_space=pl.ANY),
                pl.BlockSpec(memory_space=pl.ANY),
            ],
            out_specs=[
                pl.BlockSpec(memory_space=pl.ANY),
                held((rows, 1)),
                held((slots, width // 2)),
            ],
            scratch_shapes=[
                pltpu.VMEM(w_own.shape, BF16),
                pltpu.VMEM(w_other.shape, BF16),
                pltpu.VMEM((rows, width), F32),
                pltpu.SemaphoreType.DMA((2, parts)),
                pltpu.SemaphoreType.DMA,
            ],
        ),
        out_shape=[
            jax.ShapeDtypeStruct((rows, width), F32),
            jax.ShapeDtypeStruct((rows, 1), F32),
            jax.ShapeDtypeStruct((slots, width // 2), BF16),
        ],
        cost_estimate=pl.CostEstimate(
            flops=2 * 2 * rows * heads * width, bytes_accessed=16_000_000, transcendentals=0
        ),
        compiler_params=pltpu.CompilerParams(vmem_limit_bytes=VMEM_LIMIT),
    )(mp_index, own, other, latents, gain_out.reshape(1, width), routes, w_own, w_other)


def attention_backward(
    counts_ref,
    d_attn,
    k_ref,
    v_ref,
    q_ref,
    lk_ref,
    lv_ref,
    p_ref,
    pl_ref,
    inv_row_ref,
    pair_ref,
    scaled_ref,
    lat_ref,
):
    groups, patch_rows, _ = k_ref.shape
    latent_rows = lk_ref.shape[1]
    stacked = q_ref.shape[1]
    per_group = stacked // latent_rows
    key_width = groups * HD
    query_width = groups * per_group * HD
    first_count = counts_ref[0, 0]
    both_count = first_count + counts_ref[0, 1]
    position = lax.broadcasted_iota(jnp.int32, (1, patch_rows), 1)
    in_first = position < first_count
    rows_at = lax.broadcasted_iota(jnp.int32, (patch_rows, HD), 0)
    row_first = rows_at < first_count
    row_second = jnp.logical_and(rows_at >= first_count, rows_at < both_count)
    scale_row = inv_row_ref[:1]
    row_dot = jnp.zeros((1, patch_rows), F32)
    for g in range(groups):
        d_first = jnp.concatenate(
            [
                d_attn[:latent_rows, head * HD : (head + 1) * HD]
                for head in range(g * per_group, (g + 1) * per_group)
            ],
            axis=0,
        )
        d_second = jnp.concatenate(
            [
                d_attn[latent_rows:, head * HD : (head + 1) * HD]
                for head in range(g * per_group, (g + 1) * per_group)
            ],
            axis=0,
        )
        q = q_ref[g, :, :HD]
        k = k_ref[g, :, :HD]
        v = v_ref[g, :, :HD]
        lk = lk_ref[g, :, :HD]
        lv = lv_ref[g, :, :HD]
        p_low = p_ref[g]
        p = p_low.astype(F32)
        zero = jnp.zeros_like(v)
        d_p = dot_general(d_first, jnp.where(row_first, v, zero), 1, 1) + dot_general(
            d_second, jnp.where(row_second, v, zero), 1, 1
        )
        product = p * d_p
        lat_first = pl_ref[g, :, :latent_rows]
        lat_second = pl_ref[g, :, latent_rows:]
        d_lat_first = dot_general(d_first, lv, 1, 1)
        d_lat_second = dot_general(d_second, lv, 1, 1)
        lat_product_first = lat_first.astype(F32) * d_lat_first
        lat_product_second = lat_second.astype(F32) * d_lat_second
        whole_sum = jnp.sum(product, axis=-1, keepdims=True)
        first_sum = jnp.sum(jnp.where(in_first, product, 0.0), axis=-1, keepdims=True)
        delta_first = first_sum + jnp.sum(lat_product_first, axis=-1, keepdims=True)
        delta_second = (whole_sum - first_sum) + jnp.sum(
            lat_product_second, axis=-1, keepdims=True
        )
        ds = product - p * jnp.where(in_first, delta_first, delta_second)
        ds_low = ds.astype(BF16)
        dsl = (
            lat_product_first
            - lat_first.astype(F32) * delta_first
            + lat_product_second
            - lat_second.astype(F32) * delta_second
        ).astype(BF16)
        scores = dot_general(q, k, 1, 1)
        row_dot = row_dot + jnp.sum(ds * scores + product, axis=0, keepdims=True)
        d_q = (
            jnp.dot(ds_low, k, preferred_element_type=F32)
            + jnp.dot(dsl, lk, preferred_element_type=F32)
        ).astype(BF16)
        for h in range(per_group):
            head = g * per_group + h
            lat_ref[:latent_rows, head * HD : (head + 1) * HD] = d_q[
                h * latent_rows : (h + 1) * latent_rows
            ]
        d_k = dot_general(q, ds_low, 0, 0)
        nothing = jnp.zeros_like(p_low)
        d_v = dot_general(d_first, jnp.where(in_first, p_low, nothing), 0, 0) + dot_general(
            d_second, jnp.where(in_first, nothing, p_low), 0, 0
        )
        k_at = slice(g * HD, (g + 1) * HD)
        v_at = slice(key_width + g * HD, key_width + (g + 1) * HD)
        pair_ref[k_at, :] = d_k.astype(BF16)
        pair_ref[v_at, :] = d_v.astype(BF16)
        scaled_ref[k_at, :] = (d_k * scale_row).astype(BF16)
        scaled_ref[v_at, :] = (d_v * scale_row).astype(BF16)
        d_lk = dot_general(dsl, q, 0, 0)
        d_lv = dot_general(lat_first, d_first, 0, 0) + dot_general(lat_second, d_second, 0, 0)
        lat_ref[:latent_rows, query_width + g * HD : query_width + (g + 1) * HD] = d_lk.astype(BF16)
        at = query_width + key_width + g * HD
        lat_ref[:latent_rows, at : at + HD] = d_lv.astype(BF16)
    high = row_dot.astype(BF16)
    low = (row_dot - high.astype(F32)).astype(BF16)
    rest = pair_ref.shape[0] - 2 * key_width - 2
    pair_ref[2 * key_width :, :] = jnp.concatenate(
        [high.astype(F32), low.astype(F32), jnp.zeros((rest, patch_rows), F32)], axis=0
    ).astype(BF16)


def backward_kernel(
    slot_count,
    where_ref,
    counts_ref,
    inv_out_ref,
    gain_ref,
    routes_ref,
    inv_row_ref,
    got_own_hbm,
    got_other_hbm,
    hat_hbm,
    w_out_hbm,
    k_hbm,
    v_hbm,
    q_hbm,
    lk_hbm,
    lv_hbm,
    p_hbm,
    pl_hbm,
    x_hbm,
    line_own_hbm,
    line_low_hbm,
    line_high_hbm,
    line_both_hbm,
    pair_hbm,
    lat_hbm,
    value_going_hbm,
    value_kept_hbm,
    key_going_hbm,
    key_kept_hbm,
    got_own_ref,
    got_other_ref,
    hat_ref,
    w_out_ref,
    k_ref,
    v_ref,
    q_ref,
    lk_ref,
    lv_ref,
    p_ref,
    pl_ref,
    x_ref,
    d_final_ref,
    branch_ref,
    scaled_ref,
    line_own_ref,
    line_low_ref,
    line_high_ref,
    line_both_ref,
    pair_ref,
    lat_ref,
    value_ref,
    key_ref,
    sems,
    out_sems,
    value_sems,
    key_sems,
):
    sources = (
        got_own_hbm,
        got_other_hbm,
        hat_hbm,
        w_out_hbm,
        k_hbm,
        v_hbm,
        q_hbm,
        lk_hbm,
        lv_hbm,
        p_hbm,
        pl_hbm,
        x_hbm,
    )
    targets = (
        got_own_ref,
        got_other_ref,
        hat_ref,
        w_out_ref,
        k_ref,
        v_ref,
        q_ref,
        lk_ref,
        lv_ref,
        p_ref,
        pl_ref,
        x_ref,
    )
    copies = [
        pltpu.make_async_copy(source, target, sems.at[i])
        for i, (source, target) in enumerate(zip(sources, targets))
    ]
    for copy in copies[:4]:
        copy.start()
    rows, width = hat_ref.shape
    half = width // 2
    slots = got_own_ref.shape[0]
    latent_rows = lk_ref.shape[1]
    key_width, own = value_ref.shape[2:]

    place = slots_of(routes_ref, slot_count, False)
    table = jnp.where(
        lax.broadcasted_iota(jnp.int32, (rows, slots), 1) == place, 1.0, 0.0
    ).astype(BF16)
    total = jnp.zeros((rows, 1), F32)
    chunk = 512
    for copy in copies[:3]:
        copy.wait()
    for copy in copies[4:]:
        copy.start()
    for got_ref, which in ((got_own_ref, where_ref[1]), (got_other_ref, 1 - where_ref[1])):
        for c in range(half // chunk):
            at = pl.ds(pl.multiple_of(which * half + c * chunk, chunk), chunk)
            d_final = jnp.dot(
                table, got_ref[:, c * chunk : (c + 1) * chunk], preferred_element_type=F32
            )
            product = d_final * hat_ref[:, at]
            total = total + jnp.sum(product * gain_ref[:, at], axis=-1, keepdims=True)
            d_final_ref[:, at] = d_final
    total = total / width
    lat_ref[latent_rows:, :] = jnp.zeros_like(lat_ref[latent_rows:, :])
    highs, lows = [], []
    part = width // 4
    for c in range(width // chunk):
        at = slice(c * chunk, (c + 1) * chunk)
        d_final = d_final_ref[:, at]
        hat = hat_ref[:, at]
        term = jnp.sum(d_final * hat, axis=0, keepdims=True)
        high = term.astype(BF16).astype(F32)
        highs.append(high)
        lows.append(term - high)
        branch_ref[:, at] = (
            inv_out_ref[...] * (d_final * gain_ref[:, at] - hat * total)
        ).astype(BF16)
    per_row = part // chunk
    lines = [
        jnp.concatenate(group[i * per_row : (i + 1) * per_row], axis=1)
        for group in (highs, lows)
        for i in range(4)
    ]
    lat_ref[latent_rows : latent_rows + 16, :part] = jnp.concatenate(
        lines + [jnp.zeros((8, part), F32)], axis=0
    ).astype(BF16)
    z = where_ref[0] >> 2
    some = pl.ds(pl.multiple_of(where_ref[1] * (rows // 2), rows // 2), rows // 2)
    line_own_ref[...] = branch_ref[:, pl.ds(pl.multiple_of(z * part, part), part)]
    for turn, ref in ((1, line_low_ref), (2, line_high_ref), (3, line_both_ref)):
        ref[...] = branch_ref[some, pl.ds(pl.multiple_of((z ^ turn) * part, part), part)]
    results = [
        pltpu.make_async_copy(source, target, out_sems.at[i])
        for i, (source, target) in enumerate(
            (
                (line_low_ref, line_low_hbm),
                (line_high_ref, line_high_hbm),
                (line_both_ref, line_both_hbm),
                (line_own_ref, line_own_hbm),
                (pair_ref, pair_hbm),
                (lat_ref, lat_hbm),
            )
        )
    ]
    for copy in results[:4]:
        copy.start()

    copies[3].wait()
    d_attn = dot_general(branch_ref[...], w_out_ref[...], 1, 1).astype(BF16)
    for copy in copies[4:11]:
        copy.wait()
    attention_backward(
        counts_ref,
        d_attn,
        k_ref,
        v_ref,
        q_ref,
        lk_ref,
        lv_ref,
        p_ref,
        pl_ref,
        inv_row_ref,
        pair_ref,
        scaled_ref,
        lat_ref,
    )
    for copy in results[4:]:
        copy.start()
    copies[11].wait()

    me = where_ref[0]
    odd = me & 1
    for j in range(8):
        y = ((me >> 1) & 1) ^ (1 - (j >> 2))
        z = (me >> 2) ^ ((1 - ((j >> 1) & 1)) + 2 * (1 - (j & 1)))
        first = 4 * z + 2 * y
        line = j & 3
        key_hbm = key_kept_hbm if j >> 2 else key_going_hbm
        grad = jnp.dot(
            scaled_ref[...],
            x_ref[:, pl.ds(pl.multiple_of(first * own, 2 * own), 2 * own)],
            preferred_element_type=F32,
        ).astype(BF16)
        for x_same, value_hbm in enumerate((value_going_hbm, value_kept_hbm)):
            block = jnp.where(odd == x_same, grad[:, own:], grad[:, :own])
            value_ref[x_same, j] = block[key_width:]
            key_ref[x_same, j] = block[:key_width]
            for copy in (
                pltpu.make_async_copy(
                    value_ref.at[x_same, j], value_hbm.at[j], value_sems.at[x_same, j]
                ),
                pltpu.make_async_copy(
                    key_ref.at[x_same, j], key_hbm.at[x_same, line], key_sems.at[x_same, j]
                ),
            ):
                copy.start()
                results.append(copy)
    for copy in results:
        copy.wait()


def backward_call(
    where, counts, got_own, got_other, hat, inv_out, gain_out, routes, w_out, kept, context, slot_count
):
    k, v, q, lk, lv, p, lat_p, inv_row = kept
    rows, width = hat.shape
    patch_rows = context.shape[0]
    heads = w_out.shape[0]
    key_width = k.shape[0] * HD
    latent_rows = lk.shape[1]
    own = width // 16
    large = (got_own, got_other, hat, w_out, k, v, q, lk, lv, p, lat_p, context)
    out = [
        (rows, width // 4),
        (rows // 2, width // 4),
        (rows // 2, width // 4),
        (rows // 2, width // 4),
        (2 * key_width + 16, patch_rows),
        (latent_rows + 16, heads + 2 * key_width),
        (8, key_width, own),
        (8, key_width, own),
        (2, 4, key_width, own),
        (2, 4, key_width, own),
    ]
    return pl.pallas_call(
        functools.partial(backward_kernel, slot_count),
        name="attention_backward",
        grid_spec=pltpu.PrefetchScalarGridSpec(
            num_scalar_prefetch=1,
            grid=(1,),
            in_specs=[
                pl.BlockSpec(memory_space=pltpu.SMEM),
                held(inv_out.shape),
                held((1, width)),
                held(routes.shape),
                held(inv_row.shape),
            ]
            + [pl.BlockSpec(memory_space=pl.ANY)] * len(large),
            out_specs=[pl.BlockSpec(memory_space=pl.ANY)] * len(out),
            scratch_shapes=[pltpu.VMEM(a.shape, a.dtype) for a in large]
            + [
                pltpu.VMEM((rows, width), F32),
                pltpu.VMEM((rows, width), BF16),
                pltpu.VMEM((2 * key_width, patch_rows), BF16),
            ]
            + [pltpu.VMEM(shape, BF16) for shape in out[:6]]
            + [
                pltpu.VMEM((2, 8, key_width, own), BF16),
                pltpu.VMEM((2, 8, key_width, own), BF16),
                pltpu.SemaphoreType.DMA((len(large),)),
                pltpu.SemaphoreType.DMA((6,)),
                pltpu.SemaphoreType.DMA((2, 8)),
                pltpu.SemaphoreType.DMA((2, 8)),
            ],
        ),
        out_shape=[jax.ShapeDtypeStruct(shape, BF16) for shape in out],
        cost_estimate=pl.CostEstimate(
            flops=5_000_000_000, bytes_accessed=26_000_000, transcendentals=0
        ),
        compiler_params=pltpu.CompilerParams(vmem_limit_bytes=VMEM_LIMIT),
    )(where, counts, inv_out, gain_out.reshape(1, width), routes, inv_row, *large)


def patch_kernel(
    width,
    mp_ref,
    own_ref,
    other_ref,
    wk_ref,
    wv_ref,
    wk_other_ref,
    wv_other_ref,
    x_ref,
    inv_row_ref,
    gain_ref,
    out_ref,
    turned_ref,
    inv_ref,
    dot_ref,
    w_ref,
):
    step = pl.program_id(0)
    key_width = wk_ref.shape[0]
    patch_rows = turned_ref.shape[0]
    pair = 2 * key_width

    @pl.when(step == 0)
    def _():
        row_dot = jnp.zeros((patch_rows, 1), F32)
        for i, ref in enumerate((own_ref, other_ref)):
            turned = jnp.transpose(ref[...])
            turned_ref[:, i * pair : (i + 1) * pair] = turned[:, :pair]
            row_dot = row_dot + turned[:, pair : pair + 1].astype(F32)
            row_dot = row_dot + turned[:, pair + 1 : pair + 2].astype(F32)
        inverse = jnp.transpose(jnp.broadcast_to(inv_row_ref[:1], (128, patch_rows)))[:, :1]
        inv_ref[...] = inverse
        dot_ref[...] = row_dot * (inverse * inverse / width)
        for i, ref in enumerate((wk_ref, wv_ref, wk_other_ref, wv_other_ref)):
            w_ref[i * key_width : (i + 1) * key_width, :] = ref[...]

    rows = x_ref.shape[0]
    at = pl.ds(pl.multiple_of(step * rows, rows), rows)
    d_in = jnp.dot(turned_ref[at, :], w_ref[...], preferred_element_type=F32)
    out_ref[...] = (
        d_in * gain_ref[...] * inv_ref[at, :] - x_ref[...].astype(F32) * dot_ref[at, :]
    ).astype(BF16)


def patch_call(mp_index, own, other, wk, wv, wk_other, wv_other, context, inv_row, gain_ctx):
    patch_rows, width = context.shape
    half = width // 2
    steps = 4
    rows = patch_rows // steps
    key_width = wk.shape[0]
    once = pl.Buffered(1)
    w_spec = pl.BlockSpec((key_width, half), lambda i, mp: (0, mp[0]), pipeline_mode=once)
    return pl.pallas_call(
        functools.partial(patch_kernel, width),
        name="patch_gradient",
        grid_spec=pltpu.PrefetchScalarGridSpec(
            num_scalar_prefetch=1,
            grid=(steps,),
            in_specs=[
                held(own.shape),
                held(other.shape),
                w_spec,
                w_spec,
                w_spec,
                w_spec,
                pl.BlockSpec((rows, half), lambda i, mp: (i, mp[0])),
                held(inv_row.shape),
                pl.BlockSpec((1, half), lambda i, mp: (0, mp[0])),
            ],
            out_specs=pl.BlockSpec((rows, half), lambda i, mp: (i, 0)),
            scratch_shapes=[
                pltpu.VMEM((patch_rows, 4 * key_width), BF16),
                pltpu.VMEM((patch_rows, 1), F32),
                pltpu.VMEM((patch_rows, 1), F32),
                pltpu.VMEM((4 * key_width, half), BF16),
            ],
        ),
        out_shape=jax.ShapeDtypeStruct((patch_rows, half), BF16),
        cost_estimate=pl.CostEstimate(
            flops=3_300_000_000, bytes_accessed=14_000_000, transcendentals=0
        ),
        compiler_params=pltpu.CompilerParams(vmem_limit_bytes=VMEM_LIMIT),
    )(mp_index, own, other, wk, wv, wk_other, wv_other, context, inv_row, gain_ctx.reshape(1, width))


def out_kernel(
    where_ref,
    a0_ref,
    a1_ref,
    a2_ref,
    a3_ref,
    d0_ref,
    d1_ref,
    d2_ref,
    d3_ref,
    e1_ref,
    e2_ref,
    e3_ref,
    first_going_ref,
    first_kept_ref,
    second_going_ref,
    second_kept_ref,
    attn_ref,
    line_ref,
    resid_ref,
):
    rows, heads = a0_ref.shape
    columns = line_ref.shape[1]
    own = columns // 4
    latent_rows = rows // 2
    mine = where_ref[1]
    for i, ref in enumerate((a0_ref, a1_ref, a2_ref, a3_ref)):
        attn_ref[i * rows : (i + 1) * rows, :] = ref[...]
    line_ref[:rows, :] = d0_ref[...]
    half = rows // 2
    for i, (ref, other) in enumerate(((d1_ref, e1_ref), (d2_ref, e2_ref), (d3_ref, e3_ref))):
        at = (i + 1) * rows
        line_ref[pl.ds(pl.multiple_of(at + mine * half, half), half), :] = ref[...]
        line_ref[pl.ds(pl.multiple_of(at + (1 - mine) * half, half), half), :] = other[...]
    resid = jnp.zeros((latent_rows, columns), F32)
    for i in range(8):
        resid = resid + line_ref[i * latent_rows : (i + 1) * latent_rows, :].astype(F32)
    resid_ref[...] = resid
    odd = where_ref[0] & 1
    upper = (where_ref[0] >> 1) & 1
    cut = heads // 2
    share = own // 2
    for turn in range(4):
        x_differs, y_differs = 1 - (turn & 1), 1 - (turn >> 1)
        owner = 2 * (upper ^ y_differs) + (odd ^ x_differs)
        at = pl.ds(pl.multiple_of(owner * own, own), own)
        grad = dot_general(attn_ref[...], line_ref[:, at], 0, 0).astype(BF16)
        mine_at = pl.ds(pl.multiple_of(owner * own + mine * share, share), share)
        part = resid_ref[:, mine_at]
        part = jnp.concatenate([part[: latent_rows // 2], part[latent_rows // 2 :]], axis=1)
        ref = first_going_ref if x_differs else first_kept_ref
        ref[1 - y_differs, :cut, :] = grad[:cut]
        ref[1 - y_differs, cut:, :] = part.astype(BF16)
        ref = second_going_ref if y_differs else second_kept_ref
        ref[1 - x_differs] = grad[cut:]


def out_call(where, attn, line, line_other):
    rows, heads = attn[0].shape
    columns = line[0].shape[1]
    own = columns // 4
    first = (2, heads // 2 + rows // 4, own)
    second = (2, heads // 2, own)
    shapes = [first, first, second, second]
    return pl.pallas_call(
        out_kernel,
        name="output_projection_gradient",
        grid_spec=pltpu.PrefetchScalarGridSpec(
            num_scalar_prefetch=1,
            grid=(1,),
            in_specs=[held(a.shape) for a in (*attn, *line, *line_other)],
            out_specs=[held(shape) for shape in shapes],
            scratch_shapes=[
                pltpu.VMEM((4 * rows, heads), BF16),
                pltpu.VMEM((4 * rows, columns), BF16),
                pltpu.VMEM((rows // 2, columns), F32),
            ],
        ),
        out_shape=[jax.ShapeDtypeStruct(shape, BF16) for shape in shapes],
        cost_estimate=pl.CostEstimate(
            flops=8 * rows * heads * columns, bytes_accessed=4_000_000, transcendentals=0
        ),
        compiler_params=pltpu.CompilerParams(vmem_limit_bytes=VMEM_LIMIT),
    )(where, *attn, *line, *line_other)


def latent_kernel(
    where_ref,
    sum_ref,
    got_ref,
    proj_ref,
    lat_ref,
    gain_ref,
    wq_ref,
    wk_ref,
    wv_ref,
    query_ref,
    pair_ref,
    message_ref,
    gain_out_ref,
    total_ref,
):
    latent_rows, width = lat_ref.shape
    own, query_width = wq_ref.shape
    key_width = wk_ref.shape[0]
    scaling = HD ** (-0.5)
    total_ref[...] = sum_ref[...] + got_ref[...].astype(F32)
    total = total_ref[:latent_rows, :]
    low = total.astype(BF16)
    at = pl.ds(pl.multiple_of(where_ref[0] * own, own), own)
    lat = lat_ref[...].astype(F32)
    inverse = lax.rsqrt(jnp.mean(lat * lat, axis=-1, keepdims=True) + EPSILON)
    gain = gain_ref[:, at]
    normed = (lat_ref[:, at].astype(F32) * inverse * gain).astype(BF16)
    query = dot_general(normed, low[:, :query_width], 0, 0) * scaling
    query_ref[...] = query
    pair = dot_general(low[:, query_width:], normed, 0, 0)
    pair_ref[...] = pair
    wq = wq_ref[...]
    wk = wk_ref[...]
    wv = wv_ref[...]
    gain_term = jnp.transpose(
        jnp.broadcast_to(jnp.sum(wq.astype(F32) * query, axis=1, keepdims=True), (own, 128))
    )[:1]
    gain_term = gain_term + jnp.sum(wk.astype(F32) * pair[:key_width], axis=0, keepdims=True)
    gain_term = gain_term + jnp.sum(wv.astype(F32) * pair[key_width:], axis=0, keepdims=True)
    scaled = (total[:, :query_width] * scaling).astype(BF16)
    d_lat = dot_general(scaled, wq, 1, 1)
    d_lat = d_lat + jnp.dot(
        low[:, query_width : query_width + key_width], wk, preferred_element_type=F32
    )
    d_lat = d_lat + jnp.dot(low[:, query_width + key_width :], wv, preferred_element_type=F32)
    message_ref[:latent_rows, :own] = d_lat
    message_ref[:latent_rows, own:] = jnp.broadcast_to(
        jnp.sum(total * proj_ref[...], axis=-1, keepdims=True), (latent_rows, 128)
    )
    message_ref[latent_rows:, :own] = jnp.broadcast_to(gain_term / gain, (8, own))
    message_ref[latent_rows:, own:] = jnp.zeros((8, 128), F32)
    part = width // 4
    share = own // 2
    first = where_ref[0] * own + where_ref[1] * share
    line = first // part
    mine = pl.ds(pl.multiple_of(first % part, share), share)
    gain_out_ref[...] = jnp.sum(
        jnp.where(
            lax.broadcasted_iota(jnp.int32, (8, share), 0) % 4 == line,
            total_ref[latent_rows : latent_rows + 8, mine],
            0.0,
        ),
        axis=0,
        keepdims=True,
    )


def latent_call(where, sums, got, proj, latents, gain_lat, w_query, wk, wv, own):
    latent_rows, width = latents.shape
    query_width = w_query.shape[1]
    key_width = wk.shape[0]
    return pl.pallas_call(
        latent_kernel,
        name="latent_gradients",
        grid_spec=pltpu.PrefetchScalarGridSpec(
            num_scalar_prefetch=1,
            grid=(1,),
            in_specs=[
                held(sums.shape),
                held(got.shape),
                held(proj.shape),
                held(latents.shape),
                held((1, width)),
                pl.BlockSpec((own, query_width), lambda i, w: (w[0], 0)),
                pl.BlockSpec((key_width, own), lambda i, w: (0, w[0])),
                pl.BlockSpec((key_width, own), lambda i, w: (0, w[0])),
            ],
            out_specs=[
                held((own, query_width)),
                held((2 * key_width, own)),
                held((latent_rows + 8, own + 128)),
                held((1, own // 2)),
            ],
            scratch_shapes=[pltpu.VMEM(sums.shape, F32)],
        ),
        out_shape=[
            jax.ShapeDtypeStruct((own, query_width), F32),
            jax.ShapeDtypeStruct((2 * key_width, own), F32),
            jax.ShapeDtypeStruct((latent_rows + 8, own + 128), F32),
            jax.ShapeDtypeStruct((1, own // 2), F32),
        ],
        cost_estimate=pl.CostEstimate(
            flops=100_000_000, bytes_accessed=3_000_000, transcendentals=0
        ),
        compiler_params=pltpu.CompilerParams(vmem_limit_bytes=VMEM_LIMIT),
    )(where, sums, got, proj, latents, gain_lat.reshape(1, width), w_query, wk, wv)


def plane_kernel(
    value_ref,
    value_got_ref,
    key_ref,
    key_got_ref,
    both_ref,
    low_ref,
    high_ref,
    kept_ref,
):
    key_width = value_ref.shape[1]
    for i, ref in enumerate((both_ref, low_ref, high_ref, kept_ref)):
        ref[:key_width, :] = (key_ref[i] + key_got_ref[i].astype(F32)).astype(ref.dtype)
        ref[key_width:, :] = (value_ref[i] + value_got_ref[i].astype(F32)).astype(ref.dtype)


def plane_call(value, value_got, key, key_got):
    _, key_width, own = value.shape
    shape = (2 * key_width, own)
    return pl.pallas_call(
        plane_kernel,
        name="plane_sum",
        out_shape=[jax.ShapeDtypeStruct(shape, BF16)] * 3 + [jax.ShapeDtypeStruct(shape, F32)],
        cost_estimate=pl.CostEstimate(flops=1_000_000, bytes_accessed=5_000_000, transcendentals=0),
        compiler_params=pltpu.CompilerParams(vmem_limit_bytes=VMEM_LIMIT),
    )(value, value_got, key, key_got)


def halve_kernel(kept_ref, got_ref, going_ref, rest_ref):
    half = going_ref.shape[0]
    going_ref[...] = (kept_ref[:half].astype(F32) + got_ref[:half].astype(F32)).astype(BF16)
    rest_ref[...] = kept_ref[half:].astype(F32) + got_ref[half:].astype(F32)


def halve_call(kept, got):
    shape = (kept.shape[0] // 2,) + kept.shape[1:]
    return pl.pallas_call(
        halve_kernel,
        name="halve_sum",
        out_shape=[jax.ShapeDtypeStruct(shape, BF16), jax.ShapeDtypeStruct(shape, F32)],
        cost_estimate=pl.CostEstimate(flops=1_000_000, bytes_accessed=4_000_000, transcendentals=0),
        compiler_params=pltpu.CompilerParams(vmem_limit_bytes=VMEM_LIMIT),
    )(kept, got)


def final_kernel(
    where_ref,
    kept_ref,
    both_ref,
    low_ref,
    high_ref,
    gain_ref,
    pair_ref,
    wk_ref,
    wv_ref,
    key_grad_ref,
    value_grad_ref,
    gain_term_ref,
):
    key_width = wk_ref.shape[0]
    total = (
        kept_ref[...]
        + both_ref[...].astype(F32)
        + low_ref[...].astype(F32)
        + high_ref[...].astype(F32)
    )
    term = jnp.sum(wk_ref[...].astype(F32) * total[:key_width], axis=0, keepdims=True)
    term = term + jnp.sum(wv_ref[...].astype(F32) * total[key_width:], axis=0, keepdims=True)
    gain_term_ref[...] = jnp.broadcast_to(term, gain_term_ref.shape)
    total = total * gain_ref[...] + pair_ref[...]
    key_grad_ref[...] = total[:key_width]
    value_grad_ref[...] = total[key_width:]


def final_call(where, kept, both, low, high, gain_ctx, pair, wk, wv):
    rows, own = kept.shape
    width = gain_ctx.shape[0]
    key_width = rows // 2
    w_spec = pl.BlockSpec((key_width, own), lambda i, w: (0, w[0]))
    return pl.pallas_call(
        final_kernel,
        name="key_value_gradients",
        grid_spec=pltpu.PrefetchScalarGridSpec(
            num_scalar_prefetch=1,
            grid=(1,),
            in_specs=[held(kept.shape)] * 4
            + [pl.BlockSpec((1, own), lambda i, w: (0, w[0])), held(pair.shape), w_spec, w_spec],
            out_specs=[held((key_width, own)), held((key_width, own)), held((8, own))],
        ),
        out_shape=[
            jax.ShapeDtypeStruct((key_width, own), F32),
            jax.ShapeDtypeStruct((key_width, own), F32),
            jax.ShapeDtypeStruct((8, own), F32),
        ],
        cost_estimate=pl.CostEstimate(flops=1_000_000, bytes_accessed=3_000_000, transcendentals=0),
        compiler_params=pltpu.CompilerParams(vmem_limit_bytes=VMEM_LIMIT),
    )(where, kept, both, low, high, gain_ctx.reshape(1, width), pair, wk, wv)


def add_halves(left, right):
    return left.astype(F32) + right.astype(F32)


def local(
    context,
    counts,
    routes,
    w_query,
    w_key,
    w_value,
    w_out,
    latents,
    gain_ctx,
    gain_lat,
    gain_out,
    cotangent,
):
    dp_count = lax.axis_size("dp")
    mp_index = lax.axis_index("mp")
    dp_index = lax.axis_index("dp")
    patch_rows, width = context.shape
    half_width = width // 2
    own_width = width // dp_count
    latent_rows = latents.shape[0]
    slot_count = cotangent.shape[0] // dp_count
    slots = dp_count * slot_count
    query_width = w_query.shape[1]

    def swap(array, turn):
        return lax.ppermute(array, "dp", [(i, i ^ turn) for i in range(dp_count)])

    def exchange(array):
        blocks = array.reshape(dp_count, slot_count, half_width)
        return lax.all_to_all(blocks, "dp", split_axis=0, concat_axis=0, tiled=True).reshape(
            slots, half_width
        )

    wk = w_key.T
    wv = w_value.T
    turned_routes = routes.reshape(1, -1)
    mp_scalar = mp_index.reshape(1)
    where = jnp.stack([dp_index, mp_index])

    returned = exchange(cotangent)
    w_out_other = swap_cores(w_out)
    wk_other = swap_cores(wk)
    wv_other = swap_cores(wv)

    (attn_rows, k, v, inv_row, q, lat_k, lat_v, lat_proj, p, lat_p) = forward_call(
        context, counts, w_query, wk, wv, latents, gain_ctx, gain_lat
    )
    attn_other = swap_cores(attn_rows)
    out_hat, out_inv, outgoing = branch_call(
        mp_scalar,
        attn_rows,
        attn_other,
        w_out,
        w_out_other,
        latents,
        gain_out,
        turned_routes,
        slots,
        slot_count,
    )
    routed = exchange(outgoing)

    returned, out_inv = lax.optimization_barrier((returned, out_inv))
    returned_other = swap_cores(returned)
    (
        line_own,
        line_low,
        line_high,
        line_both,
        pair,
        lat_terms,
        value_going,
        value_kept,
        key_going,
        key_kept,
    ) = backward_call(
        where,
        counts,
        returned,
        returned_other,
        out_hat,
        out_inv,
        gain_out,
        turned_routes,
        w_out,
        (k, v, q, lat_k, lat_v, p, lat_p, inv_row),
        context,
        slot_count,
    )

    value_got = swap(value_going, 1)
    key_got = swap(key_going, 2)

    pair_other = swap_cores(pair)
    ctx_grad = patch_call(
        mp_scalar, pair, pair_other, wk, wv, wk_other, wv_other, context, inv_row, gain_ctx
    )

    line_low, line_high, line_both, attn_line, pair_other = lax.optimization_barrier(
        (line_low, line_high, line_both, attn_rows, pair_other)
    )
    got_low = swap(line_low, 4)
    got_high = swap(line_high, 8)
    got_both = swap(line_both, 12)
    attn_high = swap(attn_line, 8)
    attn_low = swap(attn_line, 4)
    attn_both = swap(attn_high, 4)

    value_got, key_got, ctx_grad, routed = lax.optimization_barrier(
        (value_got, key_got, ctx_grad, routed)
    )
    key_kept = key_kept.reshape((8,) + key_kept.shape[2:])
    key_got = key_got.reshape((8,) + key_got.shape[2:])
    value_going = add_halves(value_kept[:4], value_got[:4]).astype(BF16)
    key_going = add_halves(key_kept[:4], key_got[:4]).astype(BF16)
    value_kept = add_halves(value_kept[4:], value_got[4:])
    key_kept = add_halves(key_kept[4:], key_got[4:])
    value_got = swap(value_going, 2)
    key_got = swap(key_going, 1)

    lat_terms, got_low, got_high, got_both, value_kept, key_kept = lax.optimization_barrier(
        (lat_terms, got_low, got_high, got_both, value_kept, key_kept)
    )
    lat_sum = lat_terms.astype(F32)
    for turn in (4, 8, 1):
        lat_sum = lat_sum + swap(lat_sum.astype(BF16), turn).astype(F32)
    lat_got = swap(lat_sum.astype(BF16), 2)

    first_going, first_kept, second_going, second_kept = out_call(
        where,
        (attn_rows, attn_low, attn_high, attn_both),
        (line_own, got_low, got_high, got_both),
        (swap_cores(got_low), swap_cores(got_high), swap_cores(got_both)),
    )

    both, low, high, kept = plane_call(value_kept, value_got, key_kept, key_got)
    first_going, second_going, kept = lax.optimization_barrier((first_going, second_going, kept))
    both = swap(both, 12)
    low = swap(low, 4)
    high = swap(high, 8)

    first_got = swap(first_going, 1)
    second_got = swap(second_going, 2)
    first = swap(add_halves(first_kept[0], first_got[0]).astype(BF16), 2)
    second = swap(add_halves(second_kept[0], second_got[0]).astype(BF16), 1)
    first = add_halves(first_kept[1], first_got[1]) + first.astype(F32)
    second = add_halves(second_kept[1], second_got[1]) + second.astype(F32)
    cut = query_width // 2
    grad_w_out = jnp.concatenate([first[:cut], second], axis=0)
    share = own_width // 2
    resid_sum = jnp.concatenate([first[cut:, :share], first[cut:, share:]], axis=0)

    grad_w_query, pair_lat, message, grad_gain_out = latent_call(
        where, lat_sum, lat_got, lat_proj, latents, gain_lat, w_query, wk, wv, own_width
    )
    message = message + swap_cores(message)

    grad_key, grad_value, gain_term = final_call(
        where, kept, both, low, high, gain_ctx, pair_lat, wk, wv
    )
    gain_term = gain_term + swap_cores(gain_term)

    def mine_of(array, axis):
        return lax.dynamic_slice_in_dim(
            array, dp_index * own_width + mp_index * share, share, axis
        )

    lat_hat, lat_inv = norm_parts(latents.astype(F32))
    mine = lax.dynamic_slice_in_dim(message, mp_index * share, share, 1)
    lat_dot = message[:latent_rows, own_width : own_width + 1] / width
    grad_latents = resid_sum + lat_inv * (
        mine_of(gain_lat, 0) * mine[:latent_rows] - mine_of(lat_hat, 1) * lat_dot
    )
    return (
        routed,
        ctx_grad,
        grad_w_query,
        grad_key.T,
        grad_value.T,
        grad_w_out,
        grad_latents,
        lax.dynamic_slice_in_dim(gain_term, mp_index * share, share, 1)[0],
        mine[latent_rows],
        grad_gain_out[0],
    )


def local_general(
    context,
    counts,
    routes,
    w_query,
    w_key,
    w_value,
    w_out,
    latents,
    gain_ctx,
    gain_lat,
    gain_out,
    cotangent,
):
    dp_count = lax.axis_size("dp")
    mp_count = lax.axis_size("mp")
    mp_index = lax.axis_index("mp")
    dp_index = lax.axis_index("dp")
    bits = dp_count.bit_length() - 1
    gather_bits = [bits - 1, bits - 2]
    scatter_bits = list(range(bits - 2))
    order_one = list(range(bits))
    order_two = [1, 0] + order_one[2:]
    patch_rows, width = context.shape
    half_width = width // mp_count
    own_width = width // dp_count
    head_local = w_query.shape[1] // HD
    group_local = w_key.shape[1] // HD
    per_group = head_local // group_local
    latent_rows = latents.shape[0]
    image_slots = counts.shape[1]
    out_rows = image_slots * latent_rows
    slot_count = cotangent.shape[0] // dp_count
    key_width = w_key.shape[1]
    query_width = w_query.shape[1]
    scaling = HD ** (-0.5)

    returned = lax.all_to_all(
        cotangent.reshape(dp_count, slot_count, half_width),
        "dp",
        split_axis=0,
        concat_axis=0,
        tiled=True,
    ).reshape(dp_count * slot_count, half_width)
    returned_other = swap_cores(returned)
    w_out_other = swap_cores(w_out)
    w_pair = jnp.concatenate([w_key, w_value], axis=1)
    w_pair_half = lax.dynamic_slice_in_dim(w_pair, mp_index * half_width, half_width, 0)
    w_pair_other = swap_cores(
        lax.dynamic_slice_in_dim(w_pair, (1 - mp_index) * half_width, half_width, 0)
    )

    patch_hat, patch_inv = norm_parts(context.astype(F32))
    normed_ctx = (patch_hat * gain_ctx).astype(BF16)
    key_f32 = jnp.dot(normed_ctx, w_key, preferred_element_type=F32)
    value_f32 = jnp.dot(normed_ctx, w_value, preferred_element_type=F32)
    key_rows = key_f32.astype(BF16)
    value_rows = value_f32.astype(BF16)
    lat_float = latents.astype(F32)
    lat_hat, lat_inv = norm_parts(lat_float)
    normed_lat = (lat_hat * gain_lat).astype(BF16)
    lat_key_f32 = jnp.dot(normed_lat, w_key, preferred_element_type=F32)
    lat_value_f32 = jnp.dot(normed_lat, w_value, preferred_element_type=F32)
    lat_keys = lat_key_f32.astype(BF16)
    lat_values = lat_value_f32.astype(BF16)
    query_f32 = jnp.dot(normed_lat, w_query, preferred_element_type=F32) * scaling
    query_rows = query_f32.astype(BF16)
    query_heads = query_rows.reshape(latent_rows, group_local, per_group, HD)
    key_heads = key_rows.reshape(patch_rows, group_local, HD)
    value_heads = value_rows.reshape(patch_rows, group_local, HD)
    lat_key_heads = lat_keys.reshape(latent_rows, group_local, HD)
    lat_value_heads = lat_values.reshape(latent_rows, group_local, HD)
    scores = jnp.einsum(
        "rkgd,tkd->kgrt", query_heads, key_heads, preferred_element_type=jnp.float32
    )
    lat_scores = jnp.einsum(
        "rkgd,skd->kgrs", query_heads, lat_key_heads, preferred_element_type=jnp.float32
    )
    position = jnp.arange(patch_rows, dtype=jnp.int32)
    image_count = counts[0]
    image_start = jnp.cumsum(image_count) - image_count
    member = (position[None, :] >= image_start[:, None]) & (
        position[None, :] < (image_start + image_count)[:, None]
    )
    member_wide = member[:, None, None, None, :]
    masked = jnp.where(member_wide, scores[None], NEGATIVE)
    row_max = jnp.maximum(
        jnp.max(masked, axis=-1, keepdims=True), jnp.max(lat_scores, axis=-1, keepdims=True)[None]
    )
    exponent = jnp.where(member_wide, jnp.exp(masked - row_max), 0.0)
    lat_exponent = jnp.exp(lat_scores[None] - row_max)
    total = jnp.sum(exponent, axis=-1, keepdims=True) + jnp.sum(
        lat_exponent, axis=-1, keepdims=True
    )
    attention = exponent / total
    lat_attention = lat_exponent / total
    attention_low = attention.astype(BF16)
    lat_attention_low = lat_attention.astype(BF16)
    mixed = jnp.einsum(
        "ikgrt,tkd->irkgd", attention_low, value_heads, preferred_element_type=jnp.float32
    )
    mixed = mixed + jnp.einsum(
        "ikgrs,skd->irkgd", lat_attention_low, lat_value_heads, preferred_element_type=jnp.float32
    )
    attn_rows = mixed.reshape(out_rows, query_width).astype(BF16)
    attn_other = swap_cores(attn_rows)
    branch = jnp.dot(attn_rows, w_out, preferred_element_type=F32) + jnp.dot(
        attn_other, w_out_other, preferred_element_type=F32
    )
    resid = jnp.tile(lat_float, (image_slots, 1)) + branch
    out_hat, out_inv = norm_parts(resid)
    final_rows = (out_hat * gain_out).astype(BF16)
    shard_of = routes[:, 0]
    shard_hot = (shard_of[:, None] == jnp.arange(dp_count, dtype=jnp.int32)[None, :]).astype(
        jnp.int32
    )
    rank = jnp.sum((jnp.cumsum(shard_hot, axis=0) - shard_hot) * shard_hot, axis=1)
    place = shard_of * slot_count + rank
    scatter_table = (
        jnp.arange(dp_count * slot_count, dtype=jnp.int32)[:, None] == place[None, :]
    ).astype(BF16)
    final_half = lax.dynamic_slice_in_dim(final_rows, mp_index * half_width, half_width, 1)
    outgoing = jnp.dot(scatter_table, final_half, preferred_element_type=F32).astype(BF16)
    routed = lax.all_to_all(
        outgoing.reshape(dp_count, slot_count, half_width),
        "dp",
        split_axis=0,
        concat_axis=0,
        tiled=True,
    ).reshape(dp_count * slot_count, half_width)

    attn_line = attn_rows
    for bit in gather_bits:
        attn_line = jnp.concatenate([attn_line, swap_bit(attn_line, bit, dp_count)], axis=0)

    first = jnp.where(mp_index == 0, returned, returned_other)
    second = jnp.where(mp_index == 0, returned_other, returned)
    d_final = jnp.concatenate(
        [dot_general(scatter_table, first, 0, 0), dot_general(scatter_table, second, 0, 0)], axis=1
    )
    d_hat = d_final * gain_out
    d_resid = out_inv * (d_hat - out_hat * jnp.mean(d_hat * out_hat, axis=1, keepdims=True))
    gain_out_term = jnp.sum(d_final * out_hat, axis=0)
    d_branch = d_resid.astype(BF16)
    d_attn = dot_general(d_branch, w_out, 1, 1).astype(BF16)

    d_attn_heads = d_attn.reshape(image_slots, latent_rows, group_local, per_group, HD)
    d_probs = jnp.einsum(
        "irkgd,tkd->ikgrt", d_attn_heads, value_heads, preferred_element_type=jnp.float32
    )
    d_lat_probs = jnp.einsum(
        "irkgd,skd->ikgrs", d_attn_heads, lat_value_heads, preferred_element_type=jnp.float32
    )
    row_delta = jnp.sum(attention * d_probs, axis=-1, keepdims=True) + jnp.sum(
        lat_attention * d_lat_probs, axis=-1, keepdims=True
    )
    d_scores = jnp.sum(attention * (d_probs - row_delta), axis=0).astype(BF16)
    d_lat_scores = jnp.sum(lat_attention * (d_lat_probs - row_delta), axis=0).astype(BF16)
    d_query = jnp.einsum("kgrt,tkd->rkgd", d_scores, key_heads, preferred_element_type=jnp.float32)
    d_query = d_query + jnp.einsum(
        "kgrs,skd->rkgd", d_lat_scores, lat_key_heads, preferred_element_type=jnp.float32
    )
    d_query = d_query.reshape(latent_rows, query_width).astype(BF16)
    d_keys = jnp.einsum("kgrt,rkgd->tkd", d_scores, query_heads, preferred_element_type=jnp.float32)
    d_keys = d_keys.reshape(patch_rows, key_width).astype(BF16)
    d_values = jnp.einsum(
        "ikgrt,irkgd->tkd", attention_low, d_attn_heads, preferred_element_type=jnp.float32
    )
    d_values = d_values.reshape(patch_rows, key_width).astype(BF16)
    d_lat_keys = jnp.einsum(
        "kgrs,rkgd->skd", d_lat_scores, query_heads, preferred_element_type=jnp.float32
    )
    d_lat_keys = d_lat_keys.reshape(latent_rows, key_width).astype(BF16)
    d_lat_values = jnp.einsum(
        "ikgrs,irkgd->skd", lat_attention_low, d_attn_heads, preferred_element_type=jnp.float32
    )
    d_lat_values = d_lat_values.reshape(latent_rows, key_width).astype(BF16)
    d_pair = jnp.concatenate([d_keys, d_values], axis=1)

    value_grad = dot_general(d_values, normed_ctx, 0, 0).reshape(key_width, dp_count, own_width)
    key_grad = dot_general(d_keys, normed_ctx, 0, 0).reshape(key_width, dp_count, own_width)
    value_block = scatter_sum(value_grad, order_one, dp_count)
    key_block = scatter_sum(key_grad, order_two, dp_count)

    row_dot = jnp.sum(d_keys.astype(F32) * key_f32, axis=1) + jnp.sum(
        d_values.astype(F32) * value_f32, axis=1
    )
    row_dot = (row_dot + swap_cores(row_dot)) / width
    d_pair_other = swap_cores(d_pair)
    d_ctx_in = dot_general(d_pair, w_pair_half, 1, 1) + dot_general(
        d_pair_other, w_pair_other, 1, 1
    )
    gain_ctx_half = lax.dynamic_slice_in_dim(gain_ctx, mp_index * half_width, half_width, 0)
    hat_half = lax.dynamic_slice_in_dim(patch_hat, mp_index * half_width, half_width, 1)
    ctx_grad = (patch_inv * (d_ctx_in * gain_ctx_half - hat_half * row_dot[:, None])).astype(BF16)

    high = gain_out_term.astype(BF16)
    low = (gain_out_term - high.astype(F32)).astype(BF16)
    lat_sum = jnp.concatenate(
        [
            d_query,
            d_lat_keys,
            d_lat_values,
            high.reshape(latent_rows, width // latent_rows),
            low.reshape(latent_rows, width // latent_rows),
        ],
        axis=1,
    ).astype(F32)
    for bit in gather_bits + scatter_bits:
        lat_sum = lat_sum + swap_bit(lat_sum.astype(BF16), bit, dp_count).astype(F32)
    pair_sum = lat_sum[:, query_width : query_width + 2 * key_width]
    query_sum = lat_sum[:, :query_width]
    gains_at = query_width + 2 * key_width
    gain_step = width // latent_rows
    gain_out_full = (
        lat_sum[:, gains_at : gains_at + gain_step]
        + lat_sum[:, gains_at + gain_step : gains_at + 2 * gain_step]
    ).reshape(width)

    plane = dp_count // 4
    row_half = out_rows // mp_count
    d_block = lax.dynamic_slice_in_dim(d_branch, mp_index * row_half, row_half, 0)
    d_line = d_block.reshape(1, row_half, 2, 2, plane * own_width)
    for step, bit in enumerate(gather_bits):
        mine = (dp_index >> bit) & 1
        going = lax.dynamic_index_in_dim(d_line, 1 - mine, 2, keepdims=False)
        kept = lax.dynamic_index_in_dim(d_line, mine, 2, keepdims=False)
        d_line = jnp.concatenate([kept, swap_bit(going, bit, dp_count)], axis=0)
    d_line_other = swap_cores(d_line)
    d_line = jnp.concatenate(
        [
            jnp.where(mp_index == 0, d_line, d_line_other),
            jnp.where(mp_index == 0, d_line_other, d_line),
        ],
        axis=1,
    )
    out_part = dot_general(attn_line, d_line.reshape(4 * out_rows, plane * own_width), 0, 0)
    resid_part = jnp.sum(
        d_line.astype(F32).reshape(4 * image_slots, latent_rows, plane * own_width), axis=0
    )
    resid_part = lax.dynamic_index_in_dim(
        resid_part.reshape(2, latent_rows // 2, plane, mp_count, own_width // mp_count),
        mp_index,
        3,
        keepdims=False,
    )
    resid_part = jnp.transpose(resid_part, (1, 2, 0, 3)).reshape(
        latent_rows // 2, plane, own_width
    )
    out_part = jnp.concatenate([out_part.reshape(query_width, plane, own_width), resid_part], axis=0)
    cut = out_part.shape[0] // 2
    out_block = jnp.concatenate(
        [
            scatter_sum(out_part[:cut], scatter_bits, dp_count),
            scatter_sum(out_part[cut:], [1, 0] + scatter_bits[2:], dp_count),
        ],
        axis=0,
    )
    grad_w_out = out_block[:query_width]
    resid_sum = (
        out_block[query_width:]
        .reshape(latent_rows // 2, 2, own_width // mp_count)
        .transpose(1, 0, 2)
        .reshape(latent_rows, own_width // mp_count)
    )

    def own(array, axis):
        return lax.dynamic_slice_in_dim(array, dp_index * own_width, own_width, axis)

    lat_own = own(normed_lat, 1)
    pair_ctx = jnp.concatenate([key_block, value_block], axis=0).T
    query_grad = dot_general(lat_own, query_sum.astype(BF16), 0, 0) * scaling
    pair_lat = dot_general(lat_own, pair_sum.astype(BF16), 0, 0)
    pair_all = pair_ctx + pair_lat
    wq_own = own(w_query, 0)
    pair_own = own(w_pair, 0)
    gain_ctx_part = jnp.sum(pair_own.astype(F32) * pair_ctx, axis=1) / own(gain_ctx, 0)
    gain_lat_part = (
        jnp.sum(wq_own.astype(F32) * query_grad, axis=1)
        + jnp.sum(pair_own.astype(F32) * pair_lat, axis=1)
    ) / own(gain_lat, 0)
    d_lat_part = dot_general(
        (query_sum * scaling).astype(BF16), wq_own, 1, 1
    ) + dot_general(pair_sum.astype(BF16), pair_own, 1, 1)
    lat_dot_part = (
        jnp.sum(query_sum * query_f32, axis=1)
        + jnp.sum(pair_sum[:, :key_width] * lat_key_f32, axis=1)
        + jnp.sum(pair_sum[:, key_width:] * lat_value_f32, axis=1)
    )
    small = jnp.concatenate(
        [
            d_lat_part,
            jnp.broadcast_to(lat_dot_part[:, None], (latent_rows, own_width)),
            jnp.broadcast_to(gain_ctx_part[None, :], (8, own_width)),
            jnp.broadcast_to(gain_lat_part[None, :], (8, own_width)),
        ],
        axis=0,
    )
    small = small + swap_cores(small)
    share = own_width // mp_count
    small = lax.dynamic_slice_in_dim(small, mp_index * share, share, 1)
    d_lat_in = small[:latent_rows]
    lat_dot = small[latent_rows : 2 * latent_rows] / width

    def mine_of(array, axis):
        return lax.dynamic_slice_in_dim(
            array, dp_index * own_width + mp_index * share, share, axis
        )

    grad_latents = resid_sum + lat_inv * (
        mine_of(gain_lat, 0) * d_lat_in - mine_of(lat_hat, 1) * lat_dot
    )
    return (
        routed,
        ctx_grad,
        query_grad,
        pair_all[:, :key_width],
        pair_all[:, key_width:],
        grad_w_out,
        grad_latents,
        small[2 * latent_rows],
        small[2 * latent_rows + 8],
        mine_of(gain_out_full, 0),
    )


def solution(mesh):
    placed = (
        P("dp", None),
        P("dp", None),
        P("dp", None),
        P(None, "mp"),
        P(None, "mp"),
        P(None, "mp"),
        P("mp", None),
        P(),
        P(),
        P(),
        P(),
        P("dp", "mp"),
    )
    return jax.shard_map(
        local if mesh.shape["dp"] == 16 else local_general,
        mesh=mesh,
        in_specs=placed,
        out_specs=(
            P("dp", "mp"),
            P("dp", "mp"),
            P("dp", "mp"),
            P("dp", "mp"),
            P("dp", "mp"),
            P("mp", "dp"),
            P(None, ("dp", "mp")),
            P(("dp", "mp")),
            P(("dp", "mp")),
            P(("dp", "mp")),
        ),
        check_vma=False,
    )
```

```python
import functools

import jax
import jax.numpy as jnp
from jax import lax
from jax.experimental import pallas as pl
from jax.experimental.pallas import tpu as pltpu
from jax.sharding import PartitionSpec as P

HD = 96
EPSILON = 1e-06
NEGATIVE = -1e30
BF16 = jnp.bfloat16
F32 = jnp.float32
VMEM_LIMIT = 63 << 20


def dot_general(left, right, left_dim, right_dim):
    return lax.dot_general(
        left, right, (((left_dim,), (right_dim,)), ((), ())), preferred_element_type=F32
    )


def norm_parts(values_in):
    inverse = lax.rsqrt(jnp.mean(values_in * values_in, axis=-1, keepdims=True) + EPSILON)
    return (values_in * inverse, inverse)


def swap_cores(array):
    return lax.ppermute(array, "mp", [(0, 1), (1, 0)])


def swap_bit(array, bit, dp_count):
    return lax.ppermute(array, "dp", [(i, i ^ (1 << bit)) for i in range(dp_count)])


def halve(array, axis, bit, dp_count):
    mine = (lax.axis_index("dp") >> bit) & 1
    going = lax.dynamic_index_in_dim(array, 1 - mine, axis, keepdims=False)
    kept = lax.dynamic_index_in_dim(array, mine, axis, keepdims=False)
    return kept.astype(F32) + swap_bit(going.astype(BF16), bit, dp_count).astype(F32)


def scatter_sum(array, bits, dp_count):
    rows, owners, columns = array.shape
    left = sorted(bits, reverse=True)
    array = array.reshape((rows,) + (2,) * len(left) + (columns,))
    for bit in bits:
        axis = left.index(bit)
        array = halve(array, 1 + axis, bit, dp_count)
        left.pop(axis)
    return array


def forward_kernel(
    counts_ref,
    gain_ctx_ref,
    gain_lat_ref,
    lat_hbm,
    wk_hbm,
    wv_hbm,
    x_hbm,
    wq_hbm,
    attn_hbm,
    k_hbm,
    v_hbm,
    inv_row_hbm,
    q_hbm,
    lk_hbm,
    lv_hbm,
    lat_proj_hbm,
    p_hbm,
    pl_hbm,
    lat_ref,
    wk_ref,
    wv_ref,
    x_ref,
    wq_ref,
    attn_ref,
    k_ref,
    v_ref,
    inv_row_ref,
    q_ref,
    lk_ref,
    lv_ref,
    lat_proj_ref,
    p_ref,
    pl_ref,
    lat_normed_ref,
    last_ref,
    gained_ref,
    sems,
    out_sems,
):
    patch_rows, width = x_ref.shape
    chunks = sems.shape[0] - 4
    rows = patch_rows // chunks
    groups = k_ref.shape[0]
    latent_rows = lat_ref.shape[0]
    key_width = wk_ref.shape[0]
    query_width = wq_ref.shape[1]
    per_group = query_width // key_width

    def fetch(source, target, i):
        return pltpu.make_async_copy(source, target, sems.at[i])

    def fetch_rows(i):
        at = pl.ds(i * rows, rows)
        return fetch(x_hbm.at[at], x_ref.at[at], i)

    weights = [
        fetch(source, target, chunks + i)
        for i, (source, target) in enumerate(
            ((lat_hbm, lat_ref), (wk_hbm, wk_ref), (wv_hbm, wv_ref), (wq_hbm, wq_ref))
        )
    ]
    for copy in weights[:3]:
        copy.start()
    blocks = [fetch_rows(i) for i in range(chunks)]
    for copy in blocks + weights[3:]:
        copy.start()
    results = {}
    for i, (name, source, target) in enumerate(
        (
            ("attn", attn_ref, attn_hbm),
            ("k", k_ref, k_hbm),
            ("v", v_ref, v_hbm),
            ("inv_row", inv_row_ref, inv_row_hbm),
            ("q", q_ref, q_hbm),
            ("lk", lk_ref, lk_hbm),
            ("lv", lv_ref, lv_hbm),
            ("lat_proj", lat_proj_ref, lat_proj_hbm),
            ("p0", p_ref.at[0], p_hbm.at[0]),
            ("p1", p_ref.at[1], p_hbm.at[1]),
            ("pl", pl_ref, pl_hbm),
        )
    ):
        results[name] = pltpu.make_async_copy(source, target, out_sems.at[i])

    weights[0].wait()
    lat = lat_ref[...].astype(F32)
    lat_inverse = lax.rsqrt(jnp.mean(lat * lat, axis=-1, keepdims=True) + EPSILON)
    lat_normed = lat * lat_inverse * gain_lat_ref[...]
    lat_normed_ref[...] = lat_normed.astype(BF16)
    last_ref[rows:, :] = (lat_normed / gain_ctx_ref[...]).astype(BF16)
    for i, ref in enumerate((wk_ref, wv_ref)):
        weights[1 + i].wait()
        gained_ref[i * key_width : (i + 1) * key_width, :] = (
            ref[...].astype(F32) * gain_ctx_ref[...]
        ).astype(BF16)
    for i in range(chunks):
        blocks[i].wait()
        at = slice(i * rows, (i + 1) * rows)
        squares = jnp.zeros((rows, 128), F32)
        for c in range(width // 128):
            part = x_ref[at, c * 128 : (c + 1) * 128].astype(F32)
            squares = squares + part * part
        inverse = lax.rsqrt(jnp.sum(squares, axis=-1, keepdims=True) / width + EPSILON)
        if i < chunks - 1:
            pair = dot_general(x_ref[at, :], gained_ref[...], 1, 1)
        else:
            last_ref[:rows, :] = x_ref[at, :]
            pair = dot_general(last_ref[...], gained_ref[...], 1, 1)
            projected = pair[rows:]
        pair = (pair[:rows] * inverse).astype(BF16)
        inv_row_ref[:, at] = jnp.transpose(jnp.broadcast_to(inverse, (rows, 128)))[:8]
        for g in range(groups):
            k_ref[g, at, :HD] = pair[:, g * HD : (g + 1) * HD]
            v_ref[g, at, :HD] = pair[:, key_width + g * HD : key_width + (g + 1) * HD]
    lat_proj_ref[:, query_width:] = projected
    for i, ref in enumerate((lk_ref, lv_ref)):
        for g in range(groups):
            at = i * key_width + g * HD
            ref[g, :, :HD] = projected[:, at : at + HD].astype(BF16)
    for name in ("k", "v", "inv_row", "lk", "lv"):
        results[name].start()
    weights[3].wait()
    query = jnp.dot(lat_normed_ref[...], wq_ref[...], preferred_element_type=F32) * HD ** (-0.5)
    lat_proj_ref[:, :query_width] = query
    first_count = counts_ref[0, 0]
    both_count = first_count + counts_ref[0, 1]
    position = lax.broadcasted_iota(jnp.int32, (1, patch_rows), 1)
    in_first = position < first_count
    in_second = jnp.logical_and(position >= first_count, position < both_count)
    rows_at = lax.broadcasted_iota(jnp.int32, (patch_rows, HD), 0)
    row_first = rows_at < first_count
    row_second = jnp.logical_and(rows_at >= first_count, rows_at < both_count)
    for g in range(groups):
        for h in range(per_group):
            head = g * per_group + h
            q_ref[g, h * latent_rows : (h + 1) * latent_rows, :HD] = query[
                :, head * HD : (head + 1) * HD
            ].astype(BF16)
    results["lat_proj"].start()
    results["q"].start()
    for g in range(groups):
        q = q_ref[g, :, :HD]
        scores = dot_general(q, k_ref[g, :, :HD], 1, 1)
        lat_scores = dot_general(q, lk_ref[g, :, :HD], 1, 1)
        lat_max = jnp.max(lat_scores, axis=-1, keepdims=True)
        max_first = jnp.maximum(
            jnp.max(jnp.where(in_first, scores, NEGATIVE), axis=-1, keepdims=True), lat_max
        )
        max_second = jnp.maximum(
            jnp.max(jnp.where(in_second, scores, NEGATIVE), axis=-1, keepdims=True), lat_max
        )
        masked = jnp.where(
            in_first, scores - max_first, jnp.where(in_second, scores - max_second, NEGATIVE)
        )
        exponent = jnp.exp(masked)
        lat_first = jnp.exp(lat_scores - max_first)
        lat_second = jnp.exp(lat_scores - max_second)
        sum_first = jnp.sum(
            jnp.where(in_first, exponent, 0.0), axis=-1, keepdims=True
        ) + jnp.sum(lat_first, axis=-1, keepdims=True)
        sum_second = jnp.sum(
            jnp.where(in_second, exponent, 0.0), axis=-1, keepdims=True
        ) + jnp.sum(lat_second, axis=-1, keepdims=True)
        per_first = 1.0 / sum_first
        per_second = 1.0 / sum_second
        p = (exponent * jnp.where(in_first, per_first, per_second)).astype(BF16)
        p_ref[g] = p
        results[f"p{g}"].start()
        lat_p_first = (lat_first * per_first).astype(BF16)
        lat_p_second = (lat_second * per_second).astype(BF16)
        pl_ref[g, :, :latent_rows] = lat_p_first
        pl_ref[g, :, latent_rows:] = lat_p_second
        v = v_ref[g, :, :HD]
        zero = jnp.zeros_like(v)
        lv = lv_ref[g, :, :HD]
        for j, (row_mask, lat_p) in enumerate(
            ((row_first, lat_p_first), (row_second, lat_p_second))
        ):
            mixed = jnp.dot(
                p, jnp.where(row_mask, v, zero), preferred_element_type=F32
            ) + jnp.dot(lat_p, lv, preferred_element_type=F32)
            mixed = mixed.astype(BF16)
            for h in range(per_group):
                head = g * per_group + h
                attn_ref[
                    j * latent_rows : (j + 1) * latent_rows, head * HD : (head + 1) * HD
                ] = mixed[h * latent_rows : (h + 1) * latent_rows]
    for name in ("attn", "pl"):
        results[name].start()
    for copy in results.values():
        copy.wait()


def whole(shape):
    return pl.BlockSpec(shape, lambda *_: (0,) * len(shape))


def held(shape):
    return pl.BlockSpec(shape, lambda *_: (0,) * len(shape), pipeline_mode=pl.Buffered(1))


def forward_call(context, counts, w_query, w_key, w_value, latents, gain_ctx, gain_lat):
    patch_rows, width = context.shape
    chunks = 4
    key_width = w_key.shape[0]
    query_width = w_query.shape[1]
    groups = key_width // HD
    latent_rows = latents.shape[0]
    stacked = query_width // key_width * latent_rows
    large = (latents, w_key, w_value, context, w_query)
    out = [
        ((2 * latent_rows, query_width), BF16),
        ((groups, patch_rows, 128), BF16),
        ((groups, patch_rows, 128), BF16),
        ((8, patch_rows), F32),
        ((groups, stacked, 128), BF16),
        ((groups, latent_rows, 128), BF16),
        ((groups, latent_rows, 128), BF16),
        ((latent_rows, query_width + 2 * key_width), F32),
        ((groups, stacked, patch_rows), BF16),
        ((groups, stacked, 2 * latent_rows), BF16),
    ]
    return pl.pallas_call(
        forward_kernel,
        name="forward_attention",
        in_specs=[
            pl.BlockSpec(memory_space=pltpu.SMEM),
            pl.BlockSpec(memory_space=pltpu.VMEM),
            pl.BlockSpec(memory_space=pltpu.VMEM),
        ]
        + [pl.BlockSpec(memory_space=pl.ANY)] * len(large),
        out_specs=[pl.BlockSpec(memory_space=pl.ANY)] * len(out),
        out_shape=[jax.ShapeDtypeStruct(shape, dtype) for shape, dtype in out],
        scratch_shapes=[pltpu.VMEM(a.shape, a.dtype) for a in large]
        + [pltpu.VMEM(shape, dtype) for shape, dtype in out]
        + [
            pltpu.VMEM((latent_rows, width), BF16),
            pltpu.VMEM((patch_rows // chunks + latent_rows, width), BF16),
            pltpu.VMEM((2 * key_width, width), BF16),
            pltpu.SemaphoreType.DMA((chunks + 4,)),
            pltpu.SemaphoreType.DMA((len(out) + 1,)),
        ],
        cost_estimate=pl.CostEstimate(
            flops=5_000_000_000, bytes_accessed=24_000_000, transcendentals=600_000
        ),
        compiler_params=pltpu.CompilerParams(vmem_limit_bytes=VMEM_LIMIT),
    )(counts, gain_ctx.reshape(1, width), gain_lat.reshape(1, width), *large)


def slots_of(routes_ref, slot_count, as_row):
    rows = routes_ref.shape[1]
    turned = jnp.broadcast_to(routes_ref[...].astype(F32), (rows, rows))
    shard = jnp.transpose(turned)
    down = lax.broadcasted_iota(jnp.int32, (rows, rows), 0)
    across = lax.broadcasted_iota(jnp.int32, (rows, rows), 1)
    same = shard == turned
    if as_row:
        rank = jnp.sum(jnp.where(same & (down < across), 1.0, 0.0), axis=0, keepdims=True)
        return (turned[:1] * slot_count + rank).astype(jnp.int32)
    rank = jnp.sum(jnp.where(same & (across < down), 1.0, 0.0), axis=1, keepdims=True)
    return (shard[:, :1] * slot_count + rank).astype(jnp.int32)


def branch_kernel(
    slot_count,
    where_ref,
    own_ref,
    other_ref,
    lat_ref,
    gain_ref,
    routes_ref,
    w_own_hbm,
    w_other_hbm,
    hat_hbm,
    inv_ref,
    out_ref,
    w_own_ref,
    w_other_ref,
    hat_ref,
    sems,
    hat_sem,
):
    rows, width = hat_ref.shape
    slots, half = out_ref.shape
    parts = sems.shape[1]
    size = width // parts
    copies = []
    for part in range(parts):
        at = pl.ds(part * size, size)
        for i, (source, target) in enumerate(
            ((w_own_hbm, w_own_ref), (w_other_hbm, w_other_ref))
        ):
            copies.append(
                pltpu.make_async_copy(source.at[:, at], target.at[:, at], sems.at[i, part])
            )
    for copy in copies:
        copy.start()
    place = slots_of(routes_ref, slot_count, True)
    table = jnp.where(
        lax.broadcasted_iota(jnp.int32, (slots, rows), 0) == place, 1.0, 0.0
    ).astype(BF16)
    squares = jnp.zeros((rows, 128), F32)
    for part in range(parts):
        at = slice(part * size, (part + 1) * size)
        copies[2 * part].wait()
        copies[2 * part + 1].wait()
        lat = lat_ref[:, at].astype(F32)
        resid = (
            jnp.concatenate([lat, lat], axis=0)
            + jnp.dot(own_ref[...], w_own_ref[:, at], preferred_element_type=F32)
            + jnp.dot(other_ref[...], w_other_ref[:, at], preferred_element_type=F32)
        )
        hat_ref[:, at] = resid
        for c in range(size // 128):
            piece = resid[:, c * 128 : (c + 1) * 128]
            squares = squares + piece * piece
    inverse = lax.rsqrt(jnp.sum(squares, axis=-1, keepdims=True) / width + EPSILON)
    inv_ref[...] = inverse
    hat_ref[...] = hat_ref[...] * inverse
    hat_copy = pltpu.make_async_copy(hat_ref, hat_hbm, hat_sem)
    hat_copy.start()
    at = pl.ds(pl.multiple_of(where_ref[1] * half, half), half)
    final = (hat_ref[:, at] * gain_ref[:, at]).astype(BF16)
    out_ref[...] = jnp.dot(table, final, preferred_element_type=F32).astype(BF16)
    hat_copy.wait()


def branch_call(where, own, other, w_own, w_other, latents, gain_out, routes, slots, slot_count):
    width = w_own.shape[1]
    rows, heads = own.shape
    parts = 4
    return pl.pallas_call(
        functools.partial(branch_kernel, slot_count),
        name="branch_norm",
        grid_spec=pltpu.PrefetchScalarGridSpec(
            num_scalar_prefetch=1,
            grid=(1,),
            in_specs=[
                held((rows, heads)),
                held((rows, heads)),
                held(latents.shape),
                held((1, width)),
                held((1, rows)),
                pl.BlockSpec(memory_space=pl.ANY),
                pl.BlockSpec(memory_space=pl.ANY),
            ],
            out_specs=[
                pl.BlockSpec(memory_space=pl.ANY),
                held((rows, 1)),
                held((slots, width // 2)),
            ],
            scratch_shapes=[
                pltpu.VMEM(w_own.shape, BF16),
                pltpu.VMEM(w_other.shape, BF16),
                pltpu.VMEM((rows, width), F32),
                pltpu.SemaphoreType.DMA((2, parts)),
                pltpu.SemaphoreType.DMA,
            ],
        ),
        out_shape=[
            jax.ShapeDtypeStruct((rows, width), F32),
            jax.ShapeDtypeStruct((rows, 1), F32),
            jax.ShapeDtypeStruct((slots, width // 2), BF16),
        ],
        cost_estimate=pl.CostEstimate(
            flops=2 * 2 * rows * heads * width, bytes_accessed=16_000_000, transcendentals=0
        ),
        compiler_params=pltpu.CompilerParams(vmem_limit_bytes=VMEM_LIMIT),
    )(where, own, other, latents, gain_out.reshape(1, width), routes, w_own, w_other)


def attention_backward(
    counts_ref,
    d_attn,
    k_ref,
    v_ref,
    q_ref,
    lk_ref,
    lv_ref,
    p_ref,
    pl_ref,
    inv_row_ref,
    pair_ref,
    scaled_ref,
    lat_ref,
):
    groups, patch_rows, _ = k_ref.shape
    latent_rows = lk_ref.shape[1]
    stacked = q_ref.shape[1]
    per_group = stacked // latent_rows
    key_width = groups * HD
    query_width = groups * per_group * HD
    first_count = counts_ref[0, 0]
    both_count = first_count + counts_ref[0, 1]
    position = lax.broadcasted_iota(jnp.int32, (1, patch_rows), 1)
    in_first = position < first_count
    rows_at = lax.broadcasted_iota(jnp.int32, (patch_rows, HD), 0)
    row_first = rows_at < first_count
    row_second = jnp.logical_and(rows_at >= first_count, rows_at < both_count)
    scale_row = inv_row_ref[:1]
    row_dot = jnp.zeros((1, patch_rows), F32)
    for g in range(groups):
        d_first = jnp.concatenate(
            [
                d_attn[:latent_rows, head * HD : (head + 1) * HD]
                for head in range(g * per_group, (g + 1) * per_group)
            ],
            axis=0,
        )
        d_second = jnp.concatenate(
            [
                d_attn[latent_rows:, head * HD : (head + 1) * HD]
                for head in range(g * per_group, (g + 1) * per_group)
            ],
            axis=0,
        )
        q = q_ref[g, :, :HD]
        k = k_ref[g, :, :HD]
        v = v_ref[g, :, :HD]
        lk = lk_ref[g, :, :HD]
        lv = lv_ref[g, :, :HD]
        p_low = p_ref[g]
        p = p_low.astype(F32)
        zero = jnp.zeros_like(v)
        d_p = dot_general(d_first, jnp.where(row_first, v, zero), 1, 1) + dot_general(
            d_second, jnp.where(row_second, v, zero), 1, 1
        )
        product = p * d_p
        lat_first = pl_ref[g, :, :latent_rows]
        lat_second = pl_ref[g, :, latent_rows:]
        d_lat_first = dot_general(d_first, lv, 1, 1)
        d_lat_second = dot_general(d_second, lv, 1, 1)
        lat_product_first = lat_first.astype(F32) * d_lat_first
        lat_product_second = lat_second.astype(F32) * d_lat_second
        whole_sum = jnp.sum(product, axis=-1, keepdims=True)
        first_sum = jnp.sum(jnp.where(in_first, product, 0.0), axis=-1, keepdims=True)
        delta_first = first_sum + jnp.sum(lat_product_first, axis=-1, keepdims=True)
        delta_second = (whole_sum - first_sum) + jnp.sum(
            lat_product_second, axis=-1, keepdims=True
        )
        ds = product - p * jnp.where(in_first, delta_first, delta_second)
        ds_low = ds.astype(BF16)
        dsl = (
            lat_product_first
            - lat_first.astype(F32) * delta_first
            + lat_product_second
            - lat_second.astype(F32) * delta_second
        ).astype(BF16)
        scores = dot_general(q, k, 1, 1)
        row_dot = row_dot + jnp.sum(ds * scores + product, axis=0, keepdims=True)
        d_q = (
            jnp.dot(ds_low, k, preferred_element_type=F32)
            + jnp.dot(dsl, lk, preferred_element_type=F32)
        ).astype(BF16)
        for h in range(per_group):
            head = g * per_group + h
            lat_ref[:latent_rows, head * HD : (head + 1) * HD] = d_q[
                h * latent_rows : (h + 1) * latent_rows
            ]
        d_k = dot_general(q, ds_low, 0, 0)
        nothing = jnp.zeros_like(p_low)
        d_v = dot_general(d_first, jnp.where(in_first, p_low, nothing), 0, 0) + dot_general(
            d_second, jnp.where(in_first, nothing, p_low), 0, 0
        )
        k_at = slice(g * HD, (g + 1) * HD)
        v_at = slice(key_width + g * HD, key_width + (g + 1) * HD)
        pair_ref[k_at, :] = d_k.astype(BF16)
        pair_ref[v_at, :] = d_v.astype(BF16)
        scaled_ref[k_at, :] = (d_k * scale_row).astype(BF16)
        scaled_ref[v_at, :] = (d_v * scale_row).astype(BF16)
        d_lk = dot_general(dsl, q, 0, 0)
        d_lv = dot_general(lat_first, d_first, 0, 0) + dot_general(lat_second, d_second, 0, 0)
        lat_ref[:latent_rows, query_width + g * HD : query_width + (g + 1) * HD] = d_lk.astype(BF16)
        at = query_width + key_width + g * HD
        lat_ref[:latent_rows, at : at + HD] = d_lv.astype(BF16)
    high = row_dot.astype(BF16)
    low = (row_dot - high.astype(F32)).astype(BF16)
    rest = pair_ref.shape[0] - 2 * key_width - 2
    pair_ref[2 * key_width :, :] = jnp.concatenate(
        [high.astype(F32), low.astype(F32), jnp.zeros((rest, patch_rows), F32)], axis=0
    ).astype(BF16)


def backward_kernel(
    slot_count,
    where_ref,
    counts_ref,
    inv_out_ref,
    gain_ref,
    routes_ref,
    inv_row_ref,
    attn_ref,
    got_own_hbm,
    got_other_hbm,
    hat_hbm,
    w_out_hbm,
    k_hbm,
    v_hbm,
    q_hbm,
    lk_hbm,
    lv_hbm,
    p_hbm,
    pl_hbm,
    x_hbm,
    line_own_hbm,
    line_high_hbm,
    pair_hbm,
    message_hbm,
    value_going_hbm,
    value_kept_hbm,
    key_going_hbm,
    key_kept_hbm,
    got_own_ref,
    got_other_ref,
    hat_ref,
    w_out_ref,
    k_ref,
    v_ref,
    q_ref,
    lk_ref,
    lv_ref,
    p_ref,
    pl_ref,
    x_ref,
    d_final_ref,
    branch_ref,
    scaled_ref,
    line_own_ref,
    line_high_ref,
    pair_ref,
    message_ref,
    value_ref,
    key_ref,
    sems,
    out_sems,
    value_sems,
    key_sems,
):
    sources = (
        got_own_hbm,
        got_other_hbm,
        hat_hbm,
        w_out_hbm,
        k_hbm,
        v_hbm,
        q_hbm,
        lk_hbm,
        lv_hbm,
        p_hbm,
        pl_hbm,
        x_hbm,
    )
    targets = (
        got_own_ref,
        got_other_ref,
        hat_ref,
        w_out_ref,
        k_ref,
        v_ref,
        q_ref,
        lk_ref,
        lv_ref,
        p_ref,
        pl_ref,
        x_ref,
    )
    copies = [
        pltpu.make_async_copy(source, target, sems.at[i])
        for i, (source, target) in enumerate(zip(sources, targets))
    ]
    for copy in copies[:4]:
        copy.start()
    rows, width = hat_ref.shape
    half = width // 2
    slots = got_own_ref.shape[0]
    latent_rows = lk_ref.shape[1]
    key_width, own = value_ref.shape[2:]
    lat_at = message_ref.shape[1] - (key_width * 2 + attn_ref.shape[1])
    lat_ref = message_ref.at[:, pl.ds(lat_at, message_ref.shape[1] - lat_at)]

    place = slots_of(routes_ref, slot_count, False)
    table = jnp.where(
        lax.broadcasted_iota(jnp.int32, (rows, slots), 1) == place, 1.0, 0.0
    ).astype(BF16)
    total = jnp.zeros((rows, 1), F32)
    chunk = 512
    for copy in copies[:3]:
        copy.wait()
    for copy in copies[4:]:
        copy.start()
    for got_ref, which in ((got_own_ref, where_ref[1]), (got_other_ref, 1 - where_ref[1])):
        for c in range(half // chunk):
            at = pl.ds(pl.multiple_of(which * half + c * chunk, chunk), chunk)
            d_final = jnp.dot(
                table, got_ref[:, c * chunk : (c + 1) * chunk], preferred_element_type=F32
            )
            product = d_final * hat_ref[:, at]
            total = total + jnp.sum(product * gain_ref[:, at], axis=-1, keepdims=True)
            d_final_ref[:, at] = d_final
    total = total / width
    lat_ref[latent_rows:, :] = jnp.zeros_like(lat_ref[latent_rows:, :])
    highs, lows = [], []
    part = width // 4
    for c in range(width // chunk):
        at = slice(c * chunk, (c + 1) * chunk)
        d_final = d_final_ref[:, at]
        hat = hat_ref[:, at]
        term = jnp.sum(d_final * hat, axis=0, keepdims=True)
        high = term.astype(BF16).astype(F32)
        highs.append(high)
        lows.append(term - high)
        branch_ref[:, at] = (
            inv_out_ref[...] * (d_final * gain_ref[:, at] - hat * total)
        ).astype(BF16)
    per_row = part // chunk
    lines = [
        jnp.concatenate(group[i * per_row : (i + 1) * per_row], axis=1)
        for group in (highs, lows)
        for i in range(4)
    ]
    lat_ref[latent_rows : latent_rows + 16, :part] = jnp.concatenate(
        lines + [jnp.zeros((8, part), F32)], axis=0
    ).astype(BF16)
    z = where_ref[0] >> 2
    some = pl.ds(pl.multiple_of(where_ref[1] * (rows // 2), rows // 2), rows // 2)
    line_own_ref[...] = branch_ref[:, pl.ds(pl.multiple_of(z * part, part), part)]
    message_ref[rows // 2 :, :lat_at] = jnp.zeros_like(message_ref[rows // 2 :, :lat_at])
    heads = attn_ref.shape[1]
    for turn, ref, first in (
        (1, message_ref, 0),
        (2, line_high_ref, 0),
        (3, line_high_ref, part + 2 * heads),
    ):
        ref[: rows // 2, first : first + part] = branch_ref[
            some, pl.ds(pl.multiple_of((z ^ turn) * part, part), part)
        ]
    for ref in (message_ref, line_high_ref):
        ref[: rows // 2, part : part + heads] = attn_ref[: rows // 2, :]
        ref[: rows // 2, part + heads : part + 2 * heads] = attn_ref[rows // 2 :, :]
    results = [
        pltpu.make_async_copy(source, target, out_sems.at[i])
        for i, (source, target) in enumerate(
            (
                (line_high_ref, line_high_hbm),
                (line_own_ref, line_own_hbm),
                (pair_ref, pair_hbm),
                (message_ref, message_hbm),
            )
        )
    ]
    for copy in results[:2]:
        copy.start()

    copies[3].wait()
    d_attn = dot_general(branch_ref[...], w_out_ref[...], 1, 1).astype(BF16)
    for copy in copies[4:11]:
        copy.wait()
    attention_backward(
        counts_ref,
        d_attn,
        k_ref,
        v_ref,
        q_ref,
        lk_ref,
        lv_ref,
        p_ref,
        pl_ref,
        inv_row_ref,
        pair_ref,
        scaled_ref,
        lat_ref,
    )
    for copy in results[2:]:
        copy.start()
    copies[11].wait()

    me = where_ref[0]
    odd = me & 1
    for j in range(8):
        y = ((me >> 1) & 1) ^ (1 - (j >> 2))
        z = (me >> 2) ^ ((1 - ((j >> 1) & 1)) + 2 * (1 - (j & 1)))
        first = 4 * z + 2 * y
        line = j & 3
        key_hbm = key_kept_hbm if j >> 2 else key_going_hbm
        grad = jnp.dot(
            scaled_ref[...],
            x_ref[:, pl.ds(pl.multiple_of(first * own, 2 * own), 2 * own)],
            preferred_element_type=F32,
        ).astype(BF16)
        for x_same, value_hbm in enumerate((value_going_hbm, value_kept_hbm)):
            block = jnp.where(odd == x_same, grad[:, own:], grad[:, :own])
            value_ref[x_same, j] = block[key_width:]
            key_ref[x_same, j] = block[:key_width]
            for copy in (
                pltpu.make_async_copy(
                    value_ref.at[x_same, j], value_hbm.at[j], value_sems.at[x_same, j]
                ),
                pltpu.make_async_copy(
                    key_ref.at[x_same, j], key_hbm.at[x_same, line], key_sems.at[x_same, j]
                ),
            ):
                copy.start()
                results.append(copy)
    for copy in results:
        copy.wait()


def backward_call(
    where, counts, attn, got_own, got_other, hat, inv_out, gain_out, routes, w_out, kept, context, slot_count
):
    k, v, q, lk, lv, p, lat_p, inv_row = kept
    rows, width = hat.shape
    patch_rows = context.shape[0]
    heads = w_out.shape[0]
    key_width = k.shape[0] * HD
    latent_rows = lk.shape[1]
    own = width // 16
    large = (got_own, got_other, hat, w_out, k, v, q, lk, lv, p, lat_p, context)
    out = [
        (rows, width // 4),
        (rows // 2, width // 2 + 2 * heads),
        (2 * key_width + 16, patch_rows),
        (latent_rows + 16, width // 4 + 3 * heads + 2 * key_width),
        (8, key_width, own),
        (8, key_width, own),
        (2, 4, key_width, own),
        (2, 4, key_width, own),
    ]
    return pl.pallas_call(
        functools.partial(backward_kernel, slot_count),
        name="attention_backward",
        grid_spec=pltpu.PrefetchScalarGridSpec(
            num_scalar_prefetch=1,
            grid=(1,),
            in_specs=[
                pl.BlockSpec(memory_space=pltpu.SMEM),
                held(inv_out.shape),
                held((1, width)),
                held(routes.shape),
                held(inv_row.shape),
                held(attn.shape),
            ]
            + [pl.BlockSpec(memory_space=pl.ANY)] * len(large),
            out_specs=[pl.BlockSpec(memory_space=pl.ANY)] * len(out),
            scratch_shapes=[pltpu.VMEM(a.shape, a.dtype) for a in large]
            + [
                pltpu.VMEM((rows, width), F32),
                pltpu.VMEM((rows, width), BF16),
                pltpu.VMEM((2 * key_width, patch_rows), BF16),
            ]
            + [pltpu.VMEM(shape, BF16) for shape in out[:4]]
            + [
                pltpu.VMEM((2, 8, key_width, own), BF16),
                pltpu.VMEM((2, 8, key_width, own), BF16),
                pltpu.SemaphoreType.DMA((len(large),)),
                pltpu.SemaphoreType.DMA((4,)),
                pltpu.SemaphoreType.DMA((2, 8)),
                pltpu.SemaphoreType.DMA((2, 8)),
            ],
        ),
        out_shape=[jax.ShapeDtypeStruct(shape, BF16) for shape in out],
        cost_estimate=pl.CostEstimate(
            flops=5_000_000_000, bytes_accessed=26_000_000, transcendentals=0
        ),
        compiler_params=pltpu.CompilerParams(vmem_limit_bytes=VMEM_LIMIT),
    )(where, counts, inv_out, gain_out.reshape(1, width), routes, inv_row, attn, *large)


def patch_kernel(
    width,
    where_ref,
    own_ref,
    other_ref,
    wk_ref,
    wv_ref,
    wk_other_ref,
    wv_other_ref,
    x_ref,
    inv_row_ref,
    gain_ref,
    out_ref,
    turned_ref,
    inv_ref,
    dot_ref,
    w_ref,
):
    step = pl.program_id(0)
    key_width = wk_ref.shape[0]
    patch_rows = turned_ref.shape[0]
    pair = 2 * key_width

    @pl.when(step == 0)
    def _():
        row_dot = jnp.zeros((patch_rows, 1), F32)
        for i, ref in enumerate((own_ref, other_ref)):
            turned = jnp.transpose(ref[...])
            turned_ref[:, i * pair : (i + 1) * pair] = turned[:, :pair]
            row_dot = row_dot + turned[:, pair : pair + 1].astype(F32)
            row_dot = row_dot + turned[:, pair + 1 : pair + 2].astype(F32)
        inverse = jnp.transpose(jnp.broadcast_to(inv_row_ref[:1], (128, patch_rows)))[:, :1]
        inv_ref[...] = inverse
        dot_ref[...] = row_dot * (inverse * inverse / width)
        for i, ref in enumerate((wk_ref, wv_ref, wk_other_ref, wv_other_ref)):
            w_ref[i * key_width : (i + 1) * key_width, :] = ref[...]

    rows = x_ref.shape[0]
    at = pl.ds(pl.multiple_of(step * rows, rows), rows)
    d_in = jnp.dot(turned_ref[at, :], w_ref[...], preferred_element_type=F32)
    out_ref[...] = (
        d_in * gain_ref[...] * inv_ref[at, :] - x_ref[...].astype(F32) * dot_ref[at, :]
    ).astype(BF16)


def patch_call(where, own, other, wk, wv, wk_other, wv_other, context, inv_row, gain_ctx):
    patch_rows, width = context.shape
    half = width // 2
    steps = 4
    rows = patch_rows // steps
    key_width = wk.shape[0]
    once = pl.Buffered(1)
    w_spec = pl.BlockSpec((key_width, half), lambda i, w: (0, w[1]), pipeline_mode=once)
    return pl.pallas_call(
        functools.partial(patch_kernel, width),
        name="patch_gradient",
        grid_spec=pltpu.PrefetchScalarGridSpec(
            num_scalar_prefetch=1,
            grid=(steps,),
            in_specs=[
                held(own.shape),
                held(other.shape),
                w_spec,
                w_spec,
                w_spec,
                w_spec,
                pl.BlockSpec((rows, half), lambda i, w: (i, w[1])),
                held(inv_row.shape),
                pl.BlockSpec((1, half), lambda i, w: (0, w[1])),
            ],
            out_specs=pl.BlockSpec((rows, half), lambda i, w: (i, 0)),
            scratch_shapes=[
                pltpu.VMEM((patch_rows, 4 * key_width), BF16),
                pltpu.VMEM((patch_rows, 1), F32),
                pltpu.VMEM((patch_rows, 1), F32),
                pltpu.VMEM((4 * key_width, half), BF16),
            ],
        ),
        out_shape=jax.ShapeDtypeStruct((patch_rows, half), BF16),
        cost_estimate=pl.CostEstimate(
            flops=3_300_000_000, bytes_accessed=14_000_000, transcendentals=0
        ),
        compiler_params=pltpu.CompilerParams(vmem_limit_bytes=VMEM_LIMIT),
    )(where, own, other, wk, wv, wk_other, wv_other, context, inv_row, gain_ctx.reshape(1, width))


def out_kernel(
    where_ref,
    attn_own_ref,
    line_own_ref,
    low_ref,
    high_ref,
    forwarded_ref,
    other_low_ref,
    other_high_ref,
    other_forwarded_ref,
    first_going_ref,
    first_kept_ref,
    second_going_ref,
    second_kept_ref,
    attn_ref,
    line_ref,
    resid_ref,
):
    rows, heads = attn_own_ref.shape
    columns = line_ref.shape[1]
    own = columns // 4
    latent_rows = rows // 2
    mine = where_ref[1]
    half = rows // 2
    attn_ref[:rows, :] = attn_own_ref[...]
    line_ref[:rows, :] = line_own_ref[...]
    for i, (ref, other, first) in enumerate(
        (
            (low_ref, other_low_ref, 0),
            (high_ref, other_high_ref, 0),
            (forwarded_ref, other_forwarded_ref, columns + 2 * heads),
        )
    ):
        at = (i + 1) * rows
        attn_ref[at : at + half, :] = ref[:half, columns : columns + heads]
        attn_ref[at + half : at + rows, :] = ref[:half, columns + heads : columns + 2 * heads]
        for holder, which in ((ref, mine), (other, 1 - mine)):
            line_ref[pl.ds(pl.multiple_of(at + which * half, half), half), :] = holder[
                :half, first : first + columns
            ]
    resid = jnp.zeros((latent_rows, columns), F32)
    for i in range(8):
        resid = resid + line_ref[i * latent_rows : (i + 1) * latent_rows, :].astype(F32)
    resid_ref[...] = resid
    odd = where_ref[0] & 1
    upper = (where_ref[0] >> 1) & 1
    share = own // 2
    cut = heads // 2
    for turn in range(4):
        x_differs, y_differs = 1 - (turn & 1), 1 - (turn >> 1)
        owner = 2 * (upper ^ y_differs) + (odd ^ x_differs)
        at = pl.ds(pl.multiple_of(owner * own, own), own)
        grad = dot_general(attn_ref[...], line_ref[:, at], 0, 0).astype(BF16)
        mine_at = pl.ds(pl.multiple_of(owner * own + mine * share, share), share)
        part = resid_ref[:, mine_at]
        part = jnp.concatenate([part[: latent_rows // 2], part[latent_rows // 2 :]], axis=1)
        ref = first_going_ref if x_differs else first_kept_ref
        ref[1 - y_differs, :cut, :] = grad[:cut]
        ref[1 - y_differs, cut:, :] = part.astype(BF16)
        ref = second_going_ref if y_differs else second_kept_ref
        ref[1 - x_differs] = grad[cut:]


def out_call(where, attn, line, received, others):
    rows, heads = attn.shape
    columns = line.shape[1]
    own = columns // 4
    first = (2, heads // 2 + rows // 4, own)
    second = (2, heads // 2, own)
    shapes = [first, first, second, second]
    operands = (attn, line, *received, *others)
    return pl.pallas_call(
        out_kernel,
        name="output_projection_gradient",
        grid_spec=pltpu.PrefetchScalarGridSpec(
            num_scalar_prefetch=1,
            grid=(1,),
            in_specs=[held(a.shape) for a in operands],
            out_specs=[held(shape) for shape in shapes],
            scratch_shapes=[
                pltpu.VMEM((4 * rows, heads), BF16),
                pltpu.VMEM((4 * rows, columns), BF16),
                pltpu.VMEM((rows // 2, columns), F32),
            ],
        ),
        out_shape=[jax.ShapeDtypeStruct(shape, BF16) for shape in shapes],
        cost_estimate=pl.CostEstimate(
            flops=8 * rows * heads * columns, bytes_accessed=4_000_000, transcendentals=0
        ),
        compiler_params=pltpu.CompilerParams(vmem_limit_bytes=VMEM_LIMIT),
    )(where, *operands)


def latent_kernel(
    where_ref,
    sum_ref,
    got_ref,
    proj_ref,
    lat_ref,
    gain_ref,
    wq_ref,
    wk_ref,
    wv_ref,
    routed_hbm,
    query_ref,
    pair_ref,
    message_ref,
    gain_out_ref,
    routed_out_hbm,
    total_ref,
    routed_ref,
    sems,
):
    arrive = pltpu.make_async_copy(routed_hbm, routed_ref, sems.at[0])
    leave = pltpu.make_async_copy(routed_ref, routed_out_hbm, sems.at[1])
    arrive.start()
    latent_rows, width = lat_ref.shape
    own, query_width = wq_ref.shape
    key_width = wk_ref.shape[0]
    scaling = HD ** (-0.5)
    total_ref[...] = sum_ref[...].astype(F32) + got_ref[...].astype(F32)
    total = total_ref[:latent_rows, :]
    low = total.astype(BF16)
    at = pl.ds(pl.multiple_of(where_ref[0] * own, own), own)
    lat = lat_ref[...].astype(F32)
    inverse = lax.rsqrt(jnp.mean(lat * lat, axis=-1, keepdims=True) + EPSILON)
    gain = gain_ref[:, at]
    normed = (lat_ref[:, at].astype(F32) * inverse * gain).astype(BF16)
    query = dot_general(normed, low[:, :query_width], 0, 0) * scaling
    query_ref[...] = query
    pair = dot_general(low[:, query_width:], normed, 0, 0)
    pair_ref[...] = pair
    wq = wq_ref[...]
    wk = wk_ref[...]
    wv = wv_ref[...]
    gain_term = jnp.transpose(
        jnp.broadcast_to(jnp.sum(wq.astype(F32) * query, axis=1, keepdims=True), (own, 128))
    )[:1]
    gain_term = gain_term + jnp.sum(wk.astype(F32) * pair[:key_width], axis=0, keepdims=True)
    gain_term = gain_term + jnp.sum(wv.astype(F32) * pair[key_width:], axis=0, keepdims=True)
    arrive.wait()
    leave.start()
    scaled = (total[:, :query_width] * scaling).astype(BF16)
    d_lat = dot_general(scaled, wq, 1, 1)
    d_lat = d_lat + jnp.dot(
        low[:, query_width : query_width + key_width], wk, preferred_element_type=F32
    )
    d_lat = d_lat + jnp.dot(low[:, query_width + key_width :], wv, preferred_element_type=F32)
    message_ref[:latent_rows, :own] = d_lat
    message_ref[:latent_rows, own:] = jnp.broadcast_to(
        jnp.sum(total * proj_ref[...], axis=-1, keepdims=True), (latent_rows, 128)
    )
    message_ref[latent_rows:, :own] = jnp.broadcast_to(gain_term / gain, (8, own))
    message_ref[latent_rows:, own:] = jnp.zeros((8, 128), F32)
    part = width // 4
    share = own // 2
    first = where_ref[0] * own + where_ref[1] * share
    line = first // part
    mine = pl.ds(pl.multiple_of(first % part, share), share)
    gain_out_ref[...] = jnp.sum(
        jnp.where(
            lax.broadcasted_iota(jnp.int32, (8, share), 0) % 4 == line,
            total_ref[latent_rows : latent_rows + 8, mine],
            0.0,
        ),
        axis=0,
        keepdims=True,
    )
    leave.wait()


def latent_call(where, sums, parts, proj, latents, gain_lat, w_query, wk, wv, own, routed):
    latent_rows, width = latents.shape
    query_width = w_query.shape[1]
    key_width = wk.shape[0]
    return pl.pallas_call(
        latent_kernel,
        name="latent_gradients",
        grid_spec=pltpu.PrefetchScalarGridSpec(
            num_scalar_prefetch=1,
            grid=(1,),
            in_specs=[
                held(sums.shape),
                *(held(part.shape) for part in parts),
                held(proj.shape),
                held(latents.shape),
                held((1, width)),
                pl.BlockSpec((own, query_width), lambda i, w: (w[0], 0)),
                pl.BlockSpec((key_width, own), lambda i, w: (0, w[0])),
                pl.BlockSpec((key_width, own), lambda i, w: (0, w[0])),
                pl.BlockSpec(memory_space=pl.ANY),
            ],
            out_specs=[
                held((own, query_width)),
                held((2 * key_width, own)),
                held((latent_rows + 8, own + 128)),
                held((1, own // 2)),
                pl.BlockSpec(memory_space=pl.ANY),
            ],
            scratch_shapes=[
                pltpu.VMEM(sums.shape, F32),
                pltpu.VMEM(routed.shape, BF16),
                pltpu.SemaphoreType.DMA((2,)),
            ],
        ),
        out_shape=[
            jax.ShapeDtypeStruct((own, query_width), F32),
            jax.ShapeDtypeStruct((2 * key_width, own), F32),
            jax.ShapeDtypeStruct((latent_rows + 8, own + 128), F32),
            jax.ShapeDtypeStruct((1, own // 2), F32),
            jax.ShapeDtypeStruct(routed.shape, BF16),
        ],
        cost_estimate=pl.CostEstimate(
            flops=100_000_000, bytes_accessed=3_000_000, transcendentals=0
        ),
        compiler_params=pltpu.CompilerParams(vmem_limit_bytes=VMEM_LIMIT),
    )(where, sums, *parts, proj, latents, gain_lat.reshape(1, width), w_query, wk, wv, routed)


def plane_kernel(
    value_ref,
    value_got_ref,
    value_last_ref,
    key_ref,
    key_got_ref,
    key_last_ref,
    going_ref,
    high_ref,
):
    key_width = value_ref.shape[-2]
    for i, ref in enumerate((going_ref.at[0], going_ref.at[1], high_ref)):
        for j, parts in enumerate(
            (
                (key_ref, key_got_ref, key_last_ref),
                (value_ref, value_got_ref, value_last_ref),
            )
        ):
            total = sum(part[i].astype(F32) for part in parts)
            ref[j * key_width : (j + 1) * key_width, :] = total.astype(ref.dtype)


def plane_call(value, value_got, value_last, key, key_got, key_last):
    _, key_width, own = value.shape
    upper = pl.BlockSpec((4, key_width, own), lambda i: (1, 0, 0))
    last = pl.BlockSpec((4, key_width, own), lambda i: (0, 0, 0))
    shape = (2 * key_width, own)
    return pl.pallas_call(
        plane_kernel,
        name="plane_sum",
        grid=(1,),
        in_specs=[upper, upper, last] * 2,
        out_specs=[held((2, *shape)), held(shape)],
        out_shape=[
            jax.ShapeDtypeStruct((2, *shape), BF16),
            jax.ShapeDtypeStruct(shape, F32),
        ],
        cost_estimate=pl.CostEstimate(flops=1_000_000, bytes_accessed=3_000_000, transcendentals=0),
        compiler_params=pltpu.CompilerParams(vmem_limit_bytes=VMEM_LIMIT),
    )(value, value_got, value_last, key, key_got, key_last)


def final_kernel(
    where_ref,
    value_ref,
    value_got_ref,
    value_last_ref,
    key_ref,
    key_got_ref,
    key_last_ref,
    low_ref,
    high_ref,
    gain_ref,
    pair_ref,
    wk_ref,
    wv_ref,
    key_grad_ref,
    value_grad_ref,
    gain_term_ref,
):
    key_width = wk_ref.shape[0]
    term = jnp.zeros((1, wk_ref.shape[1]), F32)
    for j, (w_ref, out_ref, parts) in enumerate(
        (
            (wk_ref, key_grad_ref, (key_ref, key_got_ref, key_last_ref)),
            (wv_ref, value_grad_ref, (value_ref, value_got_ref, value_last_ref)),
        )
    ):
        at = slice(j * key_width, (j + 1) * key_width)
        total = sum(part[0].astype(F32) for part in parts)
        total = total + low_ref[0, at, :].astype(F32) + high_ref[at, :].astype(F32)
        term = term + jnp.sum(w_ref[...].astype(F32) * total, axis=0, keepdims=True)
        out_ref[...] = total * gain_ref[...] + pair_ref[at, :]
    gain_term_ref[...] = jnp.broadcast_to(term, gain_term_ref.shape)


def final_call(where, value, value_got, value_last, key, key_got, key_last, line, gain_ctx, pair, wk, wv):
    rows, own = pair.shape
    width = gain_ctx.shape[0]
    key_width = rows // 2
    w_spec = pl.BlockSpec((key_width, own), lambda i, w: (0, w[0]))
    end = pl.BlockSpec((1, key_width, own), lambda i, w: (7, 0, 0))
    last = pl.BlockSpec((1, key_width, own), lambda i, w: (3, 0, 0))
    return pl.pallas_call(
        final_kernel,
        name="key_value_gradients",
        grid_spec=pltpu.PrefetchScalarGridSpec(
            num_scalar_prefetch=1,
            grid=(1,),
            in_specs=[end, end, last] * 2
            + [pl.BlockSpec((1, rows, own), lambda i, w: (1, 0, 0)), held(pair.shape)]
            + [pl.BlockSpec((1, own), lambda i, w: (0, w[0])), held(pair.shape), w_spec, w_spec],
            out_specs=[held((key_width, own)), held((key_width, own)), held((8, own))],
        ),
        out_shape=[
            jax.ShapeDtypeStruct((key_width, own), F32),
            jax.ShapeDtypeStruct((key_width, own), F32),
            jax.ShapeDtypeStruct((8, own), F32),
        ],
        cost_estimate=pl.CostEstimate(flops=1_000_000, bytes_accessed=3_000_000, transcendentals=0),
        compiler_params=pltpu.CompilerParams(vmem_limit_bytes=VMEM_LIMIT),
    )(
        where,
        value,
        value_got,
        value_last,
        key,
        key_got,
        key_last,
        *line,
        gain_ctx.reshape(1, width),
        pair,
        wk,
        wv,
    )


def out_final_kernel(
    where_ref,
    first_kept_ref,
    first_got_ref,
    first_last_ref,
    second_kept_ref,
    second_got_ref,
    second_last_ref,
    message_ref,
    message_got_ref,
    lat_ref,
    gain_ref,
    out_ref,
    latent_ref,
    gain_lat_ref,
):
    heads, own = out_ref.shape
    latent_rows, width = lat_ref.shape
    share = own // 2
    cut = heads // 2
    first = sum(
        part.astype(F32) for part in (first_kept_ref[0], first_got_ref[0], first_last_ref[...])
    )
    out_ref[:cut, :] = first[:cut]
    out_ref[cut:, :] = sum(
        part.astype(F32) for part in (second_kept_ref[0], second_got_ref[0], second_last_ref[...])
    )
    resid = first[cut:]
    resid = jnp.concatenate([resid[:, :share], resid[:, share:]], axis=0)
    mine = pl.ds(pl.multiple_of(where_ref[1] * share, share), share)
    d_lat = message_ref[:, mine] + message_got_ref[:, mine]
    lat_dot = message_ref[:latent_rows, own : own + 1] + message_got_ref[:latent_rows, own : own + 1]
    lat = lat_ref[...].astype(F32)
    inverse = lax.rsqrt(jnp.mean(lat * lat, axis=-1, keepdims=True) + EPSILON)
    at = pl.ds(pl.multiple_of(where_ref[0] * own + where_ref[1] * share, share), share)
    hat = lat_ref[:, at].astype(F32) * inverse
    latent_ref[...] = resid + inverse * (gain_ref[:, at] * d_lat[:latent_rows] - hat * (lat_dot / width))
    gain_lat_ref[...] = d_lat[latent_rows : latent_rows + 1]


def out_final_call(where, parts, message, message_got, latents, gain_lat):
    _, rows, own = parts[0].shape
    latent_rows, width = latents.shape
    heads = 2 * (rows - latent_rows // 2)
    shapes = [(heads, own), (latent_rows, own // 2), (1, own // 2)]
    return pl.pallas_call(
        out_final_kernel,
        name="output_gradient_sum",
        grid_spec=pltpu.PrefetchScalarGridSpec(
            num_scalar_prefetch=1,
            grid=(1,),
            in_specs=[
                pl.BlockSpec((1, *part.shape[1:]), lambda i, w: (1, 0, 0))
                if part.ndim == 3
                else held(part.shape)
                for part in parts
            ]
            + [held(a.shape) for a in (message, message_got, latents)]
            + [held((1, width))],
            out_specs=[held(shape) for shape in shapes],
        ),
        out_shape=[jax.ShapeDtypeStruct(shape, F32) for shape in shapes],
        cost_estimate=pl.CostEstimate(flops=1_000_000, bytes_accessed=3_000_000, transcendentals=0),
        compiler_params=pltpu.CompilerParams(vmem_limit_bytes=VMEM_LIMIT),
    )(where, *parts, message, message_got, latents, gain_lat.reshape(1, width))


def add_halves(left, right):
    return left.astype(F32) + right.astype(F32)


def local(
    context,
    counts,
    routes,
    w_query,
    w_key,
    w_value,
    w_out,
    latents,
    gain_ctx,
    gain_lat,
    gain_out,
    cotangent,
):
    dp_count = lax.axis_size("dp")
    mp_index = lax.axis_index("mp")
    dp_index = lax.axis_index("dp")
    patch_rows, width = context.shape
    half_width = width // 2
    own_width = width // dp_count
    latent_rows = latents.shape[0]
    slot_count = cotangent.shape[0] // dp_count
    slots = dp_count * slot_count
    query_width = w_query.shape[1]

    def swap(array, turn):
        return lax.ppermute(array, "dp", [(i, i ^ turn) for i in range(dp_count)])

    def exchange(array):
        blocks = array.reshape(dp_count, slot_count, half_width)
        return lax.all_to_all(blocks, "dp", split_axis=0, concat_axis=0, tiled=True).reshape(
            slots, half_width
        )

    wk = w_key.T
    wv = w_value.T
    turned_routes = routes.reshape(1, -1)
    where = jnp.stack([dp_index, mp_index])

    returned = exchange(cotangent)
    w_out_other = swap_cores(w_out)
    wk_other = swap_cores(wk)
    wv_other = swap_cores(wv)

    (attn_rows, k, v, inv_row, q, lat_k, lat_v, lat_proj, p, lat_p) = forward_call(
        context, counts, w_query, wk, wv, latents, gain_ctx, gain_lat
    )
    wk_other, wv_other, attn_rows = lax.optimization_barrier((wk_other, wv_other, attn_rows))
    attn_other = swap_cores(attn_rows)
    out_hat, out_inv, outgoing = branch_call(
        where,
        attn_rows,
        attn_other,
        w_out,
        w_out_other,
        latents,
        gain_out,
        turned_routes,
        slots,
        slot_count,
    )

    routed = exchange(outgoing)
    returned, out_inv = lax.optimization_barrier((returned, out_inv))
    returned_other = swap_cores(returned)
    backward = backward_call(
        where,
        counts,
        attn_rows,
        returned,
        returned_other,
        out_hat,
        out_inv,
        gain_out,
        turned_routes,
        w_out,
        (k, v, q, lat_k, lat_v, p, lat_p, inv_row),
        context,
        slot_count,
    )
    backward = lax.optimization_barrier(backward)
    (
        line_own,
        line_high,
        pair,
        message,
        value_going,
        value_kept,
        key_going,
        key_kept,
    ) = backward

    value_got = swap(value_going, 1)
    key_got = swap(key_going, 2)
    pair_other = swap_cores(pair)

    ctx_grad = patch_call(
        where, pair, pair_other, wk, wv, wk_other, wv_other, context, inv_row, gain_ctx
    )

    line_high, message, pair_other = lax.optimization_barrier((line_high, message, pair_other))
    got_high = swap(line_high, 8)
    got_low = swap(message, 4)
    value_got, key_got, ctx_grad, routed = lax.optimization_barrier(
        (value_got, key_got, ctx_grad, routed)
    )
    key_kept = key_kept.reshape((8,) + key_kept.shape[2:])
    key_got = key_got.reshape((8,) + key_got.shape[2:])
    value_going = add_halves(value_kept[:4], value_got[:4]).astype(BF16)
    key_going = add_halves(key_kept[:4], key_got[:4]).astype(BF16)
    value_last = swap(value_going, 2)
    key_last = swap(key_going, 1)

    got_low, got_high, value_going, key_going = lax.optimization_barrier(
        (got_low, got_high, value_going, key_going)
    )
    lat_at = message.shape[1] - lat_proj.shape[1]
    lat_sum = add_halves(message[:, lat_at:], got_low[:, lat_at:])
    lat_got = swap(lat_sum.astype(BF16), 8)
    forwarded = swap(got_high, 4)
    other_low = swap_cores(got_low)
    other_high = swap_cores(got_high)

    planes = plane_call(value_kept, value_got, value_last, key_kept, key_got, key_last)
    (going, high), lat_got, forwarded = lax.optimization_barrier((planes, lat_got, forwarded))
    low = swap(going, 4)
    other_forwarded = swap_cores(forwarded)
    lat_sum = add_halves(lat_sum, lat_got)
    lat_sum = add_halves(lat_sum, swap(lat_sum.astype(BF16), 1)).astype(BF16)
    lat_parts = (swap(lat_sum, 2),)

    first_going, first_kept, second_going, second_kept = out_call(
        where,
        attn_rows,
        line_own,
        (got_low, got_high, forwarded),
        (other_low, other_high, other_forwarded),
    )
    low, lat_parts, first_going, second_going = lax.optimization_barrier(
        (low, lat_parts, first_going, second_going)
    )
    high = swap(add_halves(high, low[0]).astype(BF16), 8)
    first_got = swap(first_going, 1)
    second_got = swap(second_going, 2)

    grad_w_query, pair_lat, message, grad_gain_out, routed = latent_call(
        where, lat_sum, lat_parts, lat_proj, latents, gain_lat, w_query, wk, wv, own_width, routed
    )
    first_got, second_got, high, message, pair_lat = lax.optimization_barrier(
        (first_got, second_got, high, message, pair_lat)
    )
    first_last = swap(add_halves(first_kept[0], first_got[0]).astype(BF16), 2)
    second_last = swap(add_halves(second_kept[0], second_got[0]).astype(BF16), 1)
    message_got = swap_cores(message)

    low, high, pair_lat, message_got = lax.optimization_barrier((low, high, pair_lat, message_got))
    grad_key, grad_value, gain_term = final_call(
        where,
        value_kept,
        value_got,
        value_last,
        key_kept,
        key_got,
        key_last,
        (low, high),
        gain_ctx,
        pair_lat,
        wk,
        wv,
    )
    gain_got = swap_cores(gain_term)
    first_last, second_last, gain_term = lax.optimization_barrier(
        (first_last, second_last, gain_term)
    )
    grad_w_out, grad_latents, grad_gain_lat = out_final_call(
        where,
        (first_kept, first_got, first_last, second_kept, second_got, second_last),
        message,
        message_got,
        latents,
        gain_lat,
    )
    share = own_width // 2
    return (
        routed,
        ctx_grad,
        grad_w_query,
        grad_key.T,
        grad_value.T,
        grad_w_out,
        grad_latents,
        lax.dynamic_slice_in_dim(gain_term + gain_got, mp_index * share, share, 1)[0],
        grad_gain_lat[0],
        grad_gain_out[0],
    )


def local_general(
    context,
    counts,
    routes,
    w_query,
    w_key,
    w_value,
    w_out,
    latents,
    gain_ctx,
    gain_lat,
    gain_out,
    cotangent,
):
    dp_count = lax.axis_size("dp")
    mp_count = lax.axis_size("mp")
    mp_index = lax.axis_index("mp")
    dp_index = lax.axis_index("dp")
    bits = dp_count.bit_length() - 1
    gather_bits = [bits - 1, bits - 2]
    scatter_bits = list(range(bits - 2))
    order_one = list(range(bits))
    order_two = [1, 0] + order_one[2:]
    patch_rows, width = context.shape
    half_width = width // mp_count
    own_width = width // dp_count
    head_local = w_query.shape[1] // HD
    group_local = w_key.shape[1] // HD
    per_group = head_local // group_local
    latent_rows = latents.shape[0]
    image_slots = counts.shape[1]
    out_rows = image_slots * latent_rows
    slot_count = cotangent.shape[0] // dp_count
    key_width = w_key.shape[1]
    query_width = w_query.shape[1]
    scaling = HD ** (-0.5)

    returned = lax.all_to_all(
        cotangent.reshape(dp_count, slot_count, half_width),
        "dp",
        split_axis=0,
        concat_axis=0,
        tiled=True,
    ).reshape(dp_count * slot_count, half_width)
    returned_other = swap_cores(returned)
    w_out_other = swap_cores(w_out)
    w_pair = jnp.concatenate([w_key, w_value], axis=1)
    w_pair_half = lax.dynamic_slice_in_dim(w_pair, mp_index * half_width, half_width, 0)
    w_pair_other = swap_cores(
        lax.dynamic_slice_in_dim(w_pair, (1 - mp_index) * half_width, half_width, 0)
    )

    patch_hat, patch_inv = norm_parts(context.astype(F32))
    normed_ctx = (patch_hat * gain_ctx).astype(BF16)
    key_f32 = jnp.dot(normed_ctx, w_key, preferred_element_type=F32)
    value_f32 = jnp.dot(normed_ctx, w_value, preferred_element_type=F32)
    key_rows = key_f32.astype(BF16)
    value_rows = value_f32.astype(BF16)
    lat_float = latents.astype(F32)
    lat_hat, lat_inv = norm_parts(lat_float)
    normed_lat = (lat_hat * gain_lat).astype(BF16)
    lat_key_f32 = jnp.dot(normed_lat, w_key, preferred_element_type=F32)
    lat_value_f32 = jnp.dot(normed_lat, w_value, preferred_element_type=F32)
    lat_keys = lat_key_f32.astype(BF16)
    lat_values = lat_value_f32.astype(BF16)
    query_f32 = jnp.dot(normed_lat, w_query, preferred_element_type=F32) * scaling
    query_rows = query_f32.astype(BF16)
    query_heads = query_rows.reshape(latent_rows, group_local, per_group, HD)
    key_heads = key_rows.reshape(patch_rows, group_local, HD)
    value_heads = value_rows.reshape(patch_rows, group_local, HD)
    lat_key_heads = lat_keys.reshape(latent_rows, group_local, HD)
    lat_value_heads = lat_values.reshape(latent_rows, group_local, HD)
    scores = jnp.einsum(
        "rkgd,tkd->kgrt", query_heads, key_heads, preferred_element_type=jnp.float32
    )
    lat_scores = jnp.einsum(
        "rkgd,skd->kgrs", query_heads, lat_key_heads, preferred_element_type=jnp.float32
    )
    position = jnp.arange(patch_rows, dtype=jnp.int32)
    image_count = counts[0]
    image_start = jnp.cumsum(image_count) - image_count
    member = (position[None, :] >= image_start[:, None]) & (
        position[None, :] < (image_start + image_count)[:, None]
    )
    member_wide = member[:, None, None, None, :]
    masked = jnp.where(member_wide, scores[None], NEGATIVE)
    row_max = jnp.maximum(
        jnp.max(masked, axis=-1, keepdims=True), jnp.max(lat_scores, axis=-1, keepdims=True)[None]
    )
    exponent = jnp.where(member_wide, jnp.exp(masked - row_max), 0.0)
    lat_exponent = jnp.exp(lat_scores[None] - row_max)
    total = jnp.sum(exponent, axis=-1, keepdims=True) + jnp.sum(
        lat_exponent, axis=-1, keepdims=True
    )
    attention = exponent / total
    lat_attention = lat_exponent / total
    attention_low = attention.astype(BF16)
    lat_attention_low = lat_attention.astype(BF16)
    mixed = jnp.einsum(
        "ikgrt,tkd->irkgd", attention_low, value_heads, preferred_element_type=jnp.float32
    )
    mixed = mixed + jnp.einsum(
        "ikgrs,skd->irkgd", lat_attention_low, lat_value_heads, preferred_element_type=jnp.float32
    )
    attn_rows = mixed.reshape(out_rows, query_width).astype(BF16)
    attn_other = swap_cores(attn_rows)
    branch = jnp.dot(attn_rows, w_out, preferred_element_type=F32) + jnp.dot(
        attn_other, w_out_other, preferred_element_type=F32
    )
    resid = jnp.tile(lat_float, (image_slots, 1)) + branch
    out_hat, out_inv = norm_parts(resid)
    final_rows = (out_hat * gain_out).astype(BF16)
    shard_of = routes[:, 0]
    shard_hot = (shard_of[:, None] == jnp.arange(dp_count, dtype=jnp.int32)[None, :]).astype(
        jnp.int32
    )
    rank = jnp.sum((jnp.cumsum(shard_hot, axis=0) - shard_hot) * shard_hot, axis=1)
    place = shard_of * slot_count + rank
    scatter_table = (
        jnp.arange(dp_count * slot_count, dtype=jnp.int32)[:, None] == place[None, :]
    ).astype(BF16)
    final_half = lax.dynamic_slice_in_dim(final_rows, mp_index * half_width, half_width, 1)
    outgoing = jnp.dot(scatter_table, final_half, preferred_element_type=F32).astype(BF16)
    routed = lax.all_to_all(
        outgoing.reshape(dp_count, slot_count, half_width),
        "dp",
        split_axis=0,
        concat_axis=0,
        tiled=True,
    ).reshape(dp_count * slot_count, half_width)

    attn_line = attn_rows
    for bit in gather_bits:
        attn_line = jnp.concatenate([attn_line, swap_bit(attn_line, bit, dp_count)], axis=0)

    first = jnp.where(mp_index == 0, returned, returned_other)
    second = jnp.where(mp_index == 0, returned_other, returned)
    d_final = jnp.concatenate(
        [dot_general(scatter_table, first, 0, 0), dot_general(scatter_table, second, 0, 0)], axis=1
    )
    d_hat = d_final * gain_out
    d_resid = out_inv * (d_hat - out_hat * jnp.mean(d_hat * out_hat, axis=1, keepdims=True))
    gain_out_term = jnp.sum(d_final * out_hat, axis=0)
    d_branch = d_resid.astype(BF16)
    d_attn = dot_general(d_branch, w_out, 1, 1).astype(BF16)

    d_attn_heads = d_attn.reshape(image_slots, latent_rows, group_local, per_group, HD)
    d_probs = jnp.einsum(
        "irkgd,tkd->ikgrt", d_attn_heads, value_heads, preferred_element_type=jnp.float32
    )
    d_lat_probs = jnp.einsum(
        "irkgd,skd->ikgrs", d_attn_heads, lat_value_heads, preferred_element_type=jnp.float32
    )
    row_delta = jnp.sum(attention * d_probs, axis=-1, keepdims=True) + jnp.sum(
        lat_attention * d_lat_probs, axis=-1, keepdims=True
    )
    d_scores = jnp.sum(attention * (d_probs - row_delta), axis=0).astype(BF16)
    d_lat_scores = jnp.sum(lat_attention * (d_lat_probs - row_delta), axis=0).astype(BF16)
    d_query = jnp.einsum("kgrt,tkd->rkgd", d_scores, key_heads, preferred_element_type=jnp.float32)
    d_query = d_query + jnp.einsum(
        "kgrs,skd->rkgd", d_lat_scores, lat_key_heads, preferred_element_type=jnp.float32
    )
    d_query = d_query.reshape(latent_rows, query_width).astype(BF16)
    d_keys = jnp.einsum("kgrt,rkgd->tkd", d_scores, query_heads, preferred_element_type=jnp.float32)
    d_keys = d_keys.reshape(patch_rows, key_width).astype(BF16)
    d_values = jnp.einsum(
        "ikgrt,irkgd->tkd", attention_low, d_attn_heads, preferred_element_type=jnp.float32
    )
    d_values = d_values.reshape(patch_rows, key_width).astype(BF16)
    d_lat_keys = jnp.einsum(
        "kgrs,rkgd->skd", d_lat_scores, query_heads, preferred_element_type=jnp.float32
    )
    d_lat_keys = d_lat_keys.reshape(latent_rows, key_width).astype(BF16)
    d_lat_values = jnp.einsum(
        "ikgrs,irkgd->skd", lat_attention_low, d_attn_heads, preferred_element_type=jnp.float32
    )
    d_lat_values = d_lat_values.reshape(latent_rows, key_width).astype(BF16)
    d_pair = jnp.concatenate([d_keys, d_values], axis=1)

    value_grad = dot_general(d_values, normed_ctx, 0, 0).reshape(key_width, dp_count, own_width)
    key_grad = dot_general(d_keys, normed_ctx, 0, 0).reshape(key_width, dp_count, own_width)
    value_block = scatter_sum(value_grad, order_one, dp_count)
    key_block = scatter_sum(key_grad, order_two, dp_count)

    row_dot = jnp.sum(d_keys.astype(F32) * key_f32, axis=1) + jnp.sum(
        d_values.astype(F32) * value_f32, axis=1
    )
    row_dot = (row_dot + swap_cores(row_dot)) / width
    d_pair_other = swap_cores(d_pair)
    d_ctx_in = dot_general(d_pair, w_pair_half, 1, 1) + dot_general(
        d_pair_other, w_pair_other, 1, 1
    )
    gain_ctx_half = lax.dynamic_slice_in_dim(gain_ctx, mp_index * half_width, half_width, 0)
    hat_half = lax.dynamic_slice_in_dim(patch_hat, mp_index * half_width, half_width, 1)
    ctx_grad = (patch_inv * (d_ctx_in * gain_ctx_half - hat_half * row_dot[:, None])).astype(BF16)

    high = gain_out_term.astype(BF16)
    low = (gain_out_term - high.astype(F32)).astype(BF16)
    lat_sum = jnp.concatenate(
        [
            d_query,
            d_lat_keys,
            d_lat_values,
            high.reshape(latent_rows, width // latent_rows),
            low.reshape(latent_rows, width // latent_rows),
        ],
        axis=1,
    ).astype(F32)
    for bit in gather_bits + scatter_bits:
        lat_sum = lat_sum + swap_bit(lat_sum.astype(BF16), bit, dp_count).astype(F32)
    pair_sum = lat_sum[:, query_width : query_width + 2 * key_width]
    query_sum = lat_sum[:, :query_width]
    gains_at = query_width + 2 * key_width
    gain_step = width // latent_rows
    gain_out_full = (
        lat_sum[:, gains_at : gains_at + gain_step]
        + lat_sum[:, gains_at + gain_step : gains_at + 2 * gain_step]
    ).reshape(width)

    plane = dp_count // 4
    row_half = out_rows // mp_count
    d_block = lax.dynamic_slice_in_dim(d_branch, mp_index * row_half, row_half, 0)
    d_line = d_block.reshape(1, row_half, 2, 2, plane * own_width)
    for step, bit in enumerate(gather_bits):
        mine = (dp_index >> bit) & 1
        going = lax.dynamic_index_in_dim(d_line, 1 - mine, 2, keepdims=False)
        kept = lax.dynamic_index_in_dim(d_line, mine, 2, keepdims=False)
        d_line = jnp.concatenate([kept, swap_bit(going, bit, dp_count)], axis=0)
    d_line_other = swap_cores(d_line)
    d_line = jnp.concatenate(
        [
            jnp.where(mp_index == 0, d_line, d_line_other),
            jnp.where(mp_index == 0, d_line_other, d_line),
        ],
        axis=1,
    )
    out_part = dot_general(attn_line, d_line.reshape(4 * out_rows, plane * own_width), 0, 0)
    resid_part = jnp.sum(
        d_line.astype(F32).reshape(4 * image_slots, latent_rows, plane * own_width), axis=0
    )
    resid_part = lax.dynamic_index_in_dim(
        resid_part.reshape(2, latent_rows // 2, plane, mp_count, own_width // mp_count),
        mp_index,
        3,
        keepdims=False,
    )
    resid_part = jnp.transpose(resid_part, (1, 2, 0, 3)).reshape(
        latent_rows // 2, plane, own_width
    )
    out_part = jnp.concatenate([out_part.reshape(query_width, plane, own_width), resid_part], axis=0)
    cut = out_part.shape[0] // 2
    out_block = jnp.concatenate(
        [
            scatter_sum(out_part[:cut], scatter_bits, dp_count),
            scatter_sum(out_part[cut:], [1, 0] + scatter_bits[2:], dp_count),
        ],
        axis=0,
    )
    grad_w_out = out_block[:query_width]
    resid_sum = (
        out_block[query_width:]
        .reshape(latent_rows // 2, 2, own_width // mp_count)
        .transpose(1, 0, 2)
        .reshape(latent_rows, own_width // mp_count)
    )

    def own(array, axis):
        return lax.dynamic_slice_in_dim(array, dp_index * own_width, own_width, axis)

    lat_own = own(normed_lat, 1)
    pair_ctx = jnp.concatenate([key_block, value_block], axis=0).T
    query_grad = dot_general(lat_own, query_sum.astype(BF16), 0, 0) * scaling
    pair_lat = dot_general(lat_own, pair_sum.astype(BF16), 0, 0)
    pair_all = pair_ctx + pair_lat
    wq_own = own(w_query, 0)
    pair_own = own(w_pair, 0)
    gain_ctx_part = jnp.sum(pair_own.astype(F32) * pair_ctx, axis=1) / own(gain_ctx, 0)
    gain_lat_part = (
        jnp.sum(wq_own.astype(F32) * query_grad, axis=1)
        + jnp.sum(pair_own.astype(F32) * pair_lat, axis=1)
    ) / own(gain_lat, 0)
    d_lat_part = dot_general(
        (query_sum * scaling).astype(BF16), wq_own, 1, 1
    ) + dot_general(pair_sum.astype(BF16), pair_own, 1, 1)
    lat_dot_part = (
        jnp.sum(query_sum * query_f32, axis=1)
        + jnp.sum(pair_sum[:, :key_width] * lat_key_f32, axis=1)
        + jnp.sum(pair_sum[:, key_width:] * lat_value_f32, axis=1)
    )
    small = jnp.concatenate(
        [
            d_lat_part,
            jnp.broadcast_to(lat_dot_part[:, None], (latent_rows, own_width)),
            jnp.broadcast_to(gain_ctx_part[None, :], (8, own_width)),
            jnp.broadcast_to(gain_lat_part[None, :], (8, own_width)),
        ],
        axis=0,
    )
    small = small + swap_cores(small)
    share = own_width // mp_count
    small = lax.dynamic_slice_in_dim(small, mp_index * share, share, 1)
    d_lat_in = small[:latent_rows]
    lat_dot = small[latent_rows : 2 * latent_rows] / width

    def mine_of(array, axis):
        return lax.dynamic_slice_in_dim(
            array, dp_index * own_width + mp_index * share, share, axis
        )

    grad_latents = resid_sum + lat_inv * (
        mine_of(gain_lat, 0) * d_lat_in - mine_of(lat_hat, 1) * lat_dot
    )
    return (
        routed,
        ctx_grad,
        query_grad,
        pair_all[:, :key_width],
        pair_all[:, key_width:],
        grad_w_out,
        grad_latents,
        small[2 * latent_rows],
        small[2 * latent_rows + 8],
        mine_of(gain_out_full, 0),
    )


def solution(mesh):
    placed = (
        P("dp", None),
        P("dp", None),
        P("dp", None),
        P(None, "mp"),
        P(None, "mp"),
        P(None, "mp"),
        P("mp", None),
        P(),
        P(),
        P(),
        P(),
        P("dp", "mp"),
    )
    return jax.shard_map(
        local if mesh.shape["dp"] == 16 else local_general,
        mesh=mesh,
        in_specs=placed,
        out_specs=(
            P("dp", "mp"),
            P("dp", "mp"),
            P("dp", "mp"),
            P("dp", "mp"),
            P("dp", "mp"),
            P("mp", "dp"),
            P(None, ("dp", "mp")),
            P(("dp", "mp")),
            P(("dp", "mp")),
            P(("dp", "mp")),
        ),
        check_vma=False,
    )
```

```python
import functools

import jax
import jax.numpy as jnp
from jax import lax
from jax.experimental import pallas as pl
from jax.experimental.pallas import tpu as pltpu
from jax.sharding import PartitionSpec as P

HD = 96
EPSILON = 1e-06
NEGATIVE = -1e30
BF16 = jnp.bfloat16
F32 = jnp.float32
VMEM_LIMIT = 63 << 20


def dot_general(left, right, left_dim, right_dim):
    return lax.dot_general(
        left, right, (((left_dim,), (right_dim,)), ((), ())), preferred_element_type=F32
    )


def norm_parts(values_in):
    inverse = lax.rsqrt(jnp.mean(values_in * values_in, axis=-1, keepdims=True) + EPSILON)
    return (values_in * inverse, inverse)


def swap_cores(array):
    return lax.ppermute(array, "mp", [(0, 1), (1, 0)])


def swap_bit(array, bit, dp_count):
    return lax.ppermute(array, "dp", [(i, i ^ (1 << bit)) for i in range(dp_count)])


def halve(array, axis, bit, dp_count):
    mine = (lax.axis_index("dp") >> bit) & 1
    going = lax.dynamic_index_in_dim(array, 1 - mine, axis, keepdims=False)
    kept = lax.dynamic_index_in_dim(array, mine, axis, keepdims=False)
    return kept.astype(F32) + swap_bit(going.astype(BF16), bit, dp_count).astype(F32)


def scatter_sum(array, bits, dp_count):
    rows, owners, columns = array.shape
    left = sorted(bits, reverse=True)
    array = array.reshape((rows,) + (2,) * len(left) + (columns,))
    for bit in bits:
        axis = left.index(bit)
        array = halve(array, 1 + axis, bit, dp_count)
        left.pop(axis)
    return array


def forward_kernel(
    counts_ref,
    gain_ctx_hbm,
    gain_lat_hbm,
    lat_hbm,
    wk_hbm,
    wv_hbm,
    x_hbm,
    wq_hbm,
    attn_hbm,
    k_hbm,
    v_hbm,
    inv_row_hbm,
    q_hbm,
    lk_hbm,
    lv_hbm,
    lat_proj_hbm,
    p_hbm,
    pl_hbm,
    gain_ctx_ref,
    gain_lat_ref,
    lat_ref,
    wk_ref,
    wv_ref,
    x_ref,
    wq_ref,
    attn_ref,
    k_ref,
    v_ref,
    inv_row_ref,
    q_ref,
    lk_ref,
    lv_ref,
    lat_proj_ref,
    p_ref,
    pl_ref,
    lat_normed_ref,
    last_ref,
    gained_ref,
    sems,
    out_sems,
):
    patch_rows, width = x_ref.shape
    chunks = sems.shape[0] - 6
    rows = patch_rows // chunks
    groups = k_ref.shape[0]
    latent_rows = lat_ref.shape[0]
    key_width = wk_ref.shape[0]
    query_width = wq_ref.shape[1]
    per_group = query_width // key_width

    def fetch(source, target, i):
        return pltpu.make_async_copy(source, target, sems.at[i])

    def fetch_rows(i):
        at = pl.ds(i * rows, rows)
        return fetch(x_hbm.at[at], x_ref.at[at], i)

    weights = [
        fetch(source, target, chunks + i)
        for i, (source, target) in enumerate(
            ((lat_hbm, lat_ref), (wk_hbm, wk_ref), (wv_hbm, wv_ref), (wq_hbm, wq_ref))
        )
    ]
    gains = [
        fetch(gain_ctx_hbm, gain_ctx_ref, chunks + 4),
        fetch(gain_lat_hbm, gain_lat_ref, chunks + 5),
    ]
    for copy in (*gains, *weights[:3]):
        copy.start()
    blocks = [fetch_rows(i) for i in range(chunks)]
    for copy in blocks + weights[3:]:
        copy.start()
    results = {}
    for i, (name, source, target) in enumerate(
        (
            ("attn", attn_ref, attn_hbm),
            ("k", k_ref, k_hbm),
            ("v", v_ref, v_hbm),
            ("inv_row", inv_row_ref, inv_row_hbm),
            ("q", q_ref, q_hbm),
            ("lk", lk_ref, lk_hbm),
            ("lv", lv_ref, lv_hbm),
            ("lat_proj", lat_proj_ref, lat_proj_hbm),
            ("p0", p_ref.at[0], p_hbm.at[0]),
            ("p1", p_ref.at[1], p_hbm.at[1]),
            ("pl", pl_ref, pl_hbm),
        )
    ):
        results[name] = pltpu.make_async_copy(source, target, out_sems.at[i])

    for copy in (*gains, weights[0]):
        copy.wait()
    lat = lat_ref[...].astype(F32)
    lat_inverse = lax.rsqrt(jnp.mean(lat * lat, axis=-1, keepdims=True) + EPSILON)
    lat_normed = lat * lat_inverse * gain_lat_ref[...]
    lat_normed_ref[...] = lat_normed.astype(BF16)
    last_ref[rows:, :] = (lat_normed / gain_ctx_ref[...]).astype(BF16)
    for i, ref in enumerate((wk_ref, wv_ref)):
        weights[1 + i].wait()
        gained_ref[i * key_width : (i + 1) * key_width, :] = (
            ref[...].astype(F32) * gain_ctx_ref[...]
        ).astype(BF16)
    for i in range(chunks):
        blocks[i].wait()
        at = slice(i * rows, (i + 1) * rows)
        squares = jnp.zeros((rows, 128), F32)
        for c in range(width // 128):
            part = x_ref[at, c * 128 : (c + 1) * 128].astype(F32)
            squares = squares + part * part
        inverse = lax.rsqrt(jnp.sum(squares, axis=-1, keepdims=True) / width + EPSILON)
        if i < chunks - 1:
            pair = dot_general(x_ref[at, :], gained_ref[...], 1, 1)
        else:
            last_ref[:rows, :] = x_ref[at, :]
            pair = dot_general(last_ref[...], gained_ref[...], 1, 1)
            projected = pair[rows:]
        pair = (pair[:rows] * inverse).astype(BF16)
        inv_row_ref[:, at] = jnp.transpose(jnp.broadcast_to(inverse, (rows, 128)))[:8]
        for g in range(groups):
            k_ref[g, at, :HD] = pair[:, g * HD : (g + 1) * HD]
            v_ref[g, at, :HD] = pair[:, key_width + g * HD : key_width + (g + 1) * HD]
    lat_proj_ref[:, query_width:] = projected
    for i, ref in enumerate((lk_ref, lv_ref)):
        for g in range(groups):
            at = i * key_width + g * HD
            ref[g, :, :HD] = projected[:, at : at + HD].astype(BF16)
    for name in ("k", "v", "inv_row", "lk", "lv"):
        results[name].start()
    weights[3].wait()
    query = jnp.dot(lat_normed_ref[...], wq_ref[...], preferred_element_type=F32) * HD ** (-0.5)
    lat_proj_ref[:, :query_width] = query
    first_count = counts_ref[0, 0]
    both_count = first_count + counts_ref[0, 1]
    position = lax.broadcasted_iota(jnp.int32, (1, patch_rows), 1)
    in_first = position < first_count
    in_second = jnp.logical_and(position >= first_count, position < both_count)
    rows_at = lax.broadcasted_iota(jnp.int32, (patch_rows, HD), 0)
    row_first = rows_at < first_count
    row_second = jnp.logical_and(rows_at >= first_count, rows_at < both_count)
    for g in range(groups):
        for h in range(per_group):
            head = g * per_group + h
            q_ref[g, h * latent_rows : (h + 1) * latent_rows, :HD] = query[
                :, head * HD : (head + 1) * HD
            ].astype(BF16)
    results["lat_proj"].start()
    results["q"].start()
    for g in range(groups):
        q = q_ref[g, :, :HD]
        scores = dot_general(q, k_ref[g, :, :HD], 1, 1)
        lat_scores = dot_general(q, lk_ref[g, :, :HD], 1, 1)
        lat_max = jnp.max(lat_scores, axis=-1, keepdims=True)
        max_first = jnp.maximum(
            jnp.max(jnp.where(in_first, scores, NEGATIVE), axis=-1, keepdims=True), lat_max
        )
        max_second = jnp.maximum(
            jnp.max(jnp.where(in_second, scores, NEGATIVE), axis=-1, keepdims=True), lat_max
        )
        masked = jnp.where(
            in_first, scores - max_first, jnp.where(in_second, scores - max_second, NEGATIVE)
        )
        exponent = jnp.exp(masked)
        lat_first = jnp.exp(lat_scores - max_first)
        lat_second = jnp.exp(lat_scores - max_second)
        sum_first = jnp.sum(
            jnp.where(in_first, exponent, 0.0), axis=-1, keepdims=True
        ) + jnp.sum(lat_first, axis=-1, keepdims=True)
        sum_second = jnp.sum(
            jnp.where(in_second, exponent, 0.0), axis=-1, keepdims=True
        ) + jnp.sum(lat_second, axis=-1, keepdims=True)
        per_first = 1.0 / sum_first
        per_second = 1.0 / sum_second
        p = (exponent * jnp.where(in_first, per_first, per_second)).astype(BF16)
        p_ref[g] = p
        results[f"p{g}"].start()
        lat_p_first = (lat_first * per_first).astype(BF16)
        lat_p_second = (lat_second * per_second).astype(BF16)
        pl_ref[g, :, :latent_rows] = lat_p_first
        pl_ref[g, :, latent_rows:] = lat_p_second
        v = v_ref[g, :, :HD]
        zero = jnp.zeros_like(v)
        lv = lv_ref[g, :, :HD]
        for j, (row_mask, lat_p) in enumerate(
            ((row_first, lat_p_first), (row_second, lat_p_second))
        ):
            mixed = jnp.dot(
                p, jnp.where(row_mask, v, zero), preferred_element_type=F32
            ) + jnp.dot(lat_p, lv, preferred_element_type=F32)
            mixed = mixed.astype(BF16)
            for h in range(per_group):
                head = g * per_group + h
                attn_ref[
                    j * latent_rows : (j + 1) * latent_rows, head * HD : (head + 1) * HD
                ] = mixed[h * latent_rows : (h + 1) * latent_rows]
    for name in ("attn", "pl"):
        results[name].start()
    for copy in results.values():
        copy.wait()


def whole(shape):
    return pl.BlockSpec(shape, lambda *_: (0,) * len(shape))


def held(shape):
    return pl.BlockSpec(shape, lambda *_: (0,) * len(shape), pipeline_mode=pl.Buffered(1))


def forward_call(context, counts, w_query, w_key, w_value, latents, gain_ctx, gain_lat):
    patch_rows, width = context.shape
    chunks = 4
    key_width = w_key.shape[0]
    query_width = w_query.shape[1]
    groups = key_width // HD
    latent_rows = latents.shape[0]
    stacked = query_width // key_width * latent_rows
    large = (latents, w_key, w_value, context, w_query)
    out = [
        ((2 * latent_rows, query_width), BF16),
        ((groups, patch_rows, 128), BF16),
        ((groups, patch_rows, 128), BF16),
        ((8, patch_rows), F32),
        ((groups, stacked, 128), BF16),
        ((groups, latent_rows, 128), BF16),
        ((groups, latent_rows, 128), BF16),
        ((latent_rows, query_width + 2 * key_width), F32),
        ((groups, stacked, patch_rows), BF16),
        ((groups, stacked, 2 * latent_rows), BF16),
    ]
    return pl.pallas_call(
        forward_kernel,
        name="forward_attention",
        in_specs=[
            pl.BlockSpec(memory_space=pltpu.SMEM),
            pl.BlockSpec(memory_space=pl.ANY),
            pl.BlockSpec(memory_space=pl.ANY),
        ]
        + [pl.BlockSpec(memory_space=pl.ANY)] * len(large),
        out_specs=[pl.BlockSpec(memory_space=pl.ANY)] * len(out),
        out_shape=[jax.ShapeDtypeStruct(shape, dtype) for shape, dtype in out],
        scratch_shapes=[pltpu.VMEM((1, width), F32)] * 2
        + [pltpu.VMEM(a.shape, a.dtype) for a in large]
        + [pltpu.VMEM(shape, dtype) for shape, dtype in out]
        + [
            pltpu.VMEM((latent_rows, width), BF16),
            pltpu.VMEM((patch_rows // chunks + latent_rows, width), BF16),
            pltpu.VMEM((2 * key_width, width), BF16),
            pltpu.SemaphoreType.DMA((chunks + 6,)),
            pltpu.SemaphoreType.DMA((len(out) + 1,)),
        ],
        cost_estimate=pl.CostEstimate(
            flops=5_000_000_000, bytes_accessed=24_000_000, transcendentals=600_000
        ),
        compiler_params=pltpu.CompilerParams(vmem_limit_bytes=VMEM_LIMIT),
    )(counts, gain_ctx.reshape(1, width), gain_lat.reshape(1, width), *large)


def slots_of(routes_ref, slot_count, as_row):
    rows = routes_ref.shape[1]
    turned = jnp.broadcast_to(routes_ref[...].astype(F32), (rows, rows))
    shard = jnp.transpose(turned)
    down = lax.broadcasted_iota(jnp.int32, (rows, rows), 0)
    across = lax.broadcasted_iota(jnp.int32, (rows, rows), 1)
    same = shard == turned
    if as_row:
        rank = jnp.sum(jnp.where(same & (down < across), 1.0, 0.0), axis=0, keepdims=True)
        return (turned[:1] * slot_count + rank).astype(jnp.int32)
    rank = jnp.sum(jnp.where(same & (across < down), 1.0, 0.0), axis=1, keepdims=True)
    return (shard[:, :1] * slot_count + rank).astype(jnp.int32)


def branch_kernel(
    slot_count,
    own_hbm,
    other_hbm,
    lat_hbm,
    gain_hbm,
    routes_hbm,
    w_own_hbm,
    w_other_hbm,
    hat_hbm,
    inv_hbm,
    out_hbm,
    own_ref,
    other_ref,
    lat_ref,
    gain_ref,
    routes_ref,
    w_own_ref,
    w_other_ref,
    hat_ref,
    low_ref,
    inv_ref,
    out_ref,
    sems,
    out_sems,
    small_sems,
):
    rows, width = hat_ref.shape
    slots, half = out_ref.shape
    parts = sems.shape[1]
    size = width // parts
    small = [
        pltpu.make_async_copy(source, target, small_sems.at[i])
        for i, (source, target) in enumerate(
            (
                (routes_hbm, routes_ref),
                (own_hbm, own_ref),
                (other_hbm, other_ref),
                (lat_hbm, lat_ref),
                (gain_hbm, gain_ref),
            )
        )
    ]
    for copy in small:
        copy.start()
    copies = []
    for part in range(parts):
        at = pl.ds(part * size, size)
        for i, (source, target) in enumerate(
            ((w_own_hbm, w_own_ref), (w_other_hbm, w_other_ref))
        ):
            copies.append(
                pltpu.make_async_copy(source.at[:, at], target.at[:, at], sems.at[i, part])
            )
    for copy in copies:
        copy.start()
    small[0].wait()
    place = slots_of(routes_ref, slot_count, True)
    for copy in small[1:]:
        copy.wait()
    table = jnp.where(
        lax.broadcasted_iota(jnp.int32, (slots, rows), 0) == place, 1.0, 0.0
    ).astype(BF16)
    squares = jnp.zeros((rows, 128), F32)
    for part in range(parts):
        at = slice(part * size, (part + 1) * size)
        copies[2 * part].wait()
        copies[2 * part + 1].wait()
        lat = lat_ref[:, at].astype(F32)
        resid = (
            jnp.concatenate([lat, lat], axis=0)
            + jnp.dot(own_ref[...], w_own_ref[:, at], preferred_element_type=F32)
            + jnp.dot(other_ref[...], w_other_ref[:, at], preferred_element_type=F32)
        )
        hat_ref[:, at] = resid
        for c in range(size // 128):
            piece = resid[:, c * 128 : (c + 1) * 128]
            squares = squares + piece * piece
    inverse = lax.rsqrt(jnp.sum(squares, axis=-1, keepdims=True) / width + EPSILON)
    inv_ref[...] = inverse
    low_ref[...] = (hat_ref[...] * inverse).astype(BF16)
    results = [
        pltpu.make_async_copy(source, target, out_sems.at[i])
        for i, (source, target) in enumerate(
            ((low_ref, hat_hbm), (inv_ref, inv_hbm), (out_ref, out_hbm))
        )
    ]
    for copy in results[:2]:
        copy.start()
    at = pl.ds(pl.multiple_of(lax.axis_index("mp") * half, half), half)
    final = (hat_ref[:, at] * inverse * gain_ref[:, at]).astype(BF16)
    out_ref[...] = jnp.dot(table, final, preferred_element_type=F32).astype(BF16)
    results[2].start()
    for copy in results:
        copy.wait()


def branch_call(own, other, w_own, w_other, latents, gain_out, routes, slots, slot_count):
    width = w_own.shape[1]
    rows, heads = own.shape
    parts = 4
    return pl.pallas_call(
        functools.partial(branch_kernel, slot_count),
        name="branch_norm",
        **dict(
            in_specs=[pl.BlockSpec(memory_space=pl.ANY)] * 7,
            out_specs=[pl.BlockSpec(memory_space=pl.ANY)] * 3,
            scratch_shapes=[
                pltpu.VMEM((rows, heads), BF16),
                pltpu.VMEM((rows, heads), BF16),
                pltpu.VMEM(latents.shape, BF16),
                pltpu.VMEM((1, width), F32),
                pltpu.VMEM((1, rows), jnp.int32),
                pltpu.VMEM(w_own.shape, BF16),
                pltpu.VMEM(w_other.shape, BF16),
                pltpu.VMEM((rows, width), F32),
                pltpu.VMEM((rows, width), BF16),
                pltpu.VMEM((rows, 1), F32),
                pltpu.VMEM((slots, width // 2), BF16),
                pltpu.SemaphoreType.DMA((2, parts)),
                pltpu.SemaphoreType.DMA((3,)),
                pltpu.SemaphoreType.DMA((5,)),
            ],
        ),
        out_shape=[
            jax.ShapeDtypeStruct((rows, width), BF16),
            jax.ShapeDtypeStruct((rows, 1), F32),
            jax.ShapeDtypeStruct((slots, width // 2), BF16),
        ],
        cost_estimate=pl.CostEstimate(
            flops=2 * 2 * rows * heads * width, bytes_accessed=16_000_000, transcendentals=0
        ),
        compiler_params=pltpu.CompilerParams(vmem_limit_bytes=VMEM_LIMIT),
    )(own, other, latents, gain_out.reshape(1, width), routes, w_own, w_other)


def attention_backward(
    counts_ref,
    d_attn,
    k_ref,
    v_ref,
    q_ref,
    lk_ref,
    lv_ref,
    p_ref,
    pl_ref,
    inv_row_ref,
    pair_ref,
    scaled_ref,
    lat_ref,
):
    groups, patch_rows, _ = k_ref.shape
    latent_rows = lk_ref.shape[1]
    stacked = q_ref.shape[1]
    per_group = stacked // latent_rows
    key_width = groups * HD
    query_width = groups * per_group * HD
    first_count = counts_ref[0, 0]
    both_count = first_count + counts_ref[0, 1]
    position = lax.broadcasted_iota(jnp.int32, (1, patch_rows), 1)
    in_first = position < first_count
    rows_at = lax.broadcasted_iota(jnp.int32, (patch_rows, HD), 0)
    row_first = rows_at < first_count
    row_second = jnp.logical_and(rows_at >= first_count, rows_at < both_count)
    scale_row = inv_row_ref[:1]
    row_dot = jnp.zeros((1, patch_rows), F32)
    for g in range(groups):
        d_first = jnp.concatenate(
            [
                d_attn[:latent_rows, head * HD : (head + 1) * HD]
                for head in range(g * per_group, (g + 1) * per_group)
            ],
            axis=0,
        )
        d_second = jnp.concatenate(
            [
                d_attn[latent_rows:, head * HD : (head + 1) * HD]
                for head in range(g * per_group, (g + 1) * per_group)
            ],
            axis=0,
        )
        q = q_ref[g, :, :HD]
        k = k_ref[g, :, :HD]
        v = v_ref[g, :, :HD]
        lk = lk_ref[g, :, :HD]
        lv = lv_ref[g, :, :HD]
        p_low = p_ref[g]
        p = p_low.astype(F32)
        zero = jnp.zeros_like(v)
        d_p = dot_general(d_first, jnp.where(row_first, v, zero), 1, 1) + dot_general(
            d_second, jnp.where(row_second, v, zero), 1, 1
        )
        product = p * d_p
        lat_first = pl_ref[g, :, :latent_rows]
        lat_second = pl_ref[g, :, latent_rows:]
        d_lat_first = dot_general(d_first, lv, 1, 1)
        d_lat_second = dot_general(d_second, lv, 1, 1)
        lat_product_first = lat_first.astype(F32) * d_lat_first
        lat_product_second = lat_second.astype(F32) * d_lat_second
        whole_sum = jnp.sum(product, axis=-1, keepdims=True)
        first_sum = jnp.sum(jnp.where(in_first, product, 0.0), axis=-1, keepdims=True)
        delta_first = first_sum + jnp.sum(lat_product_first, axis=-1, keepdims=True)
        delta_second = (whole_sum - first_sum) + jnp.sum(
            lat_product_second, axis=-1, keepdims=True
        )
        ds = product - p * jnp.where(in_first, delta_first, delta_second)
        ds_low = ds.astype(BF16)
        dsl = (
            lat_product_first
            - lat_first.astype(F32) * delta_first
            + lat_product_second
            - lat_second.astype(F32) * delta_second
        ).astype(BF16)
        scores = dot_general(q, k, 1, 1)
        row_dot = row_dot + jnp.sum(ds * scores + product, axis=0, keepdims=True)
        d_q = (
            jnp.dot(ds_low, k, preferred_element_type=F32)
            + jnp.dot(dsl, lk, preferred_element_type=F32)
        ).astype(BF16)
        for h in range(per_group):
            head = g * per_group + h
            lat_ref[:latent_rows, head * HD : (head + 1) * HD] = d_q[
                h * latent_rows : (h + 1) * latent_rows
            ]
        d_k = dot_general(q, ds_low, 0, 0)
        nothing = jnp.zeros_like(p_low)
        d_v = dot_general(d_first, jnp.where(in_first, p_low, nothing), 0, 0) + dot_general(
            d_second, jnp.where(in_first, nothing, p_low), 0, 0
        )
        k_at = slice(g * HD, (g + 1) * HD)
        v_at = slice(key_width + g * HD, key_width + (g + 1) * HD)
        pair_ref[k_at, :] = d_k.astype(BF16)
        pair_ref[v_at, :] = d_v.astype(BF16)
        scaled_ref[k_at, :] = (d_k * scale_row).astype(BF16)
        scaled_ref[v_at, :] = (d_v * scale_row).astype(BF16)
        d_lk = dot_general(dsl, q, 0, 0)
        d_lv = dot_general(lat_first, d_first, 0, 0) + dot_general(lat_second, d_second, 0, 0)
        lat_ref[:latent_rows, query_width + g * HD : query_width + (g + 1) * HD] = d_lk.astype(BF16)
        at = query_width + key_width + g * HD
        lat_ref[:latent_rows, at : at + HD] = d_lv.astype(BF16)
    high = row_dot.astype(BF16)
    low = (row_dot - high.astype(F32)).astype(BF16)
    rest = pair_ref.shape[0] - 2 * key_width - 2
    pair_ref[2 * key_width :, :] = jnp.concatenate(
        [high.astype(F32), low.astype(F32), jnp.zeros((rest, patch_rows), F32)], axis=0
    ).astype(BF16)


def backward_kernel(
    slot_count,
    counts_ref,
    inv_out_hbm,
    gain_hbm,
    routes_hbm,
    inv_row_hbm,
    attn_hbm,
    got_own_hbm,
    got_other_hbm,
    hat_hbm,
    w_out_hbm,
    k_hbm,
    v_hbm,
    q_hbm,
    lk_hbm,
    lv_hbm,
    p_hbm,
    pl_hbm,
    x_hbm,
    line_own_hbm,
    line_high_hbm,
    pair_hbm,
    message_hbm,
    lat_hbm,
    value_going_hbm,
    value_kept_hbm,
    key_going_hbm,
    key_kept_hbm,
    inv_out_ref,
    gain_ref,
    routes_ref,
    inv_row_ref,
    attn_ref,
    got_own_ref,
    got_other_ref,
    hat_ref,
    w_out_ref,
    k_ref,
    v_ref,
    q_ref,
    lk_ref,
    lv_ref,
    p_ref,
    pl_ref,
    x_ref,
    d_final_ref,
    branch_ref,
    scaled_ref,
    line_own_ref,
    line_high_ref,
    pair_ref,
    message_ref,
    lat_ref,
    value_ref,
    key_ref,
    sems,
    out_sems,
    value_sems,
    key_sems,
    small_sems,
):
    small = [
        pltpu.make_async_copy(source, target, small_sems.at[i])
        for i, (source, target) in enumerate(
            (
                (routes_hbm, routes_ref),
                (inv_out_hbm, inv_out_ref),
                (gain_hbm, gain_ref),
                (inv_row_hbm, inv_row_ref),
                (attn_hbm, attn_ref),
            )
        )
    ]
    for copy in small:
        copy.start()
    sources = (
        got_own_hbm,
        got_other_hbm,
        hat_hbm,
        w_out_hbm,
        k_hbm,
        v_hbm,
        q_hbm,
        lk_hbm,
        lv_hbm,
        p_hbm,
        pl_hbm,
        x_hbm,
    )
    targets = (
        got_own_ref,
        got_other_ref,
        hat_ref,
        w_out_ref,
        k_ref,
        v_ref,
        q_ref,
        lk_ref,
        lv_ref,
        p_ref,
        pl_ref,
        x_ref,
    )
    copies = [
        pltpu.make_async_copy(source, target, sems.at[i])
        for i, (source, target) in enumerate(zip(sources, targets))
    ]
    for copy in copies[:4]:
        copy.start()
    me, core = lax.axis_index("dp"), lax.axis_index("mp")
    rows, width = hat_ref.shape
    half = width // 2
    slots = got_own_ref.shape[0]
    latent_rows = lk_ref.shape[1]
    key_width, own = value_ref.shape[2:]

    small[0].wait()
    place = slots_of(routes_ref, slot_count, False)
    for copy in small[1:]:
        copy.wait()
    table = jnp.where(
        lax.broadcasted_iota(jnp.int32, (rows, slots), 1) == place, 1.0, 0.0
    ).astype(BF16)
    total = jnp.zeros((rows, 1), F32)
    chunk = 512
    for copy in copies[:3]:
        copy.wait()
    for copy in copies[4:]:
        copy.start()
    for got_ref, which in ((got_own_ref, core), (got_other_ref, 1 - core)):
        for c in range(half // chunk):
            at = pl.ds(pl.multiple_of(which * half + c * chunk, chunk), chunk)
            d_final = jnp.dot(
                table, got_ref[:, c * chunk : (c + 1) * chunk], preferred_element_type=F32
            )
            product = d_final * hat_ref[:, at].astype(F32)
            total = total + jnp.sum(product * gain_ref[:, at], axis=-1, keepdims=True)
            d_final_ref[:, at] = d_final
    total = total / width
    lat_ref[latent_rows:, :] = jnp.zeros_like(lat_ref[latent_rows:, :])
    highs, lows = [], []
    part = width // 4
    for c in range(width // chunk):
        at = slice(c * chunk, (c + 1) * chunk)
        d_final = d_final_ref[:, at]
        hat = hat_ref[:, at].astype(F32)
        term = jnp.sum(d_final * hat, axis=0, keepdims=True)
        high = term.astype(BF16).astype(F32)
        highs.append(high)
        lows.append(term - high)
        branch_ref[:, at] = (
            inv_out_ref[...] * (d_final * gain_ref[:, at] - hat * total)
        ).astype(BF16)
    per_row = part // chunk
    lines = [
        jnp.concatenate(group[i * per_row : (i + 1) * per_row], axis=1)
        for group in (highs, lows)
        for i in range(4)
    ]
    lat_ref[latent_rows : latent_rows + 16, :part] = jnp.concatenate(
        lines + [jnp.zeros((8, part), F32)], axis=0
    ).astype(BF16)
    z = me >> 2
    some = pl.ds(pl.multiple_of(core * (rows // 2), rows // 2), rows // 2)
    line_own_ref[...] = branch_ref[:, pl.ds(pl.multiple_of(z * part, part), part)]
    heads = attn_ref.shape[1]
    for turn, ref, first in (
        (1, message_ref, 0),
        (2, line_high_ref, 0),
        (3, line_high_ref, part + 2 * heads),
    ):
        ref[: rows // 2, first : first + part] = branch_ref[
            some, pl.ds(pl.multiple_of((z ^ turn) * part, part), part)
        ]
    for ref in (message_ref, line_high_ref):
        ref[: rows // 2, part : part + heads] = attn_ref[: rows // 2, :]
        ref[: rows // 2, part + heads : part + 2 * heads] = attn_ref[rows // 2 :, :]
    results = [
        pltpu.make_async_copy(source, target, out_sems.at[i])
        for i, (source, target) in enumerate(
            (
                (line_high_ref, line_high_hbm),
                (message_ref, message_hbm),
                (line_own_ref, line_own_hbm),
                (pair_ref, pair_hbm),
                (lat_ref, lat_hbm),
            )
        )
    ]
    for copy in results[:3]:
        copy.start()

    copies[3].wait()
    d_attn = dot_general(branch_ref[...], w_out_ref[...], 1, 1).astype(BF16)
    for copy in copies[4:11]:
        copy.wait()
    attention_backward(
        counts_ref,
        d_attn,
        k_ref,
        v_ref,
        q_ref,
        lk_ref,
        lv_ref,
        p_ref,
        pl_ref,
        inv_row_ref,
        pair_ref,
        scaled_ref,
        lat_ref,
    )
    for copy in results[3:]:
        copy.start()
    copies[11].wait()

    odd = me & 1
    for j in range(8):
        y = ((me >> 1) & 1) ^ (1 - (j >> 2))
        z = (me >> 2) ^ ((1 - ((j >> 1) & 1)) + 2 * (1 - (j & 1)))
        first = 4 * z + 2 * y
        line = j & 3
        key_hbm = key_kept_hbm if j >> 2 else key_going_hbm
        grad = jnp.dot(
            scaled_ref[...],
            x_ref[:, pl.ds(pl.multiple_of(first * own, 2 * own), 2 * own)],
            preferred_element_type=F32,
        ).astype(BF16)
        for x_same, value_hbm in enumerate((value_going_hbm, value_kept_hbm)):
            block = jnp.where(odd == x_same, grad[:, own:], grad[:, :own])
            value_ref[x_same, j] = block[key_width:]
            key_ref[x_same, j] = block[:key_width]
            for copy in (
                pltpu.make_async_copy(
                    value_ref.at[x_same, j], value_hbm.at[j], value_sems.at[x_same, j]
                ),
                pltpu.make_async_copy(
                    key_ref.at[x_same, j], key_hbm.at[x_same, line], key_sems.at[x_same, j]
                ),
            ):
                copy.start()
                results.append(copy)
    for copy in results:
        copy.wait()


def backward_call(
    counts, attn, got_own, got_other, hat, inv_out, gain_out, routes, w_out, kept, context, slot_count
):
    k, v, q, lk, lv, p, lat_p, inv_row = kept
    rows, width = hat.shape
    patch_rows = context.shape[0]
    heads = w_out.shape[0]
    key_width = k.shape[0] * HD
    latent_rows = lk.shape[1]
    own = width // 16
    large = (got_own, got_other, hat, w_out, k, v, q, lk, lv, p, lat_p, context)
    small = (inv_out, gain_out.reshape(1, width), routes, inv_row, attn)
    out = [
        (rows, width // 4),
        (rows // 2, width // 2 + 2 * heads),
        (2 * key_width + 16, patch_rows),
        (rows // 2, width // 4 + 2 * heads),
        (latent_rows + 16, heads + 2 * key_width),
        (8, key_width, own),
        (8, key_width, own),
        (2, 4, key_width, own),
        (2, 4, key_width, own),
    ]
    return pl.pallas_call(
        functools.partial(backward_kernel, slot_count),
        name="attention_backward",
        **dict(
            in_specs=[
                pl.BlockSpec(memory_space=pltpu.SMEM),
            ]
            + [pl.BlockSpec(memory_space=pl.ANY)] * (5 + len(large)),
            out_specs=[pl.BlockSpec(memory_space=pl.ANY)] * len(out),
            scratch_shapes=[pltpu.VMEM(a.shape, a.dtype) for a in (*small, *large)]
            + [
                pltpu.VMEM((rows, width), F32),
                pltpu.VMEM((rows, width), BF16),
                pltpu.VMEM((2 * key_width, patch_rows), BF16),
            ]
            + [pltpu.VMEM(shape, BF16) for shape in out[:5]]
            + [
                pltpu.VMEM((2, 8, key_width, own), BF16),
                pltpu.VMEM((2, 8, key_width, own), BF16),
                pltpu.SemaphoreType.DMA((len(large),)),
                pltpu.SemaphoreType.DMA((5,)),
                pltpu.SemaphoreType.DMA((2, 8)),
                pltpu.SemaphoreType.DMA((2, 8)),
                pltpu.SemaphoreType.DMA((5,)),
            ],
        ),
        out_shape=[jax.ShapeDtypeStruct(shape, BF16) for shape in out],
        cost_estimate=pl.CostEstimate(
            flops=5_000_000_000, bytes_accessed=26_000_000, transcendentals=0
        ),
        compiler_params=pltpu.CompilerParams(vmem_limit_bytes=VMEM_LIMIT),
    )(counts, *small, *large)


def patch_kernel(
    width,
    where_ref,
    own_ref,
    other_ref,
    wk_ref,
    wv_ref,
    wk_other_ref,
    wv_other_ref,
    x_ref,
    inv_row_ref,
    gain_ref,
    out_ref,
    turned_ref,
    inv_ref,
    dot_ref,
    w_ref,
):
    step = pl.program_id(0)
    key_width = wk_ref.shape[0]
    patch_rows = turned_ref.shape[0]
    pair = 2 * key_width

    @pl.when(step == 0)
    def _():
        row_dot = jnp.zeros((patch_rows, 1), F32)
        for i, ref in enumerate((own_ref, other_ref)):
            turned = jnp.transpose(ref[...])
            turned_ref[:, i * pair : (i + 1) * pair] = turned[:, :pair]
            row_dot = row_dot + turned[:, pair : pair + 1].astype(F32)
            row_dot = row_dot + turned[:, pair + 1 : pair + 2].astype(F32)
        inverse = jnp.transpose(jnp.broadcast_to(inv_row_ref[:1], (128, patch_rows)))[:, :1]
        inv_ref[...] = inverse
        dot_ref[...] = row_dot * (inverse * inverse / width)
        for i, ref in enumerate((wk_ref, wv_ref, wk_other_ref, wv_other_ref)):
            w_ref[i * key_width : (i + 1) * key_width, :] = ref[...]

    rows = x_ref.shape[0]
    at = pl.ds(pl.multiple_of(step * rows, rows), rows)
    d_in = jnp.dot(turned_ref[at, :], w_ref[...], preferred_element_type=F32)
    out_ref[...] = (
        d_in * gain_ref[...] * inv_ref[at, :] - x_ref[...].astype(F32) * dot_ref[at, :]
    ).astype(BF16)


def patch_call(where, own, other, wk, wv, wk_other, wv_other, context, inv_row, gain_ctx):
    patch_rows, width = context.shape
    half = width // 2
    steps = 4
    rows = patch_rows // steps
    key_width = wk.shape[0]
    once = pl.Buffered(1)
    w_spec = pl.BlockSpec((key_width, half), lambda i, w: (0, w[1]), pipeline_mode=once)
    return pl.pallas_call(
        functools.partial(patch_kernel, width),
        name="patch_gradient",
        grid_spec=pltpu.PrefetchScalarGridSpec(
            num_scalar_prefetch=1,
            grid=(steps,),
            in_specs=[
                held(own.shape),
                held(other.shape),
                w_spec,
                w_spec,
                w_spec,
                w_spec,
                pl.BlockSpec((rows, half), lambda i, w: (i, w[1])),
                held(inv_row.shape),
                pl.BlockSpec((1, half), lambda i, w: (0, w[1])),
            ],
            out_specs=pl.BlockSpec((rows, half), lambda i, w: (i, 0)),
            scratch_shapes=[
                pltpu.VMEM((patch_rows, 4 * key_width), BF16),
                pltpu.VMEM((patch_rows, 1), F32),
                pltpu.VMEM((patch_rows, 1), F32),
                pltpu.VMEM((4 * key_width, half), BF16),
            ],
        ),
        out_shape=jax.ShapeDtypeStruct((patch_rows, half), BF16),
        cost_estimate=pl.CostEstimate(
            flops=3_300_000_000, bytes_accessed=14_000_000, transcendentals=0
        ),
        compiler_params=pltpu.CompilerParams(vmem_limit_bytes=VMEM_LIMIT),
    )(where, own, other, wk, wv, wk_other, wv_other, context, inv_row, gain_ctx.reshape(1, width))


def out_kernel(
    where_ref,
    attn_own_ref,
    line_own_ref,
    low_ref,
    high_ref,
    forwarded_ref,
    other_low_ref,
    other_high_ref,
    other_forwarded_ref,
    first_going_ref,
    first_kept_ref,
    second_going_ref,
    second_kept_ref,
    attn_ref,
    line_ref,
    resid_ref,
):
    rows, heads = attn_own_ref.shape
    columns = line_ref.shape[1]
    own = columns // 4
    latent_rows = rows // 2
    mine = where_ref[1]
    half = rows // 2
    attn_ref[:rows, :] = attn_own_ref[...]
    line_ref[:rows, :] = line_own_ref[...]
    for i, (ref, other, first, attn_at) in enumerate(
        (
            (low_ref, other_low_ref, 0, columns),
            (high_ref, other_high_ref, 0, columns),
            (forwarded_ref, other_forwarded_ref, 2 * heads, 0),
        )
    ):
        at = (i + 1) * rows
        attn_ref[at : at + half, :] = ref[:half, attn_at : attn_at + heads]
        attn_ref[at + half : at + rows, :] = ref[:half, attn_at + heads : attn_at + 2 * heads]
        for holder, which in ((ref, mine), (other, 1 - mine)):
            line_ref[pl.ds(pl.multiple_of(at + which * half, half), half), :] = holder[
                :half, first : first + columns
            ]
    resid = jnp.zeros((latent_rows, columns), F32)
    for i in range(8):
        resid = resid + line_ref[i * latent_rows : (i + 1) * latent_rows, :].astype(F32)
    resid_ref[...] = resid
    odd = where_ref[0] & 1
    upper = (where_ref[0] >> 1) & 1
    share = own // 2
    cut = heads // 2
    for turn in range(4):
        x_differs, y_differs = 1 - (turn & 1), 1 - (turn >> 1)
        owner = 2 * (upper ^ y_differs) + (odd ^ x_differs)
        at = pl.ds(pl.multiple_of(owner * own, own), own)
        grad = dot_general(attn_ref[...], line_ref[:, at], 0, 0).astype(BF16)
        mine_at = pl.ds(pl.multiple_of(owner * own + mine * share, share), share)
        part = resid_ref[:, mine_at]
        part = jnp.concatenate([part[: latent_rows // 2], part[latent_rows // 2 :]], axis=1)
        ref = first_going_ref if x_differs else first_kept_ref
        ref[1 - y_differs, :cut, :] = grad[:cut]
        ref[1 - y_differs, cut:, :] = part.astype(BF16)
        ref = second_going_ref if y_differs else second_kept_ref
        ref[1 - x_differs] = grad[cut:]


def out_call(where, attn, line, received, others):
    rows, heads = attn.shape
    columns = line.shape[1]
    own = columns // 4
    first = (2, heads // 2 + rows // 4, own)
    second = (2, heads // 2, own)
    shapes = [first, first, second, second]
    operands = (attn, line, *received, *others)
    return pl.pallas_call(
        out_kernel,
        name="output_projection_gradient",
        grid_spec=pltpu.PrefetchScalarGridSpec(
            num_scalar_prefetch=1,
            grid=(1,),
            in_specs=[held(a.shape) for a in operands],
            out_specs=[held(shape) for shape in shapes],
            scratch_shapes=[
                pltpu.VMEM((4 * rows, heads), BF16),
                pltpu.VMEM((4 * rows, columns), BF16),
                pltpu.VMEM((rows // 2, columns), F32),
            ],
        ),
        out_shape=[jax.ShapeDtypeStruct(shape, BF16) for shape in shapes],
        cost_estimate=pl.CostEstimate(
            flops=8 * rows * heads * columns, bytes_accessed=4_000_000, transcendentals=0
        ),
        compiler_params=pltpu.CompilerParams(vmem_limit_bytes=VMEM_LIMIT),
    )(where, *operands)


def latent_kernel(
    where_ref,
    sum_ref,
    across_ref,
    along_ref,
    corner_ref,
    proj_ref,
    lat_ref,
    gain_ref,
    wq_ref,
    wk_ref,
    wv_ref,
    routed_hbm,
    query_ref,
    pair_ref,
    message_ref,
    gain_out_ref,
    routed_out_hbm,
    total_ref,
    routed_ref,
    sems,
):
    arrive = pltpu.make_async_copy(routed_hbm, routed_ref, sems.at[0])
    leave = pltpu.make_async_copy(routed_ref, routed_out_hbm, sems.at[1])
    arrive.start()
    latent_rows, width = lat_ref.shape
    own, query_width = wq_ref.shape
    key_width = wk_ref.shape[0]
    scaling = HD ** (-0.5)
    total_ref[...] = sum(
        ref[...].astype(F32) for ref in (sum_ref, across_ref, along_ref, corner_ref)
    )
    total = total_ref[:latent_rows, :]
    low = total.astype(BF16)
    at = pl.ds(pl.multiple_of(where_ref[0] * own, own), own)
    lat = lat_ref[...].astype(F32)
    inverse = lax.rsqrt(jnp.mean(lat * lat, axis=-1, keepdims=True) + EPSILON)
    gain = gain_ref[:, at]
    normed = (lat_ref[:, at].astype(F32) * inverse * gain).astype(BF16)
    query = dot_general(normed, low[:, :query_width], 0, 0) * scaling
    query_ref[...] = query
    pair = dot_general(low[:, query_width:], normed, 0, 0)
    pair_ref[...] = pair
    wq = wq_ref[...]
    wk = wk_ref[...]
    wv = wv_ref[...]
    gain_term = jnp.transpose(
        jnp.broadcast_to(jnp.sum(wq.astype(F32) * query, axis=1, keepdims=True), (own, 128))
    )[:1]
    gain_term = gain_term + jnp.sum(wk.astype(F32) * pair[:key_width], axis=0, keepdims=True)
    gain_term = gain_term + jnp.sum(wv.astype(F32) * pair[key_width:], axis=0, keepdims=True)
    arrive.wait()
    leave.start()
    scaled = (total[:, :query_width] * scaling).astype(BF16)
    d_lat = dot_general(scaled, wq, 1, 1)
    d_lat = d_lat + jnp.dot(
        low[:, query_width : query_width + key_width], wk, preferred_element_type=F32
    )
    d_lat = d_lat + jnp.dot(low[:, query_width + key_width :], wv, preferred_element_type=F32)
    message_ref[:latent_rows, :own] = d_lat
    message_ref[:latent_rows, own:] = jnp.broadcast_to(
        jnp.sum(total * proj_ref[...], axis=-1, keepdims=True), (latent_rows, 128)
    )
    message_ref[latent_rows:, :own] = jnp.broadcast_to(gain_term / gain, (8, own))
    message_ref[latent_rows:, own:] = jnp.zeros((8, 128), F32)
    part = width // 4
    share = own // 2
    first = where_ref[0] * own + where_ref[1] * share
    line = first // part
    mine = pl.ds(pl.multiple_of(first % part, share), share)
    gain_out_ref[...] = jnp.sum(
        jnp.where(
            lax.broadcasted_iota(jnp.int32, (8, share), 0) % 4 == line,
            total_ref[latent_rows : latent_rows + 8, mine],
            0.0,
        ),
        axis=0,
        keepdims=True,
    )
    leave.wait()


def latent_call(where, sums, parts, proj, latents, gain_lat, w_query, wk, wv, own, routed):
    latent_rows, width = latents.shape
    query_width = w_query.shape[1]
    key_width = wk.shape[0]
    return pl.pallas_call(
        latent_kernel,
        name="latent_gradients",
        grid_spec=pltpu.PrefetchScalarGridSpec(
            num_scalar_prefetch=1,
            grid=(1,),
            in_specs=[
                held(sums.shape),
                *(held(part.shape) for part in parts),
                held(proj.shape),
                held(latents.shape),
                held((1, width)),
                pl.BlockSpec((own, query_width), lambda i, w: (w[0], 0)),
                pl.BlockSpec((key_width, own), lambda i, w: (0, w[0])),
                pl.BlockSpec((key_width, own), lambda i, w: (0, w[0])),
                pl.BlockSpec(memory_space=pl.ANY),
            ],
            out_specs=[
                held((own, query_width)),
                held((2 * key_width, own)),
                held((latent_rows + 8, own + 128)),
                held((1, own // 2)),
                pl.BlockSpec(memory_space=pl.ANY),
            ],
            scratch_shapes=[
                pltpu.VMEM(sums.shape, F32),
                pltpu.VMEM(routed.shape, BF16),
                pltpu.SemaphoreType.DMA((2,)),
            ],
        ),
        out_shape=[
            jax.ShapeDtypeStruct((own, query_width), F32),
            jax.ShapeDtypeStruct((2 * key_width, own), F32),
            jax.ShapeDtypeStruct((latent_rows + 8, own + 128), F32),
            jax.ShapeDtypeStruct((1, own // 2), F32),
            jax.ShapeDtypeStruct(routed.shape, BF16),
        ],
        cost_estimate=pl.CostEstimate(
            flops=100_000_000, bytes_accessed=3_000_000, transcendentals=0
        ),
        compiler_params=pltpu.CompilerParams(vmem_limit_bytes=VMEM_LIMIT),
    )(where, sums, *parts, proj, latents, gain_lat.reshape(1, width), w_query, wk, wv, routed)


def plane_kernel(
    value_ref,
    value_got_ref,
    value_last_ref,
    key_ref,
    key_got_ref,
    key_last_ref,
    going_ref,
    high_ref,
):
    key_width = value_ref.shape[-2]
    for i, ref in enumerate((going_ref.at[0], going_ref.at[1], high_ref)):
        for j, parts in enumerate(
            (
                (key_ref, key_got_ref, key_last_ref),
                (value_ref, value_got_ref, value_last_ref),
            )
        ):
            total = sum(part[i].astype(F32) for part in parts)
            ref[j * key_width : (j + 1) * key_width, :] = total.astype(ref.dtype)


def plane_call(value, value_got, value_last, key, key_got, key_last):
    _, key_width, own = value.shape
    upper = pl.BlockSpec((4, key_width, own), lambda i: (1, 0, 0))
    last = pl.BlockSpec((4, key_width, own), lambda i: (0, 0, 0))
    shape = (2 * key_width, own)
    return pl.pallas_call(
        plane_kernel,
        name="plane_sum",
        grid=(1,),
        in_specs=[upper, upper, last] * 2,
        out_specs=[held((2, *shape)), held(shape)],
        out_shape=[
            jax.ShapeDtypeStruct((2, *shape), BF16),
            jax.ShapeDtypeStruct(shape, F32),
        ],
        cost_estimate=pl.CostEstimate(flops=1_000_000, bytes_accessed=3_000_000, transcendentals=0),
        compiler_params=pltpu.CompilerParams(vmem_limit_bytes=VMEM_LIMIT),
    )(value, value_got, value_last, key, key_got, key_last)


def final_kernel(
    where_ref,
    value_ref,
    value_got_ref,
    value_last_ref,
    key_ref,
    key_got_ref,
    key_last_ref,
    low_ref,
    high_ref,
    gain_ref,
    pair_ref,
    wk_ref,
    wv_ref,
    key_grad_ref,
    value_grad_ref,
    gain_term_ref,
):
    key_width = wk_ref.shape[0]
    term = jnp.zeros((1, wk_ref.shape[1]), F32)
    for j, (w_ref, out_ref, parts) in enumerate(
        (
            (wk_ref, key_grad_ref, (key_ref, key_got_ref, key_last_ref)),
            (wv_ref, value_grad_ref, (value_ref, value_got_ref, value_last_ref)),
        )
    ):
        at = slice(j * key_width, (j + 1) * key_width)
        total = sum(part[0].astype(F32) for part in parts)
        total = total + low_ref[0, at, :].astype(F32) + high_ref[at, :].astype(F32)
        term = term + jnp.sum(w_ref[...].astype(F32) * total, axis=0, keepdims=True)
        out_ref[...] = total * gain_ref[...] + pair_ref[at, :]
    gain_term_ref[...] = jnp.broadcast_to(term, gain_term_ref.shape)


def final_call(where, value, value_got, value_last, key, key_got, key_last, line, gain_ctx, pair, wk, wv):
    rows, own = pair.shape
    width = gain_ctx.shape[0]
    key_width = rows // 2
    w_spec = pl.BlockSpec((key_width, own), lambda i, w: (0, w[0]))
    end = pl.BlockSpec((1, key_width, own), lambda i, w: (7, 0, 0))
    last = pl.BlockSpec((1, key_width, own), lambda i, w: (3, 0, 0))
    return pl.pallas_call(
        final_kernel,
        name="key_value_gradients",
        grid_spec=pltpu.PrefetchScalarGridSpec(
            num_scalar_prefetch=1,
            grid=(1,),
            in_specs=[end, end, last] * 2
            + [pl.BlockSpec((1, rows, own), lambda i, w: (1, 0, 0)), held(pair.shape)]
            + [pl.BlockSpec((1, own), lambda i, w: (0, w[0])), held(pair.shape), w_spec, w_spec],
            out_specs=[held((key_width, own)), held((key_width, own)), held((8, own))],
        ),
        out_shape=[
            jax.ShapeDtypeStruct((key_width, own), F32),
            jax.ShapeDtypeStruct((key_width, own), F32),
            jax.ShapeDtypeStruct((8, own), F32),
        ],
        cost_estimate=pl.CostEstimate(flops=1_000_000, bytes_accessed=3_000_000, transcendentals=0),
        compiler_params=pltpu.CompilerParams(vmem_limit_bytes=VMEM_LIMIT),
    )(
        where,
        value,
        value_got,
        value_last,
        key,
        key_got,
        key_last,
        *line,
        gain_ctx.reshape(1, width),
        pair,
        wk,
        wv,
    )


def out_final_kernel(
    where_ref,
    first_kept_ref,
    first_got_ref,
    first_last_ref,
    second_kept_ref,
    second_got_ref,
    second_last_ref,
    message_ref,
    message_got_ref,
    term_ref,
    term_got_ref,
    lat_ref,
    gain_ref,
    out_ref,
    latent_ref,
    gain_lat_ref,
    gain_ctx_ref,
):
    heads, own = out_ref.shape
    latent_rows, width = lat_ref.shape
    share = own // 2
    cut = heads // 2
    first = sum(
        part.astype(F32) for part in (first_kept_ref[0], first_got_ref[0], first_last_ref[...])
    )
    out_ref[:cut, :] = first[:cut]
    out_ref[cut:, :] = sum(
        part.astype(F32) for part in (second_kept_ref[0], second_got_ref[0], second_last_ref[...])
    )
    resid = first[cut:]
    resid = jnp.concatenate([resid[:, :share], resid[:, share:]], axis=0)
    mine = pl.ds(pl.multiple_of(where_ref[1] * share, share), share)
    d_lat = message_ref[:, mine] + message_got_ref[:, mine]
    lat_dot = message_ref[:latent_rows, own : own + 1] + message_got_ref[:latent_rows, own : own + 1]
    lat = lat_ref[...].astype(F32)
    inverse = lax.rsqrt(jnp.mean(lat * lat, axis=-1, keepdims=True) + EPSILON)
    at = pl.ds(pl.multiple_of(where_ref[0] * own + where_ref[1] * share, share), share)
    hat = lat_ref[:, at].astype(F32) * inverse
    latent_ref[...] = resid + inverse * (gain_ref[:, at] * d_lat[:latent_rows] - hat * (lat_dot / width))
    gain_lat_ref[...] = d_lat[latent_rows : latent_rows + 1]
    gain_ctx_ref[...] = term_ref[:1, mine] + term_got_ref[:1, mine]


def out_final_call(where, parts, message, message_got, term, term_got, latents, gain_lat):
    _, rows, own = parts[0].shape
    latent_rows, width = latents.shape
    heads = 2 * (rows - latent_rows // 2)
    shapes = [(heads, own), (latent_rows, own // 2), (1, own // 2), (1, own // 2)]
    return pl.pallas_call(
        out_final_kernel,
        name="output_gradient_sum",
        grid_spec=pltpu.PrefetchScalarGridSpec(
            num_scalar_prefetch=1,
            grid=(1,),
            in_specs=[
                pl.BlockSpec((1, *part.shape[1:]), lambda i, w: (1, 0, 0))
                if part.ndim == 3
                else held(part.shape)
                for part in parts
            ]
            + [held(a.shape) for a in (message, message_got, term, term_got, latents)]
            + [held((1, width))],
            out_specs=[held(shape) for shape in shapes],
        ),
        out_shape=[jax.ShapeDtypeStruct(shape, F32) for shape in shapes],
        cost_estimate=pl.CostEstimate(flops=1_000_000, bytes_accessed=3_000_000, transcendentals=0),
        compiler_params=pltpu.CompilerParams(vmem_limit_bytes=VMEM_LIMIT),
    )(
        where,
        *parts,
        message,
        message_got,
        term,
        term_got,
        latents,
        gain_lat.reshape(1, width),
    )


def add_halves(left, right):
    return left.astype(F32) + right.astype(F32)


def local(
    context,
    counts,
    routes,
    w_query,
    w_key,
    w_value,
    w_out,
    latents,
    gain_ctx,
    gain_lat,
    gain_out,
    cotangent,
):
    dp_count = lax.axis_size("dp")
    mp_index = lax.axis_index("mp")
    dp_index = lax.axis_index("dp")
    patch_rows, width = context.shape
    half_width = width // 2
    own_width = width // dp_count
    latent_rows = latents.shape[0]
    slot_count = cotangent.shape[0] // dp_count
    slots = dp_count * slot_count
    query_width = w_query.shape[1]

    def swap(array, turn):
        return lax.ppermute(array, "dp", [(i, i ^ turn) for i in range(dp_count)])

    def exchange(array):
        blocks = array.reshape(dp_count, slot_count, half_width)
        return lax.all_to_all(blocks, "dp", split_axis=0, concat_axis=0, tiled=True).reshape(
            slots, half_width
        )

    wk = w_key.T
    wv = w_value.T
    turned_routes = routes.reshape(1, -1)
    where = jnp.stack([dp_index, mp_index])

    returned = exchange(cotangent)
    w_out_other = swap_cores(w_out)
    wk_other = swap_cores(wk)
    wv_other = swap_cores(wv)

    (attn_rows, k, v, inv_row, q, lat_k, lat_v, lat_proj, p, lat_p) = forward_call(
        context, counts, w_query, wk, wv, latents, gain_ctx, gain_lat
    )
    wk_other, wv_other, attn_rows = lax.optimization_barrier((wk_other, wv_other, attn_rows))
    attn_other = swap_cores(attn_rows)
    out_hat, out_inv, outgoing = branch_call(
        attn_rows,
        attn_other,
        w_out,
        w_out_other,
        latents,
        gain_out,
        turned_routes,
        slots,
        slot_count,
    )

    routed = exchange(outgoing)
    returned, out_inv = lax.optimization_barrier((returned, out_inv))
    returned_other = swap_cores(returned)
    backward = backward_call(
        counts,
        attn_rows,
        returned,
        returned_other,
        out_hat,
        out_inv,
        gain_out,
        turned_routes,
        w_out,
        (k, v, q, lat_k, lat_v, p, lat_p, inv_row),
        context,
        slot_count,
    )
    backward = lax.optimization_barrier(backward)
    (
        line_own,
        line_high,
        pair,
        message,
        lat_terms,
        value_going,
        value_kept,
        key_going,
        key_kept,
    ) = backward

    value_got = swap(value_going, 1)
    key_got = swap(key_going, 2)
    pair_other = swap_cores(pair)

    line_high, message, lat_terms, pair_other = lax.optimization_barrier(
        (line_high, message, lat_terms, pair_other)
    )
    lat_got = swap(lat_terms, 4)
    got_high = swap(line_high, 8)
    got_low = swap(message, 4)

    ctx_grad = patch_call(
        where, pair, pair_other, wk, wv, wk_other, wv_other, context, inv_row, gain_ctx
    )

    lat_got, ctx_grad = lax.optimization_barrier((lat_got, ctx_grad))
    lat_sum = add_halves(lat_terms, lat_got)
    lat_low = lat_sum.astype(BF16)
    value_got, key_got, ctx_grad, routed, lat_low = lax.optimization_barrier(
        (value_got, key_got, ctx_grad, routed, lat_low)
    )
    key_kept = key_kept.reshape((8,) + key_kept.shape[2:])
    key_got = key_got.reshape((8,) + key_got.shape[2:])
    value_going = add_halves(value_kept[:4], value_got[:4]).astype(BF16)
    key_going = add_halves(key_kept[:4], key_got[:4]).astype(BF16)
    value_last = swap(value_going, 2)
    key_last = swap(key_going, 1)

    got_low, got_high, value_going, key_going, lat_low = lax.optimization_barrier(
        (got_low, got_high, value_going, key_going, lat_low)
    )
    lat_got = swap(lat_low, 8)
    forwarded = swap(got_high[:, width // 4 :], 4)
    other_low = swap_cores(got_low)
    other_high = swap_cores(got_high)

    planes = plane_call(value_kept, value_got, value_last, key_kept, key_got, key_last)
    (going, high), lat_got, forwarded = lax.optimization_barrier((planes, lat_got, forwarded))
    low = swap(going, 4)
    other_forwarded = swap_cores(forwarded)
    lat_sum = add_halves(lat_sum, lat_got).astype(BF16)
    lat_parts = (swap(lat_sum, 1), swap(lat_sum, 2), swap(lat_sum, 3))

    first_going, first_kept, second_going, second_kept = out_call(
        where,
        attn_rows,
        line_own,
        (got_low, got_high, forwarded),
        (other_low, other_high, other_forwarded),
    )
    low, first_going, second_going = lax.optimization_barrier((low, first_going, second_going))
    high = add_halves(high, low[0]).astype(BF16)
    high, lat_parts, first_going, second_going = lax.optimization_barrier(
        (high, lat_parts, first_going, second_going)
    )
    high = swap(high, 8)
    first_got = swap(first_going, 1)
    second_got = swap(second_going, 2)

    grad_w_query, pair_lat, message, grad_gain_out, routed = latent_call(
        where, lat_sum, lat_parts, lat_proj, latents, gain_lat, w_query, wk, wv, own_width, routed
    )
    first_got, second_got, high, message, pair_lat = lax.optimization_barrier(
        (first_got, second_got, high, message, pair_lat)
    )
    first_last = swap(add_halves(first_kept[0], first_got[0]).astype(BF16), 2)
    second_last = swap(add_halves(second_kept[0], second_got[0]).astype(BF16), 1)
    message_got = swap_cores(message)

    grad_key, grad_value, gain_term = final_call(
        where,
        value_kept,
        value_got,
        value_last,
        key_kept,
        key_got,
        key_last,
        (low, high),
        gain_ctx,
        pair_lat,
        wk,
        wv,
    )
    gain_got = swap_cores(gain_term)
    first_last, second_last, gain_term = lax.optimization_barrier(
        (first_last, second_last, gain_term)
    )
    grad_w_out, grad_latents, grad_gain_lat, grad_gain_ctx = out_final_call(
        where,
        (first_kept, first_got, first_last, second_kept, second_got, second_last),
        message,
        message_got,
        gain_term,
        gain_got,
        latents,
        gain_lat,
    )
    return (
        routed,
        ctx_grad,
        grad_w_query,
        grad_key.T,
        grad_value.T,
        grad_w_out,
        grad_latents,
        grad_gain_ctx[0],
        grad_gain_lat[0],
        grad_gain_out[0],
    )


def local_general(
    context,
    counts,
    routes,
    w_query,
    w_key,
    w_value,
    w_out,
    latents,
    gain_ctx,
    gain_lat,
    gain_out,
    cotangent,
):
    dp_count = lax.axis_size("dp")
    mp_count = lax.axis_size("mp")
    mp_index = lax.axis_index("mp")
    dp_index = lax.axis_index("dp")
    bits = dp_count.bit_length() - 1
    gather_bits = [bits - 1, bits - 2]
    scatter_bits = list(range(bits - 2))
    order_one = list(range(bits))
    order_two = [1, 0] + order_one[2:]
    patch_rows, width = context.shape
    half_width = width // mp_count
    own_width = width // dp_count
    head_local = w_query.shape[1] // HD
    group_local = w_key.shape[1] // HD
    per_group = head_local // group_local
    latent_rows = latents.shape[0]
    image_slots = counts.shape[1]
    out_rows = image_slots * latent_rows
    slot_count = cotangent.shape[0] // dp_count
    key_width = w_key.shape[1]
    query_width = w_query.shape[1]
    scaling = HD ** (-0.5)

    returned = lax.all_to_all(
        cotangent.reshape(dp_count, slot_count, half_width),
        "dp",
        split_axis=0,
        concat_axis=0,
        tiled=True,
    ).reshape(dp_count * slot_count, half_width)
    returned_other = swap_cores(returned)
    w_out_other = swap_cores(w_out)
    w_pair = jnp.concatenate([w_key, w_value], axis=1)
    w_pair_half = lax.dynamic_slice_in_dim(w_pair, mp_index * half_width, half_width, 0)
    w_pair_other = swap_cores(
        lax.dynamic_slice_in_dim(w_pair, (1 - mp_index) * half_width, half_width, 0)
    )

    patch_hat, patch_inv = norm_parts(context.astype(F32))
    normed_ctx = (patch_hat * gain_ctx).astype(BF16)
    key_f32 = jnp.dot(normed_ctx, w_key, preferred_element_type=F32)
    value_f32 = jnp.dot(normed_ctx, w_value, preferred_element_type=F32)
    key_rows = key_f32.astype(BF16)
    value_rows = value_f32.astype(BF16)
    lat_float = latents.astype(F32)
    lat_hat, lat_inv = norm_parts(lat_float)
    normed_lat = (lat_hat * gain_lat).astype(BF16)
    lat_key_f32 = jnp.dot(normed_lat, w_key, preferred_element_type=F32)
    lat_value_f32 = jnp.dot(normed_lat, w_value, preferred_element_type=F32)
    lat_keys = lat_key_f32.astype(BF16)
    lat_values = lat_value_f32.astype(BF16)
    query_f32 = jnp.dot(normed_lat, w_query, preferred_element_type=F32) * scaling
    query_rows = query_f32.astype(BF16)
    query_heads = query_rows.reshape(latent_rows, group_local, per_group, HD)
    key_heads = key_rows.reshape(patch_rows, group_local, HD)
    value_heads = value_rows.reshape(patch_rows, group_local, HD)
    lat_key_heads = lat_keys.reshape(latent_rows, group_local, HD)
    lat_value_heads = lat_values.reshape(latent_rows, group_local, HD)
    scores = jnp.einsum(
        "rkgd,tkd->kgrt", query_heads, key_heads, preferred_element_type=jnp.float32
    )
    lat_scores = jnp.einsum(
        "rkgd,skd->kgrs", query_heads, lat_key_heads, preferred_element_type=jnp.float32
    )
    position = jnp.arange(patch_rows, dtype=jnp.int32)
    image_count = counts[0]
    image_start = jnp.cumsum(image_count) - image_count
    member = (position[None, :] >= image_start[:, None]) & (
        position[None, :] < (image_start + image_count)[:, None]
    )
    member_wide = member[:, None, None, None, :]
    masked = jnp.where(member_wide, scores[None], NEGATIVE)
    row_max = jnp.maximum(
        jnp.max(masked, axis=-1, keepdims=True), jnp.max(lat_scores, axis=-1, keepdims=True)[None]
    )
    exponent = jnp.where(member_wide, jnp.exp(masked - row_max), 0.0)
    lat_exponent = jnp.exp(lat_scores[None] - row_max)
    total = jnp.sum(exponent, axis=-1, keepdims=True) + jnp.sum(
        lat_exponent, axis=-1, keepdims=True
    )
    attention = exponent / total
    lat_attention = lat_exponent / total
    attention_low = attention.astype(BF16)
    lat_attention_low = lat_attention.astype(BF16)
    mixed = jnp.einsum(
        "ikgrt,tkd->irkgd", attention_low, value_heads, preferred_element_type=jnp.float32
    )
    mixed = mixed + jnp.einsum(
        "ikgrs,skd->irkgd", lat_attention_low, lat_value_heads, preferred_element_type=jnp.float32
    )
    attn_rows = mixed.reshape(out_rows, query_width).astype(BF16)
    attn_other = swap_cores(attn_rows)
    branch = jnp.dot(attn_rows, w_out, preferred_element_type=F32) + jnp.dot(
        attn_other, w_out_other, preferred_element_type=F32
    )
    resid = jnp.tile(lat_float, (image_slots, 1)) + branch
    out_hat, out_inv = norm_parts(resid)
    final_rows = (out_hat * gain_out).astype(BF16)
    shard_of = routes[:, 0]
    shard_hot = (shard_of[:, None] == jnp.arange(dp_count, dtype=jnp.int32)[None, :]).astype(
        jnp.int32
    )
    rank = jnp.sum((jnp.cumsum(shard_hot, axis=0) - shard_hot) * shard_hot, axis=1)
    place = shard_of * slot_count + rank
    scatter_table = (
        jnp.arange(dp_count * slot_count, dtype=jnp.int32)[:, None] == place[None, :]
    ).astype(BF16)
    final_half = lax.dynamic_slice_in_dim(final_rows, mp_index * half_width, half_width, 1)
    outgoing = jnp.dot(scatter_table, final_half, preferred_element_type=F32).astype(BF16)
    routed = lax.all_to_all(
        outgoing.reshape(dp_count, slot_count, half_width),
        "dp",
        split_axis=0,
        concat_axis=0,
        tiled=True,
    ).reshape(dp_count * slot_count, half_width)

    attn_line = attn_rows
    for bit in gather_bits:
        attn_line = jnp.concatenate([attn_line, swap_bit(attn_line, bit, dp_count)], axis=0)

    first = jnp.where(mp_index == 0, returned, returned_other)
    second = jnp.where(mp_index == 0, returned_other, returned)
    d_final = jnp.concatenate(
        [dot_general(scatter_table, first, 0, 0), dot_general(scatter_table, second, 0, 0)], axis=1
    )
    d_hat = d_final * gain_out
    d_resid = out_inv * (d_hat - out_hat * jnp.mean(d_hat * out_hat, axis=1, keepdims=True))
    gain_out_term = jnp.sum(d_final * out_hat, axis=0)
    d_branch = d_resid.astype(BF16)
    d_attn = dot_general(d_branch, w_out, 1, 1).astype(BF16)

    d_attn_heads = d_attn.reshape(image_slots, latent_rows, group_local, per_group, HD)
    d_probs = jnp.einsum(
        "irkgd,tkd->ikgrt", d_attn_heads, value_heads, preferred_element_type=jnp.float32
    )
    d_lat_probs = jnp.einsum(
        "irkgd,skd->ikgrs", d_attn_heads, lat_value_heads, preferred_element_type=jnp.float32
    )
    row_delta = jnp.sum(attention * d_probs, axis=-1, keepdims=True) + jnp.sum(
        lat_attention * d_lat_probs, axis=-1, keepdims=True
    )
    d_scores = jnp.sum(attention * (d_probs - row_delta), axis=0).astype(BF16)
    d_lat_scores = jnp.sum(lat_attention * (d_lat_probs - row_delta), axis=0).astype(BF16)
    d_query = jnp.einsum("kgrt,tkd->rkgd", d_scores, key_heads, preferred_element_type=jnp.float32)
    d_query = d_query + jnp.einsum(
        "kgrs,skd->rkgd", d_lat_scores, lat_key_heads, preferred_element_type=jnp.float32
    )
    d_query = d_query.reshape(latent_rows, query_width).astype(BF16)
    d_keys = jnp.einsum("kgrt,rkgd->tkd", d_scores, query_heads, preferred_element_type=jnp.float32)
    d_keys = d_keys.reshape(patch_rows, key_width).astype(BF16)
    d_values = jnp.einsum(
        "ikgrt,irkgd->tkd", attention_low, d_attn_heads, preferred_element_type=jnp.float32
    )
    d_values = d_values.reshape(patch_rows, key_width).astype(BF16)
    d_lat_keys = jnp.einsum(
        "kgrs,rkgd->skd", d_lat_scores, query_heads, preferred_element_type=jnp.float32
    )
    d_lat_keys = d_lat_keys.reshape(latent_rows, key_width).astype(BF16)
    d_lat_values = jnp.einsum(
        "ikgrs,irkgd->skd", lat_attention_low, d_attn_heads, preferred_element_type=jnp.float32
    )
    d_lat_values = d_lat_values.reshape(latent_rows, key_width).astype(BF16)
    d_pair = jnp.concatenate([d_keys, d_values], axis=1)

    value_grad = dot_general(d_values, normed_ctx, 0, 0).reshape(key_width, dp_count, own_width)
    key_grad = dot_general(d_keys, normed_ctx, 0, 0).reshape(key_width, dp_count, own_width)
    value_block = scatter_sum(value_grad, order_one, dp_count)
    key_block = scatter_sum(key_grad, order_two, dp_count)

    row_dot = jnp.sum(d_keys.astype(F32) * key_f32, axis=1) + jnp.sum(
        d_values.astype(F32) * value_f32, axis=1
    )
    row_dot = (row_dot + swap_cores(row_dot)) / width
    d_pair_other = swap_cores(d_pair)
    d_ctx_in = dot_general(d_pair, w_pair_half, 1, 1) + dot_general(
        d_pair_other, w_pair_other, 1, 1
    )
    gain_ctx_half = lax.dynamic_slice_in_dim(gain_ctx, mp_index * half_width, half_width, 0)
    hat_half = lax.dynamic_slice_in_dim(patch_hat, mp_index * half_width, half_width, 1)
    ctx_grad = (patch_inv * (d_ctx_in * gain_ctx_half - hat_half * row_dot[:, None])).astype(BF16)

    high = gain_out_term.astype(BF16)
    low = (gain_out_term - high.astype(F32)).astype(BF16)
    lat_sum = jnp.concatenate(
        [
            d_query,
            d_lat_keys,
            d_lat_values,
            high.reshape(latent_rows, width // latent_rows),
            low.reshape(latent_rows, width // latent_rows),
        ],
        axis=1,
    ).astype(F32)
    for bit in gather_bits + scatter_bits:
        lat_sum = lat_sum + swap_bit(lat_sum.astype(BF16), bit, dp_count).astype(F32)
    pair_sum = lat_sum[:, query_width : query_width + 2 * key_width]
    query_sum = lat_sum[:, :query_width]
    gains_at = query_width + 2 * key_width
    gain_step = width // latent_rows
    gain_out_full = (
        lat_sum[:, gains_at : gains_at + gain_step]
        + lat_sum[:, gains_at + gain_step : gains_at + 2 * gain_step]
    ).reshape(width)

    plane = dp_count // 4
    row_half = out_rows // mp_count
    d_block = lax.dynamic_slice_in_dim(d_branch, mp_index * row_half, row_half, 0)
    d_line = d_block.reshape(1, row_half, 2, 2, plane * own_width)
    for step, bit in enumerate(gather_bits):
        mine = (dp_index >> bit) & 1
        going = lax.dynamic_index_in_dim(d_line, 1 - mine, 2, keepdims=False)
        kept = lax.dynamic_index_in_dim(d_line, mine, 2, keepdims=False)
        d_line = jnp.concatenate([kept, swap_bit(going, bit, dp_count)], axis=0)
    d_line_other = swap_cores(d_line)
    d_line = jnp.concatenate(
        [
            jnp.where(mp_index == 0, d_line, d_line_other),
            jnp.where(mp_index == 0, d_line_other, d_line),
        ],
        axis=1,
    )
    out_part = dot_general(attn_line, d_line.reshape(4 * out_rows, plane * own_width), 0, 0)
    resid_part = jnp.sum(
        d_line.astype(F32).reshape(4 * image_slots, latent_rows, plane * own_width), axis=0
    )
    resid_part = lax.dynamic_index_in_dim(
        resid_part.reshape(2, latent_rows // 2, plane, mp_count, own_width // mp_count),
        mp_index,
        3,
        keepdims=False,
    )
    resid_part = jnp.transpose(resid_part, (1, 2, 0, 3)).reshape(
        latent_rows // 2, plane, own_width
    )
    out_part = jnp.concatenate([out_part.reshape(query_width, plane, own_width), resid_part], axis=0)
    cut = out_part.shape[0] // 2
    out_block = jnp.concatenate(
        [
            scatter_sum(out_part[:cut], scatter_bits, dp_count),
            scatter_sum(out_part[cut:], [1, 0] + scatter_bits[2:], dp_count),
        ],
        axis=0,
    )
    grad_w_out = out_block[:query_width]
    resid_sum = (
        out_block[query_width:]
        .reshape(latent_rows // 2, 2, own_width // mp_count)
        .transpose(1, 0, 2)
        .reshape(latent_rows, own_width // mp_count)
    )

    def own(array, axis):
        return lax.dynamic_slice_in_dim(array, dp_index * own_width, own_width, axis)

    lat_own = own(normed_lat, 1)
    pair_ctx = jnp.concatenate([key_block, value_block], axis=0).T
    query_grad = dot_general(lat_own, query_sum.astype(BF16), 0, 0) * scaling
    pair_lat = dot_general(lat_own, pair_sum.astype(BF16), 0, 0)
    pair_all = pair_ctx + pair_lat
    wq_own = own(w_query, 0)
    pair_own = own(w_pair, 0)
    gain_ctx_part = jnp.sum(pair_own.astype(F32) * pair_ctx, axis=1) / own(gain_ctx, 0)
    gain_lat_part = (
        jnp.sum(wq_own.astype(F32) * query_grad, axis=1)
        + jnp.sum(pair_own.astype(F32) * pair_lat, axis=1)
    ) / own(gain_lat, 0)
    d_lat_part = dot_general(
        (query_sum * scaling).astype(BF16), wq_own, 1, 1
    ) + dot_general(pair_sum.astype(BF16), pair_own, 1, 1)
    lat_dot_part = (
        jnp.sum(query_sum * query_f32, axis=1)
        + jnp.sum(pair_sum[:, :key_width] * lat_key_f32, axis=1)
        + jnp.sum(pair_sum[:, key_width:] * lat_value_f32, axis=1)
    )
    small = jnp.concatenate(
        [
            d_lat_part,
            jnp.broadcast_to(lat_dot_part[:, None], (latent_rows, own_width)),
            jnp.broadcast_to(gain_ctx_part[None, :], (8, own_width)),
            jnp.broadcast_to(gain_lat_part[None, :], (8, own_width)),
        ],
        axis=0,
    )
    small = small + swap_cores(small)
    share = own_width // mp_count
    small = lax.dynamic_slice_in_dim(small, mp_index * share, share, 1)
    d_lat_in = small[:latent_rows]
    lat_dot = small[latent_rows : 2 * latent_rows] / width

    def mine_of(array, axis):
        return lax.dynamic_slice_in_dim(
            array, dp_index * own_width + mp_index * share, share, axis
        )

    grad_latents = resid_sum + lat_inv * (
        mine_of(gain_lat, 0) * d_lat_in - mine_of(lat_hat, 1) * lat_dot
    )
    return (
        routed,
        ctx_grad,
        query_grad,
        pair_all[:, :key_width],
        pair_all[:, key_width:],
        grad_w_out,
        grad_latents,
        small[2 * latent_rows],
        small[2 * latent_rows + 8],
        mine_of(gain_out_full, 0),
    )


def solution(mesh):
    placed = (
        P("dp", None),
        P("dp", None),
        P("dp", None),
        P(None, "mp"),
        P(None, "mp"),
        P(None, "mp"),
        P("mp", None),
        P(),
        P(),
        P(),
        P(),
        P("dp", "mp"),
    )
    return jax.shard_map(
        local if mesh.shape["dp"] == 16 else local_general,
        mesh=mesh,
        in_specs=placed,
        out_specs=(
            P("dp", "mp"),
            P("dp", "mp"),
            P("dp", "mp"),
            P("dp", "mp"),
            P("dp", "mp"),
            P("mp", "dp"),
            P(None, ("dp", "mp")),
            P(("dp", "mp")),
            P(("dp", "mp")),
            P(("dp", "mp")),
        ),
        check_vma=False,
    )
```

```python
import functools

import jax
import jax.numpy as jnp
from jax import lax
from jax.experimental import pallas as pl
from jax.experimental.pallas import tpu as pltpu
from jax.sharding import PartitionSpec as P

HD = 96
EPSILON = 1e-06
NEGATIVE = -1e30
BF16 = jnp.bfloat16
F32 = jnp.float32
VMEM_LIMIT = 63 << 20


def dot_general(left, right, left_dim, right_dim):
    return lax.dot_general(
        left, right, (((left_dim,), (right_dim,)), ((), ())), preferred_element_type=F32
    )


def norm_parts(values_in):
    inverse = lax.rsqrt(jnp.mean(values_in * values_in, axis=-1, keepdims=True) + EPSILON)
    return (values_in * inverse, inverse)


def swap_cores(array):
    return lax.ppermute(array, "mp", [(0, 1), (1, 0)])


def swap_bit(array, bit, dp_count):
    return lax.ppermute(array, "dp", [(i, i ^ (1 << bit)) for i in range(dp_count)])


def halve(array, axis, bit, dp_count):
    mine = (lax.axis_index("dp") >> bit) & 1
    going = lax.dynamic_index_in_dim(array, 1 - mine, axis, keepdims=False)
    kept = lax.dynamic_index_in_dim(array, mine, axis, keepdims=False)
    return kept.astype(F32) + swap_bit(going.astype(BF16), bit, dp_count).astype(F32)


def scatter_sum(array, bits, dp_count):
    rows, owners, columns = array.shape
    left = sorted(bits, reverse=True)
    array = array.reshape((rows,) + (2,) * len(left) + (columns,))
    for bit in bits:
        axis = left.index(bit)
        array = halve(array, 1 + axis, bit, dp_count)
        left.pop(axis)
    return array


def forward_kernel(
    counts_ref,
    gain_ctx_hbm,
    gain_lat_hbm,
    lat_hbm,
    wk_hbm,
    wv_hbm,
    x_hbm,
    wq_hbm,
    attn_hbm,
    k_hbm,
    v_hbm,
    inv_row_hbm,
    q_hbm,
    lk_hbm,
    lv_hbm,
    lat_proj_hbm,
    p_hbm,
    pl_hbm,
    gain_ctx_ref,
    gain_lat_ref,
    lat_ref,
    wk_ref,
    wv_ref,
    x_ref,
    wq_ref,
    attn_ref,
    k_ref,
    v_ref,
    inv_row_ref,
    q_ref,
    lk_ref,
    lv_ref,
    lat_proj_ref,
    p_ref,
    pl_ref,
    lat_normed_ref,
    last_ref,
    gained_ref,
    sems,
    out_sems,
):
    patch_rows, width = x_ref.shape
    chunks = sems.shape[0] - 6
    rows = patch_rows // chunks
    groups = k_ref.shape[0]
    latent_rows = lat_ref.shape[0]
    key_width = wk_ref.shape[0]
    query_width = wq_ref.shape[1]
    per_group = query_width // key_width

    def fetch(source, target, i):
        return pltpu.make_async_copy(source, target, sems.at[i])

    def fetch_rows(i):
        at = pl.ds(i * rows, rows)
        return fetch(x_hbm.at[at], x_ref.at[at], i)

    weights = [
        fetch(source, target, chunks + i)
        for i, (source, target) in enumerate(
            ((lat_hbm, lat_ref), (wk_hbm, wk_ref), (wv_hbm, wv_ref), (wq_hbm, wq_ref))
        )
    ]
    gains = [
        fetch(gain_ctx_hbm, gain_ctx_ref, chunks + 4),
        fetch(gain_lat_hbm, gain_lat_ref, chunks + 5),
    ]
    for copy in (*gains, *weights[:3]):
        copy.start()
    blocks = [fetch_rows(i) for i in range(chunks)]
    for copy in blocks + weights[3:]:
        copy.start()
    results = {}
    for i, (name, source, target) in enumerate(
        (
            ("attn", attn_ref, attn_hbm),
            ("k", k_ref, k_hbm),
            ("v", v_ref, v_hbm),
            ("inv_row", inv_row_ref, inv_row_hbm),
            ("q", q_ref, q_hbm),
            ("lk", lk_ref, lk_hbm),
            ("lv", lv_ref, lv_hbm),
            ("lat_proj", lat_proj_ref, lat_proj_hbm),
            ("p0", p_ref.at[0], p_hbm.at[0]),
            ("p1", p_ref.at[1], p_hbm.at[1]),
            ("pl", pl_ref, pl_hbm),
        )
    ):
        results[name] = pltpu.make_async_copy(source, target, out_sems.at[i])

    for copy in (*gains, weights[0]):
        copy.wait()
    lat = lat_ref[...].astype(F32)
    lat_inverse = lax.rsqrt(jnp.mean(lat * lat, axis=-1, keepdims=True) + EPSILON)
    lat_normed = lat * lat_inverse * gain_lat_ref[...]
    lat_normed_ref[...] = lat_normed.astype(BF16)
    last_ref[rows:, :] = (lat_normed / gain_ctx_ref[...]).astype(BF16)
    for i, ref in enumerate((wk_ref, wv_ref)):
        weights[1 + i].wait()
        gained_ref[i * key_width : (i + 1) * key_width, :] = (
            ref[...].astype(F32) * gain_ctx_ref[...]
        ).astype(BF16)
    for i in range(chunks):
        blocks[i].wait()
        at = slice(i * rows, (i + 1) * rows)
        squares = jnp.zeros((rows, 128), F32)
        for c in range(width // 128):
            part = x_ref[at, c * 128 : (c + 1) * 128].astype(F32)
            squares = squares + part * part
        inverse = lax.rsqrt(jnp.sum(squares, axis=-1, keepdims=True) / width + EPSILON)
        if i < chunks - 1:
            pair = dot_general(x_ref[at, :], gained_ref[...], 1, 1)
        else:
            last_ref[:rows, :] = x_ref[at, :]
            pair = dot_general(last_ref[...], gained_ref[...], 1, 1)
            projected = pair[rows:]
        pair = (pair[:rows] * inverse).astype(BF16)
        inv_row_ref[:, at] = jnp.transpose(jnp.broadcast_to(inverse, (rows, 128)))[:8]
        for g in range(groups):
            k_ref[g, at, :HD] = pair[:, g * HD : (g + 1) * HD]
            v_ref[g, at, :HD] = pair[:, key_width + g * HD : key_width + (g + 1) * HD]
    lat_proj_ref[:, query_width:] = projected
    for i, ref in enumerate((lk_ref, lv_ref)):
        for g in range(groups):
            at = i * key_width + g * HD
            ref[g, :, :HD] = projected[:, at : at + HD].astype(BF16)
    for name in ("k", "v", "inv_row", "lk", "lv"):
        results[name].start()
    weights[3].wait()
    query = jnp.dot(lat_normed_ref[...], wq_ref[...], preferred_element_type=F32) * HD ** (-0.5)
    lat_proj_ref[:, :query_width] = query
    first_count = counts_ref[0, 0]
    both_count = first_count + counts_ref[0, 1]
    position = lax.broadcasted_iota(jnp.int32, (1, patch_rows), 1)
    in_first = position < first_count
    in_second = jnp.logical_and(position >= first_count, position < both_count)
    rows_at = lax.broadcasted_iota(jnp.int32, (patch_rows, HD), 0)
    row_first = rows_at < first_count
    row_second = jnp.logical_and(rows_at >= first_count, rows_at < both_count)
    for g in range(groups):
        for h in range(per_group):
            head = g * per_group + h
            q_ref[g, h * latent_rows : (h + 1) * latent_rows, :HD] = query[
                :, head * HD : (head + 1) * HD
            ].astype(BF16)
    results["lat_proj"].start()
    results["q"].start()
    for g in range(groups):
        q = q_ref[g, :, :HD]
        scores = dot_general(q, k_ref[g, :, :HD], 1, 1)
        lat_scores = dot_general(q, lk_ref[g, :, :HD], 1, 1)
        lat_max = jnp.max(lat_scores, axis=-1, keepdims=True)
        max_first = jnp.maximum(
            jnp.max(jnp.where(in_first, scores, NEGATIVE), axis=-1, keepdims=True), lat_max
        )
        max_second = jnp.maximum(
            jnp.max(jnp.where(in_second, scores, NEGATIVE), axis=-1, keepdims=True), lat_max
        )
        masked = jnp.where(
            in_first, scores - max_first, jnp.where(in_second, scores - max_second, NEGATIVE)
        )
        exponent = jnp.exp(masked)
        lat_first = jnp.exp(lat_scores - max_first)
        lat_second = jnp.exp(lat_scores - max_second)
        sum_first = jnp.sum(
            jnp.where(in_first, exponent, 0.0), axis=-1, keepdims=True
        ) + jnp.sum(lat_first, axis=-1, keepdims=True)
        sum_second = jnp.sum(
            jnp.where(in_second, exponent, 0.0), axis=-1, keepdims=True
        ) + jnp.sum(lat_second, axis=-1, keepdims=True)
        per_first = 1.0 / sum_first
        per_second = 1.0 / sum_second
        p = (exponent * jnp.where(in_first, per_first, per_second)).astype(BF16)
        p_ref[g] = p
        results[f"p{g}"].start()
        lat_p_first = (lat_first * per_first).astype(BF16)
        lat_p_second = (lat_second * per_second).astype(BF16)
        pl_ref[g, :, :latent_rows] = lat_p_first
        pl_ref[g, :, latent_rows:] = lat_p_second
        v = v_ref[g, :, :HD]
        zero = jnp.zeros_like(v)
        lv = lv_ref[g, :, :HD]
        for j, (row_mask, lat_p) in enumerate(
            ((row_first, lat_p_first), (row_second, lat_p_second))
        ):
            mixed = jnp.dot(
                p, jnp.where(row_mask, v, zero), preferred_element_type=F32
            ) + jnp.dot(lat_p, lv, preferred_element_type=F32)
            mixed = mixed.astype(BF16)
            for h in range(per_group):
                head = g * per_group + h
                attn_ref[
                    j * latent_rows : (j + 1) * latent_rows, head * HD : (head + 1) * HD
                ] = mixed[h * latent_rows : (h + 1) * latent_rows]
    for name in ("attn", "pl"):
        results[name].start()
    for copy in results.values():
        copy.wait()


def whole(shape):
    return pl.BlockSpec(shape, lambda *_: (0,) * len(shape))


def held(shape):
    return pl.BlockSpec(shape, lambda *_: (0,) * len(shape), pipeline_mode=pl.Buffered(1))


def forward_call(context, counts, w_query, w_key, w_value, latents, gain_ctx, gain_lat):
    patch_rows, width = context.shape
    chunks = 4
    key_width = w_key.shape[0]
    query_width = w_query.shape[1]
    groups = key_width // HD
    latent_rows = latents.shape[0]
    stacked = query_width // key_width * latent_rows
    large = (latents, w_key, w_value, context, w_query)
    out = [
        ((2 * latent_rows, query_width), BF16),
        ((groups, patch_rows, 128), BF16),
        ((groups, patch_rows, 128), BF16),
        ((8, patch_rows), F32),
        ((groups, stacked, 128), BF16),
        ((groups, latent_rows, 128), BF16),
        ((groups, latent_rows, 128), BF16),
        ((latent_rows, query_width + 2 * key_width), F32),
        ((groups, stacked, patch_rows), BF16),
        ((groups, stacked, 2 * latent_rows), BF16),
    ]
    return pl.pallas_call(
        forward_kernel,
        name="forward_attention",
        in_specs=[
            pl.BlockSpec(memory_space=pltpu.SMEM),
            pl.BlockSpec(memory_space=pl.ANY),
            pl.BlockSpec(memory_space=pl.ANY),
        ]
        + [pl.BlockSpec(memory_space=pl.ANY)] * len(large),
        out_specs=[pl.BlockSpec(memory_space=pl.ANY)] * len(out),
        out_shape=[jax.ShapeDtypeStruct(shape, dtype) for shape, dtype in out],
        scratch_shapes=[pltpu.VMEM((1, width), F32)] * 2
        + [pltpu.VMEM(a.shape, a.dtype) for a in large]
        + [pltpu.VMEM(shape, dtype) for shape, dtype in out]
        + [
            pltpu.VMEM((latent_rows, width), BF16),
            pltpu.VMEM((patch_rows // chunks + latent_rows, width), BF16),
            pltpu.VMEM((2 * key_width, width), BF16),
            pltpu.SemaphoreType.DMA((chunks + 6,)),
            pltpu.SemaphoreType.DMA((len(out) + 1,)),
        ],
        cost_estimate=pl.CostEstimate(
            flops=5_000_000_000, bytes_accessed=24_000_000, transcendentals=600_000
        ),
        compiler_params=pltpu.CompilerParams(vmem_limit_bytes=VMEM_LIMIT),
    )(counts, gain_ctx.reshape(1, width), gain_lat.reshape(1, width), *large)


def slots_of(routes_ref, slot_count, as_row):
    rows = routes_ref.shape[1]
    turned = jnp.broadcast_to(routes_ref[...].astype(F32), (rows, rows))
    shard = jnp.transpose(turned)
    down = lax.broadcasted_iota(jnp.int32, (rows, rows), 0)
    across = lax.broadcasted_iota(jnp.int32, (rows, rows), 1)
    same = shard == turned
    if as_row:
        rank = jnp.sum(jnp.where(same & (down < across), 1.0, 0.0), axis=0, keepdims=True)
        return (turned[:1] * slot_count + rank).astype(jnp.int32)
    rank = jnp.sum(jnp.where(same & (across < down), 1.0, 0.0), axis=1, keepdims=True)
    return (shard[:, :1] * slot_count + rank).astype(jnp.int32)


def branch_kernel(
    slot_count,
    own_hbm,
    other_hbm,
    lat_hbm,
    gain_hbm,
    routes_hbm,
    w_own_hbm,
    w_other_hbm,
    hat_hbm,
    inv_hbm,
    out_hbm,
    own_ref,
    other_ref,
    lat_ref,
    gain_ref,
    routes_ref,
    w_own_ref,
    w_other_ref,
    hat_ref,
    low_ref,
    inv_ref,
    out_ref,
    sems,
    out_sems,
    small_sems,
):
    rows, width = hat_ref.shape
    slots, half = out_ref.shape
    parts = sems.shape[1]
    size = width // parts
    small = [
        pltpu.make_async_copy(source, target, small_sems.at[i])
        for i, (source, target) in enumerate(
            (
                (routes_hbm, routes_ref),
                (own_hbm, own_ref),
                (other_hbm, other_ref),
                (lat_hbm, lat_ref),
                (gain_hbm, gain_ref),
            )
        )
    ]
    for copy in small:
        copy.start()
    copies = []
    for part in range(parts):
        at = pl.ds(part * size, size)
        for i, (source, target) in enumerate(
            ((w_own_hbm, w_own_ref), (w_other_hbm, w_other_ref))
        ):
            copies.append(
                pltpu.make_async_copy(source.at[:, at], target.at[:, at], sems.at[i, part])
            )
    for copy in copies:
        copy.start()
    small[0].wait()
    place = slots_of(routes_ref, slot_count, True)
    for copy in small[1:]:
        copy.wait()
    table = jnp.where(
        lax.broadcasted_iota(jnp.int32, (slots, rows), 0) == place, 1.0, 0.0
    ).astype(BF16)
    squares = jnp.zeros((rows, 128), F32)
    for part in range(parts):
        at = slice(part * size, (part + 1) * size)
        copies[2 * part].wait()
        copies[2 * part + 1].wait()
        lat = lat_ref[:, at].astype(F32)
        resid = (
            jnp.concatenate([lat, lat], axis=0)
            + jnp.dot(own_ref[...], w_own_ref[:, at], preferred_element_type=F32)
            + jnp.dot(other_ref[...], w_other_ref[:, at], preferred_element_type=F32)
        )
        hat_ref[:, at] = resid
        for c in range(size // 128):
            piece = resid[:, c * 128 : (c + 1) * 128]
            squares = squares + piece * piece
    inverse = lax.rsqrt(jnp.sum(squares, axis=-1, keepdims=True) / width + EPSILON)
    inv_ref[...] = inverse
    low_ref[...] = (hat_ref[...] * inverse).astype(BF16)
    results = [
        pltpu.make_async_copy(source, target, out_sems.at[i])
        for i, (source, target) in enumerate(
            ((low_ref, hat_hbm), (inv_ref, inv_hbm), (out_ref, out_hbm))
        )
    ]
    for copy in results[:2]:
        copy.start()
    at = pl.ds(pl.multiple_of(lax.axis_index("mp") * half, half), half)
    final = (hat_ref[:, at] * inverse * gain_ref[:, at]).astype(BF16)
    out_ref[...] = jnp.dot(table, final, preferred_element_type=F32).astype(BF16)
    results[2].start()
    for copy in results:
        copy.wait()


def branch_call(own, other, w_own, w_other, latents, gain_out, routes, slots, slot_count):
    width = w_own.shape[1]
    rows, heads = own.shape
    parts = 4
    return pl.pallas_call(
        functools.partial(branch_kernel, slot_count),
        name="branch_norm",
        **dict(
            in_specs=[pl.BlockSpec(memory_space=pl.ANY)] * 7,
            out_specs=[pl.BlockSpec(memory_space=pl.ANY)] * 3,
            scratch_shapes=[
                pltpu.VMEM((rows, heads), BF16),
                pltpu.VMEM((rows, heads), BF16),
                pltpu.VMEM(latents.shape, BF16),
                pltpu.VMEM((1, width), F32),
                pltpu.VMEM((1, rows), jnp.int32),
                pltpu.VMEM(w_own.shape, BF16),
                pltpu.VMEM(w_other.shape, BF16),
                pltpu.VMEM((rows, width), F32),
                pltpu.VMEM((rows, width), BF16),
                pltpu.VMEM((rows, 1), F32),
                pltpu.VMEM((slots, width // 2), BF16),
                pltpu.SemaphoreType.DMA((2, parts)),
                pltpu.SemaphoreType.DMA((3,)),
                pltpu.SemaphoreType.DMA((5,)),
            ],
        ),
        out_shape=[
            jax.ShapeDtypeStruct((rows, width), BF16),
            jax.ShapeDtypeStruct((rows, 1), F32),
            jax.ShapeDtypeStruct((slots, width // 2), BF16),
        ],
        cost_estimate=pl.CostEstimate(
            flops=2 * 2 * rows * heads * width, bytes_accessed=16_000_000, transcendentals=0
        ),
        compiler_params=pltpu.CompilerParams(vmem_limit_bytes=VMEM_LIMIT),
    )(own, other, latents, gain_out.reshape(1, width), routes, w_own, w_other)


def attention_backward(
    counts_ref,
    d_attn,
    k_ref,
    v_ref,
    q_ref,
    lk_ref,
    lv_ref,
    p_ref,
    pl_ref,
    inv_row_ref,
    pair_ref,
    scaled_ref,
    lat_ref,
):
    groups, patch_rows, _ = k_ref.shape
    latent_rows = lk_ref.shape[1]
    stacked = q_ref.shape[1]
    per_group = stacked // latent_rows
    key_width = groups * HD
    query_width = groups * per_group * HD
    first_count = counts_ref[0, 0]
    both_count = first_count + counts_ref[0, 1]
    position = lax.broadcasted_iota(jnp.int32, (1, patch_rows), 1)
    in_first = position < first_count
    rows_at = lax.broadcasted_iota(jnp.int32, (patch_rows, HD), 0)
    row_first = rows_at < first_count
    row_second = jnp.logical_and(rows_at >= first_count, rows_at < both_count)
    scale_row = inv_row_ref[:1]
    row_dot = jnp.zeros((1, patch_rows), F32)
    for g in range(groups):
        d_first = jnp.concatenate(
            [
                d_attn[:latent_rows, head * HD : (head + 1) * HD]
                for head in range(g * per_group, (g + 1) * per_group)
            ],
            axis=0,
        )
        d_second = jnp.concatenate(
            [
                d_attn[latent_rows:, head * HD : (head + 1) * HD]
                for head in range(g * per_group, (g + 1) * per_group)
            ],
            axis=0,
        )
        q = q_ref[g, :, :HD]
        k = k_ref[g, :, :HD]
        v = v_ref[g, :, :HD]
        lk = lk_ref[g, :, :HD]
        lv = lv_ref[g, :, :HD]
        p_low = p_ref[g]
        p = p_low.astype(F32)
        zero = jnp.zeros_like(v)
        d_p = dot_general(d_first, jnp.where(row_first, v, zero), 1, 1) + dot_general(
            d_second, jnp.where(row_second, v, zero), 1, 1
        )
        product = p * d_p
        lat_first = pl_ref[g, :, :latent_rows]
        lat_second = pl_ref[g, :, latent_rows:]
        d_lat_first = dot_general(d_first, lv, 1, 1)
        d_lat_second = dot_general(d_second, lv, 1, 1)
        lat_product_first = lat_first.astype(F32) * d_lat_first
        lat_product_second = lat_second.astype(F32) * d_lat_second
        whole_sum = jnp.sum(product, axis=-1, keepdims=True)
        first_sum = jnp.sum(jnp.where(in_first, product, 0.0), axis=-1, keepdims=True)
        delta_first = first_sum + jnp.sum(lat_product_first, axis=-1, keepdims=True)
        delta_second = (whole_sum - first_sum) + jnp.sum(
            lat_product_second, axis=-1, keepdims=True
        )
        ds = product - p * jnp.where(in_first, delta_first, delta_second)
        ds_low = ds.astype(BF16)
        dsl = (
            lat_product_first
            - lat_first.astype(F32) * delta_first
            + lat_product_second
            - lat_second.astype(F32) * delta_second
        ).astype(BF16)
        scores = dot_general(q, k, 1, 1)
        row_dot = row_dot + jnp.sum(ds * scores + product, axis=0, keepdims=True)
        d_q = (
            jnp.dot(ds_low, k, preferred_element_type=F32)
            + jnp.dot(dsl, lk, preferred_element_type=F32)
        ).astype(BF16)
        for h in range(per_group):
            head = g * per_group + h
            lat_ref[:latent_rows, head * HD : (head + 1) * HD] = d_q[
                h * latent_rows : (h + 1) * latent_rows
            ]
        d_k = dot_general(q, ds_low, 0, 0)
        nothing = jnp.zeros_like(p_low)
        d_v = dot_general(d_first, jnp.where(in_first, p_low, nothing), 0, 0) + dot_general(
            d_second, jnp.where(in_first, nothing, p_low), 0, 0
        )
        k_at = slice(g * HD, (g + 1) * HD)
        v_at = slice(key_width + g * HD, key_width + (g + 1) * HD)
        pair_ref[k_at, :] = d_k.astype(BF16)
        pair_ref[v_at, :] = d_v.astype(BF16)
        scaled_ref[k_at, :] = (d_k * scale_row).astype(BF16)
        scaled_ref[v_at, :] = (d_v * scale_row).astype(BF16)
        d_lk = dot_general(dsl, q, 0, 0)
        d_lv = dot_general(lat_first, d_first, 0, 0) + dot_general(lat_second, d_second, 0, 0)
        lat_ref[:latent_rows, query_width + g * HD : query_width + (g + 1) * HD] = d_lk.astype(BF16)
        at = query_width + key_width + g * HD
        lat_ref[:latent_rows, at : at + HD] = d_lv.astype(BF16)
    high = row_dot.astype(BF16)
    low = (row_dot - high.astype(F32)).astype(BF16)
    rest = pair_ref.shape[0] - 2 * key_width - 2
    pair_ref[2 * key_width :, :] = jnp.concatenate(
        [high.astype(F32), low.astype(F32), jnp.zeros((rest, patch_rows), F32)], axis=0
    ).astype(BF16)


def backward_kernel(
    slot_count,
    counts_ref,
    inv_out_hbm,
    gain_hbm,
    routes_hbm,
    inv_row_hbm,
    attn_hbm,
    got_own_hbm,
    got_other_hbm,
    hat_hbm,
    w_out_hbm,
    k_hbm,
    v_hbm,
    q_hbm,
    lk_hbm,
    lv_hbm,
    p_hbm,
    pl_hbm,
    x_hbm,
    line_own_hbm,
    line_high_hbm,
    pair_hbm,
    message_hbm,
    lat_hbm,
    value_going_hbm,
    value_kept_hbm,
    key_going_hbm,
    key_kept_hbm,
    inv_out_ref,
    gain_ref,
    routes_ref,
    inv_row_ref,
    attn_ref,
    got_own_ref,
    got_other_ref,
    hat_ref,
    w_out_ref,
    k_ref,
    v_ref,
    q_ref,
    lk_ref,
    lv_ref,
    p_ref,
    pl_ref,
    x_ref,
    d_final_ref,
    branch_ref,
    scaled_ref,
    line_own_ref,
    line_high_ref,
    pair_ref,
    message_ref,
    lat_ref,
    value_ref,
    key_ref,
    sems,
    out_sems,
    value_sems,
    key_sems,
    small_sems,
):
    small = [
        pltpu.make_async_copy(source, target, small_sems.at[i])
        for i, (source, target) in enumerate(
            (
                (routes_hbm, routes_ref),
                (inv_out_hbm, inv_out_ref),
                (gain_hbm, gain_ref),
                (inv_row_hbm, inv_row_ref),
                (attn_hbm, attn_ref),
            )
        )
    ]
    for copy in small:
        copy.start()
    sources = (
        got_own_hbm,
        got_other_hbm,
        hat_hbm,
        w_out_hbm,
        k_hbm,
        v_hbm,
        q_hbm,
        lk_hbm,
        lv_hbm,
        p_hbm,
        pl_hbm,
        x_hbm,
    )
    targets = (
        got_own_ref,
        got_other_ref,
        hat_ref,
        w_out_ref,
        k_ref,
        v_ref,
        q_ref,
        lk_ref,
        lv_ref,
        p_ref,
        pl_ref,
        x_ref,
    )
    copies = [
        pltpu.make_async_copy(source, target, sems.at[i])
        for i, (source, target) in enumerate(zip(sources, targets))
    ]
    for copy in copies[:4]:
        copy.start()
    me, core = lax.axis_index("dp"), lax.axis_index("mp")
    rows, width = hat_ref.shape
    half = width // 2
    slots = got_own_ref.shape[0]
    latent_rows = lk_ref.shape[1]
    key_width, own = value_ref.shape[2:]

    small[0].wait()
    place = slots_of(routes_ref, slot_count, False)
    for copy in small[1:]:
        copy.wait()
    table = jnp.where(
        lax.broadcasted_iota(jnp.int32, (rows, slots), 1) == place, 1.0, 0.0
    ).astype(BF16)
    total = jnp.zeros((rows, 1), F32)
    chunk = 512
    for copy in copies[:3]:
        copy.wait()
    for copy in copies[4:]:
        copy.start()
    for got_ref, which in ((got_own_ref, core), (got_other_ref, 1 - core)):
        for c in range(half // chunk):
            at = pl.ds(pl.multiple_of(which * half + c * chunk, chunk), chunk)
            d_final = jnp.dot(
                table, got_ref[:, c * chunk : (c + 1) * chunk], preferred_element_type=F32
            )
            product = d_final * hat_ref[:, at].astype(F32)
            total = total + jnp.sum(product * gain_ref[:, at], axis=-1, keepdims=True)
            d_final_ref[:, at] = d_final
    total = total / width
    lat_ref[latent_rows:, :] = jnp.zeros_like(lat_ref[latent_rows:, :])
    highs, lows = [], []
    part = width // 4
    for c in range(width // chunk):
        at = slice(c * chunk, (c + 1) * chunk)
        d_final = d_final_ref[:, at]
        hat = hat_ref[:, at].astype(F32)
        term = jnp.sum(d_final * hat, axis=0, keepdims=True)
        high = term.astype(BF16).astype(F32)
        highs.append(high)
        lows.append(term - high)
        branch_ref[:, at] = (
            inv_out_ref[...] * (d_final * gain_ref[:, at] - hat * total)
        ).astype(BF16)
    per_row = part // chunk
    lines = [
        jnp.concatenate(group[i * per_row : (i + 1) * per_row], axis=1)
        for group in (highs, lows)
        for i in range(4)
    ]
    lat_ref[latent_rows : latent_rows + 16, :part] = jnp.concatenate(
        lines + [jnp.zeros((8, part), F32)], axis=0
    ).astype(BF16)
    z = me >> 2
    some = pl.ds(pl.multiple_of(core * (rows // 2), rows // 2), rows // 2)
    line_own_ref[...] = branch_ref[:, pl.ds(pl.multiple_of(z * part, part), part)]
    heads = attn_ref.shape[1]
    for turn, ref, first in (
        (1, message_ref, 0),
        (2, line_high_ref, 0),
        (3, line_high_ref, part + 2 * heads),
    ):
        ref[: rows // 2, first : first + part] = branch_ref[
            some, pl.ds(pl.multiple_of((z ^ turn) * part, part), part)
        ]
    for ref in (message_ref, line_high_ref):
        ref[: rows // 2, part : part + heads] = attn_ref[: rows // 2, :]
        ref[: rows // 2, part + heads : part + 2 * heads] = attn_ref[rows // 2 :, :]
    results = [
        pltpu.make_async_copy(source, target, out_sems.at[i])
        for i, (source, target) in enumerate(
            (
                (line_high_ref, line_high_hbm),
                (message_ref, message_hbm),
                (line_own_ref, line_own_hbm),
                (pair_ref, pair_hbm),
                (lat_ref, lat_hbm),
            )
        )
    ]
    for copy in results[:3]:
        copy.start()

    copies[3].wait()
    d_attn = dot_general(branch_ref[...], w_out_ref[...], 1, 1).astype(BF16)
    for copy in copies[4:11]:
        copy.wait()
    attention_backward(
        counts_ref,
        d_attn,
        k_ref,
        v_ref,
        q_ref,
        lk_ref,
        lv_ref,
        p_ref,
        pl_ref,
        inv_row_ref,
        pair_ref,
        scaled_ref,
        lat_ref,
    )
    for copy in results[3:]:
        copy.start()
    copies[11].wait()

    odd = me & 1
    for j in range(8):
        y = ((me >> 1) & 1) ^ (1 - (j >> 2))
        z = (me >> 2) ^ ((1 - ((j >> 1) & 1)) + 2 * (1 - (j & 1)))
        first = 4 * z + 2 * y
        line = j & 3
        key_hbm = key_kept_hbm if j >> 2 else key_going_hbm
        grad = jnp.dot(
            scaled_ref[...],
            x_ref[:, pl.ds(pl.multiple_of(first * own, 2 * own), 2 * own)],
            preferred_element_type=F32,
        ).astype(BF16)
        for x_same, value_hbm in enumerate((value_going_hbm, value_kept_hbm)):
            block = jnp.where(odd == x_same, grad[:, own:], grad[:, :own])
            value_ref[x_same, j] = block[key_width:]
            key_ref[x_same, j] = block[:key_width]
            for copy in (
                pltpu.make_async_copy(
                    value_ref.at[x_same, j], value_hbm.at[j], value_sems.at[x_same, j]
                ),
                pltpu.make_async_copy(
                    key_ref.at[x_same, j], key_hbm.at[x_same, line], key_sems.at[x_same, j]
                ),
            ):
                copy.start()
                results.append(copy)
    for copy in results:
        copy.wait()


def backward_call(
    counts, attn, got_own, got_other, hat, inv_out, gain_out, routes, w_out, kept, context, slot_count
):
    k, v, q, lk, lv, p, lat_p, inv_row = kept
    rows, width = hat.shape
    patch_rows = context.shape[0]
    heads = w_out.shape[0]
    key_width = k.shape[0] * HD
    latent_rows = lk.shape[1]
    own = width // 16
    large = (got_own, got_other, hat, w_out, k, v, q, lk, lv, p, lat_p, context)
    small = (inv_out, gain_out.reshape(1, width), routes, inv_row, attn)
    out = [
        (rows, width // 4),
        (rows // 2, width // 2 + 2 * heads),
        (2 * key_width + 16, patch_rows),
        (rows // 2, width // 4 + 2 * heads),
        (latent_rows + 16, heads + 2 * key_width),
        (8, key_width, own),
        (8, key_width, own),
        (2, 4, key_width, own),
        (2, 4, key_width, own),
    ]
    return pl.pallas_call(
        functools.partial(backward_kernel, slot_count),
        name="attention_backward",
        **dict(
            in_specs=[
                pl.BlockSpec(memory_space=pltpu.SMEM),
            ]
            + [pl.BlockSpec(memory_space=pl.ANY)] * (5 + len(large)),
            out_specs=[pl.BlockSpec(memory_space=pl.ANY)] * len(out),
            scratch_shapes=[pltpu.VMEM(a.shape, a.dtype) for a in (*small, *large)]
            + [
                pltpu.VMEM((rows, width), F32),
                pltpu.VMEM((rows, width), BF16),
                pltpu.VMEM((2 * key_width, patch_rows), BF16),
            ]
            + [pltpu.VMEM(shape, BF16) for shape in out[:5]]
            + [
                pltpu.VMEM((2, 8, key_width, own), BF16),
                pltpu.VMEM((2, 8, key_width, own), BF16),
                pltpu.SemaphoreType.DMA((len(large),)),
                pltpu.SemaphoreType.DMA((5,)),
                pltpu.SemaphoreType.DMA((2, 8)),
                pltpu.SemaphoreType.DMA((2, 8)),
                pltpu.SemaphoreType.DMA((5,)),
            ],
        ),
        out_shape=[jax.ShapeDtypeStruct(shape, BF16) for shape in out],
        cost_estimate=pl.CostEstimate(
            flops=5_000_000_000, bytes_accessed=26_000_000, transcendentals=0
        ),
        compiler_params=pltpu.CompilerParams(vmem_limit_bytes=VMEM_LIMIT),
    )(counts, *small, *large)


def patch_kernel(
    width,
    where_ref,
    own_ref,
    other_ref,
    wk_ref,
    wv_ref,
    wk_other_ref,
    wv_other_ref,
    x_ref,
    inv_row_ref,
    gain_ref,
    out_ref,
    turned_ref,
    inv_ref,
    dot_ref,
    w_ref,
):
    step = pl.program_id(0)
    key_width = wk_ref.shape[0]
    patch_rows = turned_ref.shape[0]
    pair = 2 * key_width

    @pl.when(step == 0)
    def _():
        row_dot = jnp.zeros((patch_rows, 1), F32)
        for i, ref in enumerate((own_ref, other_ref)):
            turned = jnp.transpose(ref[...])
            turned_ref[:, i * pair : (i + 1) * pair] = turned[:, :pair]
            row_dot = row_dot + turned[:, pair : pair + 1].astype(F32)
            row_dot = row_dot + turned[:, pair + 1 : pair + 2].astype(F32)
        inverse = jnp.transpose(jnp.broadcast_to(inv_row_ref[:1], (128, patch_rows)))[:, :1]
        inv_ref[...] = inverse
        dot_ref[...] = row_dot * (inverse * inverse / width)
        for i, ref in enumerate((wk_ref, wv_ref, wk_other_ref, wv_other_ref)):
            w_ref[i * key_width : (i + 1) * key_width, :] = ref[...]

    rows = x_ref.shape[0]
    at = pl.ds(pl.multiple_of(step * rows, rows), rows)
    d_in = jnp.dot(turned_ref[at, :], w_ref[...], preferred_element_type=F32)
    out_ref[...] = (
        d_in * gain_ref[...] * inv_ref[at, :] - x_ref[...].astype(F32) * dot_ref[at, :]
    ).astype(BF16)


def patch_call(where, own, other, wk, wv, wk_other, wv_other, context, inv_row, gain_ctx):
    patch_rows, width = context.shape
    half = width // 2
    steps = 4
    rows = patch_rows // steps
    key_width = wk.shape[0]
    once = pl.Buffered(1)
    w_spec = pl.BlockSpec((key_width, half), lambda i, w: (0, w[1]), pipeline_mode=once)
    return pl.pallas_call(
        functools.partial(patch_kernel, width),
        name="patch_gradient",
        grid_spec=pltpu.PrefetchScalarGridSpec(
            num_scalar_prefetch=1,
            grid=(steps,),
            in_specs=[
                held(own.shape),
                held(other.shape),
                w_spec,
                w_spec,
                w_spec,
                w_spec,
                pl.BlockSpec((rows, half), lambda i, w: (i, w[1])),
                held(inv_row.shape),
                pl.BlockSpec((1, half), lambda i, w: (0, w[1])),
            ],
            out_specs=pl.BlockSpec((rows, half), lambda i, w: (i, 0)),
            scratch_shapes=[
                pltpu.VMEM((patch_rows, 4 * key_width), BF16),
                pltpu.VMEM((patch_rows, 1), F32),
                pltpu.VMEM((patch_rows, 1), F32),
                pltpu.VMEM((4 * key_width, half), BF16),
            ],
        ),
        out_shape=jax.ShapeDtypeStruct((patch_rows, half), BF16),
        cost_estimate=pl.CostEstimate(
            flops=3_300_000_000, bytes_accessed=14_000_000, transcendentals=0
        ),
        compiler_params=pltpu.CompilerParams(vmem_limit_bytes=VMEM_LIMIT),
    )(where, own, other, wk, wv, wk_other, wv_other, context, inv_row, gain_ctx.reshape(1, width))


def out_kernel(
    where_ref,
    attn_own_ref,
    line_own_ref,
    low_ref,
    high_ref,
    forwarded_ref,
    other_low_ref,
    other_high_ref,
    other_forwarded_ref,
    first_onward_ref,
    first_last_ref,
    first_kept_ref,
    second_onward_ref,
    second_last_ref,
    second_kept_ref,
    attn_ref,
    line_ref,
    resid_ref,
):
    rows, heads = attn_own_ref.shape
    columns = line_ref.shape[1]
    own = columns // 4
    latent_rows = rows // 2
    mine = where_ref[1]
    half = rows // 2
    attn_ref[:rows, :] = attn_own_ref[...]
    line_ref[:rows, :] = line_own_ref[...]
    for i, (ref, other, first, attn_at) in enumerate(
        (
            (low_ref, other_low_ref, 0, columns),
            (high_ref, other_high_ref, 0, columns),
            (forwarded_ref, other_forwarded_ref, 2 * heads, 0),
        )
    ):
        at = (i + 1) * rows
        attn_ref[at : at + half, :] = ref[:half, attn_at : attn_at + heads]
        attn_ref[at + half : at + rows, :] = ref[:half, attn_at + heads : attn_at + 2 * heads]
        for holder, which in ((ref, mine), (other, 1 - mine)):
            line_ref[pl.ds(pl.multiple_of(at + which * half, half), half), :] = holder[
                :half, first : first + columns
            ]
    resid = jnp.zeros((latent_rows, columns), F32)
    for i in range(8):
        resid = resid + line_ref[i * latent_rows : (i + 1) * latent_rows, :].astype(F32)
    resid_ref[...] = resid
    odd = where_ref[0] & 1
    upper = (where_ref[0] >> 1) & 1
    share = own // 2
    cut = heads // 2
    for turn in range(4):
        x_differs, y_differs = 1 - (turn & 1), 1 - (turn >> 1)
        owner = 2 * (upper ^ y_differs) + (odd ^ x_differs)
        at = pl.ds(pl.multiple_of(owner * own, own), own)
        grad = dot_general(attn_ref[...], line_ref[:, at], 0, 0).astype(BF16)
        mine_at = pl.ds(pl.multiple_of(owner * own + mine * share, share), share)
        part = resid_ref[:, mine_at]
        part = jnp.concatenate([part[: latent_rows // 2], part[latent_rows // 2 :]], axis=1)
        ends = 1 - y_differs
        ref = (first_onward_ref, first_last_ref)[ends] if x_differs else first_kept_ref.at[ends]
        ref[:cut, :] = grad[:cut]
        ref[cut:, :] = part.astype(BF16)
        ends = 1 - x_differs
        ref = (second_onward_ref, second_last_ref)[ends] if y_differs else second_kept_ref.at[ends]
        ref[...] = grad[cut:]


def out_call(where, attn, line, received, others):
    rows, heads = attn.shape
    columns = line.shape[1]
    own = columns // 4
    first = (heads // 2 + rows // 4, own)
    second = (heads // 2, own)
    shapes = [first, first, (2, *first), second, second, (2, *second)]
    operands = (attn, line, *received, *others)
    return pl.pallas_call(
        out_kernel,
        name="output_projection_gradient",
        grid_spec=pltpu.PrefetchScalarGridSpec(
            num_scalar_prefetch=1,
            grid=(1,),
            in_specs=[held(a.shape) for a in operands],
            out_specs=[held(shape) for shape in shapes],
            scratch_shapes=[
                pltpu.VMEM((4 * rows, heads), BF16),
                pltpu.VMEM((4 * rows, columns), BF16),
                pltpu.VMEM((rows // 2, columns), F32),
            ],
        ),
        out_shape=[jax.ShapeDtypeStruct(shape, BF16) for shape in shapes],
        cost_estimate=pl.CostEstimate(
            flops=8 * rows * heads * columns, bytes_accessed=4_000_000, transcendentals=0
        ),
        compiler_params=pltpu.CompilerParams(vmem_limit_bytes=VMEM_LIMIT),
    )(where, *operands)


def latent_kernel(
    where_ref,
    sum_ref,
    across_ref,
    along_ref,
    corner_ref,
    proj_ref,
    lat_ref,
    gain_ref,
    wq_ref,
    wk_ref,
    wv_ref,
    routed_hbm,
    query_ref,
    pair_ref,
    message_ref,
    gain_out_ref,
    routed_out_hbm,
    total_ref,
    routed_ref,
    sems,
):
    arrive = pltpu.make_async_copy(routed_hbm, routed_ref, sems.at[0])
    leave = pltpu.make_async_copy(routed_ref, routed_out_hbm, sems.at[1])
    arrive.start()
    latent_rows, width = lat_ref.shape
    own, query_width = wq_ref.shape
    key_width = wk_ref.shape[0]
    scaling = HD ** (-0.5)
    total_ref[...] = sum(
        ref[...].astype(F32) for ref in (sum_ref, across_ref, along_ref, corner_ref)
    )
    total = total_ref[:latent_rows, :]
    low = total.astype(BF16)
    at = pl.ds(pl.multiple_of(where_ref[0] * own, own), own)
    lat = lat_ref[...].astype(F32)
    inverse = lax.rsqrt(jnp.mean(lat * lat, axis=-1, keepdims=True) + EPSILON)
    gain = gain_ref[:, at]
    normed = (lat_ref[:, at].astype(F32) * inverse * gain).astype(BF16)
    query = dot_general(normed, low[:, :query_width], 0, 0) * scaling
    query_ref[...] = query
    pair = dot_general(low[:, query_width:], normed, 0, 0)
    pair_ref[...] = pair
    wq = wq_ref[...]
    wk = wk_ref[...]
    wv = wv_ref[...]
    gain_term = jnp.transpose(
        jnp.broadcast_to(jnp.sum(wq.astype(F32) * query, axis=1, keepdims=True), (own, 128))
    )[:1]
    gain_term = gain_term + jnp.sum(wk.astype(F32) * pair[:key_width], axis=0, keepdims=True)
    gain_term = gain_term + jnp.sum(wv.astype(F32) * pair[key_width:], axis=0, keepdims=True)
    arrive.wait()
    leave.start()
    scaled = (total[:, :query_width] * scaling).astype(BF16)
    d_lat = dot_general(scaled, wq, 1, 1)
    d_lat = d_lat + jnp.dot(
        low[:, query_width : query_width + key_width], wk, preferred_element_type=F32
    )
    d_lat = d_lat + jnp.dot(low[:, query_width + key_width :], wv, preferred_element_type=F32)
    message_ref[:latent_rows, :own] = d_lat
    message_ref[:latent_rows, own:] = jnp.broadcast_to(
        jnp.sum(total * proj_ref[...], axis=-1, keepdims=True), (latent_rows, 128)
    )
    message_ref[latent_rows:, :own] = jnp.broadcast_to(gain_term / gain, (8, own))
    message_ref[latent_rows:, own:] = jnp.zeros((8, 128), F32)
    part = width // 4
    share = own // 2
    first = where_ref[0] * own + where_ref[1] * share
    line = first // part
    mine = pl.ds(pl.multiple_of(first % part, share), share)
    gain_out_ref[...] = jnp.sum(
        jnp.where(
            lax.broadcasted_iota(jnp.int32, (8, share), 0) % 4 == line,
            total_ref[latent_rows : latent_rows + 8, mine],
            0.0,
        ),
        axis=0,
        keepdims=True,
    )
    leave.wait()


def latent_call(where, sums, parts, proj, latents, gain_lat, w_query, wk, wv, own, routed):
    latent_rows, width = latents.shape
    query_width = w_query.shape[1]
    key_width = wk.shape[0]
    return pl.pallas_call(
        latent_kernel,
        name="latent_gradients",
        grid_spec=pltpu.PrefetchScalarGridSpec(
            num_scalar_prefetch=1,
            grid=(1,),
            in_specs=[
                held(sums.shape),
                *(held(part.shape) for part in parts),
                held(proj.shape),
                held(latents.shape),
                held((1, width)),
                pl.BlockSpec((own, query_width), lambda i, w: (w[0], 0)),
                pl.BlockSpec((key_width, own), lambda i, w: (0, w[0])),
                pl.BlockSpec((key_width, own), lambda i, w: (0, w[0])),
                pl.BlockSpec(memory_space=pl.ANY),
            ],
            out_specs=[
                held((own, query_width)),
                held((2 * key_width, own)),
                held((latent_rows + 8, own + 128)),
                held((1, own // 2)),
                pl.BlockSpec(memory_space=pl.ANY),
            ],
            scratch_shapes=[
                pltpu.VMEM(sums.shape, F32),
                pltpu.VMEM(routed.shape, BF16),
                pltpu.SemaphoreType.DMA((2,)),
            ],
        ),
        out_shape=[
            jax.ShapeDtypeStruct((own, query_width), F32),
            jax.ShapeDtypeStruct((2 * key_width, own), F32),
            jax.ShapeDtypeStruct((latent_rows + 8, own + 128), F32),
            jax.ShapeDtypeStruct((1, own // 2), F32),
            jax.ShapeDtypeStruct(routed.shape, BF16),
        ],
        cost_estimate=pl.CostEstimate(
            flops=100_000_000, bytes_accessed=3_000_000, transcendentals=0
        ),
        compiler_params=pltpu.CompilerParams(vmem_limit_bytes=VMEM_LIMIT),
    )(where, sums, *parts, proj, latents, gain_lat.reshape(1, width), w_query, wk, wv, routed)


def plane_kernel(
    value_ref,
    value_got_ref,
    value_last_ref,
    key_ref,
    key_got_ref,
    key_last_ref,
    going_ref,
    high_ref,
):
    key_width = value_ref.shape[-2]
    for i, ref in enumerate((going_ref.at[0], going_ref.at[1], high_ref)):
        for j, parts in enumerate(
            (
                (key_ref, key_got_ref, key_last_ref),
                (value_ref, value_got_ref, value_last_ref),
            )
        ):
            total = sum(part[i].astype(F32) for part in parts)
            ref[j * key_width : (j + 1) * key_width, :] = total.astype(ref.dtype)


def plane_call(value, value_got, value_last, key, key_got, key_last):
    _, key_width, own = value.shape
    upper = pl.BlockSpec((4, key_width, own), lambda i: (1, 0, 0))
    last = pl.BlockSpec((4, key_width, own), lambda i: (0, 0, 0))
    shape = (2 * key_width, own)
    return pl.pallas_call(
        plane_kernel,
        name="plane_sum",
        grid=(1,),
        in_specs=[upper, upper, last] * 2,
        out_specs=[held((2, *shape)), held(shape)],
        out_shape=[
            jax.ShapeDtypeStruct((2, *shape), BF16),
            jax.ShapeDtypeStruct(shape, F32),
        ],
        cost_estimate=pl.CostEstimate(flops=1_000_000, bytes_accessed=3_000_000, transcendentals=0),
        compiler_params=pltpu.CompilerParams(vmem_limit_bytes=VMEM_LIMIT),
    )(value, value_got, value_last, key, key_got, key_last)


def final_kernel(
    where_ref,
    value_ref,
    value_got_ref,
    value_last_ref,
    key_ref,
    key_got_ref,
    key_last_ref,
    low_ref,
    high_ref,
    gain_ref,
    pair_ref,
    wk_ref,
    wv_ref,
    key_grad_ref,
    value_grad_ref,
    gain_term_ref,
):
    key_width = wk_ref.shape[0]
    term = jnp.zeros((1, wk_ref.shape[1]), F32)
    for j, (w_ref, out_ref, parts) in enumerate(
        (
            (wk_ref, key_grad_ref, (key_ref, key_got_ref, key_last_ref)),
            (wv_ref, value_grad_ref, (value_ref, value_got_ref, value_last_ref)),
        )
    ):
        at = slice(j * key_width, (j + 1) * key_width)
        total = sum(part[0].astype(F32) for part in parts)
        total = total + low_ref[0, at, :].astype(F32) + high_ref[at, :].astype(F32)
        term = term + jnp.sum(w_ref[...].astype(F32) * total, axis=0, keepdims=True)
        out_ref[...] = total * gain_ref[...] + pair_ref[at, :]
    gain_term_ref[...] = jnp.broadcast_to(term, gain_term_ref.shape)


def final_call(where, value, value_got, value_last, key, key_got, key_last, line, gain_ctx, pair, wk, wv):
    rows, own = pair.shape
    width = gain_ctx.shape[0]
    key_width = rows // 2
    w_spec = pl.BlockSpec((key_width, own), lambda i, w: (0, w[0]))
    end = pl.BlockSpec((1, key_width, own), lambda i, w: (7, 0, 0))
    last = pl.BlockSpec((1, key_width, own), lambda i, w: (3, 0, 0))
    return pl.pallas_call(
        final_kernel,
        name="key_value_gradients",
        grid_spec=pltpu.PrefetchScalarGridSpec(
            num_scalar_prefetch=1,
            grid=(1,),
            in_specs=[end, end, last] * 2
            + [pl.BlockSpec((1, rows, own), lambda i, w: (1, 0, 0)), held(pair.shape)]
            + [pl.BlockSpec((1, own), lambda i, w: (0, w[0])), held(pair.shape), w_spec, w_spec],
            out_specs=[held((key_width, own)), held((key_width, own)), held((8, own))],
        ),
        out_shape=[
            jax.ShapeDtypeStruct((key_width, own), F32),
            jax.ShapeDtypeStruct((key_width, own), F32),
            jax.ShapeDtypeStruct((8, own), F32),
        ],
        cost_estimate=pl.CostEstimate(flops=1_000_000, bytes_accessed=3_000_000, transcendentals=0),
        compiler_params=pltpu.CompilerParams(vmem_limit_bytes=VMEM_LIMIT),
    )(
        where,
        value,
        value_got,
        value_last,
        key,
        key_got,
        key_last,
        *line,
        gain_ctx.reshape(1, width),
        pair,
        wk,
        wv,
    )


def out_final_kernel(
    where_ref,
    first_kept_ref,
    first_got_ref,
    first_last_ref,
    second_kept_ref,
    second_got_ref,
    second_last_ref,
    message_ref,
    message_got_ref,
    term_ref,
    term_got_ref,
    lat_ref,
    gain_ref,
    out_ref,
    latent_ref,
    gain_lat_ref,
    gain_ctx_ref,
):
    heads, own = out_ref.shape
    latent_rows, width = lat_ref.shape
    share = own // 2
    cut = heads // 2
    first = sum(
        part.astype(F32) for part in (first_kept_ref[0], first_got_ref[...], first_last_ref[...])
    )
    out_ref[:cut, :] = first[:cut]
    out_ref[cut:, :] = sum(
        part.astype(F32) for part in (second_kept_ref[0], second_got_ref[...], second_last_ref[...])
    )
    resid = first[cut:]
    resid = jnp.concatenate([resid[:, :share], resid[:, share:]], axis=0)
    mine = pl.ds(pl.multiple_of(where_ref[1] * share, share), share)
    d_lat = message_ref[:, mine] + message_got_ref[:, mine]
    lat_dot = message_ref[:latent_rows, own : own + 1] + message_got_ref[:latent_rows, own : own + 1]
    lat = lat_ref[...].astype(F32)
    inverse = lax.rsqrt(jnp.mean(lat * lat, axis=-1, keepdims=True) + EPSILON)
    at = pl.ds(pl.multiple_of(where_ref[0] * own + where_ref[1] * share, share), share)
    hat = lat_ref[:, at].astype(F32) * inverse
    latent_ref[...] = resid + inverse * (gain_ref[:, at] * d_lat[:latent_rows] - hat * (lat_dot / width))
    gain_lat_ref[...] = d_lat[latent_rows : latent_rows + 1]
    gain_ctx_ref[...] = term_ref[:1, mine] + term_got_ref[:1, mine]


def out_final_call(where, parts, message, message_got, term, term_got, latents, gain_lat):
    _, rows, own = parts[0].shape
    latent_rows, width = latents.shape
    heads = 2 * (rows - latent_rows // 2)
    shapes = [(heads, own), (latent_rows, own // 2), (1, own // 2), (1, own // 2)]
    return pl.pallas_call(
        out_final_kernel,
        name="output_gradient_sum",
        grid_spec=pltpu.PrefetchScalarGridSpec(
            num_scalar_prefetch=1,
            grid=(1,),
            in_specs=[
                pl.BlockSpec((1, *part.shape[1:]), lambda i, w: (1, 0, 0))
                if part.ndim == 3
                else held(part.shape)
                for part in parts
            ]
            + [held(a.shape) for a in (message, message_got, term, term_got, latents)]
            + [held((1, width))],
            out_specs=[held(shape) for shape in shapes],
        ),
        out_shape=[jax.ShapeDtypeStruct(shape, F32) for shape in shapes],
        cost_estimate=pl.CostEstimate(flops=1_000_000, bytes_accessed=3_000_000, transcendentals=0),
        compiler_params=pltpu.CompilerParams(vmem_limit_bytes=VMEM_LIMIT),
    )(
        where,
        *parts,
        message,
        message_got,
        term,
        term_got,
        latents,
        gain_lat.reshape(1, width),
    )


def add_halves(left, right):
    return left.astype(F32) + right.astype(F32)


def local(
    context,
    counts,
    routes,
    w_query,
    w_key,
    w_value,
    w_out,
    latents,
    gain_ctx,
    gain_lat,
    gain_out,
    cotangent,
):
    dp_count = lax.axis_size("dp")
    mp_index = lax.axis_index("mp")
    dp_index = lax.axis_index("dp")
    patch_rows, width = context.shape
    half_width = width // 2
    own_width = width // dp_count
    latent_rows = latents.shape[0]
    slot_count = cotangent.shape[0] // dp_count
    slots = dp_count * slot_count
    query_width = w_query.shape[1]

    def swap(array, turn):
        return lax.ppermute(array, "dp", [(i, i ^ turn) for i in range(dp_count)])

    def exchange(array):
        blocks = array.reshape(dp_count, slot_count, half_width)
        return lax.all_to_all(blocks, "dp", split_axis=0, concat_axis=0, tiled=True).reshape(
            slots, half_width
        )

    wk = w_key.T
    wv = w_value.T
    turned_routes = routes.reshape(1, -1)
    where = jnp.stack([dp_index, mp_index])

    returned = exchange(cotangent)
    w_out_other = swap_cores(w_out)
    wk_other = swap_cores(wk)
    wv_other = swap_cores(wv)

    (attn_rows, k, v, inv_row, q, lat_k, lat_v, lat_proj, p, lat_p) = forward_call(
        context, counts, w_query, wk, wv, latents, gain_ctx, gain_lat
    )
    wk_other, wv_other, attn_rows = lax.optimization_barrier((wk_other, wv_other, attn_rows))
    attn_other = swap_cores(attn_rows)
    out_hat, out_inv, outgoing = branch_call(
        attn_rows,
        attn_other,
        w_out,
        w_out_other,
        latents,
        gain_out,
        turned_routes,
        slots,
        slot_count,
    )

    routed = exchange(outgoing)
    returned, out_inv = lax.optimization_barrier((returned, out_inv))
    returned_other = swap_cores(returned)
    backward = backward_call(
        counts,
        attn_rows,
        returned,
        returned_other,
        out_hat,
        out_inv,
        gain_out,
        turned_routes,
        w_out,
        (k, v, q, lat_k, lat_v, p, lat_p, inv_row),
        context,
        slot_count,
    )
    backward = lax.optimization_barrier(backward)
    (
        line_own,
        line_high,
        pair,
        message,
        lat_terms,
        value_going,
        value_kept,
        key_going,
        key_kept,
    ) = backward

    value_got = swap(value_going, 1)
    key_got = swap(key_going, 2)
    pair_other = swap_cores(pair)

    line_high, message, lat_terms, pair_other = lax.optimization_barrier(
        (line_high, message, lat_terms, pair_other)
    )
    lat_got = swap(lat_terms, 4)
    got_high = swap(line_high, 8)
    got_low = swap(message, 4)

    ctx_grad = patch_call(
        where, pair, pair_other, wk, wv, wk_other, wv_other, context, inv_row, gain_ctx
    )

    lat_got, ctx_grad = lax.optimization_barrier((lat_got, ctx_grad))
    lat_sum = add_halves(lat_terms, lat_got)
    lat_low = lat_sum.astype(BF16)
    value_got, key_got, ctx_grad, routed, lat_low = lax.optimization_barrier(
        (value_got, key_got, ctx_grad, routed, lat_low)
    )
    key_kept = key_kept.reshape((8,) + key_kept.shape[2:])
    key_got = key_got.reshape((8,) + key_got.shape[2:])
    value_going = add_halves(value_kept[:4], value_got[:4]).astype(BF16)
    key_going = add_halves(key_kept[:4], key_got[:4]).astype(BF16)
    value_last = swap(value_going, 2)
    key_last = swap(key_going, 1)

    got_low, got_high, value_going, key_going, lat_low = lax.optimization_barrier(
        (got_low, got_high, value_going, key_going, lat_low)
    )
    lat_got = swap(lat_low, 8)
    forwarded = swap(got_high[:, width // 4 :], 4)
    other_low = swap_cores(got_low)
    other_high = swap_cores(got_high)

    planes = plane_call(value_kept, value_got, value_last, key_kept, key_got, key_last)
    low = swap(planes[0], 4)
    (_, high), lat_got, forwarded = lax.optimization_barrier((planes, lat_got, forwarded))
    other_forwarded = swap_cores(forwarded)
    lat_sum = add_halves(lat_sum, lat_got).astype(BF16)
    lat_parts = (swap(lat_sum, 1), swap(lat_sum, 2), swap(lat_sum, 3))

    first_onward, first_end, first_kept, second_onward, second_end, second_kept = out_call(
        where,
        attn_rows,
        line_own,
        (got_low, got_high, forwarded),
        (other_low, other_high, other_forwarded),
    )
    low, first_onward, second_onward, first_end, second_end = lax.optimization_barrier(
        (low, first_onward, second_onward, first_end, second_end)
    )
    high = add_halves(high, low[0]).astype(BF16)
    high, lat_parts = lax.optimization_barrier((high, lat_parts))
    high = swap(high, 8)
    first_onward = swap(first_onward, 1)
    second_onward = swap(second_onward, 2)
    first_end = swap(first_end, 1)
    second_end = swap(second_end, 2)

    grad_w_query, pair_lat, message, grad_gain_out, routed = latent_call(
        where, lat_sum, lat_parts, lat_proj, latents, gain_lat, w_query, wk, wv, own_width, routed
    )
    first_onward, second_onward, message, pair_lat = lax.optimization_barrier(
        (first_onward, second_onward, message, pair_lat)
    )
    high, pair_lat = lax.optimization_barrier((high, pair_lat))
    first_last = swap(add_halves(first_kept[0], first_onward).astype(BF16), 2)
    second_last = swap(add_halves(second_kept[0], second_onward).astype(BF16), 1)
    message_got = swap_cores(message)

    grad_key, grad_value, gain_term = final_call(
        where,
        value_kept,
        value_got,
        value_last,
        key_kept,
        key_got,
        key_last,
        (low, high),
        gain_ctx,
        pair_lat,
        wk,
        wv,
    )
    gain_got = swap_cores(gain_term)
    first_last, second_last, gain_term = lax.optimization_barrier(
        (first_last, second_last, gain_term)
    )
    grad_w_out, grad_latents, grad_gain_lat, grad_gain_ctx = out_final_call(
        where,
        (first_kept, first_end, first_last, second_kept, second_end, second_last),
        message,
        message_got,
        gain_term,
        gain_got,
        latents,
        gain_lat,
    )
    return (
        routed,
        ctx_grad,
        grad_w_query,
        grad_key.T,
        grad_value.T,
        grad_w_out,
        grad_latents,
        grad_gain_ctx[0],
        grad_gain_lat[0],
        grad_gain_out[0],
    )


def local_general(
    context,
    counts,
    routes,
    w_query,
    w_key,
    w_value,
    w_out,
    latents,
    gain_ctx,
    gain_lat,
    gain_out,
    cotangent,
):
    dp_count = lax.axis_size("dp")
    mp_count = lax.axis_size("mp")
    mp_index = lax.axis_index("mp")
    dp_index = lax.axis_index("dp")
    bits = dp_count.bit_length() - 1
    gather_bits = [bits - 1, bits - 2]
    scatter_bits = list(range(bits - 2))
    order_one = list(range(bits))
    order_two = [1, 0] + order_one[2:]
    patch_rows, width = context.shape
    half_width = width // mp_count
    own_width = width // dp_count
    head_local = w_query.shape[1] // HD
    group_local = w_key.shape[1] // HD
    per_group = head_local // group_local
    latent_rows = latents.shape[0]
    image_slots = counts.shape[1]
    out_rows = image_slots * latent_rows
    slot_count = cotangent.shape[0] // dp_count
    key_width = w_key.shape[1]
    query_width = w_query.shape[1]
    scaling = HD ** (-0.5)

    returned = lax.all_to_all(
        cotangent.reshape(dp_count, slot_count, half_width),
        "dp",
        split_axis=0,
        concat_axis=0,
        tiled=True,
    ).reshape(dp_count * slot_count, half_width)
    returned_other = swap_cores(returned)
    w_out_other = swap_cores(w_out)
    w_pair = jnp.concatenate([w_key, w_value], axis=1)
    w_pair_half = lax.dynamic_slice_in_dim(w_pair, mp_index * half_width, half_width, 0)
    w_pair_other = swap_cores(
        lax.dynamic_slice_in_dim(w_pair, (1 - mp_index) * half_width, half_width, 0)
    )

    patch_hat, patch_inv = norm_parts(context.astype(F32))
    normed_ctx = (patch_hat * gain_ctx).astype(BF16)
    key_f32 = jnp.dot(normed_ctx, w_key, preferred_element_type=F32)
    value_f32 = jnp.dot(normed_ctx, w_value, preferred_element_type=F32)
    key_rows = key_f32.astype(BF16)
    value_rows = value_f32.astype(BF16)
    lat_float = latents.astype(F32)
    lat_hat, lat_inv = norm_parts(lat_float)
    normed_lat = (lat_hat * gain_lat).astype(BF16)
    lat_key_f32 = jnp.dot(normed_lat, w_key, preferred_element_type=F32)
    lat_value_f32 = jnp.dot(normed_lat, w_value, preferred_element_type=F32)
    lat_keys = lat_key_f32.astype(BF16)
    lat_values = lat_value_f32.astype(BF16)
    query_f32 = jnp.dot(normed_lat, w_query, preferred_element_type=F32) * scaling
    query_rows = query_f32.astype(BF16)
    query_heads = query_rows.reshape(latent_rows, group_local, per_group, HD)
    key_heads = key_rows.reshape(patch_rows, group_local, HD)
    value_heads = value_rows.reshape(patch_rows, group_local, HD)
    lat_key_heads = lat_keys.reshape(latent_rows, group_local, HD)
    lat_value_heads = lat_values.reshape(latent_rows, group_local, HD)
    scores = jnp.einsum(
        "rkgd,tkd->kgrt", query_heads, key_heads, preferred_element_type=jnp.float32
    )
    lat_scores = jnp.einsum(
        "rkgd,skd->kgrs", query_heads, lat_key_heads, preferred_element_type=jnp.float32
    )
    position = jnp.arange(patch_rows, dtype=jnp.int32)
    image_count = counts[0]
    image_start = jnp.cumsum(image_count) - image_count
    member = (position[None, :] >= image_start[:, None]) & (
        position[None, :] < (image_start + image_count)[:, None]
    )
    member_wide = member[:, None, None, None, :]
    masked = jnp.where(member_wide, scores[None], NEGATIVE)
    row_max = jnp.maximum(
        jnp.max(masked, axis=-1, keepdims=True), jnp.max(lat_scores, axis=-1, keepdims=True)[None]
    )
    exponent = jnp.where(member_wide, jnp.exp(masked - row_max), 0.0)
    lat_exponent = jnp.exp(lat_scores[None] - row_max)
    total = jnp.sum(exponent, axis=-1, keepdims=True) + jnp.sum(
        lat_exponent, axis=-1, keepdims=True
    )
    attention = exponent / total
    lat_attention = lat_exponent / total
    attention_low = attention.astype(BF16)
    lat_attention_low = lat_attention.astype(BF16)
    mixed = jnp.einsum(
        "ikgrt,tkd->irkgd", attention_low, value_heads, preferred_element_type=jnp.float32
    )
    mixed = mixed + jnp.einsum(
        "ikgrs,skd->irkgd", lat_attention_low, lat_value_heads, preferred_element_type=jnp.float32
    )
    attn_rows = mixed.reshape(out_rows, query_width).astype(BF16)
    attn_other = swap_cores(attn_rows)
    branch = jnp.dot(attn_rows, w_out, preferred_element_type=F32) + jnp.dot(
        attn_other, w_out_other, preferred_element_type=F32
    )
    resid = jnp.tile(lat_float, (image_slots, 1)) + branch
    out_hat, out_inv = norm_parts(resid)
    final_rows = (out_hat * gain_out).astype(BF16)
    shard_of = routes[:, 0]
    shard_hot = (shard_of[:, None] == jnp.arange(dp_count, dtype=jnp.int32)[None, :]).astype(
        jnp.int32
    )
    rank = jnp.sum((jnp.cumsum(shard_hot, axis=0) - shard_hot) * shard_hot, axis=1)
    place = shard_of * slot_count + rank
    scatter_table = (
        jnp.arange(dp_count * slot_count, dtype=jnp.int32)[:, None] == place[None, :]
    ).astype(BF16)
    final_half = lax.dynamic_slice_in_dim(final_rows, mp_index * half_width, half_width, 1)
    outgoing = jnp.dot(scatter_table, final_half, preferred_element_type=F32).astype(BF16)
    routed = lax.all_to_all(
        outgoing.reshape(dp_count, slot_count, half_width),
        "dp",
        split_axis=0,
        concat_axis=0,
        tiled=True,
    ).reshape(dp_count * slot_count, half_width)

    attn_line = attn_rows
    for bit in gather_bits:
        attn_line = jnp.concatenate([attn_line, swap_bit(attn_line, bit, dp_count)], axis=0)

    first = jnp.where(mp_index == 0, returned, returned_other)
    second = jnp.where(mp_index == 0, returned_other, returned)
    d_final = jnp.concatenate(
        [dot_general(scatter_table, first, 0, 0), dot_general(scatter_table, second, 0, 0)], axis=1
    )
    d_hat = d_final * gain_out
    d_resid = out_inv * (d_hat - out_hat * jnp.mean(d_hat * out_hat, axis=1, keepdims=True))
    gain_out_term = jnp.sum(d_final * out_hat, axis=0)
    d_branch = d_resid.astype(BF16)
    d_attn = dot_general(d_branch, w_out, 1, 1).astype(BF16)

    d_attn_heads = d_attn.reshape(image_slots, latent_rows, group_local, per_group, HD)
    d_probs = jnp.einsum(
        "irkgd,tkd->ikgrt", d_attn_heads, value_heads, preferred_element_type=jnp.float32
    )
    d_lat_probs = jnp.einsum(
        "irkgd,skd->ikgrs", d_attn_heads, lat_value_heads, preferred_element_type=jnp.float32
    )
    row_delta = jnp.sum(attention * d_probs, axis=-1, keepdims=True) + jnp.sum(
        lat_attention * d_lat_probs, axis=-1, keepdims=True
    )
    d_scores = jnp.sum(attention * (d_probs - row_delta), axis=0).astype(BF16)
    d_lat_scores = jnp.sum(lat_attention * (d_lat_probs - row_delta), axis=0).astype(BF16)
    d_query = jnp.einsum("kgrt,tkd->rkgd", d_scores, key_heads, preferred_element_type=jnp.float32)
    d_query = d_query + jnp.einsum(
        "kgrs,skd->rkgd", d_lat_scores, lat_key_heads, preferred_element_type=jnp.float32
    )
    d_query = d_query.reshape(latent_rows, query_width).astype(BF16)
    d_keys = jnp.einsum("kgrt,rkgd->tkd", d_scores, query_heads, preferred_element_type=jnp.float32)
    d_keys = d_keys.reshape(patch_rows, key_width).astype(BF16)
    d_values = jnp.einsum(
        "ikgrt,irkgd->tkd", attention_low, d_attn_heads, preferred_element_type=jnp.float32
    )
    d_values = d_values.reshape(patch_rows, key_width).astype(BF16)
    d_lat_keys = jnp.einsum(
        "kgrs,rkgd->skd", d_lat_scores, query_heads, preferred_element_type=jnp.float32
    )
    d_lat_keys = d_lat_keys.reshape(latent_rows, key_width).astype(BF16)
    d_lat_values = jnp.einsum(
        "ikgrs,irkgd->skd", lat_attention_low, d_attn_heads, preferred_element_type=jnp.float32
    )
    d_lat_values = d_lat_values.reshape(latent_rows, key_width).astype(BF16)
    d_pair = jnp.concatenate([d_keys, d_values], axis=1)

    value_grad = dot_general(d_values, normed_ctx, 0, 0).reshape(key_width, dp_count, own_width)
    key_grad = dot_general(d_keys, normed_ctx, 0, 0).reshape(key_width, dp_count, own_width)
    value_block = scatter_sum(value_grad, order_one, dp_count)
    key_block = scatter_sum(key_grad, order_two, dp_count)

    row_dot = jnp.sum(d_keys.astype(F32) * key_f32, axis=1) + jnp.sum(
        d_values.astype(F32) * value_f32, axis=1
    )
    row_dot = (row_dot + swap_cores(row_dot)) / width
    d_pair_other = swap_cores(d_pair)
    d_ctx_in = dot_general(d_pair, w_pair_half, 1, 1) + dot_general(
        d_pair_other, w_pair_other, 1, 1
    )
    gain_ctx_half = lax.dynamic_slice_in_dim(gain_ctx, mp_index * half_width, half_width, 0)
    hat_half = lax.dynamic_slice_in_dim(patch_hat, mp_index * half_width, half_width, 1)
    ctx_grad = (patch_inv * (d_ctx_in * gain_ctx_half - hat_half * row_dot[:, None])).astype(BF16)

    high = gain_out_term.astype(BF16)
    low = (gain_out_term - high.astype(F32)).astype(BF16)
    lat_sum = jnp.concatenate(
        [
            d_query,
            d_lat_keys,
            d_lat_values,
            high.reshape(latent_rows, width // latent_rows),
            low.reshape(latent_rows, width // latent_rows),
        ],
        axis=1,
    ).astype(F32)
    for bit in gather_bits + scatter_bits:
        lat_sum = lat_sum + swap_bit(lat_sum.astype(BF16), bit, dp_count).astype(F32)
    pair_sum = lat_sum[:, query_width : query_width + 2 * key_width]
    query_sum = lat_sum[:, :query_width]
    gains_at = query_width + 2 * key_width
    gain_step = width // latent_rows
    gain_out_full = (
        lat_sum[:, gains_at : gains_at + gain_step]
        + lat_sum[:, gains_at + gain_step : gains_at + 2 * gain_step]
    ).reshape(width)

    plane = dp_count // 4
    row_half = out_rows // mp_count
    d_block = lax.dynamic_slice_in_dim(d_branch, mp_index * row_half, row_half, 0)
    d_line = d_block.reshape(1, row_half, 2, 2, plane * own_width)
    for step, bit in enumerate(gather_bits):
        mine = (dp_index >> bit) & 1
        going = lax.dynamic_index_in_dim(d_line, 1 - mine, 2, keepdims=False)
        kept = lax.dynamic_index_in_dim(d_line, mine, 2, keepdims=False)
        d_line = jnp.concatenate([kept, swap_bit(going, bit, dp_count)], axis=0)
    d_line_other = swap_cores(d_line)
    d_line = jnp.concatenate(
        [
            jnp.where(mp_index == 0, d_line, d_line_other),
            jnp.where(mp_index == 0, d_line_other, d_line),
        ],
        axis=1,
    )
    out_part = dot_general(attn_line, d_line.reshape(4 * out_rows, plane * own_width), 0, 0)
    resid_part = jnp.sum(
        d_line.astype(F32).reshape(4 * image_slots, latent_rows, plane * own_width), axis=0
    )
    resid_part = lax.dynamic_index_in_dim(
        resid_part.reshape(2, latent_rows // 2, plane, mp_count, own_width // mp_count),
        mp_index,
        3,
        keepdims=False,
    )
    resid_part = jnp.transpose(resid_part, (1, 2, 0, 3)).reshape(
        latent_rows // 2, plane, own_width
    )
    out_part = jnp.concatenate([out_part.reshape(query_width, plane, own_width), resid_part], axis=0)
    cut = out_part.shape[0] // 2
    out_block = jnp.concatenate(
        [
            scatter_sum(out_part[:cut], scatter_bits, dp_count),
            scatter_sum(out_part[cut:], [1, 0] + scatter_bits[2:], dp_count),
        ],
        axis=0,
    )
    grad_w_out = out_block[:query_width]
    resid_sum = (
        out_block[query_width:]
        .reshape(latent_rows // 2, 2, own_width // mp_count)
        .transpose(1, 0, 2)
        .reshape(latent_rows, own_width // mp_count)
    )

    def own(array, axis):
        return lax.dynamic_slice_in_dim(array, dp_index * own_width, own_width, axis)

    lat_own = own(normed_lat, 1)
    pair_ctx = jnp.concatenate([key_block, value_block], axis=0).T
    query_grad = dot_general(lat_own, query_sum.astype(BF16), 0, 0) * scaling
    pair_lat = dot_general(lat_own, pair_sum.astype(BF16), 0, 0)
    pair_all = pair_ctx + pair_lat
    wq_own = own(w_query, 0)
    pair_own = own(w_pair, 0)
    gain_ctx_part = jnp.sum(pair_own.astype(F32) * pair_ctx, axis=1) / own(gain_ctx, 0)
    gain_lat_part = (
        jnp.sum(wq_own.astype(F32) * query_grad, axis=1)
        + jnp.sum(pair_own.astype(F32) * pair_lat, axis=1)
    ) / own(gain_lat, 0)
    d_lat_part = dot_general(
        (query_sum * scaling).astype(BF16), wq_own, 1, 1
    ) + dot_general(pair_sum.astype(BF16), pair_own, 1, 1)
    lat_dot_part = (
        jnp.sum(query_sum * query_f32, axis=1)
        + jnp.sum(pair_sum[:, :key_width] * lat_key_f32, axis=1)
        + jnp.sum(pair_sum[:, key_width:] * lat_value_f32, axis=1)
    )
    small = jnp.concatenate(
        [
            d_lat_part,
            jnp.broadcast_to(lat_dot_part[:, None], (latent_rows, own_width)),
            jnp.broadcast_to(gain_ctx_part[None, :], (8, own_width)),
            jnp.broadcast_to(gain_lat_part[None, :], (8, own_width)),
        ],
        axis=0,
    )
    small = small + swap_cores(small)
    share = own_width // mp_count
    small = lax.dynamic_slice_in_dim(small, mp_index * share, share, 1)
    d_lat_in = small[:latent_rows]
    lat_dot = small[latent_rows : 2 * latent_rows] / width

    def mine_of(array, axis):
        return lax.dynamic_slice_in_dim(
            array, dp_index * own_width + mp_index * share, share, axis
        )

    grad_latents = resid_sum + lat_inv * (
        mine_of(gain_lat, 0) * d_lat_in - mine_of(lat_hat, 1) * lat_dot
    )
    return (
        routed,
        ctx_grad,
        query_grad,
        pair_all[:, :key_width],
        pair_all[:, key_width:],
        grad_w_out,
        grad_latents,
        small[2 * latent_rows],
        small[2 * latent_rows + 8],
        mine_of(gain_out_full, 0),
    )


def solution(mesh):
    placed = (
        P("dp", None),
        P("dp", None),
        P("dp", None),
        P(None, "mp"),
        P(None, "mp"),
        P(None, "mp"),
        P("mp", None),
        P(),
        P(),
        P(),
        P(),
        P("dp", "mp"),
    )
    return jax.shard_map(
        local if mesh.shape["dp"] == 16 else local_general,
        mesh=mesh,
        in_specs=placed,
        out_specs=(
            P("dp", "mp"),
            P("dp", "mp"),
            P("dp", "mp"),
            P("dp", "mp"),
            P("dp", "mp"),
            P("mp", "dp"),
            P(None, ("dp", "mp")),
            P(("dp", "mp")),
            P(("dp", "mp")),
            P(("dp", "mp")),
        ),
        check_vma=False,
    )
```

```python
import functools

import jax
import jax.numpy as jnp
from jax import lax
from jax.experimental import pallas as pl
from jax.experimental.pallas import tpu as pltpu
from jax.sharding import PartitionSpec as P

HD = 96
EPSILON = 1e-06
NEGATIVE = -1e30
BF16 = jnp.bfloat16
F32 = jnp.float32
VMEM_LIMIT = 63 << 20


def dot_general(left, right, left_dim, right_dim):
    return lax.dot_general(
        left, right, (((left_dim,), (right_dim,)), ((), ())), preferred_element_type=F32
    )


def norm_parts(values_in):
    inverse = lax.rsqrt(jnp.mean(values_in * values_in, axis=-1, keepdims=True) + EPSILON)
    return (values_in * inverse, inverse)


def swap_cores(array):
    return lax.ppermute(array, "mp", [(0, 1), (1, 0)])


def swap_bit(array, bit, dp_count):
    return lax.ppermute(array, "dp", [(i, i ^ (1 << bit)) for i in range(dp_count)])


def halve(array, axis, bit, dp_count):
    mine = (lax.axis_index("dp") >> bit) & 1
    going = lax.dynamic_index_in_dim(array, 1 - mine, axis, keepdims=False)
    kept = lax.dynamic_index_in_dim(array, mine, axis, keepdims=False)
    return kept.astype(F32) + swap_bit(going.astype(BF16), bit, dp_count).astype(F32)


def scatter_sum(array, bits, dp_count):
    rows, owners, columns = array.shape
    left = sorted(bits, reverse=True)
    array = array.reshape((rows,) + (2,) * len(left) + (columns,))
    for bit in bits:
        axis = left.index(bit)
        array = halve(array, 1 + axis, bit, dp_count)
        left.pop(axis)
    return array


def forward_kernel(
    counts_ref,
    gain_ctx_hbm,
    gain_lat_hbm,
    lat_hbm,
    wk_hbm,
    wv_hbm,
    x_hbm,
    wq_hbm,
    attn_hbm,
    k_hbm,
    v_hbm,
    inv_row_hbm,
    q_hbm,
    lk_hbm,
    lv_hbm,
    lat_proj_hbm,
    p_hbm,
    pl_hbm,
    gain_ctx_ref,
    gain_lat_ref,
    lat_ref,
    wk_ref,
    wv_ref,
    x_ref,
    wq_ref,
    attn_ref,
    k_ref,
    v_ref,
    inv_row_ref,
    q_ref,
    lk_ref,
    lv_ref,
    lat_proj_ref,
    p_ref,
    pl_ref,
    lat_normed_ref,
    last_ref,
    gained_ref,
    sems,
    out_sems,
):
    patch_rows, width = x_ref.shape
    chunks = sems.shape[0] - 6
    rows = patch_rows // chunks
    groups = k_ref.shape[0]
    latent_rows = lat_ref.shape[0]
    key_width = wk_ref.shape[0]
    query_width = wq_ref.shape[1]
    per_group = query_width // key_width

    def fetch(source, target, i):
        return pltpu.make_async_copy(source, target, sems.at[i])

    def fetch_rows(i):
        at = pl.ds(i * rows, rows)
        return fetch(x_hbm.at[at], x_ref.at[at], i)

    weights = [
        fetch(source, target, chunks + i)
        for i, (source, target) in enumerate(
            ((lat_hbm, lat_ref), (wk_hbm, wk_ref), (wv_hbm, wv_ref), (wq_hbm, wq_ref))
        )
    ]
    gains = [
        fetch(gain_ctx_hbm, gain_ctx_ref, chunks + 4),
        fetch(gain_lat_hbm, gain_lat_ref, chunks + 5),
    ]
    for copy in (*gains, *weights[:3]):
        copy.start()
    blocks = [fetch_rows(i) for i in range(chunks)]
    for copy in blocks + weights[3:]:
        copy.start()
    results = {}
    for i, (name, source, target) in enumerate(
        (
            ("attn", attn_ref, attn_hbm),
            ("k", k_ref, k_hbm),
            ("v", v_ref, v_hbm),
            ("inv_row", inv_row_ref, inv_row_hbm),
            ("q", q_ref, q_hbm),
            ("lk", lk_ref, lk_hbm),
            ("lv", lv_ref, lv_hbm),
            ("lat_proj", lat_proj_ref, lat_proj_hbm),
            ("p0", p_ref.at[0], p_hbm.at[0]),
            ("p1", p_ref.at[1], p_hbm.at[1]),
            ("pl", pl_ref, pl_hbm),
        )
    ):
        results[name] = pltpu.make_async_copy(source, target, out_sems.at[i])

    for copy in (*gains, weights[0]):
        copy.wait()
    lat = lat_ref[...].astype(F32)
    lat_inverse = lax.rsqrt(jnp.mean(lat * lat, axis=-1, keepdims=True) + EPSILON)
    lat_normed = lat * lat_inverse * gain_lat_ref[...]
    lat_normed_ref[...] = lat_normed.astype(BF16)
    last_ref[rows:, :] = (lat_normed / gain_ctx_ref[...]).astype(BF16)
    for i, ref in enumerate((wk_ref, wv_ref)):
        weights[1 + i].wait()
        gained_ref[i * key_width : (i + 1) * key_width, :] = (
            ref[...].astype(F32) * gain_ctx_ref[...]
        ).astype(BF16)
    for i in range(chunks):
        blocks[i].wait()
        at = slice(i * rows, (i + 1) * rows)
        squares = jnp.zeros((rows, 128), F32)
        for c in range(width // 128):
            part = x_ref[at, c * 128 : (c + 1) * 128].astype(F32)
            squares = squares + part * part
        inverse = lax.rsqrt(jnp.sum(squares, axis=-1, keepdims=True) / width + EPSILON)
        if i < chunks - 1:
            pair = dot_general(x_ref[at, :], gained_ref[...], 1, 1)
        else:
            last_ref[:rows, :] = x_ref[at, :]
            pair = dot_general(last_ref[...], gained_ref[...], 1, 1)
            projected = pair[rows:]
        pair = (pair[:rows] * inverse).astype(BF16)
        inv_row_ref[:, at] = jnp.transpose(jnp.broadcast_to(inverse, (rows, 128)))[:8]
        for g in range(groups):
            k_ref[g, at, :HD] = pair[:, g * HD : (g + 1) * HD]
            v_ref[g, at, :HD] = pair[:, key_width + g * HD : key_width + (g + 1) * HD]
    lat_proj_ref[:, query_width:] = projected
    for i, ref in enumerate((lk_ref, lv_ref)):
        for g in range(groups):
            at = i * key_width + g * HD
            ref[g, :, :HD] = projected[:, at : at + HD].astype(BF16)
    for name in ("k", "v", "inv_row", "lk", "lv"):
        results[name].start()
    weights[3].wait()
    query = jnp.dot(lat_normed_ref[...], wq_ref[...], preferred_element_type=F32) * HD ** (-0.5)
    lat_proj_ref[:, :query_width] = query
    first_count = counts_ref[0, 0]
    both_count = first_count + counts_ref[0, 1]
    position = lax.broadcasted_iota(jnp.int32, (1, patch_rows), 1)
    in_first = position < first_count
    in_second = jnp.logical_and(position >= first_count, position < both_count)
    rows_at = lax.broadcasted_iota(jnp.int32, (patch_rows, HD), 0)
    row_first = rows_at < first_count
    row_second = jnp.logical_and(rows_at >= first_count, rows_at < both_count)
    for g in range(groups):
        for h in range(per_group):
            head = g * per_group + h
            q_ref[g, h * latent_rows : (h + 1) * latent_rows, :HD] = query[
                :, head * HD : (head + 1) * HD
            ].astype(BF16)
    results["lat_proj"].start()
    results["q"].start()
    for g in range(groups):
        q = q_ref[g, :, :HD]
        scores = dot_general(q, k_ref[g, :, :HD], 1, 1)
        lat_scores = dot_general(q, lk_ref[g, :, :HD], 1, 1)
        lat_max = jnp.max(lat_scores, axis=-1, keepdims=True)
        max_first = jnp.maximum(
            jnp.max(jnp.where(in_first, scores, NEGATIVE), axis=-1, keepdims=True), lat_max
        )
        max_second = jnp.maximum(
            jnp.max(jnp.where(in_second, scores, NEGATIVE), axis=-1, keepdims=True), lat_max
        )
        masked = jnp.where(
            in_first, scores - max_first, jnp.where(in_second, scores - max_second, NEGATIVE)
        )
        exponent = jnp.exp(masked)
        lat_first = jnp.exp(lat_scores - max_first)
        lat_second = jnp.exp(lat_scores - max_second)
        sum_first = jnp.sum(
            jnp.where(in_first, exponent, 0.0), axis=-1, keepdims=True
        ) + jnp.sum(lat_first, axis=-1, keepdims=True)
        sum_second = jnp.sum(
            jnp.where(in_second, exponent, 0.0), axis=-1, keepdims=True
        ) + jnp.sum(lat_second, axis=-1, keepdims=True)
        per_first = 1.0 / sum_first
        per_second = 1.0 / sum_second
        p = (exponent * jnp.where(in_first, per_first, per_second)).astype(BF16)
        p_ref[g] = p
        results[f"p{g}"].start()
        lat_p_first = (lat_first * per_first).astype(BF16)
        lat_p_second = (lat_second * per_second).astype(BF16)
        pl_ref[g, :, :latent_rows] = lat_p_first
        pl_ref[g, :, latent_rows:] = lat_p_second
        v = v_ref[g, :, :HD]
        zero = jnp.zeros_like(v)
        lv = lv_ref[g, :, :HD]
        for j, (row_mask, lat_p) in enumerate(
            ((row_first, lat_p_first), (row_second, lat_p_second))
        ):
            mixed = jnp.dot(
                p, jnp.where(row_mask, v, zero), preferred_element_type=F32
            ) + jnp.dot(lat_p, lv, preferred_element_type=F32)
            mixed = mixed.astype(BF16)
            for h in range(per_group):
                head = g * per_group + h
                attn_ref[
                    j * latent_rows : (j + 1) * latent_rows, head * HD : (head + 1) * HD
                ] = mixed[h * latent_rows : (h + 1) * latent_rows]
    for name in ("attn", "pl"):
        results[name].start()
    for copy in results.values():
        copy.wait()


def whole(shape):
    return pl.BlockSpec(shape, lambda *_: (0,) * len(shape))


def held(shape):
    return pl.BlockSpec(shape, lambda *_: (0,) * len(shape), pipeline_mode=pl.Buffered(1))


def forward_call(context, counts, w_query, w_key, w_value, latents, gain_ctx, gain_lat):
    patch_rows, width = context.shape
    chunks = 4
    key_width = w_key.shape[0]
    query_width = w_query.shape[1]
    groups = key_width // HD
    latent_rows = latents.shape[0]
    stacked = query_width // key_width * latent_rows
    large = (latents, w_key, w_value, context, w_query)
    out = [
        ((2 * latent_rows, query_width), BF16),
        ((groups, patch_rows, 128), BF16),
        ((groups, patch_rows, 128), BF16),
        ((8, patch_rows), F32),
        ((groups, stacked, 128), BF16),
        ((groups, latent_rows, 128), BF16),
        ((groups, latent_rows, 128), BF16),
        ((latent_rows, query_width + 2 * key_width), F32),
        ((groups, stacked, patch_rows), BF16),
        ((groups, stacked, 2 * latent_rows), BF16),
    ]
    return pl.pallas_call(
        forward_kernel,
        name="forward_attention",
        in_specs=[
            pl.BlockSpec(memory_space=pltpu.SMEM),
            pl.BlockSpec(memory_space=pl.ANY),
            pl.BlockSpec(memory_space=pl.ANY),
        ]
        + [pl.BlockSpec(memory_space=pl.ANY)] * len(large),
        out_specs=[pl.BlockSpec(memory_space=pl.ANY)] * len(out),
        out_shape=[jax.ShapeDtypeStruct(shape, dtype) for shape, dtype in out],
        scratch_shapes=[pltpu.VMEM((1, width), F32)] * 2
        + [pltpu.VMEM(a.shape, a.dtype) for a in large]
        + [pltpu.VMEM(shape, dtype) for shape, dtype in out]
        + [
            pltpu.VMEM((latent_rows, width), BF16),
            pltpu.VMEM((patch_rows // chunks + latent_rows, width), BF16),
            pltpu.VMEM((2 * key_width, width), BF16),
            pltpu.SemaphoreType.DMA((chunks + 6,)),
            pltpu.SemaphoreType.DMA((len(out) + 1,)),
        ],
        cost_estimate=pl.CostEstimate(
            flops=5_000_000_000, bytes_accessed=24_000_000, transcendentals=600_000
        ),
        compiler_params=pltpu.CompilerParams(vmem_limit_bytes=VMEM_LIMIT),
    )(counts, gain_ctx.reshape(1, width), gain_lat.reshape(1, width), *large)


def slots_of(routes_ref, slot_count, as_row):
    rows = routes_ref.shape[1]
    turned = jnp.broadcast_to(routes_ref[...].astype(F32), (rows, rows))
    shard = jnp.transpose(turned)
    down = lax.broadcasted_iota(jnp.int32, (rows, rows), 0)
    across = lax.broadcasted_iota(jnp.int32, (rows, rows), 1)
    same = shard == turned
    if as_row:
        rank = jnp.sum(jnp.where(same & (down < across), 1.0, 0.0), axis=0, keepdims=True)
        return (turned[:1] * slot_count + rank).astype(jnp.int32)
    rank = jnp.sum(jnp.where(same & (across < down), 1.0, 0.0), axis=1, keepdims=True)
    return (shard[:, :1] * slot_count + rank).astype(jnp.int32)


def branch_kernel(
    slot_count,
    own_hbm,
    other_hbm,
    lat_hbm,
    gain_hbm,
    routes_hbm,
    w_own_hbm,
    w_other_hbm,
    hat_hbm,
    inv_hbm,
    out_hbm,
    own_ref,
    other_ref,
    lat_ref,
    gain_ref,
    routes_ref,
    w_own_ref,
    w_other_ref,
    hat_ref,
    low_ref,
    inv_ref,
    out_ref,
    sems,
    out_sems,
    small_sems,
):
    rows, width = hat_ref.shape
    slots, half = out_ref.shape
    parts = sems.shape[1]
    size = width // parts
    small = [
        pltpu.make_async_copy(source, target, small_sems.at[i])
        for i, (source, target) in enumerate(
            (
                (routes_hbm, routes_ref),
                (own_hbm, own_ref),
                (other_hbm, other_ref),
                (lat_hbm, lat_ref),
                (gain_hbm, gain_ref),
            )
        )
    ]
    for copy in small:
        copy.start()
    copies = []
    for part in range(parts):
        at = pl.ds(part * size, size)
        for i, (source, target) in enumerate(
            ((w_own_hbm, w_own_ref), (w_other_hbm, w_other_ref))
        ):
            copies.append(
                pltpu.make_async_copy(source.at[:, at], target.at[:, at], sems.at[i, part])
            )
    for copy in copies:
        copy.start()
    small[0].wait()
    place = slots_of(routes_ref, slot_count, True)
    for copy in small[1:]:
        copy.wait()
    table = jnp.where(
        lax.broadcasted_iota(jnp.int32, (slots, rows), 0) == place, 1.0, 0.0
    ).astype(BF16)
    squares = jnp.zeros((rows, 128), F32)
    for part in range(parts):
        at = slice(part * size, (part + 1) * size)
        copies[2 * part].wait()
        copies[2 * part + 1].wait()
        lat = lat_ref[:, at].astype(F32)
        resid = (
            jnp.concatenate([lat, lat], axis=0)
            + jnp.dot(own_ref[...], w_own_ref[:, at], preferred_element_type=F32)
            + jnp.dot(other_ref[...], w_other_ref[:, at], preferred_element_type=F32)
        )
        hat_ref[:, at] = resid
        for c in range(size // 128):
            piece = resid[:, c * 128 : (c + 1) * 128]
            squares = squares + piece * piece
    inverse = lax.rsqrt(jnp.sum(squares, axis=-1, keepdims=True) / width + EPSILON)
    inv_ref[...] = inverse
    low_ref[...] = (hat_ref[...] * inverse).astype(BF16)
    results = [
        pltpu.make_async_copy(source, target, out_sems.at[i])
        for i, (source, target) in enumerate(
            ((low_ref, hat_hbm), (inv_ref, inv_hbm), (out_ref, out_hbm))
        )
    ]
    for copy in results[:2]:
        copy.start()
    at = pl.ds(pl.multiple_of(lax.axis_index("mp") * half, half), half)
    final = (hat_ref[:, at] * inverse * gain_ref[:, at]).astype(BF16)
    out_ref[...] = jnp.dot(table, final, preferred_element_type=F32).astype(BF16)
    results[2].start()
    for copy in results:
        copy.wait()


def branch_call(own, other, w_own, w_other, latents, gain_out, routes, slots, slot_count):
    width = w_own.shape[1]
    rows, heads = own.shape
    parts = 2
    return pl.pallas_call(
        functools.partial(branch_kernel, slot_count),
        name="branch_norm",
        **dict(
            in_specs=[pl.BlockSpec(memory_space=pl.ANY)] * 7,
            out_specs=[pl.BlockSpec(memory_space=pl.ANY)] * 3,
            scratch_shapes=[
                pltpu.VMEM((rows, heads), BF16),
                pltpu.VMEM((rows, heads), BF16),
                pltpu.VMEM(latents.shape, BF16),
                pltpu.VMEM((1, width), F32),
                pltpu.VMEM((1, rows), jnp.int32),
                pltpu.VMEM(w_own.shape, BF16),
                pltpu.VMEM(w_other.shape, BF16),
                pltpu.VMEM((rows, width), F32),
                pltpu.VMEM((rows, width), BF16),
                pltpu.VMEM((rows, 1), F32),
                pltpu.VMEM((slots, width // 2), BF16),
                pltpu.SemaphoreType.DMA((2, parts)),
                pltpu.SemaphoreType.DMA((3,)),
                pltpu.SemaphoreType.DMA((5,)),
            ],
        ),
        out_shape=[
            jax.ShapeDtypeStruct((rows, width), BF16),
            jax.ShapeDtypeStruct((rows, 1), F32),
            jax.ShapeDtypeStruct((slots, width // 2), BF16),
        ],
        cost_estimate=pl.CostEstimate(
            flops=2 * 2 * rows * heads * width, bytes_accessed=16_000_000, transcendentals=0
        ),
        compiler_params=pltpu.CompilerParams(vmem_limit_bytes=VMEM_LIMIT),
    )(own, other, latents, gain_out.reshape(1, width), routes, w_own, w_other)


def attention_backward(
    counts_ref,
    d_attn,
    k_ref,
    v_ref,
    q_ref,
    lk_ref,
    lv_ref,
    p_ref,
    pl_ref,
    inv_row_ref,
    pair_ref,
    scaled_ref,
    lat_ref,
):
    groups, patch_rows, _ = k_ref.shape
    latent_rows = lk_ref.shape[1]
    stacked = q_ref.shape[1]
    per_group = stacked // latent_rows
    key_width = groups * HD
    query_width = groups * per_group * HD
    first_count = counts_ref[0, 0]
    both_count = first_count + counts_ref[0, 1]
    position = lax.broadcasted_iota(jnp.int32, (1, patch_rows), 1)
    in_first = position < first_count
    rows_at = lax.broadcasted_iota(jnp.int32, (patch_rows, HD), 0)
    row_first = rows_at < first_count
    row_second = jnp.logical_and(rows_at >= first_count, rows_at < both_count)
    scale_row = inv_row_ref[:1]
    row_dot = jnp.zeros((1, patch_rows), F32)
    for g in range(groups):
        d_first = jnp.concatenate(
            [
                d_attn[:latent_rows, head * HD : (head + 1) * HD]
                for head in range(g * per_group, (g + 1) * per_group)
            ],
            axis=0,
        )
        d_second = jnp.concatenate(
            [
                d_attn[latent_rows:, head * HD : (head + 1) * HD]
                for head in range(g * per_group, (g + 1) * per_group)
            ],
            axis=0,
        )
        q = q_ref[g, :, :HD]
        k = k_ref[g, :, :HD]
        v = v_ref[g, :, :HD]
        lk = lk_ref[g, :, :HD]
        lv = lv_ref[g, :, :HD]
        p_low = p_ref[g]
        p = p_low.astype(F32)
        zero = jnp.zeros_like(v)
        d_p = dot_general(d_first, jnp.where(row_first, v, zero), 1, 1) + dot_general(
            d_second, jnp.where(row_second, v, zero), 1, 1
        )
        product = p * d_p
        lat_first = pl_ref[g, :, :latent_rows]
        lat_second = pl_ref[g, :, latent_rows:]
        d_lat_first = dot_general(d_first, lv, 1, 1)
        d_lat_second = dot_general(d_second, lv, 1, 1)
        lat_product_first = lat_first.astype(F32) * d_lat_first
        lat_product_second = lat_second.astype(F32) * d_lat_second
        whole_sum = jnp.sum(product, axis=-1, keepdims=True)
        first_sum = jnp.sum(jnp.where(in_first, product, 0.0), axis=-1, keepdims=True)
        delta_first = first_sum + jnp.sum(lat_product_first, axis=-1, keepdims=True)
        delta_second = (whole_sum - first_sum) + jnp.sum(
            lat_product_second, axis=-1, keepdims=True
        )
        ds = product - p * jnp.where(in_first, delta_first, delta_second)
        ds_low = ds.astype(BF16)
        dsl = (
            lat_product_first
            - lat_first.astype(F32) * delta_first
            + lat_product_second
            - lat_second.astype(F32) * delta_second
        ).astype(BF16)
        scores = dot_general(q, k, 1, 1)
        row_dot = row_dot + jnp.sum(ds * scores + product, axis=0, keepdims=True)
        d_q = (
            jnp.dot(ds_low, k, preferred_element_type=F32)
            + jnp.dot(dsl, lk, preferred_element_type=F32)
        ).astype(BF16)
        for h in range(per_group):
            head = g * per_group + h
            lat_ref[:latent_rows, head * HD : (head + 1) * HD] = d_q[
                h * latent_rows : (h + 1) * latent_rows
            ]
        d_k = dot_general(q, ds_low, 0, 0)
        nothing = jnp.zeros_like(p_low)
        d_v = dot_general(d_first, jnp.where(in_first, p_low, nothing), 0, 0) + dot_general(
            d_second, jnp.where(in_first, nothing, p_low), 0, 0
        )
        k_at = slice(g * HD, (g + 1) * HD)
        v_at = slice(key_width + g * HD, key_width + (g + 1) * HD)
        pair_ref[k_at, :] = d_k.astype(BF16)
        pair_ref[v_at, :] = d_v.astype(BF16)
        scaled_ref[k_at, :] = (d_k * scale_row).astype(BF16)
        scaled_ref[v_at, :] = (d_v * scale_row).astype(BF16)
        d_lk = dot_general(dsl, q, 0, 0)
        d_lv = dot_general(lat_first, d_first, 0, 0) + dot_general(lat_second, d_second, 0, 0)
        lat_ref[:latent_rows, query_width + g * HD : query_width + (g + 1) * HD] = d_lk.astype(BF16)
        at = query_width + key_width + g * HD
        lat_ref[:latent_rows, at : at + HD] = d_lv.astype(BF16)
    high = row_dot.astype(BF16)
    low = (row_dot - high.astype(F32)).astype(BF16)
    rest = pair_ref.shape[0] - 2 * key_width - 2
    pair_ref[2 * key_width :, :] = jnp.concatenate(
        [high.astype(F32), low.astype(F32), jnp.zeros((rest, patch_rows), F32)], axis=0
    ).astype(BF16)


def backward_kernel(
    slot_count,
    counts_ref,
    inv_out_hbm,
    gain_hbm,
    routes_hbm,
    inv_row_hbm,
    attn_hbm,
    got_own_hbm,
    got_other_hbm,
    hat_hbm,
    w_out_hbm,
    k_hbm,
    v_hbm,
    q_hbm,
    lk_hbm,
    lv_hbm,
    p_hbm,
    pl_hbm,
    x_hbm,
    line_own_hbm,
    line_high_hbm,
    pair_hbm,
    message_hbm,
    lat_hbm,
    value_going_hbm,
    value_kept_hbm,
    key_going_hbm,
    key_kept_hbm,
    inv_out_ref,
    gain_ref,
    routes_ref,
    inv_row_ref,
    attn_ref,
    got_own_ref,
    got_other_ref,
    hat_ref,
    w_out_ref,
    k_ref,
    v_ref,
    q_ref,
    lk_ref,
    lv_ref,
    p_ref,
    pl_ref,
    x_ref,
    d_final_ref,
    branch_ref,
    scaled_ref,
    line_own_ref,
    line_high_ref,
    pair_ref,
    message_ref,
    lat_ref,
    value_ref,
    key_ref,
    sems,
    out_sems,
    value_sems,
    key_sems,
    small_sems,
):
    small = [
        pltpu.make_async_copy(source, target, small_sems.at[i])
        for i, (source, target) in enumerate(
            (
                (routes_hbm, routes_ref),
                (inv_out_hbm, inv_out_ref),
                (gain_hbm, gain_ref),
                (inv_row_hbm, inv_row_ref),
                (attn_hbm, attn_ref),
            )
        )
    ]
    for copy in small:
        copy.start()
    sources = (
        got_own_hbm,
        got_other_hbm,
        hat_hbm,
        w_out_hbm,
        k_hbm,
        v_hbm,
        q_hbm,
        lk_hbm,
        lv_hbm,
        p_hbm,
        pl_hbm,
        x_hbm,
    )
    targets = (
        got_own_ref,
        got_other_ref,
        hat_ref,
        w_out_ref,
        k_ref,
        v_ref,
        q_ref,
        lk_ref,
        lv_ref,
        p_ref,
        pl_ref,
        x_ref,
    )
    copies = [
        pltpu.make_async_copy(source, target, sems.at[i])
        for i, (source, target) in enumerate(zip(sources, targets))
    ]
    for copy in copies[:4]:
        copy.start()
    me, core = lax.axis_index("dp"), lax.axis_index("mp")
    rows, width = hat_ref.shape
    half = width // 2
    slots = got_own_ref.shape[0]
    latent_rows = lk_ref.shape[1]
    key_width, own = value_ref.shape[2:]

    small[0].wait()
    place = slots_of(routes_ref, slot_count, False)
    for copy in small[1:]:
        copy.wait()
    table = jnp.where(
        lax.broadcasted_iota(jnp.int32, (rows, slots), 1) == place, 1.0, 0.0
    ).astype(BF16)
    total = jnp.zeros((rows, 1), F32)
    chunk = 1024
    for copy in copies[:3]:
        copy.wait()
    for copy in copies[4:]:
        copy.start()
    for got_ref, which in ((got_own_ref, core), (got_other_ref, 1 - core)):
        for c in range(half // chunk):
            at = pl.ds(pl.multiple_of(which * half + c * chunk, chunk), chunk)
            d_final = jnp.dot(
                table, got_ref[:, c * chunk : (c + 1) * chunk], preferred_element_type=F32
            )
            product = d_final * hat_ref[:, at].astype(F32)
            total = total + jnp.sum(product * gain_ref[:, at], axis=-1, keepdims=True)
            d_final_ref[:, at] = d_final.astype(BF16)
    total = total / width
    lat_ref[latent_rows:, :] = jnp.zeros_like(lat_ref[latent_rows:, :])
    highs, lows = [], []
    part = width // 4
    for c in range(width // chunk):
        at = slice(c * chunk, (c + 1) * chunk)
        d_final = d_final_ref[:, at].astype(F32)
        hat = hat_ref[:, at].astype(F32)
        term = jnp.sum(d_final * hat, axis=0, keepdims=True)
        high = term.astype(BF16).astype(F32)
        highs.append(high)
        lows.append(term - high)
        branch_ref[:, at] = (
            inv_out_ref[...] * (d_final * gain_ref[:, at] - hat * total)
        ).astype(BF16)
    per_row = part // chunk
    lines = [
        jnp.concatenate(group[i * per_row : (i + 1) * per_row], axis=1)
        for group in (highs, lows)
        for i in range(4)
    ]
    lat_ref[latent_rows : latent_rows + 16, :part] = jnp.concatenate(
        lines + [jnp.zeros((8, part), F32)], axis=0
    ).astype(BF16)
    z = me >> 2
    some = pl.ds(pl.multiple_of(core * (rows // 2), rows // 2), rows // 2)
    line_own_ref[...] = branch_ref[:, pl.ds(pl.multiple_of(z * part, part), part)]
    heads = attn_ref.shape[1]
    for turn, ref, first in (
        (1, message_ref, 0),
        (2, line_high_ref, 0),
        (3, line_high_ref, part + 2 * heads),
    ):
        ref[: rows // 2, first : first + part] = branch_ref[
            some, pl.ds(pl.multiple_of((z ^ turn) * part, part), part)
        ]
    for ref in (message_ref, line_high_ref):
        ref[: rows // 2, part : part + heads] = attn_ref[: rows // 2, :]
        ref[: rows // 2, part + heads : part + 2 * heads] = attn_ref[rows // 2 :, :]
    results = [
        pltpu.make_async_copy(source, target, out_sems.at[i])
        for i, (source, target) in enumerate(
            (
                (line_high_ref, line_high_hbm),
                (message_ref, message_hbm),
                (line_own_ref, line_own_hbm),
                (pair_ref, pair_hbm),
                (lat_ref, lat_hbm),
            )
        )
    ]
    for copy in results[:3]:
        copy.start()

    copies[3].wait()
    d_attn = dot_general(branch_ref[...], w_out_ref[...], 1, 1).astype(BF16)
    for copy in copies[4:11]:
        copy.wait()
    attention_backward(
        counts_ref,
        d_attn,
        k_ref,
        v_ref,
        q_ref,
        lk_ref,
        lv_ref,
        p_ref,
        pl_ref,
        inv_row_ref,
        pair_ref,
        scaled_ref,
        lat_ref,
    )
    for copy in results[3:]:
        copy.start()
    copies[11].wait()

    odd = me & 1
    for j in range(8):
        y = ((me >> 1) & 1) ^ (1 - (j >> 2))
        z = (me >> 2) ^ ((1 - ((j >> 1) & 1)) + 2 * (1 - (j & 1)))
        first = 4 * z + 2 * y
        line = j & 3
        key_hbm = key_kept_hbm if j >> 2 else key_going_hbm
        grad = jnp.dot(
            scaled_ref[...],
            x_ref[:, pl.ds(pl.multiple_of(first * own, 2 * own), 2 * own)],
            preferred_element_type=F32,
        ).astype(BF16)
        for x_same, value_hbm in enumerate((value_going_hbm, value_kept_hbm)):
            block = jnp.where(odd == x_same, grad[:, own:], grad[:, :own])
            value_ref[x_same, j] = block[key_width:]
            key_ref[x_same, j] = block[:key_width]
            for copy in (
                pltpu.make_async_copy(
                    value_ref.at[x_same, j], value_hbm.at[j], value_sems.at[x_same, j]
                ),
                pltpu.make_async_copy(
                    key_ref.at[x_same, j], key_hbm.at[x_same, line], key_sems.at[x_same, j]
                ),
            ):
                copy.start()
                results.append(copy)
    for copy in results:
        copy.wait()


def backward_call(
    counts, attn, got_own, got_other, hat, inv_out, gain_out, routes, w_out, kept, context, slot_count
):
    k, v, q, lk, lv, p, lat_p, inv_row = kept
    rows, width = hat.shape
    patch_rows = context.shape[0]
    heads = w_out.shape[0]
    key_width = k.shape[0] * HD
    latent_rows = lk.shape[1]
    own = width // 16
    large = (got_own, got_other, hat, w_out, k, v, q, lk, lv, p, lat_p, context)
    small = (inv_out, gain_out.reshape(1, width), routes, inv_row, attn)
    out = [
        (rows, width // 4),
        (rows // 2, width // 2 + 2 * heads),
        (2 * key_width + 16, patch_rows),
        (rows // 2, width // 4 + 2 * heads),
        (latent_rows + 16, heads + 2 * key_width),
        (8, key_width, own),
        (8, key_width, own),
        (2, 4, key_width, own),
        (2, 4, key_width, own),
    ]
    return pl.pallas_call(
        functools.partial(backward_kernel, slot_count),
        name="attention_backward",
        **dict(
            in_specs=[
                pl.BlockSpec(memory_space=pltpu.SMEM),
            ]
            + [pl.BlockSpec(memory_space=pl.ANY)] * (5 + len(large)),
            out_specs=[pl.BlockSpec(memory_space=pl.ANY)] * len(out),
            scratch_shapes=[pltpu.VMEM(a.shape, a.dtype) for a in (*small, *large)]
            + [
                pltpu.VMEM((rows, width), BF16),
                pltpu.VMEM((rows, width), BF16),
                pltpu.VMEM((2 * key_width, patch_rows), BF16),
            ]
            + [pltpu.VMEM(shape, BF16) for shape in out[:5]]
            + [
                pltpu.VMEM((2, 8, key_width, own), BF16),
                pltpu.VMEM((2, 8, key_width, own), BF16),
                pltpu.SemaphoreType.DMA((len(large),)),
                pltpu.SemaphoreType.DMA((5,)),
                pltpu.SemaphoreType.DMA((2, 8)),
                pltpu.SemaphoreType.DMA((2, 8)),
                pltpu.SemaphoreType.DMA((5,)),
            ],
        ),
        out_shape=[jax.ShapeDtypeStruct(shape, BF16) for shape in out],
        cost_estimate=pl.CostEstimate(
            flops=5_000_000_000, bytes_accessed=26_000_000, transcendentals=0
        ),
        compiler_params=pltpu.CompilerParams(vmem_limit_bytes=VMEM_LIMIT),
    )(counts, *small, *large)


def patch_kernel(
    width,
    where_ref,
    own_ref,
    other_ref,
    wk_ref,
    wv_ref,
    wk_other_ref,
    wv_other_ref,
    x_ref,
    inv_row_ref,
    gain_ref,
    out_ref,
    turned_ref,
    inv_ref,
    dot_ref,
    w_ref,
):
    step = pl.program_id(0)
    key_width = wk_ref.shape[0]
    patch_rows = turned_ref.shape[0]
    pair = 2 * key_width

    @pl.when(step == 0)
    def _():
        row_dot = jnp.zeros((patch_rows, 1), F32)
        for i, ref in enumerate((own_ref, other_ref)):
            turned = jnp.transpose(ref[...])
            turned_ref[:, i * pair : (i + 1) * pair] = turned[:, :pair]
            row_dot = row_dot + turned[:, pair : pair + 1].astype(F32)
            row_dot = row_dot + turned[:, pair + 1 : pair + 2].astype(F32)
        inverse = jnp.transpose(jnp.broadcast_to(inv_row_ref[:1], (128, patch_rows)))[:, :1]
        inv_ref[...] = inverse
        dot_ref[...] = row_dot * (inverse * inverse / width)
        for i, ref in enumerate((wk_ref, wv_ref, wk_other_ref, wv_other_ref)):
            w_ref[i * key_width : (i + 1) * key_width, :] = ref[...]

    rows = x_ref.shape[0]
    at = pl.ds(pl.multiple_of(step * rows, rows), rows)
    d_in = jnp.dot(turned_ref[at, :], w_ref[...], preferred_element_type=F32)
    out_ref[...] = (
        d_in * gain_ref[...] * inv_ref[at, :] - x_ref[...].astype(F32) * dot_ref[at, :]
    ).astype(BF16)


def patch_call(where, own, other, wk, wv, wk_other, wv_other, context, inv_row, gain_ctx):
    patch_rows, width = context.shape
    half = width // 2
    steps = 4
    rows = patch_rows // steps
    key_width = wk.shape[0]
    once = pl.Buffered(1)
    w_spec = pl.BlockSpec((key_width, half), lambda i, w: (0, w[1]), pipeline_mode=once)
    return pl.pallas_call(
        functools.partial(patch_kernel, width),
        name="patch_gradient",
        grid_spec=pltpu.PrefetchScalarGridSpec(
            num_scalar_prefetch=1,
            grid=(steps,),
            in_specs=[
                held(own.shape),
                held(other.shape),
                w_spec,
                w_spec,
                w_spec,
                w_spec,
                pl.BlockSpec((rows, half), lambda i, w: (i, w[1])),
                held(inv_row.shape),
                pl.BlockSpec((1, half), lambda i, w: (0, w[1])),
            ],
            out_specs=pl.BlockSpec((rows, half), lambda i, w: (i, 0)),
            scratch_shapes=[
                pltpu.VMEM((patch_rows, 4 * key_width), BF16),
                pltpu.VMEM((patch_rows, 1), F32),
                pltpu.VMEM((patch_rows, 1), F32),
                pltpu.VMEM((4 * key_width, half), BF16),
            ],
        ),
        out_shape=jax.ShapeDtypeStruct((patch_rows, half), BF16),
        cost_estimate=pl.CostEstimate(
            flops=3_300_000_000, bytes_accessed=14_000_000, transcendentals=0
        ),
        compiler_params=pltpu.CompilerParams(vmem_limit_bytes=VMEM_LIMIT),
    )(where, own, other, wk, wv, wk_other, wv_other, context, inv_row, gain_ctx.reshape(1, width))


def out_kernel(
    where_ref,
    attn_own_ref,
    line_own_ref,
    low_ref,
    high_ref,
    forwarded_ref,
    other_low_ref,
    other_high_ref,
    other_forwarded_ref,
    first_onward_ref,
    first_last_ref,
    first_kept_ref,
    second_onward_ref,
    second_last_ref,
    second_kept_ref,
    attn_ref,
    line_ref,
    resid_ref,
):
    rows, heads = attn_own_ref.shape
    columns = line_ref.shape[1]
    own = columns // 4
    latent_rows = rows // 2
    mine = where_ref[1]
    half = rows // 2
    attn_ref[:rows, :] = attn_own_ref[...]
    line_ref[:rows, :] = line_own_ref[...]
    for i, (ref, other, first, attn_at) in enumerate(
        (
            (low_ref, other_low_ref, 0, columns),
            (high_ref, other_high_ref, 0, columns),
            (forwarded_ref, other_forwarded_ref, 2 * heads, 0),
        )
    ):
        at = (i + 1) * rows
        attn_ref[at : at + half, :] = ref[:half, attn_at : attn_at + heads]
        attn_ref[at + half : at + rows, :] = ref[:half, attn_at + heads : attn_at + 2 * heads]
        for holder, which in ((ref, mine), (other, 1 - mine)):
            line_ref[pl.ds(pl.multiple_of(at + which * half, half), half), :] = holder[
                :half, first : first + columns
            ]
    resid = jnp.zeros((latent_rows, columns), F32)
    for i in range(8):
        resid = resid + line_ref[i * latent_rows : (i + 1) * latent_rows, :].astype(F32)
    resid_ref[...] = resid
    odd = where_ref[0] & 1
    upper = (where_ref[0] >> 1) & 1
    share = own // 2
    cut = heads // 2
    extra = latent_rows // 4
    for turn in range(4):
        x_differs, y_differs = 1 - (turn & 1), 1 - (turn >> 1)
        owner = 2 * (upper ^ y_differs) + (odd ^ x_differs)
        at = pl.ds(pl.multiple_of(owner * own, own), own)
        grad = dot_general(attn_ref[...], line_ref[:, at], 0, 0).astype(BF16)
        mine_at = pl.ds(pl.multiple_of(owner * own + mine * share, share), share)
        part = resid_ref[:, mine_at]
        part = jnp.concatenate([part[: latent_rows // 2], part[latent_rows // 2 :]], axis=1)
        ends = 1 - y_differs
        ref = (first_onward_ref, first_last_ref)[ends] if x_differs else first_kept_ref.at[ends]
        ref[:cut, :] = grad[:cut]
        ref[cut:, :] = part[:extra].astype(BF16)
        ends = 1 - x_differs
        ref = (second_onward_ref, second_last_ref)[ends] if y_differs else second_kept_ref.at[ends]
        ref[:cut, :] = grad[cut:]
        ref[cut:, :] = part[extra:].astype(BF16)


def out_call(where, attn, line, received, others):
    rows, heads = attn.shape
    columns = line.shape[1]
    own = columns // 4
    block = (heads // 2 + rows // 8, own)
    shapes = [block, block, (2, *block)] * 2
    operands = (attn, line, *received, *others)
    return pl.pallas_call(
        out_kernel,
        name="output_projection_gradient",
        grid_spec=pltpu.PrefetchScalarGridSpec(
            num_scalar_prefetch=1,
            grid=(1,),
            in_specs=[held(a.shape) for a in operands],
            out_specs=[held(shape) for shape in shapes],
            scratch_shapes=[
                pltpu.VMEM((4 * rows, heads), BF16),
                pltpu.VMEM((4 * rows, columns), BF16),
                pltpu.VMEM((rows // 2, columns), F32),
            ],
        ),
        out_shape=[jax.ShapeDtypeStruct(shape, BF16) for shape in shapes],
        cost_estimate=pl.CostEstimate(
            flops=8 * rows * heads * columns, bytes_accessed=4_000_000, transcendentals=0
        ),
        compiler_params=pltpu.CompilerParams(vmem_limit_bytes=VMEM_LIMIT),
    )(where, *operands)


def latent_kernel(
    where_ref,
    sum_ref,
    across_ref,
    along_ref,
    corner_ref,
    proj_ref,
    lat_ref,
    gain_ref,
    wq_ref,
    wk_ref,
    wv_ref,
    routed_hbm,
    query_ref,
    pair_ref,
    message_ref,
    gain_out_ref,
    routed_out_hbm,
    total_ref,
    routed_ref,
    sems,
):
    arrive = pltpu.make_async_copy(routed_hbm, routed_ref, sems.at[0])
    leave = pltpu.make_async_copy(routed_ref, routed_out_hbm, sems.at[1])
    arrive.start()
    latent_rows, width = lat_ref.shape
    own, query_width = wq_ref.shape
    key_width = wk_ref.shape[0]
    scaling = HD ** (-0.5)
    total_ref[...] = sum(
        ref[...].astype(F32) for ref in (sum_ref, across_ref, along_ref, corner_ref)
    )
    total = total_ref[:latent_rows, :]
    low = total.astype(BF16)
    at = pl.ds(pl.multiple_of(where_ref[0] * own, own), own)
    lat = lat_ref[...].astype(F32)
    inverse = lax.rsqrt(jnp.mean(lat * lat, axis=-1, keepdims=True) + EPSILON)
    gain = gain_ref[:, at]
    normed = (lat_ref[:, at].astype(F32) * inverse * gain).astype(BF16)
    query = dot_general(normed, low[:, :query_width], 0, 0) * scaling
    query_ref[...] = query
    pair = dot_general(low[:, query_width:], normed, 0, 0)
    pair_ref[...] = pair
    wq = wq_ref[...]
    wk = wk_ref[...]
    wv = wv_ref[...]
    gain_term = jnp.transpose(
        jnp.broadcast_to(jnp.sum(wq.astype(F32) * query, axis=1, keepdims=True), (own, 128))
    )[:1]
    gain_term = gain_term + jnp.sum(wk.astype(F32) * pair[:key_width], axis=0, keepdims=True)
    gain_term = gain_term + jnp.sum(wv.astype(F32) * pair[key_width:], axis=0, keepdims=True)
    arrive.wait()
    leave.start()
    scaled = (total[:, :query_width] * scaling).astype(BF16)
    d_lat = dot_general(scaled, wq, 1, 1)
    d_lat = d_lat + jnp.dot(
        low[:, query_width : query_width + key_width], wk, preferred_element_type=F32
    )
    d_lat = d_lat + jnp.dot(low[:, query_width + key_width :], wv, preferred_element_type=F32)
    message_ref[:latent_rows, :own] = d_lat
    message_ref[:latent_rows, own:] = jnp.broadcast_to(
        jnp.sum(total * proj_ref[...], axis=-1, keepdims=True), (latent_rows, 128)
    )
    message_ref[latent_rows:, :own] = jnp.broadcast_to(gain_term / gain, (8, own))
    message_ref[latent_rows:, own:] = jnp.zeros((8, 128), F32)
    part = width // 4
    share = own // 2
    first = where_ref[0] * own + where_ref[1] * share
    line = first // part
    mine = pl.ds(pl.multiple_of(first % part, share), share)
    gain_out_ref[...] = jnp.sum(
        jnp.where(
            lax.broadcasted_iota(jnp.int32, (8, share), 0) % 4 == line,
            total_ref[latent_rows : latent_rows + 8, mine],
            0.0,
        ),
        axis=0,
        keepdims=True,
    )
    leave.wait()


def latent_call(where, sums, parts, proj, latents, gain_lat, w_query, wk, wv, own, routed):
    latent_rows, width = latents.shape
    query_width = w_query.shape[1]
    key_width = wk.shape[0]
    return pl.pallas_call(
        latent_kernel,
        name="latent_gradients",
        grid_spec=pltpu.PrefetchScalarGridSpec(
            num_scalar_prefetch=1,
            grid=(1,),
            in_specs=[
                held(sums.shape),
                *(held(part.shape) for part in parts),
                held(proj.shape),
                held(latents.shape),
                held((1, width)),
                pl.BlockSpec((own, query_width), lambda i, w: (w[0], 0)),
                pl.BlockSpec((key_width, own), lambda i, w: (0, w[0])),
                pl.BlockSpec((key_width, own), lambda i, w: (0, w[0])),
                pl.BlockSpec(memory_space=pl.ANY),
            ],
            out_specs=[
                held((own, query_width)),
                held((2 * key_width, own)),
                held((latent_rows + 8, own + 128)),
                held((1, own // 2)),
                pl.BlockSpec(memory_space=pl.ANY),
            ],
            scratch_shapes=[
                pltpu.VMEM(sums.shape, F32),
                pltpu.VMEM(routed.shape, BF16),
                pltpu.SemaphoreType.DMA((2,)),
            ],
        ),
        out_shape=[
            jax.ShapeDtypeStruct((own, query_width), F32),
            jax.ShapeDtypeStruct((2 * key_width, own), F32),
            jax.ShapeDtypeStruct((latent_rows + 8, own + 128), F32),
            jax.ShapeDtypeStruct((1, own // 2), F32),
            jax.ShapeDtypeStruct(routed.shape, BF16),
        ],
        cost_estimate=pl.CostEstimate(
            flops=100_000_000, bytes_accessed=3_000_000, transcendentals=0
        ),
        compiler_params=pltpu.CompilerParams(vmem_limit_bytes=VMEM_LIMIT),
    )(where, sums, *parts, proj, latents, gain_lat.reshape(1, width), w_query, wk, wv, routed)


def plane_kernel(
    value_ref,
    value_got_ref,
    value_last_ref,
    key_ref,
    key_got_ref,
    key_last_ref,
    going_ref,
    high_ref,
):
    key_width = value_ref.shape[-2]
    for i, ref in enumerate((going_ref.at[0], going_ref.at[1], high_ref)):
        for j, parts in enumerate(
            (
                (key_ref, key_got_ref, key_last_ref),
                (value_ref, value_got_ref, value_last_ref),
            )
        ):
            total = sum(part[i].astype(F32) for part in parts)
            ref[j * key_width : (j + 1) * key_width, :] = total.astype(ref.dtype)


def plane_call(value, value_got, value_last, key, key_got, key_last):
    _, key_width, own = value.shape
    upper = pl.BlockSpec((4, key_width, own), lambda i: (1, 0, 0))
    last = pl.BlockSpec((4, key_width, own), lambda i: (0, 0, 0))
    shape = (2 * key_width, own)
    return pl.pallas_call(
        plane_kernel,
        name="plane_sum",
        grid=(1,),
        in_specs=[upper, upper, last] * 2,
        out_specs=[held((2, *shape)), held(shape)],
        out_shape=[
            jax.ShapeDtypeStruct((2, *shape), BF16),
            jax.ShapeDtypeStruct(shape, F32),
        ],
        cost_estimate=pl.CostEstimate(flops=1_000_000, bytes_accessed=3_000_000, transcendentals=0),
        compiler_params=pltpu.CompilerParams(vmem_limit_bytes=VMEM_LIMIT),
    )(value, value_got, value_last, key, key_got, key_last)


def final_kernel(
    where_ref,
    value_ref,
    value_got_ref,
    value_last_ref,
    key_ref,
    key_got_ref,
    key_last_ref,
    low_ref,
    high_ref,
    gain_ref,
    pair_ref,
    wk_ref,
    wv_ref,
    key_grad_ref,
    value_grad_ref,
    gain_term_ref,
):
    key_width = wk_ref.shape[0]
    term = jnp.zeros((1, wk_ref.shape[1]), F32)
    for j, (w_ref, out_ref, parts) in enumerate(
        (
            (wk_ref, key_grad_ref, (key_ref, key_got_ref, key_last_ref)),
            (wv_ref, value_grad_ref, (value_ref, value_got_ref, value_last_ref)),
        )
    ):
        at = slice(j * key_width, (j + 1) * key_width)
        total = sum(part[0].astype(F32) for part in parts)
        total = total + low_ref[0, at, :].astype(F32) + high_ref[at, :].astype(F32)
        term = term + jnp.sum(w_ref[...].astype(F32) * total, axis=0, keepdims=True)
        out_ref[...] = total * gain_ref[...] + pair_ref[at, :]
    gain_term_ref[...] = jnp.broadcast_to(term, gain_term_ref.shape)


def final_call(where, value, value_got, value_last, key, key_got, key_last, line, gain_ctx, pair, wk, wv):
    rows, own = pair.shape
    width = gain_ctx.shape[0]
    key_width = rows // 2
    w_spec = pl.BlockSpec((key_width, own), lambda i, w: (0, w[0]))
    end = pl.BlockSpec((1, key_width, own), lambda i, w: (7, 0, 0))
    last = pl.BlockSpec((1, key_width, own), lambda i, w: (3, 0, 0))
    return pl.pallas_call(
        final_kernel,
        name="key_value_gradients",
        grid_spec=pltpu.PrefetchScalarGridSpec(
            num_scalar_prefetch=1,
            grid=(1,),
            in_specs=[end, end, last] * 2
            + [pl.BlockSpec((1, rows, own), lambda i, w: (1, 0, 0)), held(pair.shape)]
            + [pl.BlockSpec((1, own), lambda i, w: (0, w[0])), held(pair.shape), w_spec, w_spec],
            out_specs=[held((key_width, own)), held((key_width, own)), held((8, own))],
        ),
        out_shape=[
            jax.ShapeDtypeStruct((key_width, own), F32),
            jax.ShapeDtypeStruct((key_width, own), F32),
            jax.ShapeDtypeStruct((8, own), F32),
        ],
        cost_estimate=pl.CostEstimate(flops=1_000_000, bytes_accessed=3_000_000, transcendentals=0),
        compiler_params=pltpu.CompilerParams(vmem_limit_bytes=VMEM_LIMIT),
    )(
        where,
        value,
        value_got,
        value_last,
        key,
        key_got,
        key_last,
        *line,
        gain_ctx.reshape(1, width),
        pair,
        wk,
        wv,
    )


def out_final_kernel(
    where_ref,
    first_kept_ref,
    first_got_ref,
    first_last_ref,
    second_kept_ref,
    second_got_ref,
    second_last_ref,
    message_ref,
    message_got_ref,
    term_ref,
    term_got_ref,
    lat_ref,
    gain_ref,
    out_ref,
    latent_ref,
    gain_lat_ref,
    gain_ctx_ref,
):
    heads, own = out_ref.shape
    latent_rows, width = lat_ref.shape
    share = own // 2
    cut = heads // 2
    first, second = (
        sum(part.astype(F32) for part in parts)
        for parts in (
            (first_kept_ref[0], first_got_ref[...], first_last_ref[...]),
            (second_kept_ref[0], second_got_ref[...], second_last_ref[...]),
        )
    )
    out_ref[:cut, :] = first[:cut]
    out_ref[cut:, :] = second[:cut]
    resid = jnp.concatenate([first[cut:], second[cut:]], axis=0)
    resid = jnp.concatenate([resid[:, :share], resid[:, share:]], axis=0)
    mine = pl.ds(pl.multiple_of(where_ref[1] * share, share), share)
    d_lat = message_ref[:, mine] + message_got_ref[:, mine]
    lat_dot = message_ref[:latent_rows, own : own + 1] + message_got_ref[:latent_rows, own : own + 1]
    lat = lat_ref[...].astype(F32)
    inverse = lax.rsqrt(jnp.mean(lat * lat, axis=-1, keepdims=True) + EPSILON)
    at = pl.ds(pl.multiple_of(where_ref[0] * own + where_ref[1] * share, share), share)
    hat = lat_ref[:, at].astype(F32) * inverse
    latent_ref[...] = resid + inverse * (gain_ref[:, at] * d_lat[:latent_rows] - hat * (lat_dot / width))
    gain_lat_ref[...] = d_lat[latent_rows : latent_rows + 1]
    gain_ctx_ref[...] = term_ref[:1, mine] + term_got_ref[:1, mine]


def out_final_call(where, parts, message, message_got, term, term_got, latents, gain_lat):
    _, rows, own = parts[0].shape
    latent_rows, width = latents.shape
    heads = 2 * (rows - latent_rows // 4)
    shapes = [(heads, own), (latent_rows, own // 2), (1, own // 2), (1, own // 2)]
    return pl.pallas_call(
        out_final_kernel,
        name="output_gradient_sum",
        grid_spec=pltpu.PrefetchScalarGridSpec(
            num_scalar_prefetch=1,
            grid=(1,),
            in_specs=[
                pl.BlockSpec((1, *part.shape[1:]), lambda i, w: (1, 0, 0))
                if part.ndim == 3
                else held(part.shape)
                for part in parts
            ]
            + [held(a.shape) for a in (message, message_got, term, term_got, latents)]
            + [held((1, width))],
            out_specs=[held(shape) for shape in shapes],
        ),
        out_shape=[jax.ShapeDtypeStruct(shape, F32) for shape in shapes],
        cost_estimate=pl.CostEstimate(flops=1_000_000, bytes_accessed=3_000_000, transcendentals=0),
        compiler_params=pltpu.CompilerParams(vmem_limit_bytes=VMEM_LIMIT),
    )(
        where,
        *parts,
        message,
        message_got,
        term,
        term_got,
        latents,
        gain_lat.reshape(1, width),
    )


def add_halves(left, right):
    return left.astype(F32) + right.astype(F32)


def local(
    context,
    counts,
    routes,
    w_query,
    w_key,
    w_value,
    w_out,
    latents,
    gain_ctx,
    gain_lat,
    gain_out,
    cotangent,
):
    dp_count = lax.axis_size("dp")
    mp_index = lax.axis_index("mp")
    dp_index = lax.axis_index("dp")
    patch_rows, width = context.shape
    half_width = width // 2
    own_width = width // dp_count
    latent_rows = latents.shape[0]
    slot_count = cotangent.shape[0] // dp_count
    slots = dp_count * slot_count
    query_width = w_query.shape[1]

    def swap(array, turn):
        return lax.ppermute(array, "dp", [(i, i ^ turn) for i in range(dp_count)])

    def exchange(array):
        blocks = array.reshape(dp_count, slot_count, half_width)
        return lax.all_to_all(blocks, "dp", split_axis=0, concat_axis=0, tiled=True).reshape(
            slots, half_width
        )

    wk = w_key.T
    wv = w_value.T
    turned_routes = routes.reshape(1, -1)
    where = jnp.stack([dp_index, mp_index])

    returned = exchange(cotangent)
    w_out_other = swap_cores(w_out)
    wk_other = swap_cores(wk)
    wv_other = swap_cores(wv)

    (attn_rows, k, v, inv_row, q, lat_k, lat_v, lat_proj, p, lat_p) = forward_call(
        context, counts, w_query, wk, wv, latents, gain_ctx, gain_lat
    )
    wk_other, wv_other, attn_rows = lax.optimization_barrier((wk_other, wv_other, attn_rows))
    attn_other = swap_cores(attn_rows)
    out_hat, out_inv, outgoing = branch_call(
        attn_rows,
        attn_other,
        w_out,
        w_out_other,
        latents,
        gain_out,
        turned_routes,
        slots,
        slot_count,
    )

    routed = exchange(outgoing)
    returned, out_inv = lax.optimization_barrier((returned, out_inv))
    returned_other = swap_cores(returned)
    backward = backward_call(
        counts,
        attn_rows,
        returned,
        returned_other,
        out_hat,
        out_inv,
        gain_out,
        turned_routes,
        w_out,
        (k, v, q, lat_k, lat_v, p, lat_p, inv_row),
        context,
        slot_count,
    )
    backward = lax.optimization_barrier(backward)
    (
        line_own,
        line_high,
        pair,
        message,
        lat_terms,
        value_going,
        value_kept,
        key_going,
        key_kept,
    ) = backward

    value_got = swap(value_going, 1)
    key_got = swap(key_going, 2)
    pair_other = swap_cores(pair)

    line_high, message, lat_terms, pair_other = lax.optimization_barrier(
        (line_high, message, lat_terms, pair_other)
    )
    lat_got = swap(lat_terms, 4)
    got_high = swap(line_high, 8)
    got_low = swap(message, 4)

    ctx_grad = patch_call(
        where, pair, pair_other, wk, wv, wk_other, wv_other, context, inv_row, gain_ctx
    )

    lat_got, ctx_grad = lax.optimization_barrier((lat_got, ctx_grad))
    lat_sum = add_halves(lat_terms, lat_got)
    lat_low = lat_sum.astype(BF16)
    value_got, key_got, ctx_grad, routed, lat_low = lax.optimization_barrier(
        (value_got, key_got, ctx_grad, routed, lat_low)
    )
    key_kept = key_kept.reshape((8,) + key_kept.shape[2:])
    key_got = key_got.reshape((8,) + key_got.shape[2:])
    value_going = add_halves(value_kept[:4], value_got[:4]).astype(BF16)
    key_going = add_halves(key_kept[:4], key_got[:4]).astype(BF16)
    value_last = swap(value_going, 2)
    key_last = swap(key_going, 1)

    got_low, got_high, value_going, key_going, lat_low = lax.optimization_barrier(
        (got_low, got_high, value_going, key_going, lat_low)
    )
    lat_got = swap(lat_low, 8)
    forwarded = swap(got_high[:, width // 4 :], 4)
    other_low = swap_cores(got_low)
    other_high = swap_cores(got_high)

    planes = plane_call(value_kept, value_got, value_last, key_kept, key_got, key_last)
    low = swap(planes[0], 4)
    (_, high), lat_got, forwarded = lax.optimization_barrier((planes, lat_got, forwarded))
    other_forwarded = swap_cores(forwarded)
    lat_sum = add_halves(lat_sum, lat_got).astype(BF16)
    lat_parts = (swap(lat_sum, 1), swap(lat_sum, 2), swap(lat_sum, 3))

    first_onward, first_end, first_kept, second_onward, second_end, second_kept = out_call(
        where,
        attn_rows,
        line_own,
        (got_low, got_high, forwarded),
        (other_low, other_high, other_forwarded),
    )
    low, first_onward, second_onward, first_end, second_end = lax.optimization_barrier(
        (low, first_onward, second_onward, first_end, second_end)
    )
    high = add_halves(high, low[0]).astype(BF16)
    high, lat_parts = lax.optimization_barrier((high, lat_parts))
    high = swap(high, 8)
    first_onward = swap(first_onward, 1)
    second_onward = swap(second_onward, 2)
    first_end = swap(first_end, 1)
    second_end = swap(second_end, 2)

    grad_w_query, pair_lat, message, grad_gain_out, routed = latent_call(
        where, lat_sum, lat_parts, lat_proj, latents, gain_lat, w_query, wk, wv, own_width, routed
    )
    first_onward, second_onward, first_end, second_end, message, pair_lat = (
        lax.optimization_barrier(
            (first_onward, second_onward, first_end, second_end, message, pair_lat)
        )
    )
    high, pair_lat = lax.optimization_barrier((high, pair_lat))
    first_last = swap(add_halves(first_kept[0], first_onward).astype(BF16), 2)
    second_last = swap(add_halves(second_kept[0], second_onward).astype(BF16), 1)
    message_got = swap_cores(message)

    grad_key, grad_value, gain_term = final_call(
        where,
        value_kept,
        value_got,
        value_last,
        key_kept,
        key_got,
        key_last,
        (low, high),
        gain_ctx,
        pair_lat,
        wk,
        wv,
    )
    gain_got = swap_cores(gain_term)
    first_last, second_last, gain_term = lax.optimization_barrier(
        (first_last, second_last, gain_term)
    )
    grad_w_out, grad_latents, grad_gain_lat, grad_gain_ctx = out_final_call(
        where,
        (first_kept, first_end, first_last, second_kept, second_end, second_last),
        message,
        message_got,
        gain_term,
        gain_got,
        latents,
        gain_lat,
    )
    return (
        routed,
        ctx_grad,
        grad_w_query,
        grad_key.T,
        grad_value.T,
        grad_w_out,
        grad_latents,
        grad_gain_ctx[0],
        grad_gain_lat[0],
        grad_gain_out[0],
    )


def local_general(
    context,
    counts,
    routes,
    w_query,
    w_key,
    w_value,
    w_out,
    latents,
    gain_ctx,
    gain_lat,
    gain_out,
    cotangent,
):
    dp_count = lax.axis_size("dp")
    mp_count = lax.axis_size("mp")
    mp_index = lax.axis_index("mp")
    dp_index = lax.axis_index("dp")
    bits = dp_count.bit_length() - 1
    gather_bits = [bits - 1, bits - 2]
    scatter_bits = list(range(bits - 2))
    order_one = list(range(bits))
    order_two = [1, 0] + order_one[2:]
    patch_rows, width = context.shape
    half_width = width // mp_count
    own_width = width // dp_count
    head_local = w_query.shape[1] // HD
    group_local = w_key.shape[1] // HD
    per_group = head_local // group_local
    latent_rows = latents.shape[0]
    image_slots = counts.shape[1]
    out_rows = image_slots * latent_rows
    slot_count = cotangent.shape[0] // dp_count
    key_width = w_key.shape[1]
    query_width = w_query.shape[1]
    scaling = HD ** (-0.5)

    returned = lax.all_to_all(
        cotangent.reshape(dp_count, slot_count, half_width),
        "dp",
        split_axis=0,
        concat_axis=0,
        tiled=True,
    ).reshape(dp_count * slot_count, half_width)
    returned_other = swap_cores(returned)
    w_out_other = swap_cores(w_out)
    w_pair = jnp.concatenate([w_key, w_value], axis=1)
    w_pair_half = lax.dynamic_slice_in_dim(w_pair, mp_index * half_width, half_width, 0)
    w_pair_other = swap_cores(
        lax.dynamic_slice_in_dim(w_pair, (1 - mp_index) * half_width, half_width, 0)
    )

    patch_hat, patch_inv = norm_parts(context.astype(F32))
    normed_ctx = (patch_hat * gain_ctx).astype(BF16)
    key_f32 = jnp.dot(normed_ctx, w_key, preferred_element_type=F32)
    value_f32 = jnp.dot(normed_ctx, w_value, preferred_element_type=F32)
    key_rows = key_f32.astype(BF16)
    value_rows = value_f32.astype(BF16)
    lat_float = latents.astype(F32)
    lat_hat, lat_inv = norm_parts(lat_float)
    normed_lat = (lat_hat * gain_lat).astype(BF16)
    lat_key_f32 = jnp.dot(normed_lat, w_key, preferred_element_type=F32)
    lat_value_f32 = jnp.dot(normed_lat, w_value, preferred_element_type=F32)
    lat_keys = lat_key_f32.astype(BF16)
    lat_values = lat_value_f32.astype(BF16)
    query_f32 = jnp.dot(normed_lat, w_query, preferred_element_type=F32) * scaling
    query_rows = query_f32.astype(BF16)
    query_heads = query_rows.reshape(latent_rows, group_local, per_group, HD)
    key_heads = key_rows.reshape(patch_rows, group_local, HD)
    value_heads = value_rows.reshape(patch_rows, group_local, HD)
    lat_key_heads = lat_keys.reshape(latent_rows, group_local, HD)
    lat_value_heads = lat_values.reshape(latent_rows, group_local, HD)
    scores = jnp.einsum(
        "rkgd,tkd->kgrt", query_heads, key_heads, preferred_element_type=jnp.float32
    )
    lat_scores = jnp.einsum(
        "rkgd,skd->kgrs", query_heads, lat_key_heads, preferred_element_type=jnp.float32
    )
    position = jnp.arange(patch_rows, dtype=jnp.int32)
    image_count = counts[0]
    image_start = jnp.cumsum(image_count) - image_count
    member = (position[None, :] >= image_start[:, None]) & (
        position[None, :] < (image_start + image_count)[:, None]
    )
    member_wide = member[:, None, None, None, :]
    masked = jnp.where(member_wide, scores[None], NEGATIVE)
    row_max = jnp.maximum(
        jnp.max(masked, axis=-1, keepdims=True), jnp.max(lat_scores, axis=-1, keepdims=True)[None]
    )
    exponent = jnp.where(member_wide, jnp.exp(masked - row_max), 0.0)
    lat_exponent = jnp.exp(lat_scores[None] - row_max)
    total = jnp.sum(exponent, axis=-1, keepdims=True) + jnp.sum(
        lat_exponent, axis=-1, keepdims=True
    )
    attention = exponent / total
    lat_attention = lat_exponent / total
    attention_low = attention.astype(BF16)
    lat_attention_low = lat_attention.astype(BF16)
    mixed = jnp.einsum(
        "ikgrt,tkd->irkgd", attention_low, value_heads, preferred_element_type=jnp.float32
    )
    mixed = mixed + jnp.einsum(
        "ikgrs,skd->irkgd", lat_attention_low, lat_value_heads, preferred_element_type=jnp.float32
    )
    attn_rows = mixed.reshape(out_rows, query_width).astype(BF16)
    attn_other = swap_cores(attn_rows)
    branch = jnp.dot(attn_rows, w_out, preferred_element_type=F32) + jnp.dot(
        attn_other, w_out_other, preferred_element_type=F32
    )
    resid = jnp.tile(lat_float, (image_slots, 1)) + branch
    out_hat, out_inv = norm_parts(resid)
    final_rows = (out_hat * gain_out).astype(BF16)
    shard_of = routes[:, 0]
    shard_hot = (shard_of[:, None] == jnp.arange(dp_count, dtype=jnp.int32)[None, :]).astype(
        jnp.int32
    )
    rank = jnp.sum((jnp.cumsum(shard_hot, axis=0) - shard_hot) * shard_hot, axis=1)
    place = shard_of * slot_count + rank
    scatter_table = (
        jnp.arange(dp_count * slot_count, dtype=jnp.int32)[:, None] == place[None, :]
    ).astype(BF16)
    final_half = lax.dynamic_slice_in_dim(final_rows, mp_index * half_width, half_width, 1)
    outgoing = jnp.dot(scatter_table, final_half, preferred_element_type=F32).astype(BF16)
    routed = lax.all_to_all(
        outgoing.reshape(dp_count, slot_count, half_width),
        "dp",
        split_axis=0,
        concat_axis=0,
        tiled=True,
    ).reshape(dp_count * slot_count, half_width)

    attn_line = attn_rows
    for bit in gather_bits:
        attn_line = jnp.concatenate([attn_line, swap_bit(attn_line, bit, dp_count)], axis=0)

    first = jnp.where(mp_index == 0, returned, returned_other)
    second = jnp.where(mp_index == 0, returned_other, returned)
    d_final = jnp.concatenate(
        [dot_general(scatter_table, first, 0, 0), dot_general(scatter_table, second, 0, 0)], axis=1
    )
    d_hat = d_final * gain_out
    d_resid = out_inv * (d_hat - out_hat * jnp.mean(d_hat * out_hat, axis=1, keepdims=True))
    gain_out_term = jnp.sum(d_final * out_hat, axis=0)
    d_branch = d_resid.astype(BF16)
    d_attn = dot_general(d_branch, w_out, 1, 1).astype(BF16)

    d_attn_heads = d_attn.reshape(image_slots, latent_rows, group_local, per_group, HD)
    d_probs = jnp.einsum(
        "irkgd,tkd->ikgrt", d_attn_heads, value_heads, preferred_element_type=jnp.float32
    )
    d_lat_probs = jnp.einsum(
        "irkgd,skd->ikgrs", d_attn_heads, lat_value_heads, preferred_element_type=jnp.float32
    )
    row_delta = jnp.sum(attention * d_probs, axis=-1, keepdims=True) + jnp.sum(
        lat_attention * d_lat_probs, axis=-1, keepdims=True
    )
    d_scores = jnp.sum(attention * (d_probs - row_delta), axis=0).astype(BF16)
    d_lat_scores = jnp.sum(lat_attention * (d_lat_probs - row_delta), axis=0).astype(BF16)
    d_query = jnp.einsum("kgrt,tkd->rkgd", d_scores, key_heads, preferred_element_type=jnp.float32)
    d_query = d_query + jnp.einsum(
        "kgrs,skd->rkgd", d_lat_scores, lat_key_heads, preferred_element_type=jnp.float32
    )
    d_query = d_query.reshape(latent_rows, query_width).astype(BF16)
    d_keys = jnp.einsum("kgrt,rkgd->tkd", d_scores, query_heads, preferred_element_type=jnp.float32)
    d_keys = d_keys.reshape(patch_rows, key_width).astype(BF16)
    d_values = jnp.einsum(
        "ikgrt,irkgd->tkd", attention_low, d_attn_heads, preferred_element_type=jnp.float32
    )
    d_values = d_values.reshape(patch_rows, key_width).astype(BF16)
    d_lat_keys = jnp.einsum(
        "kgrs,rkgd->skd", d_lat_scores, query_heads, preferred_element_type=jnp.float32
    )
    d_lat_keys = d_lat_keys.reshape(latent_rows, key_width).astype(BF16)
    d_lat_values = jnp.einsum(
        "ikgrs,irkgd->skd", lat_attention_low, d_attn_heads, preferred_element_type=jnp.float32
    )
    d_lat_values = d_lat_values.reshape(latent_rows, key_width).astype(BF16)
    d_pair = jnp.concatenate([d_keys, d_values], axis=1)

    value_grad = dot_general(d_values, normed_ctx, 0, 0).reshape(key_width, dp_count, own_width)
    key_grad = dot_general(d_keys, normed_ctx, 0, 0).reshape(key_width, dp_count, own_width)
    value_block = scatter_sum(value_grad, order_one, dp_count)
    key_block = scatter_sum(key_grad, order_two, dp_count)

    row_dot = jnp.sum(d_keys.astype(F32) * key_f32, axis=1) + jnp.sum(
        d_values.astype(F32) * value_f32, axis=1
    )
    row_dot = (row_dot + swap_cores(row_dot)) / width
    d_pair_other = swap_cores(d_pair)
    d_ctx_in = dot_general(d_pair, w_pair_half, 1, 1) + dot_general(
        d_pair_other, w_pair_other, 1, 1
    )
    gain_ctx_half = lax.dynamic_slice_in_dim(gain_ctx, mp_index * half_width, half_width, 0)
    hat_half = lax.dynamic_slice_in_dim(patch_hat, mp_index * half_width, half_width, 1)
    ctx_grad = (patch_inv * (d_ctx_in * gain_ctx_half - hat_half * row_dot[:, None])).astype(BF16)

    high = gain_out_term.astype(BF16)
    low = (gain_out_term - high.astype(F32)).astype(BF16)
    lat_sum = jnp.concatenate(
        [
            d_query,
            d_lat_keys,
            d_lat_values,
            high.reshape(latent_rows, width // latent_rows),
            low.reshape(latent_rows, width // latent_rows),
        ],
        axis=1,
    ).astype(F32)
    for bit in gather_bits + scatter_bits:
        lat_sum = lat_sum + swap_bit(lat_sum.astype(BF16), bit, dp_count).astype(F32)
    pair_sum = lat_sum[:, query_width : query_width + 2 * key_width]
    query_sum = lat_sum[:, :query_width]
    gains_at = query_width + 2 * key_width
    gain_step = width // latent_rows
    gain_out_full = (
        lat_sum[:, gains_at : gains_at + gain_step]
        + lat_sum[:, gains_at + gain_step : gains_at + 2 * gain_step]
    ).reshape(width)

    plane = dp_count // 4
    row_half = out_rows // mp_count
    d_block = lax.dynamic_slice_in_dim(d_branch, mp_index * row_half, row_half, 0)
    d_line = d_block.reshape(1, row_half, 2, 2, plane * own_width)
    for step, bit in enumerate(gather_bits):
        mine = (dp_index >> bit) & 1
        going = lax.dynamic_index_in_dim(d_line, 1 - mine, 2, keepdims=False)
        kept = lax.dynamic_index_in_dim(d_line, mine, 2, keepdims=False)
        d_line = jnp.concatenate([kept, swap_bit(going, bit, dp_count)], axis=0)
    d_line_other = swap_cores(d_line)
    d_line = jnp.concatenate(
        [
            jnp.where(mp_index == 0, d_line, d_line_other),
            jnp.where(mp_index == 0, d_line_other, d_line),
        ],
        axis=1,
    )
    out_part = dot_general(attn_line, d_line.reshape(4 * out_rows, plane * own_width), 0, 0)
    resid_part = jnp.sum(
        d_line.astype(F32).reshape(4 * image_slots, latent_rows, plane * own_width), axis=0
    )
    resid_part = lax.dynamic_index_in_dim(
        resid_part.reshape(2, latent_rows // 2, plane, mp_count, own_width // mp_count),
        mp_index,
        3,
        keepdims=False,
    )
    resid_part = jnp.transpose(resid_part, (1, 2, 0, 3)).reshape(
        latent_rows // 2, plane, own_width
    )
    out_part = jnp.concatenate([out_part.reshape(query_width, plane, own_width), resid_part], axis=0)
    cut = out_part.shape[0] // 2
    out_block = jnp.concatenate(
        [
            scatter_sum(out_part[:cut], scatter_bits, dp_count),
            scatter_sum(out_part[cut:], [1, 0] + scatter_bits[2:], dp_count),
        ],
        axis=0,
    )
    grad_w_out = out_block[:query_width]
    resid_sum = (
        out_block[query_width:]
        .reshape(latent_rows // 2, 2, own_width // mp_count)
        .transpose(1, 0, 2)
        .reshape(latent_rows, own_width // mp_count)
    )

    def own(array, axis):
        return lax.dynamic_slice_in_dim(array, dp_index * own_width, own_width, axis)

    lat_own = own(normed_lat, 1)
    pair_ctx = jnp.concatenate([key_block, value_block], axis=0).T
    query_grad = dot_general(lat_own, query_sum.astype(BF16), 0, 0) * scaling
    pair_lat = dot_general(lat_own, pair_sum.astype(BF16), 0, 0)
    pair_all = pair_ctx + pair_lat
    wq_own = own(w_query, 0)
    pair_own = own(w_pair, 0)
    gain_ctx_part = jnp.sum(pair_own.astype(F32) * pair_ctx, axis=1) / own(gain_ctx, 0)
    gain_lat_part = (
        jnp.sum(wq_own.astype(F32) * query_grad, axis=1)
        + jnp.sum(pair_own.astype(F32) * pair_lat, axis=1)
    ) / own(gain_lat, 0)
    d_lat_part = dot_general(
        (query_sum * scaling).astype(BF16), wq_own, 1, 1
    ) + dot_general(pair_sum.astype(BF16), pair_own, 1, 1)
    lat_dot_part = (
        jnp.sum(query_sum * query_f32, axis=1)
        + jnp.sum(pair_sum[:, :key_width] * lat_key_f32, axis=1)
        + jnp.sum(pair_sum[:, key_width:] * lat_value_f32, axis=1)
    )
    small = jnp.concatenate(
        [
            d_lat_part,
            jnp.broadcast_to(lat_dot_part[:, None], (latent_rows, own_width)),
            jnp.broadcast_to(gain_ctx_part[None, :], (8, own_width)),
            jnp.broadcast_to(gain_lat_part[None, :], (8, own_width)),
        ],
        axis=0,
    )
    small = small + swap_cores(small)
    share = own_width // mp_count
    small = lax.dynamic_slice_in_dim(small, mp_index * share, share, 1)
    d_lat_in = small[:latent_rows]
    lat_dot = small[latent_rows : 2 * latent_rows] / width

    def mine_of(array, axis):
        return lax.dynamic_slice_in_dim(
            array, dp_index * own_width + mp_index * share, share, axis
        )

    grad_latents = resid_sum + lat_inv * (
        mine_of(gain_lat, 0) * d_lat_in - mine_of(lat_hat, 1) * lat_dot
    )
    return (
        routed,
        ctx_grad,
        query_grad,
        pair_all[:, :key_width],
        pair_all[:, key_width:],
        grad_w_out,
        grad_latents,
        small[2 * latent_rows],
        small[2 * latent_rows + 8],
        mine_of(gain_out_full, 0),
    )


def solution(mesh):
    placed = (
        P("dp", None),
        P("dp", None),
        P("dp", None),
        P(None, "mp"),
        P(None, "mp"),
        P(None, "mp"),
        P("mp", None),
        P(),
        P(),
        P(),
        P(),
        P("dp", "mp"),
    )
    return jax.shard_map(
        local if mesh.shape["dp"] == 16 else local_general,
        mesh=mesh,
        in_specs=placed,
        out_specs=(
            P("dp", "mp"),
            P("dp", "mp"),
            P("dp", "mp"),
            P("dp", "mp"),
            P("dp", "mp"),
            P("mp", "dp"),
            P(None, ("dp", "mp")),
            P(("dp", "mp")),
            P(("dp", "mp")),
            P(("dp", "mp")),
        ),
        check_vma=False,
    )
```

```python
import functools

import jax
import jax.numpy as jnp
from jax import lax
from jax.experimental import pallas as pl
from jax.experimental.pallas import tpu as pltpu
from jax.sharding import PartitionSpec as P

HD = 96
EPSILON = 1e-06
NEGATIVE = -1e30
BF16 = jnp.bfloat16
F32 = jnp.float32
VMEM_LIMIT = 63 << 20


def dot_general(left, right, left_dim, right_dim):
    return lax.dot_general(
        left, right, (((left_dim,), (right_dim,)), ((), ())), preferred_element_type=F32
    )


def norm_parts(values_in):
    inverse = lax.rsqrt(jnp.mean(values_in * values_in, axis=-1, keepdims=True) + EPSILON)
    return (values_in * inverse, inverse)


def swap_cores(array):
    return lax.ppermute(array, "mp", [(0, 1), (1, 0)])


def swap_bit(array, bit, dp_count):
    return lax.ppermute(array, "dp", [(i, i ^ (1 << bit)) for i in range(dp_count)])


def halve(array, axis, bit, dp_count):
    mine = (lax.axis_index("dp") >> bit) & 1
    going = lax.dynamic_index_in_dim(array, 1 - mine, axis, keepdims=False)
    kept = lax.dynamic_index_in_dim(array, mine, axis, keepdims=False)
    return kept.astype(F32) + swap_bit(going.astype(BF16), bit, dp_count).astype(F32)


def scatter_sum(array, bits, dp_count):
    rows, owners, columns = array.shape
    left = sorted(bits, reverse=True)
    array = array.reshape((rows,) + (2,) * len(left) + (columns,))
    for bit in bits:
        axis = left.index(bit)
        array = halve(array, 1 + axis, bit, dp_count)
        left.pop(axis)
    return array


def forward_kernel(
    counts_ref,
    gain_ctx_hbm,
    gain_lat_hbm,
    lat_hbm,
    wk_hbm,
    wv_hbm,
    x_hbm,
    wq_hbm,
    attn_hbm,
    k_hbm,
    v_hbm,
    inv_row_hbm,
    q_hbm,
    lk_hbm,
    lv_hbm,
    lat_proj_hbm,
    p_hbm,
    pl_hbm,
    gain_ctx_ref,
    gain_lat_ref,
    lat_ref,
    wk_ref,
    wv_ref,
    x_ref,
    wq_ref,
    attn_ref,
    k_ref,
    v_ref,
    inv_row_ref,
    q_ref,
    lk_ref,
    lv_ref,
    lat_proj_ref,
    p_ref,
    pl_ref,
    lat_normed_ref,
    last_ref,
    gained_ref,
    sems,
    out_sems,
):
    patch_rows, width = x_ref.shape
    chunks = sems.shape[0] - 6
    rows = patch_rows // chunks
    groups = k_ref.shape[0]
    latent_rows = lat_ref.shape[0]
    key_width = wk_ref.shape[0]
    query_width = wq_ref.shape[1]
    per_group = query_width // key_width

    def fetch(source, target, i):
        return pltpu.make_async_copy(source, target, sems.at[i])

    def fetch_rows(i):
        at = pl.ds(i * rows, rows)
        return fetch(x_hbm.at[at], x_ref.at[at], i)

    weights = [
        fetch(source, target, chunks + i)
        for i, (source, target) in enumerate(
            ((lat_hbm, lat_ref), (wk_hbm, wk_ref), (wv_hbm, wv_ref), (wq_hbm, wq_ref))
        )
    ]
    gains = [
        fetch(gain_ctx_hbm, gain_ctx_ref, chunks + 4),
        fetch(gain_lat_hbm, gain_lat_ref, chunks + 5),
    ]
    for copy in (*gains, *weights[:3]):
        copy.start()
    blocks = [fetch_rows(i) for i in range(chunks)]
    for copy in blocks + weights[3:]:
        copy.start()
    results = {}
    for i, (name, source, target) in enumerate(
        (
            ("attn", attn_ref, attn_hbm),
            ("k", k_ref, k_hbm),
            ("v", v_ref, v_hbm),
            ("inv_row", inv_row_ref, inv_row_hbm),
            ("q", q_ref, q_hbm),
            ("lk", lk_ref, lk_hbm),
            ("lv", lv_ref, lv_hbm),
            ("lat_proj", lat_proj_ref, lat_proj_hbm),
            ("p0", p_ref.at[0], p_hbm.at[0]),
            ("p1", p_ref.at[1], p_hbm.at[1]),
            ("pl", pl_ref, pl_hbm),
        )
    ):
        results[name] = pltpu.make_async_copy(source, target, out_sems.at[i])

    for copy in (*gains, weights[0]):
        copy.wait()
    lat = lat_ref[...].astype(F32)
    lat_inverse = lax.rsqrt(jnp.mean(lat * lat, axis=-1, keepdims=True) + EPSILON)
    lat_normed = lat * lat_inverse * gain_lat_ref[...]
    lat_normed_ref[...] = lat_normed.astype(BF16)
    last_ref[rows:, :] = (lat_normed / gain_ctx_ref[...]).astype(BF16)
    for i, ref in enumerate((wk_ref, wv_ref)):
        weights[1 + i].wait()
        gained_ref[i * key_width : (i + 1) * key_width, :] = (
            ref[...].astype(F32) * gain_ctx_ref[...]
        ).astype(BF16)
    for i in range(chunks):
        blocks[i].wait()
        at = slice(i * rows, (i + 1) * rows)
        squares = jnp.zeros((rows, 128), F32)
        for c in range(width // 128):
            part = x_ref[at, c * 128 : (c + 1) * 128].astype(F32)
            squares = squares + part * part
        inverse = lax.rsqrt(jnp.sum(squares, axis=-1, keepdims=True) / width + EPSILON)
        if i < chunks - 1:
            pair = dot_general(x_ref[at, :], gained_ref[...], 1, 1)
        else:
            last_ref[:rows, :] = x_ref[at, :]
            pair = dot_general(last_ref[...], gained_ref[...], 1, 1)
            projected = pair[rows:]
        pair = (pair[:rows] * inverse).astype(BF16)
        inv_row_ref[:, at] = jnp.transpose(jnp.broadcast_to(inverse, (rows, 128)))[:8]
        for g in range(groups):
            k_ref[g, at, :HD] = pair[:, g * HD : (g + 1) * HD]
            v_ref[g, at, :HD] = pair[:, key_width + g * HD : key_width + (g + 1) * HD]
    lat_proj_ref[:, query_width:] = projected
    for i, ref in enumerate((lk_ref, lv_ref)):
        for g in range(groups):
            at = i * key_width + g * HD
            ref[g, :, :HD] = projected[:, at : at + HD].astype(BF16)
    for name in ("k", "v", "inv_row", "lk", "lv"):
        results[name].start()
    weights[3].wait()
    query = jnp.dot(lat_normed_ref[...], wq_ref[...], preferred_element_type=F32) * HD ** (-0.5)
    lat_proj_ref[:, :query_width] = query
    first_count = counts_ref[0, 0]
    both_count = first_count + counts_ref[0, 1]
    position = lax.broadcasted_iota(jnp.int32, (1, patch_rows), 1)
    in_first = position < first_count
    in_second = jnp.logical_and(position >= first_count, position < both_count)
    rows_at = lax.broadcasted_iota(jnp.int32, (patch_rows, HD), 0)
    row_first = rows_at < first_count
    row_second = jnp.logical_and(rows_at >= first_count, rows_at < both_count)
    for g in range(groups):
        for h in range(per_group):
            head = g * per_group + h
            q_ref[g, h * latent_rows : (h + 1) * latent_rows, :HD] = query[
                :, head * HD : (head + 1) * HD
            ].astype(BF16)
    results["lat_proj"].start()
    results["q"].start()
    for g in range(groups):
        q = q_ref[g, :, :HD]
        scores = dot_general(q, k_ref[g, :, :HD], 1, 1)
        lat_scores = dot_general(q, lk_ref[g, :, :HD], 1, 1)
        lat_max = jnp.max(lat_scores, axis=-1, keepdims=True)
        max_first = jnp.maximum(
            jnp.max(jnp.where(in_first, scores, NEGATIVE), axis=-1, keepdims=True), lat_max
        )
        max_second = jnp.maximum(
            jnp.max(jnp.where(in_second, scores, NEGATIVE), axis=-1, keepdims=True), lat_max
        )
        masked = jnp.where(
            in_first, scores - max_first, jnp.where(in_second, scores - max_second, NEGATIVE)
        )
        exponent = jnp.exp(masked)
        lat_first = jnp.exp(lat_scores - max_first)
        lat_second = jnp.exp(lat_scores - max_second)
        sum_first = jnp.sum(
            jnp.where(in_first, exponent, 0.0), axis=-1, keepdims=True
        ) + jnp.sum(lat_first, axis=-1, keepdims=True)
        sum_second = jnp.sum(
            jnp.where(in_second, exponent, 0.0), axis=-1, keepdims=True
        ) + jnp.sum(lat_second, axis=-1, keepdims=True)
        per_first = 1.0 / sum_first
        per_second = 1.0 / sum_second
        p = (exponent * jnp.where(in_first, per_first, per_second)).astype(BF16)
        p_ref[g] = p
        results[f"p{g}"].start()
        lat_p_first = (lat_first * per_first).astype(BF16)
        lat_p_second = (lat_second * per_second).astype(BF16)
        pl_ref[g, :, :latent_rows] = lat_p_first
        pl_ref[g, :, latent_rows:] = lat_p_second
        v = v_ref[g, :, :HD]
        zero = jnp.zeros_like(v)
        lv = lv_ref[g, :, :HD]
        for j, (row_mask, lat_p) in enumerate(
            ((row_first, lat_p_first), (row_second, lat_p_second))
        ):
            mixed = jnp.dot(
                p, jnp.where(row_mask, v, zero), preferred_element_type=F32
            ) + jnp.dot(lat_p, lv, preferred_element_type=F32)
            mixed = mixed.astype(BF16)
            for h in range(per_group):
                head = g * per_group + h
                attn_ref[
                    j * latent_rows : (j + 1) * latent_rows, head * HD : (head + 1) * HD
                ] = mixed[h * latent_rows : (h + 1) * latent_rows]
    for name in ("attn", "pl"):
        results[name].start()
    for copy in results.values():
        copy.wait()


def whole(shape):
    return pl.BlockSpec(shape, lambda *_: (0,) * len(shape))


def held(shape):
    return pl.BlockSpec(shape, lambda *_: (0,) * len(shape), pipeline_mode=pl.Buffered(1))


def forward_call(context, counts, w_query, w_key, w_value, latents, gain_ctx, gain_lat):
    patch_rows, width = context.shape
    chunks = 4
    key_width = w_key.shape[0]
    query_width = w_query.shape[1]
    groups = key_width // HD
    latent_rows = latents.shape[0]
    stacked = query_width // key_width * latent_rows
    large = (latents, w_key, w_value, context, w_query)
    out = [
        ((2 * latent_rows, query_width), BF16),
        ((groups, patch_rows, 128), BF16),
        ((groups, patch_rows, 128), BF16),
        ((8, patch_rows), F32),
        ((groups, stacked, 128), BF16),
        ((groups, latent_rows, 128), BF16),
        ((groups, latent_rows, 128), BF16),
        ((latent_rows, query_width + 2 * key_width), F32),
        ((groups, stacked, patch_rows), BF16),
        ((groups, stacked, 2 * latent_rows), BF16),
    ]
    return pl.pallas_call(
        forward_kernel,
        name="forward_attention",
        in_specs=[
            pl.BlockSpec(memory_space=pltpu.SMEM),
            pl.BlockSpec(memory_space=pl.ANY),
            pl.BlockSpec(memory_space=pl.ANY),
        ]
        + [pl.BlockSpec(memory_space=pl.ANY)] * len(large),
        out_specs=[pl.BlockSpec(memory_space=pl.ANY)] * len(out),
        out_shape=[jax.ShapeDtypeStruct(shape, dtype) for shape, dtype in out],
        scratch_shapes=[pltpu.VMEM((1, width), F32)] * 2
        + [pltpu.VMEM(a.shape, a.dtype) for a in large]
        + [pltpu.VMEM(shape, dtype) for shape, dtype in out]
        + [
            pltpu.VMEM((latent_rows, width), BF16),
            pltpu.VMEM((patch_rows // chunks + latent_rows, width), BF16),
            pltpu.VMEM((2 * key_width, width), BF16),
            pltpu.SemaphoreType.DMA((chunks + 6,)),
            pltpu.SemaphoreType.DMA((len(out) + 1,)),
        ],
        cost_estimate=pl.CostEstimate(
            flops=5_000_000_000, bytes_accessed=24_000_000, transcendentals=600_000
        ),
        compiler_params=pltpu.CompilerParams(vmem_limit_bytes=VMEM_LIMIT),
    )(counts, gain_ctx.reshape(1, width), gain_lat.reshape(1, width), *large)


def slots_of(routes_ref, slot_count, as_row):
    rows = routes_ref.shape[1]
    turned = jnp.broadcast_to(routes_ref[...].astype(F32), (rows, rows))
    shard = jnp.transpose(turned)
    down = lax.broadcasted_iota(jnp.int32, (rows, rows), 0)
    across = lax.broadcasted_iota(jnp.int32, (rows, rows), 1)
    same = shard == turned
    if as_row:
        rank = jnp.sum(jnp.where(same & (down < across), 1.0, 0.0), axis=0, keepdims=True)
        return (turned[:1] * slot_count + rank).astype(jnp.int32)
    rank = jnp.sum(jnp.where(same & (across < down), 1.0, 0.0), axis=1, keepdims=True)
    return (shard[:, :1] * slot_count + rank).astype(jnp.int32)


def branch_kernel(
    slot_count,
    own_hbm,
    other_hbm,
    lat_hbm,
    gain_hbm,
    routes_hbm,
    w_own_hbm,
    w_other_hbm,
    hat_hbm,
    inv_hbm,
    out_hbm,
    own_ref,
    other_ref,
    lat_ref,
    gain_ref,
    routes_ref,
    w_own_ref,
    w_other_ref,
    hat_ref,
    low_ref,
    inv_ref,
    out_ref,
    sems,
    out_sems,
    small_sems,
):
    rows, width = hat_ref.shape
    slots, half = out_ref.shape
    parts = sems.shape[1]
    size = width // parts
    small = [
        pltpu.make_async_copy(source, target, small_sems.at[i])
        for i, (source, target) in enumerate(
            (
                (routes_hbm, routes_ref),
                (own_hbm, own_ref),
                (other_hbm, other_ref),
                (lat_hbm, lat_ref),
                (gain_hbm, gain_ref),
            )
        )
    ]
    for copy in small:
        copy.start()
    copies = []
    for part in range(parts):
        at = pl.ds(part * size, size)
        for i, (source, target) in enumerate(
            ((w_own_hbm, w_own_ref), (w_other_hbm, w_other_ref))
        ):
            copies.append(
                pltpu.make_async_copy(source.at[:, at], target.at[:, at], sems.at[i, part])
            )
    for copy in copies:
        copy.start()
    small[0].wait()
    place = slots_of(routes_ref, slot_count, True)
    for copy in small[1:]:
        copy.wait()
    table = jnp.where(
        lax.broadcasted_iota(jnp.int32, (slots, rows), 0) == place, 1.0, 0.0
    ).astype(BF16)
    squares = jnp.zeros((rows, 128), F32)
    for part in range(parts):
        at = slice(part * size, (part + 1) * size)
        copies[2 * part].wait()
        copies[2 * part + 1].wait()
        lat = lat_ref[:, at].astype(F32)
        resid = (
            jnp.concatenate([lat, lat], axis=0)
            + jnp.dot(own_ref[...], w_own_ref[:, at], preferred_element_type=F32)
            + jnp.dot(other_ref[...], w_other_ref[:, at], preferred_element_type=F32)
        )
        hat_ref[:, at] = resid
        for c in range(size // 128):
            piece = resid[:, c * 128 : (c + 1) * 128]
            squares = squares + piece * piece
    inverse = lax.rsqrt(jnp.sum(squares, axis=-1, keepdims=True) / width + EPSILON)
    inv_ref[...] = inverse
    low_ref[...] = (hat_ref[...] * inverse).astype(BF16)
    results = [
        pltpu.make_async_copy(source, target, out_sems.at[i])
        for i, (source, target) in enumerate(
            ((low_ref, hat_hbm), (inv_ref, inv_hbm), (out_ref, out_hbm))
        )
    ]
    for copy in results[:2]:
        copy.start()
    at = pl.ds(pl.multiple_of(lax.axis_index("mp") * half, half), half)
    final = (hat_ref[:, at] * inverse * gain_ref[:, at]).astype(BF16)
    out_ref[...] = jnp.dot(table, final, preferred_element_type=F32).astype(BF16)
    results[2].start()
    for copy in results:
        copy.wait()


def branch_call(own, other, w_own, w_other, latents, gain_out, routes, slots, slot_count):
    width = w_own.shape[1]
    rows, heads = own.shape
    parts = 2
    return pl.pallas_call(
        functools.partial(branch_kernel, slot_count),
        name="branch_norm",
        **dict(
            in_specs=[pl.BlockSpec(memory_space=pl.ANY)] * 7,
            out_specs=[pl.BlockSpec(memory_space=pl.ANY)] * 3,
            scratch_shapes=[
                pltpu.VMEM((rows, heads), BF16),
                pltpu.VMEM((rows, heads), BF16),
                pltpu.VMEM(latents.shape, BF16),
                pltpu.VMEM((1, width), F32),
                pltpu.VMEM((1, rows), jnp.int32),
                pltpu.VMEM(w_own.shape, BF16),
                pltpu.VMEM(w_other.shape, BF16),
                pltpu.VMEM((rows, width), F32),
                pltpu.VMEM((rows, width), BF16),
                pltpu.VMEM((rows, 1), F32),
                pltpu.VMEM((slots, width // 2), BF16),
                pltpu.SemaphoreType.DMA((2, parts)),
                pltpu.SemaphoreType.DMA((3,)),
                pltpu.SemaphoreType.DMA((5,)),
            ],
        ),
        out_shape=[
            jax.ShapeDtypeStruct((rows, width), BF16),
            jax.ShapeDtypeStruct((rows, 1), F32),
            jax.ShapeDtypeStruct((slots, width // 2), BF16),
        ],
        cost_estimate=pl.CostEstimate(
            flops=2 * 2 * rows * heads * width, bytes_accessed=16_000_000, transcendentals=0
        ),
        compiler_params=pltpu.CompilerParams(vmem_limit_bytes=VMEM_LIMIT),
    )(own, other, latents, gain_out.reshape(1, width), routes, w_own, w_other)


def attention_backward(
    counts_ref,
    d_attn,
    k_ref,
    v_ref,
    q_ref,
    lk_ref,
    lv_ref,
    p_ref,
    pl_ref,
    inv_row_ref,
    pair_ref,
    scaled_ref,
    lat_ref,
):
    groups, patch_rows, _ = k_ref.shape
    latent_rows = lk_ref.shape[1]
    stacked = q_ref.shape[1]
    per_group = stacked // latent_rows
    key_width = groups * HD
    query_width = groups * per_group * HD
    first_count = counts_ref[0, 0]
    both_count = first_count + counts_ref[0, 1]
    position = lax.broadcasted_iota(jnp.int32, (1, patch_rows), 1)
    in_first = position < first_count
    rows_at = lax.broadcasted_iota(jnp.int32, (patch_rows, HD), 0)
    row_first = rows_at < first_count
    row_second = jnp.logical_and(rows_at >= first_count, rows_at < both_count)
    scale_row = inv_row_ref[:1]
    row_dot = jnp.zeros((1, patch_rows), F32)
    for g in range(groups):
        d_first = jnp.concatenate(
            [
                d_attn[:latent_rows, head * HD : (head + 1) * HD]
                for head in range(g * per_group, (g + 1) * per_group)
            ],
            axis=0,
        )
        d_second = jnp.concatenate(
            [
                d_attn[latent_rows:, head * HD : (head + 1) * HD]
                for head in range(g * per_group, (g + 1) * per_group)
            ],
            axis=0,
        )
        q = q_ref[g, :, :HD]
        k = k_ref[g, :, :HD]
        v = v_ref[g, :, :HD]
        lk = lk_ref[g, :, :HD]
        lv = lv_ref[g, :, :HD]
        p_low = p_ref[g]
        p = p_low.astype(F32)
        zero = jnp.zeros_like(v)
        d_p = dot_general(d_first, jnp.where(row_first, v, zero), 1, 1) + dot_general(
            d_second, jnp.where(row_second, v, zero), 1, 1
        )
        product = p * d_p
        lat_first = pl_ref[g, :, :latent_rows]
        lat_second = pl_ref[g, :, latent_rows:]
        d_lat_first = dot_general(d_first, lv, 1, 1)
        d_lat_second = dot_general(d_second, lv, 1, 1)
        lat_product_first = lat_first.astype(F32) * d_lat_first
        lat_product_second = lat_second.astype(F32) * d_lat_second
        whole_sum = jnp.sum(product, axis=-1, keepdims=True)
        first_sum = jnp.sum(jnp.where(in_first, product, 0.0), axis=-1, keepdims=True)
        delta_first = first_sum + jnp.sum(lat_product_first, axis=-1, keepdims=True)
        delta_second = (whole_sum - first_sum) + jnp.sum(
            lat_product_second, axis=-1, keepdims=True
        )
        ds = product - p * jnp.where(in_first, delta_first, delta_second)
        ds_low = ds.astype(BF16)
        dsl = (
            lat_product_first
            - lat_first.astype(F32) * delta_first
            + lat_product_second
            - lat_second.astype(F32) * delta_second
        ).astype(BF16)
        scores = dot_general(q, k, 1, 1)
        row_dot = row_dot + jnp.sum(ds * scores + product, axis=0, keepdims=True)
        d_q = (
            jnp.dot(ds_low, k, preferred_element_type=F32)
            + jnp.dot(dsl, lk, preferred_element_type=F32)
        ).astype(BF16)
        for h in range(per_group):
            head = g * per_group + h
            lat_ref[:latent_rows, head * HD : (head + 1) * HD] = d_q[
                h * latent_rows : (h + 1) * latent_rows
            ]
        d_k = dot_general(q, ds_low, 0, 0)
        nothing = jnp.zeros_like(p_low)
        d_v = dot_general(d_first, jnp.where(in_first, p_low, nothing), 0, 0) + dot_general(
            d_second, jnp.where(in_first, nothing, p_low), 0, 0
        )
        k_at = slice(g * HD, (g + 1) * HD)
        v_at = slice(key_width + g * HD, key_width + (g + 1) * HD)
        pair_ref[k_at, :] = d_k.astype(BF16)
        pair_ref[v_at, :] = d_v.astype(BF16)
        scaled_ref[k_at, :] = (d_k * scale_row).astype(BF16)
        scaled_ref[v_at, :] = (d_v * scale_row).astype(BF16)
        d_lk = dot_general(dsl, q, 0, 0)
        d_lv = dot_general(lat_first, d_first, 0, 0) + dot_general(lat_second, d_second, 0, 0)
        lat_ref[:latent_rows, query_width + g * HD : query_width + (g + 1) * HD] = d_lk.astype(BF16)
        at = query_width + key_width + g * HD
        lat_ref[:latent_rows, at : at + HD] = d_lv.astype(BF16)
    high = row_dot.astype(BF16)
    low = (row_dot - high.astype(F32)).astype(BF16)
    rest = pair_ref.shape[0] - 2 * key_width - 2
    pair_ref[2 * key_width :, :] = jnp.concatenate(
        [high.astype(F32), low.astype(F32), jnp.zeros((rest, patch_rows), F32)], axis=0
    ).astype(BF16)


def backward_kernel(
    slot_count,
    counts_ref,
    inv_out_hbm,
    gain_hbm,
    routes_hbm,
    inv_row_hbm,
    attn_hbm,
    got_own_hbm,
    got_other_hbm,
    hat_hbm,
    w_out_hbm,
    k_hbm,
    v_hbm,
    q_hbm,
    lk_hbm,
    lv_hbm,
    p_hbm,
    pl_hbm,
    x_hbm,
    line_own_hbm,
    line_high_hbm,
    pair_hbm,
    message_hbm,
    lat_hbm,
    value_going_hbm,
    value_kept_hbm,
    key_going_hbm,
    key_kept_hbm,
    inv_out_ref,
    gain_ref,
    routes_ref,
    inv_row_ref,
    attn_ref,
    got_own_ref,
    got_other_ref,
    hat_ref,
    w_out_ref,
    k_ref,
    v_ref,
    q_ref,
    lk_ref,
    lv_ref,
    p_ref,
    pl_ref,
    x_ref,
    d_final_ref,
    branch_ref,
    scaled_ref,
    line_own_ref,
    line_high_ref,
    pair_ref,
    message_ref,
    lat_ref,
    value_ref,
    key_ref,
    sems,
    out_sems,
    value_sems,
    key_sems,
    small_sems,
):
    small = [
        pltpu.make_async_copy(source, target, small_sems.at[i])
        for i, (source, target) in enumerate(
            (
                (routes_hbm, routes_ref),
                (inv_out_hbm, inv_out_ref),
                (gain_hbm, gain_ref),
                (inv_row_hbm, inv_row_ref),
                (attn_hbm, attn_ref),
            )
        )
    ]
    for copy in small:
        copy.start()
    sources = (
        got_own_hbm,
        got_other_hbm,
        hat_hbm,
        w_out_hbm,
        k_hbm,
        v_hbm,
        q_hbm,
        lk_hbm,
        lv_hbm,
        p_hbm,
        pl_hbm,
        x_hbm,
    )
    targets = (
        got_own_ref,
        got_other_ref,
        hat_ref,
        w_out_ref,
        k_ref,
        v_ref,
        q_ref,
        lk_ref,
        lv_ref,
        p_ref,
        pl_ref,
        x_ref,
    )
    copies = [
        pltpu.make_async_copy(source, target, sems.at[i])
        for i, (source, target) in enumerate(zip(sources, targets))
    ]
    for copy in copies[:4]:
        copy.start()
    me, core = lax.axis_index("dp"), lax.axis_index("mp")
    rows, width = hat_ref.shape
    half = width // 2
    slots = got_own_ref.shape[0]
    latent_rows = lk_ref.shape[1]
    key_width, own = value_ref.shape[2:]

    small[0].wait()
    place = slots_of(routes_ref, slot_count, False)
    for copy in small[1:]:
        copy.wait()
    table = jnp.where(
        lax.broadcasted_iota(jnp.int32, (rows, slots), 1) == place, 1.0, 0.0
    ).astype(BF16)
    total = jnp.zeros((rows, 1), F32)
    chunk = 1024
    for copy in copies[:3]:
        copy.wait()
    for copy in copies[4:]:
        copy.start()
    for got_ref, which in ((got_own_ref, core), (got_other_ref, 1 - core)):
        for c in range(half // chunk):
            at = pl.ds(pl.multiple_of(which * half + c * chunk, chunk), chunk)
            d_final = jnp.dot(
                table, got_ref[:, c * chunk : (c + 1) * chunk], preferred_element_type=F32
            )
            product = d_final * hat_ref[:, at].astype(F32)
            total = total + jnp.sum(product * gain_ref[:, at], axis=-1, keepdims=True)
            d_final_ref[:, at] = d_final.astype(BF16)
    total = total / width
    lat_ref[latent_rows:, :] = jnp.zeros_like(lat_ref[latent_rows:, :])
    highs, lows = [], []
    part = width // 4
    for c in range(width // chunk):
        at = slice(c * chunk, (c + 1) * chunk)
        d_final = d_final_ref[:, at].astype(F32)
        hat = hat_ref[:, at].astype(F32)
        term = jnp.sum(d_final * hat, axis=0, keepdims=True)
        high = term.astype(BF16).astype(F32)
        highs.append(high)
        lows.append(term - high)
        branch_ref[:, at] = (
            inv_out_ref[...] * (d_final * gain_ref[:, at] - hat * total)
        ).astype(BF16)
    per_row = part // chunk
    lines = [
        jnp.concatenate(group[i * per_row : (i + 1) * per_row], axis=1)
        for group in (highs, lows)
        for i in range(4)
    ]
    lat_ref[latent_rows : latent_rows + 16, :part] = jnp.concatenate(
        lines + [jnp.zeros((8, part), F32)], axis=0
    ).astype(BF16)
    z = me >> 2
    some = pl.ds(pl.multiple_of(core * (rows // 2), rows // 2), rows // 2)
    line_own_ref[...] = branch_ref[:, pl.ds(pl.multiple_of(z * part, part), part)]
    heads = attn_ref.shape[1]
    for turn, ref, first in (
        (1, message_ref, 0),
        (2, line_high_ref, 0),
        (3, line_high_ref, part + 2 * heads),
    ):
        ref[: rows // 2, first : first + part] = branch_ref[
            some, pl.ds(pl.multiple_of((z ^ turn) * part, part), part)
        ]
    for ref in (message_ref, line_high_ref):
        ref[: rows // 2, part : part + heads] = attn_ref[: rows // 2, :]
        ref[: rows // 2, part + heads : part + 2 * heads] = attn_ref[rows // 2 :, :]
    results = [
        pltpu.make_async_copy(source, target, out_sems.at[i])
        for i, (source, target) in enumerate(
            (
                (line_high_ref, line_high_hbm),
                (message_ref, message_hbm),
                (line_own_ref, line_own_hbm),
                (pair_ref, pair_hbm),
                (lat_ref, lat_hbm),
            )
        )
    ]
    for copy in results[:3]:
        copy.start()

    copies[3].wait()
    d_attn = dot_general(branch_ref[...], w_out_ref[...], 1, 1).astype(BF16)
    for copy in copies[4:11]:
        copy.wait()
    attention_backward(
        counts_ref,
        d_attn,
        k_ref,
        v_ref,
        q_ref,
        lk_ref,
        lv_ref,
        p_ref,
        pl_ref,
        inv_row_ref,
        pair_ref,
        scaled_ref,
        lat_ref,
    )
    for copy in results[3:]:
        copy.start()
    copies[11].wait()

    odd = me & 1
    for j in range(8):
        y = ((me >> 1) & 1) ^ (1 - (j >> 2))
        z = (me >> 2) ^ ((1 - ((j >> 1) & 1)) + 2 * (1 - (j & 1)))
        first = 4 * z + 2 * y
        line = j & 3
        key_hbm = key_kept_hbm if j >> 2 else key_going_hbm
        grad = jnp.dot(
            scaled_ref[...],
            x_ref[:, pl.ds(pl.multiple_of(first * own, 2 * own), 2 * own)],
            preferred_element_type=F32,
        ).astype(BF16)
        for x_same, value_hbm in enumerate((value_going_hbm, value_kept_hbm)):
            block = jnp.where(odd == x_same, grad[:, own:], grad[:, :own])
            value_ref[x_same, j] = block[key_width:]
            key_ref[x_same, j] = block[:key_width]
            for copy in (
                pltpu.make_async_copy(
                    value_ref.at[x_same, j], value_hbm.at[j], value_sems.at[x_same, j]
                ),
                pltpu.make_async_copy(
                    key_ref.at[x_same, j], key_hbm.at[x_same, line], key_sems.at[x_same, j]
                ),
            ):
                copy.start()
                results.append(copy)
    for copy in results:
        copy.wait()


def backward_call(
    counts, attn, got_own, got_other, hat, inv_out, gain_out, routes, w_out, kept, context, slot_count
):
    k, v, q, lk, lv, p, lat_p, inv_row = kept
    rows, width = hat.shape
    patch_rows = context.shape[0]
    heads = w_out.shape[0]
    key_width = k.shape[0] * HD
    latent_rows = lk.shape[1]
    own = width // 16
    large = (got_own, got_other, hat, w_out, k, v, q, lk, lv, p, lat_p, context)
    small = (inv_out, gain_out.reshape(1, width), routes, inv_row, attn)
    out = [
        (rows, width // 4),
        (rows // 2, width // 2 + 2 * heads),
        (2 * key_width + 16, patch_rows),
        (rows // 2, width // 4 + 2 * heads),
        (latent_rows + 16, heads + 2 * key_width),
        (8, key_width, own),
        (8, key_width, own),
        (2, 4, key_width, own),
        (2, 4, key_width, own),
    ]
    return pl.pallas_call(
        functools.partial(backward_kernel, slot_count),
        name="attention_backward",
        **dict(
            in_specs=[
                pl.BlockSpec(memory_space=pltpu.SMEM),
            ]
            + [pl.BlockSpec(memory_space=pl.ANY)] * (5 + len(large)),
            out_specs=[pl.BlockSpec(memory_space=pl.ANY)] * len(out),
            scratch_shapes=[pltpu.VMEM(a.shape, a.dtype) for a in (*small, *large)]
            + [
                pltpu.VMEM((rows, width), BF16),
                pltpu.VMEM((rows, width), BF16),
                pltpu.VMEM((2 * key_width, patch_rows), BF16),
            ]
            + [pltpu.VMEM(shape, BF16) for shape in out[:5]]
            + [
                pltpu.VMEM((2, 8, key_width, own), BF16),
                pltpu.VMEM((2, 8, key_width, own), BF16),
                pltpu.SemaphoreType.DMA((len(large),)),
                pltpu.SemaphoreType.DMA((5,)),
                pltpu.SemaphoreType.DMA((2, 8)),
                pltpu.SemaphoreType.DMA((2, 8)),
                pltpu.SemaphoreType.DMA((5,)),
            ],
        ),
        out_shape=[jax.ShapeDtypeStruct(shape, BF16) for shape in out],
        cost_estimate=pl.CostEstimate(
            flops=5_000_000_000, bytes_accessed=26_000_000, transcendentals=0
        ),
        compiler_params=pltpu.CompilerParams(vmem_limit_bytes=VMEM_LIMIT),
    )(counts, *small, *large)


def patch_kernel(
    width,
    where_ref,
    own_ref,
    other_ref,
    wk_ref,
    wv_ref,
    wk_other_ref,
    wv_other_ref,
    x_ref,
    inv_row_ref,
    gain_ref,
    out_ref,
    turned_ref,
    inv_ref,
    dot_ref,
    w_ref,
):
    step = pl.program_id(0)
    key_width = wk_ref.shape[0]
    patch_rows = turned_ref.shape[0]
    pair = 2 * key_width

    @pl.when(step == 0)
    def _():
        row_dot = jnp.zeros((patch_rows, 1), F32)
        for i, ref in enumerate((own_ref, other_ref)):
            turned = jnp.transpose(ref[...])
            turned_ref[:, i * pair : (i + 1) * pair] = turned[:, :pair]
            row_dot = row_dot + turned[:, pair : pair + 1].astype(F32)
            row_dot = row_dot + turned[:, pair + 1 : pair + 2].astype(F32)
        inverse = jnp.transpose(jnp.broadcast_to(inv_row_ref[:1], (128, patch_rows)))[:, :1]
        inv_ref[...] = inverse
        dot_ref[...] = row_dot * (inverse * inverse / width)
        for i, ref in enumerate((wk_ref, wv_ref, wk_other_ref, wv_other_ref)):
            w_ref[i * key_width : (i + 1) * key_width, :] = ref[...]

    rows = x_ref.shape[0]
    at = pl.ds(pl.multiple_of(step * rows, rows), rows)
    d_in = jnp.dot(turned_ref[at, :], w_ref[...], preferred_element_type=F32)
    out_ref[...] = (
        d_in * gain_ref[...] * inv_ref[at, :] - x_ref[...].astype(F32) * dot_ref[at, :]
    ).astype(BF16)


def patch_call(where, own, other, wk, wv, wk_other, wv_other, context, inv_row, gain_ctx):
    patch_rows, width = context.shape
    half = width // 2
    steps = 4
    rows = patch_rows // steps
    key_width = wk.shape[0]
    once = pl.Buffered(1)
    w_spec = pl.BlockSpec((key_width, half), lambda i, w: (0, w[1]), pipeline_mode=once)
    return pl.pallas_call(
        functools.partial(patch_kernel, width),
        name="patch_gradient",
        grid_spec=pltpu.PrefetchScalarGridSpec(
            num_scalar_prefetch=1,
            grid=(steps,),
            in_specs=[
                held(own.shape),
                held(other.shape),
                w_spec,
                w_spec,
                w_spec,
                w_spec,
                pl.BlockSpec((rows, half), lambda i, w: (i, w[1])),
                held(inv_row.shape),
                pl.BlockSpec((1, half), lambda i, w: (0, w[1])),
            ],
            out_specs=pl.BlockSpec((rows, half), lambda i, w: (i, 0)),
            scratch_shapes=[
                pltpu.VMEM((patch_rows, 4 * key_width), BF16),
                pltpu.VMEM((patch_rows, 1), F32),
                pltpu.VMEM((patch_rows, 1), F32),
                pltpu.VMEM((4 * key_width, half), BF16),
            ],
        ),
        out_shape=jax.ShapeDtypeStruct((patch_rows, half), BF16),
        cost_estimate=pl.CostEstimate(
            flops=3_300_000_000, bytes_accessed=14_000_000, transcendentals=0
        ),
        compiler_params=pltpu.CompilerParams(vmem_limit_bytes=VMEM_LIMIT),
    )(where, own, other, wk, wv, wk_other, wv_other, context, inv_row, gain_ctx.reshape(1, width))


def out_kernel(
    where_ref,
    attn_own_ref,
    line_own_ref,
    low_ref,
    high_ref,
    forwarded_ref,
    other_low_ref,
    other_high_ref,
    other_forwarded_ref,
    first_onward_ref,
    first_last_ref,
    first_kept_ref,
    second_onward_ref,
    second_last_ref,
    second_kept_ref,
    attn_ref,
    line_ref,
    resid_ref,
):
    rows, heads = attn_own_ref.shape
    columns = line_ref.shape[1]
    own = columns // 4
    latent_rows = rows // 2
    mine = where_ref[1]
    half = rows // 2
    attn_ref[:rows, :] = attn_own_ref[...]
    line_ref[:rows, :] = line_own_ref[...]
    for i, (ref, other, first, attn_at) in enumerate(
        (
            (low_ref, other_low_ref, 0, columns),
            (high_ref, other_high_ref, 0, columns),
            (forwarded_ref, other_forwarded_ref, 2 * heads, 0),
        )
    ):
        at = (i + 1) * rows
        attn_ref[at : at + half, :] = ref[:half, attn_at : attn_at + heads]
        attn_ref[at + half : at + rows, :] = ref[:half, attn_at + heads : attn_at + 2 * heads]
        for holder, which in ((ref, mine), (other, 1 - mine)):
            line_ref[pl.ds(pl.multiple_of(at + which * half, half), half), :] = holder[
                :half, first : first + columns
            ]
    resid = jnp.zeros((latent_rows, columns), F32)
    for i in range(8):
        resid = resid + line_ref[i * latent_rows : (i + 1) * latent_rows, :].astype(F32)
    resid_ref[...] = resid
    odd = where_ref[0] & 1
    upper = (where_ref[0] >> 1) & 1
    share = own // 2
    cut = heads // 2
    extra = latent_rows // 4
    for turn in range(4):
        x_differs, y_differs = 1 - (turn & 1), 1 - (turn >> 1)
        owner = 2 * (upper ^ y_differs) + (odd ^ x_differs)
        at = pl.ds(pl.multiple_of(owner * own, own), own)
        grad = dot_general(attn_ref[...], line_ref[:, at], 0, 0).astype(BF16)
        mine_at = pl.ds(pl.multiple_of(owner * own + mine * share, share), share)
        part = resid_ref[:, mine_at]
        part = jnp.concatenate([part[: latent_rows // 2], part[latent_rows // 2 :]], axis=1)
        ends = 1 - y_differs
        ref = (first_onward_ref, first_last_ref)[ends] if x_differs else first_kept_ref.at[ends]
        ref[:cut, :] = grad[:cut]
        ref[cut:, :] = part[:extra].astype(BF16)
        ends = 1 - x_differs
        ref = (second_onward_ref, second_last_ref)[ends] if y_differs else second_kept_ref.at[ends]
        ref[:cut, :] = grad[cut:]
        ref[cut:, :] = part[extra:].astype(BF16)


def out_call(where, attn, line, received, others):
    rows, heads = attn.shape
    columns = line.shape[1]
    own = columns // 4
    block = (heads // 2 + rows // 8, own)
    shapes = [block, block, (2, *block)] * 2
    operands = (attn, line, *received, *others)
    return pl.pallas_call(
        out_kernel,
        name="output_projection_gradient",
        grid_spec=pltpu.PrefetchScalarGridSpec(
            num_scalar_prefetch=1,
            grid=(1,),
            in_specs=[held(a.shape) for a in operands],
            out_specs=[held(shape) for shape in shapes],
            scratch_shapes=[
                pltpu.VMEM((4 * rows, heads), BF16),
                pltpu.VMEM((4 * rows, columns), BF16),
                pltpu.VMEM((rows // 2, columns), F32),
            ],
        ),
        out_shape=[jax.ShapeDtypeStruct(shape, BF16) for shape in shapes],
        cost_estimate=pl.CostEstimate(
            flops=8 * rows * heads * columns, bytes_accessed=4_000_000, transcendentals=0
        ),
        compiler_params=pltpu.CompilerParams(vmem_limit_bytes=VMEM_LIMIT),
    )(where, *operands)


def latent_kernel(
    where_ref,
    sum_ref,
    across_ref,
    along_ref,
    corner_ref,
    proj_ref,
    lat_ref,
    gain_ref,
    wq_ref,
    wk_ref,
    wv_ref,
    routed_hbm,
    query_ref,
    pair_ref,
    message_ref,
    gain_out_ref,
    terms_ref,
    routed_out_hbm,
    total_ref,
    routed_ref,
    sems,
):
    arrive = pltpu.make_async_copy(routed_hbm, routed_ref, sems.at[0])
    leave = pltpu.make_async_copy(routed_ref, routed_out_hbm, sems.at[1])
    arrive.start()
    latent_rows, width = lat_ref.shape
    own, query_width = wq_ref.shape
    key_width = wk_ref.shape[0]
    scaling = HD ** (-0.5)
    total_ref[...] = sum(
        ref[...].astype(F32) for ref in (sum_ref, across_ref, along_ref, corner_ref)
    )
    total = total_ref[:latent_rows, :]
    low = total.astype(BF16)
    at = pl.ds(pl.multiple_of(where_ref[0] * own, own), own)
    lat = lat_ref[...].astype(F32)
    inverse = lax.rsqrt(jnp.mean(lat * lat, axis=-1, keepdims=True) + EPSILON)
    gain = gain_ref[:, at]
    normed = (lat_ref[:, at].astype(F32) * inverse * gain).astype(BF16)
    query = dot_general(normed, low[:, :query_width], 0, 0) * scaling
    query_ref[...] = query
    pair = dot_general(low[:, query_width:], normed, 0, 0)
    pair_ref[...] = pair
    wq = wq_ref[...]
    wk = wk_ref[...]
    wv = wv_ref[...]
    gain_term = jnp.transpose(
        jnp.broadcast_to(jnp.sum(wq.astype(F32) * query, axis=1, keepdims=True), (own, 128))
    )[:1]
    gain_term = gain_term + jnp.sum(wk.astype(F32) * pair[:key_width], axis=0, keepdims=True)
    gain_term = gain_term + jnp.sum(wv.astype(F32) * pair[key_width:], axis=0, keepdims=True)
    arrive.wait()
    leave.start()
    share = own // 2
    own_at = pl.ds(
        pl.multiple_of(where_ref[0] * own + where_ref[1] * share, share), share
    )
    terms_ref[:latent_rows, :] = inverse * gain_ref[:, own_at]
    terms_ref[latent_rows:, :] = (
        inverse * inverse / width * lat_ref[:, own_at].astype(F32)
    )
    scaled = (total[:, :query_width] * scaling).astype(BF16)
    d_lat = dot_general(scaled, wq, 1, 1)
    d_lat = d_lat + jnp.dot(
        low[:, query_width : query_width + key_width], wk, preferred_element_type=F32
    )
    d_lat = d_lat + jnp.dot(low[:, query_width + key_width :], wv, preferred_element_type=F32)
    message_ref[:latent_rows, :own] = d_lat
    message_ref[:latent_rows, own:] = jnp.broadcast_to(
        jnp.sum(total * proj_ref[...], axis=-1, keepdims=True), (latent_rows, 128)
    )
    message_ref[latent_rows:, :own] = jnp.broadcast_to(gain_term / gain, (8, own))
    message_ref[latent_rows:, own:] = jnp.zeros((8, 128), F32)
    part = width // 4
    share = own // 2
    first = where_ref[0] * own + where_ref[1] * share
    line = first // part
    mine = pl.ds(pl.multiple_of(first % part, share), share)
    gain_out_ref[...] = jnp.sum(
        jnp.where(
            lax.broadcasted_iota(jnp.int32, (8, share), 0) % 4 == line,
            total_ref[latent_rows : latent_rows + 8, mine],
            0.0,
        ),
        axis=0,
        keepdims=True,
    )
    leave.wait()


def latent_call(where, sums, parts, proj, latents, gain_lat, w_query, wk, wv, own, routed):
    latent_rows, width = latents.shape
    query_width = w_query.shape[1]
    key_width = wk.shape[0]
    return pl.pallas_call(
        latent_kernel,
        name="latent_gradients",
        grid_spec=pltpu.PrefetchScalarGridSpec(
            num_scalar_prefetch=1,
            grid=(1,),
            in_specs=[
                held(sums.shape),
                *(held(part.shape) for part in parts),
                held(proj.shape),
                held(latents.shape),
                held((1, width)),
                pl.BlockSpec((own, query_width), lambda i, w: (w[0], 0)),
                pl.BlockSpec((key_width, own), lambda i, w: (0, w[0])),
                pl.BlockSpec((key_width, own), lambda i, w: (0, w[0])),
                pl.BlockSpec(memory_space=pl.ANY),
            ],
            out_specs=[
                held((own, query_width)),
                held((2 * key_width, own)),
                held((latent_rows + 8, own + 128)),
                held((1, own // 2)),
                held((2 * latent_rows, own // 2)),
                pl.BlockSpec(memory_space=pl.ANY),
            ],
            scratch_shapes=[
                pltpu.VMEM(sums.shape, F32),
                pltpu.VMEM(routed.shape, BF16),
                pltpu.SemaphoreType.DMA((2,)),
            ],
        ),
        out_shape=[
            jax.ShapeDtypeStruct((own, query_width), F32),
            jax.ShapeDtypeStruct((2 * key_width, own), F32),
            jax.ShapeDtypeStruct((latent_rows + 8, own + 128), F32),
            jax.ShapeDtypeStruct((1, own // 2), F32),
            jax.ShapeDtypeStruct((2 * latent_rows, own // 2), F32),
            jax.ShapeDtypeStruct(routed.shape, BF16),
        ],
        cost_estimate=pl.CostEstimate(
            flops=100_000_000, bytes_accessed=3_000_000, transcendentals=0
        ),
        compiler_params=pltpu.CompilerParams(vmem_limit_bytes=VMEM_LIMIT),
    )(where, sums, *parts, proj, latents, gain_lat.reshape(1, width), w_query, wk, wv, routed)


def plane_kernel(
    value_ref,
    value_got_ref,
    value_last_ref,
    key_ref,
    key_got_ref,
    key_last_ref,
    going_ref,
    high_ref,
):
    key_width = value_ref.shape[-2]
    for i, ref in enumerate((going_ref.at[0], going_ref.at[1], high_ref)):
        for j, parts in enumerate(
            (
                (key_ref, key_got_ref, key_last_ref),
                (value_ref, value_got_ref, value_last_ref),
            )
        ):
            total = sum(part[i].astype(F32) for part in parts)
            ref[j * key_width : (j + 1) * key_width, :] = total.astype(ref.dtype)


def plane_call(value, value_got, value_last, key, key_got, key_last):
    _, key_width, own = value.shape
    upper = pl.BlockSpec((4, key_width, own), lambda i: (1, 0, 0))
    last = pl.BlockSpec((4, key_width, own), lambda i: (0, 0, 0))
    shape = (2 * key_width, own)
    return pl.pallas_call(
        plane_kernel,
        name="plane_sum",
        grid=(1,),
        in_specs=[upper, upper, last] * 2,
        out_specs=[held((2, *shape)), held(shape)],
        out_shape=[
            jax.ShapeDtypeStruct((2, *shape), BF16),
            jax.ShapeDtypeStruct(shape, F32),
        ],
        cost_estimate=pl.CostEstimate(flops=1_000_000, bytes_accessed=3_000_000, transcendentals=0),
        compiler_params=pltpu.CompilerParams(vmem_limit_bytes=VMEM_LIMIT),
    )(value, value_got, value_last, key, key_got, key_last)


def final_kernel(
    where_ref,
    value_ref,
    value_got_ref,
    value_last_ref,
    key_ref,
    key_got_ref,
    key_last_ref,
    low_ref,
    high_ref,
    gain_ref,
    pair_ref,
    wk_ref,
    wv_ref,
    key_grad_ref,
    value_grad_ref,
    gain_term_ref,
):
    key_width = wk_ref.shape[0]
    term = jnp.zeros((1, wk_ref.shape[1]), F32)
    for j, (w_ref, out_ref, parts) in enumerate(
        (
            (wk_ref, key_grad_ref, (key_ref, key_got_ref, key_last_ref)),
            (wv_ref, value_grad_ref, (value_ref, value_got_ref, value_last_ref)),
        )
    ):
        at = slice(j * key_width, (j + 1) * key_width)
        total = sum(part[0].astype(F32) for part in parts)
        total = total + low_ref[0, at, :].astype(F32) + high_ref[at, :].astype(F32)
        term = term + jnp.sum(w_ref[...].astype(F32) * total, axis=0, keepdims=True)
        out_ref[...] = total * gain_ref[...] + pair_ref[at, :]
    gain_term_ref[...] = jnp.broadcast_to(term, gain_term_ref.shape)


def final_call(where, value, value_got, value_last, key, key_got, key_last, line, gain_ctx, pair, wk, wv):
    rows, own = pair.shape
    width = gain_ctx.shape[0]
    key_width = rows // 2
    w_spec = pl.BlockSpec((key_width, own), lambda i, w: (0, w[0]))
    end = pl.BlockSpec((1, key_width, own), lambda i, w: (7, 0, 0))
    last = pl.BlockSpec((1, key_width, own), lambda i, w: (3, 0, 0))
    return pl.pallas_call(
        final_kernel,
        name="key_value_gradients",
        grid_spec=pltpu.PrefetchScalarGridSpec(
            num_scalar_prefetch=1,
            grid=(1,),
            in_specs=[end, end, last] * 2
            + [pl.BlockSpec((1, rows, own), lambda i, w: (1, 0, 0)), held(pair.shape)]
            + [pl.BlockSpec((1, own), lambda i, w: (0, w[0])), held(pair.shape), w_spec, w_spec],
            out_specs=[held((key_width, own)), held((key_width, own)), held((8, own))],
        ),
        out_shape=[
            jax.ShapeDtypeStruct((key_width, own), F32),
            jax.ShapeDtypeStruct((key_width, own), F32),
            jax.ShapeDtypeStruct((8, own), F32),
        ],
        cost_estimate=pl.CostEstimate(flops=1_000_000, bytes_accessed=3_000_000, transcendentals=0),
        compiler_params=pltpu.CompilerParams(vmem_limit_bytes=VMEM_LIMIT),
    )(
        where,
        value,
        value_got,
        value_last,
        key,
        key_got,
        key_last,
        *line,
        gain_ctx.reshape(1, width),
        pair,
        wk,
        wv,
    )


def out_final_kernel(
    where_ref,
    first_kept_ref,
    first_got_ref,
    first_last_ref,
    second_kept_ref,
    second_got_ref,
    second_last_ref,
    message_ref,
    message_got_ref,
    term_ref,
    term_got_ref,
    terms_ref,
    out_ref,
    latent_ref,
    gain_lat_ref,
    gain_ctx_ref,
):
    heads, own = out_ref.shape
    latent_rows = latent_ref.shape[0]
    share = own // 2
    cut = heads // 2
    first, second = (
        sum(part.astype(F32) for part in parts)
        for parts in (
            (first_kept_ref[0], first_got_ref[...], first_last_ref[...]),
            (second_kept_ref[0], second_got_ref[...], second_last_ref[...]),
        )
    )
    out_ref[:cut, :] = first[:cut]
    out_ref[cut:, :] = second[:cut]
    resid = jnp.concatenate([first[cut:], second[cut:]], axis=0)
    resid = jnp.concatenate([resid[:, :share], resid[:, share:]], axis=0)
    mine = pl.ds(pl.multiple_of(where_ref[1] * share, share), share)
    d_lat = message_ref[:, mine] + message_got_ref[:, mine]
    lat_dot = message_ref[:latent_rows, own : own + 1] + message_got_ref[:latent_rows, own : own + 1]
    latent_ref[...] = (
        resid
        + terms_ref[:latent_rows, :] * d_lat[:latent_rows]
        - terms_ref[latent_rows:, :] * lat_dot
    )
    gain_lat_ref[...] = d_lat[latent_rows : latent_rows + 1]
    gain_ctx_ref[...] = term_ref[:1, mine] + term_got_ref[:1, mine]


def out_final_call(where, parts, message, message_got, term, term_got, terms):
    _, rows, own = parts[0].shape
    latent_rows = terms.shape[0] // 2
    heads = 2 * (rows - latent_rows // 4)
    shapes = [(heads, own), (latent_rows, own // 2), (1, own // 2), (1, own // 2)]
    return pl.pallas_call(
        out_final_kernel,
        name="output_gradient_sum",
        grid_spec=pltpu.PrefetchScalarGridSpec(
            num_scalar_prefetch=1,
            grid=(1,),
            in_specs=[
                pl.BlockSpec((1, *part.shape[1:]), lambda i, w: (1, 0, 0))
                if part.ndim == 3
                else held(part.shape)
                for part in parts
            ]
            + [held(a.shape) for a in (message, message_got, term, term_got, terms)],
            out_specs=[held(shape) for shape in shapes],
        ),
        out_shape=[jax.ShapeDtypeStruct(shape, F32) for shape in shapes],
        cost_estimate=pl.CostEstimate(flops=1_000_000, bytes_accessed=3_000_000, transcendentals=0),
        compiler_params=pltpu.CompilerParams(vmem_limit_bytes=VMEM_LIMIT),
    )(
        where,
        *parts,
        message,
        message_got,
        term,
        term_got,
        terms,
    )


def add_halves(left, right):
    return left.astype(F32) + right.astype(F32)


def local(
    context,
    counts,
    routes,
    w_query,
    w_key,
    w_value,
    w_out,
    latents,
    gain_ctx,
    gain_lat,
    gain_out,
    cotangent,
):
    dp_count = lax.axis_size("dp")
    mp_index = lax.axis_index("mp")
    dp_index = lax.axis_index("dp")
    patch_rows, width = context.shape
    half_width = width // 2
    own_width = width // dp_count
    latent_rows = latents.shape[0]
    slot_count = cotangent.shape[0] // dp_count
    slots = dp_count * slot_count
    query_width = w_query.shape[1]

    def swap(array, turn):
        return lax.ppermute(array, "dp", [(i, i ^ turn) for i in range(dp_count)])

    def exchange(array):
        blocks = array.reshape(dp_count, slot_count, half_width)
        return lax.all_to_all(blocks, "dp", split_axis=0, concat_axis=0, tiled=True).reshape(
            slots, half_width
        )

    wk = w_key.T
    wv = w_value.T
    turned_routes = routes.reshape(1, -1)
    where = jnp.stack([dp_index, mp_index])

    returned = exchange(cotangent)
    w_out_other = swap_cores(w_out)
    wk_other = swap_cores(wk)
    wv_other = swap_cores(wv)

    (attn_rows, k, v, inv_row, q, lat_k, lat_v, lat_proj, p, lat_p) = forward_call(
        context, counts, w_query, wk, wv, latents, gain_ctx, gain_lat
    )
    wk_other, wv_other, attn_rows = lax.optimization_barrier((wk_other, wv_other, attn_rows))
    attn_other = swap_cores(attn_rows)
    out_hat, out_inv, outgoing = branch_call(
        attn_rows,
        attn_other,
        w_out,
        w_out_other,
        latents,
        gain_out,
        turned_routes,
        slots,
        slot_count,
    )

    routed = exchange(outgoing)
    returned, out_inv = lax.optimization_barrier((returned, out_inv))
    returned_other = swap_cores(returned)
    backward = backward_call(
        counts,
        attn_rows,
        returned,
        returned_other,
        out_hat,
        out_inv,
        gain_out,
        turned_routes,
        w_out,
        (k, v, q, lat_k, lat_v, p, lat_p, inv_row),
        context,
        slot_count,
    )
    backward = lax.optimization_barrier(backward)
    (
        line_own,
        line_high,
        pair,
        message,
        lat_terms,
        value_going,
        value_kept,
        key_going,
        key_kept,
    ) = backward

    value_got = swap(value_going, 1)
    key_got = swap(key_going, 2)
    pair_other = swap_cores(pair)

    line_high, message, lat_terms, pair_other = lax.optimization_barrier(
        (line_high, message, lat_terms, pair_other)
    )
    lat_got = swap(lat_terms, 4)
    got_high = swap(line_high, 8)
    got_low = swap(message, 4)

    ctx_grad = patch_call(
        where, pair, pair_other, wk, wv, wk_other, wv_other, context, inv_row, gain_ctx
    )

    lat_got, ctx_grad = lax.optimization_barrier((lat_got, ctx_grad))
    lat_sum = add_halves(lat_terms, lat_got)
    lat_low = lat_sum.astype(BF16)
    value_got, key_got, ctx_grad, routed, lat_low = lax.optimization_barrier(
        (value_got, key_got, ctx_grad, routed, lat_low)
    )
    key_kept = key_kept.reshape((8,) + key_kept.shape[2:])
    key_got = key_got.reshape((8,) + key_got.shape[2:])
    value_going = add_halves(value_kept[:4], value_got[:4]).astype(BF16)
    key_going = add_halves(key_kept[:4], key_got[:4]).astype(BF16)
    value_last = swap(value_going, 2)
    key_last = swap(key_going, 1)

    got_low, got_high, value_going, key_going, lat_low = lax.optimization_barrier(
        (got_low, got_high, value_going, key_going, lat_low)
    )
    lat_got = swap(lat_low, 8)
    forwarded = swap(got_high[:, width // 4 :], 4)
    other_low = swap_cores(got_low)
    other_high = swap_cores(got_high)

    planes = plane_call(value_kept, value_got, value_last, key_kept, key_got, key_last)
    low = swap(planes[0], 4)
    (_, high), lat_got, forwarded = lax.optimization_barrier((planes, lat_got, forwarded))
    other_forwarded = swap_cores(forwarded)
    lat_sum = add_halves(lat_sum, lat_got).astype(BF16)
    lat_parts = (swap(lat_sum, 1), swap(lat_sum, 2), swap(lat_sum, 3))

    first_onward, first_end, first_kept, second_onward, second_end, second_kept = out_call(
        where,
        attn_rows,
        line_own,
        (got_low, got_high, forwarded),
        (other_low, other_high, other_forwarded),
    )
    low, first_onward, second_onward, first_end, second_end = lax.optimization_barrier(
        (low, first_onward, second_onward, first_end, second_end)
    )
    high = add_halves(high, low[0]).astype(BF16)
    high, lat_parts = lax.optimization_barrier((high, lat_parts))
    high = swap(high, 8)
    first_onward = swap(first_onward, 1)
    second_onward = swap(second_onward, 2)
    first_end = swap(first_end, 1)
    second_end = swap(second_end, 2)

    grad_w_query, pair_lat, message, grad_gain_out, terms, routed = latent_call(
        where, lat_sum, lat_parts, lat_proj, latents, gain_lat, w_query, wk, wv, own_width, routed
    )
    first_onward, second_onward, first_end, second_end, message, pair_lat = (
        lax.optimization_barrier(
            (first_onward, second_onward, first_end, second_end, message, pair_lat)
        )
    )
    high, pair_lat = lax.optimization_barrier((high, pair_lat))
    first_last = swap(add_halves(first_kept[0], first_onward).astype(BF16), 2)
    second_last = swap(add_halves(second_kept[0], second_onward).astype(BF16), 1)
    message_got = swap_cores(message)

    grad_key, grad_value, gain_term = final_call(
        where,
        value_kept,
        value_got,
        value_last,
        key_kept,
        key_got,
        key_last,
        (low, high),
        gain_ctx,
        pair_lat,
        wk,
        wv,
    )
    gain_got = swap_cores(gain_term)
    first_last, second_last, gain_term = lax.optimization_barrier(
        (first_last, second_last, gain_term)
    )
    grad_w_out, grad_latents, grad_gain_lat, grad_gain_ctx = out_final_call(
        where,
        (first_kept, first_end, first_last, second_kept, second_end, second_last),
        message,
        message_got,
        gain_term,
        gain_got,
        terms,
    )
    return (
        routed,
        ctx_grad,
        grad_w_query,
        grad_key.T,
        grad_value.T,
        grad_w_out,
        grad_latents,
        grad_gain_ctx[0],
        grad_gain_lat[0],
        grad_gain_out[0],
    )


def local_general(
    context,
    counts,
    routes,
    w_query,
    w_key,
    w_value,
    w_out,
    latents,
    gain_ctx,
    gain_lat,
    gain_out,
    cotangent,
):
    dp_count = lax.axis_size("dp")
    mp_count = lax.axis_size("mp")
    mp_index = lax.axis_index("mp")
    dp_index = lax.axis_index("dp")
    bits = dp_count.bit_length() - 1
    gather_bits = [bits - 1, bits - 2]
    scatter_bits = list(range(bits - 2))
    order_one = list(range(bits))
    order_two = [1, 0] + order_one[2:]
    patch_rows, width = context.shape
    half_width = width // mp_count
    own_width = width // dp_count
    head_local = w_query.shape[1] // HD
    group_local = w_key.shape[1] // HD
    per_group = head_local // group_local
    latent_rows = latents.shape[0]
    image_slots = counts.shape[1]
    out_rows = image_slots * latent_rows
    slot_count = cotangent.shape[0] // dp_count
    key_width = w_key.shape[1]
    query_width = w_query.shape[1]
    scaling = HD ** (-0.5)

    returned = lax.all_to_all(
        cotangent.reshape(dp_count, slot_count, half_width),
        "dp",
        split_axis=0,
        concat_axis=0,
        tiled=True,
    ).reshape(dp_count * slot_count, half_width)
    returned_other = swap_cores(returned)
    w_out_other = swap_cores(w_out)
    w_pair = jnp.concatenate([w_key, w_value], axis=1)
    w_pair_half = lax.dynamic_slice_in_dim(w_pair, mp_index * half_width, half_width, 0)
    w_pair_other = swap_cores(
        lax.dynamic_slice_in_dim(w_pair, (1 - mp_index) * half_width, half_width, 0)
    )

    patch_hat, patch_inv = norm_parts(context.astype(F32))
    normed_ctx = (patch_hat * gain_ctx).astype(BF16)
    key_f32 = jnp.dot(normed_ctx, w_key, preferred_element_type=F32)
    value_f32 = jnp.dot(normed_ctx, w_value, preferred_element_type=F32)
    key_rows = key_f32.astype(BF16)
    value_rows = value_f32.astype(BF16)
    lat_float = latents.astype(F32)
    lat_hat, lat_inv = norm_parts(lat_float)
    normed_lat = (lat_hat * gain_lat).astype(BF16)
    lat_key_f32 = jnp.dot(normed_lat, w_key, preferred_element_type=F32)
    lat_value_f32 = jnp.dot(normed_lat, w_value, preferred_element_type=F32)
    lat_keys = lat_key_f32.astype(BF16)
    lat_values = lat_value_f32.astype(BF16)
    query_f32 = jnp.dot(normed_lat, w_query, preferred_element_type=F32) * scaling
    query_rows = query_f32.astype(BF16)
    query_heads = query_rows.reshape(latent_rows, group_local, per_group, HD)
    key_heads = key_rows.reshape(patch_rows, group_local, HD)
    value_heads = value_rows.reshape(patch_rows, group_local, HD)
    lat_key_heads = lat_keys.reshape(latent_rows, group_local, HD)
    lat_value_heads = lat_values.reshape(latent_rows, group_local, HD)
    scores = jnp.einsum(
        "rkgd,tkd->kgrt", query_heads, key_heads, preferred_element_type=jnp.float32
    )
    lat_scores = jnp.einsum(
        "rkgd,skd->kgrs", query_heads, lat_key_heads, preferred_element_type=jnp.float32
    )
    position = jnp.arange(patch_rows, dtype=jnp.int32)
    image_count = counts[0]
    image_start = jnp.cumsum(image_count) - image_count
    member = (position[None, :] >= image_start[:, None]) & (
        position[None, :] < (image_start + image_count)[:, None]
    )
    member_wide = member[:, None, None, None, :]
    masked = jnp.where(member_wide, scores[None], NEGATIVE)
    row_max = jnp.maximum(
        jnp.max(masked, axis=-1, keepdims=True), jnp.max(lat_scores, axis=-1, keepdims=True)[None]
    )
    exponent = jnp.where(member_wide, jnp.exp(masked - row_max), 0.0)
    lat_exponent = jnp.exp(lat_scores[None] - row_max)
    total = jnp.sum(exponent, axis=-1, keepdims=True) + jnp.sum(
        lat_exponent, axis=-1, keepdims=True
    )
    attention = exponent / total
    lat_attention = lat_exponent / total
    attention_low = attention.astype(BF16)
    lat_attention_low = lat_attention.astype(BF16)
    mixed = jnp.einsum(
        "ikgrt,tkd->irkgd", attention_low, value_heads, preferred_element_type=jnp.float32
    )
    mixed = mixed + jnp.einsum(
        "ikgrs,skd->irkgd", lat_attention_low, lat_value_heads, preferred_element_type=jnp.float32
    )
    attn_rows = mixed.reshape(out_rows, query_width).astype(BF16)
    attn_other = swap_cores(attn_rows)
    branch = jnp.dot(attn_rows, w_out, preferred_element_type=F32) + jnp.dot(
        attn_other, w_out_other, preferred_element_type=F32
    )
    resid = jnp.tile(lat_float, (image_slots, 1)) + branch
    out_hat, out_inv = norm_parts(resid)
    final_rows = (out_hat * gain_out).astype(BF16)
    shard_of = routes[:, 0]
    shard_hot = (shard_of[:, None] == jnp.arange(dp_count, dtype=jnp.int32)[None, :]).astype(
        jnp.int32
    )
    rank = jnp.sum((jnp.cumsum(shard_hot, axis=0) - shard_hot) * shard_hot, axis=1)
    place = shard_of * slot_count + rank
    scatter_table = (
        jnp.arange(dp_count * slot_count, dtype=jnp.int32)[:, None] == place[None, :]
    ).astype(BF16)
    final_half = lax.dynamic_slice_in_dim(final_rows, mp_index * half_width, half_width, 1)
    outgoing = jnp.dot(scatter_table, final_half, preferred_element_type=F32).astype(BF16)
    routed = lax.all_to_all(
        outgoing.reshape(dp_count, slot_count, half_width),
        "dp",
        split_axis=0,
        concat_axis=0,
        tiled=True,
    ).reshape(dp_count * slot_count, half_width)

    attn_line = attn_rows
    for bit in gather_bits:
        attn_line = jnp.concatenate([attn_line, swap_bit(attn_line, bit, dp_count)], axis=0)

    first = jnp.where(mp_index == 0, returned, returned_other)
    second = jnp.where(mp_index == 0, returned_other, returned)
    d_final = jnp.concatenate(
        [dot_general(scatter_table, first, 0, 0), dot_general(scatter_table, second, 0, 0)], axis=1
    )
    d_hat = d_final * gain_out
    d_resid = out_inv * (d_hat - out_hat * jnp.mean(d_hat * out_hat, axis=1, keepdims=True))
    gain_out_term = jnp.sum(d_final * out_hat, axis=0)
    d_branch = d_resid.astype(BF16)
    d_attn = dot_general(d_branch, w_out, 1, 1).astype(BF16)

    d_attn_heads = d_attn.reshape(image_slots, latent_rows, group_local, per_group, HD)
    d_probs = jnp.einsum(
        "irkgd,tkd->ikgrt", d_attn_heads, value_heads, preferred_element_type=jnp.float32
    )
    d_lat_probs = jnp.einsum(
        "irkgd,skd->ikgrs", d_attn_heads, lat_value_heads, preferred_element_type=jnp.float32
    )
    row_delta = jnp.sum(attention * d_probs, axis=-1, keepdims=True) + jnp.sum(
        lat_attention * d_lat_probs, axis=-1, keepdims=True
    )
    d_scores = jnp.sum(attention * (d_probs - row_delta), axis=0).astype(BF16)
    d_lat_scores = jnp.sum(lat_attention * (d_lat_probs - row_delta), axis=0).astype(BF16)
    d_query = jnp.einsum("kgrt,tkd->rkgd", d_scores, key_heads, preferred_element_type=jnp.float32)
    d_query = d_query + jnp.einsum(
        "kgrs,skd->rkgd", d_lat_scores, lat_key_heads, preferred_element_type=jnp.float32
    )
    d_query = d_query.reshape(latent_rows, query_width).astype(BF16)
    d_keys = jnp.einsum("kgrt,rkgd->tkd", d_scores, query_heads, preferred_element_type=jnp.float32)
    d_keys = d_keys.reshape(patch_rows, key_width).astype(BF16)
    d_values = jnp.einsum(
        "ikgrt,irkgd->tkd", attention_low, d_attn_heads, preferred_element_type=jnp.float32
    )
    d_values = d_values.reshape(patch_rows, key_width).astype(BF16)
    d_lat_keys = jnp.einsum(
        "kgrs,rkgd->skd", d_lat_scores, query_heads, preferred_element_type=jnp.float32
    )
    d_lat_keys = d_lat_keys.reshape(latent_rows, key_width).astype(BF16)
    d_lat_values = jnp.einsum(
        "ikgrs,irkgd->skd", lat_attention_low, d_attn_heads, preferred_element_type=jnp.float32
    )
    d_lat_values = d_lat_values.reshape(latent_rows, key_width).astype(BF16)
    d_pair = jnp.concatenate([d_keys, d_values], axis=1)

    value_grad = dot_general(d_values, normed_ctx, 0, 0).reshape(key_width, dp_count, own_width)
    key_grad = dot_general(d_keys, normed_ctx, 0, 0).reshape(key_width, dp_count, own_width)
    value_block = scatter_sum(value_grad, order_one, dp_count)
    key_block = scatter_sum(key_grad, order_two, dp_count)

    row_dot = jnp.sum(d_keys.astype(F32) * key_f32, axis=1) + jnp.sum(
        d_values.astype(F32) * value_f32, axis=1
    )
    row_dot = (row_dot + swap_cores(row_dot)) / width
    d_pair_other = swap_cores(d_pair)
    d_ctx_in = dot_general(d_pair, w_pair_half, 1, 1) + dot_general(
        d_pair_other, w_pair_other, 1, 1
    )
    gain_ctx_half = lax.dynamic_slice_in_dim(gain_ctx, mp_index * half_width, half_width, 0)
    hat_half = lax.dynamic_slice_in_dim(patch_hat, mp_index * half_width, half_width, 1)
    ctx_grad = (patch_inv * (d_ctx_in * gain_ctx_half - hat_half * row_dot[:, None])).astype(BF16)

    high = gain_out_term.astype(BF16)
    low = (gain_out_term - high.astype(F32)).astype(BF16)
    lat_sum = jnp.concatenate(
        [
            d_query,
            d_lat_keys,
            d_lat_values,
            high.reshape(latent_rows, width // latent_rows),
            low.reshape(latent_rows, width // latent_rows),
        ],
        axis=1,
    ).astype(F32)
    for bit in gather_bits + scatter_bits:
        lat_sum = lat_sum + swap_bit(lat_sum.astype(BF16), bit, dp_count).astype(F32)
    pair_sum = lat_sum[:, query_width : query_width + 2 * key_width]
    query_sum = lat_sum[:, :query_width]
    gains_at = query_width + 2 * key_width
    gain_step = width // latent_rows
    gain_out_full = (
        lat_sum[:, gains_at : gains_at + gain_step]
        + lat_sum[:, gains_at + gain_step : gains_at + 2 * gain_step]
    ).reshape(width)

    plane = dp_count // 4
    row_half = out_rows // mp_count
    d_block = lax.dynamic_slice_in_dim(d_branch, mp_index * row_half, row_half, 0)
    d_line = d_block.reshape(1, row_half, 2, 2, plane * own_width)
    for step, bit in enumerate(gather_bits):
        mine = (dp_index >> bit) & 1
        going = lax.dynamic_index_in_dim(d_line, 1 - mine, 2, keepdims=False)
        kept = lax.dynamic_index_in_dim(d_line, mine, 2, keepdims=False)
        d_line = jnp.concatenate([kept, swap_bit(going, bit, dp_count)], axis=0)
    d_line_other = swap_cores(d_line)
    d_line = jnp.concatenate(
        [
            jnp.where(mp_index == 0, d_line, d_line_other),
            jnp.where(mp_index == 0, d_line_other, d_line),
        ],
        axis=1,
    )
    out_part = dot_general(attn_line, d_line.reshape(4 * out_rows, plane * own_width), 0, 0)
    resid_part = jnp.sum(
        d_line.astype(F32).reshape(4 * image_slots, latent_rows, plane * own_width), axis=0
    )
    resid_part = lax.dynamic_index_in_dim(
        resid_part.reshape(2, latent_rows // 2, plane, mp_count, own_width // mp_count),
        mp_index,
        3,
        keepdims=False,
    )
    resid_part = jnp.transpose(resid_part, (1, 2, 0, 3)).reshape(
        latent_rows // 2, plane, own_width
    )
    out_part = jnp.concatenate([out_part.reshape(query_width, plane, own_width), resid_part], axis=0)
    cut = out_part.shape[0] // 2
    out_block = jnp.concatenate(
        [
            scatter_sum(out_part[:cut], scatter_bits, dp_count),
            scatter_sum(out_part[cut:], [1, 0] + scatter_bits[2:], dp_count),
        ],
        axis=0,
    )
    grad_w_out = out_block[:query_width]
    resid_sum = (
        out_block[query_width:]
        .reshape(latent_rows // 2, 2, own_width // mp_count)
        .transpose(1, 0, 2)
        .reshape(latent_rows, own_width // mp_count)
    )

    def own(array, axis):
        return lax.dynamic_slice_in_dim(array, dp_index * own_width, own_width, axis)

    lat_own = own(normed_lat, 1)
    pair_ctx = jnp.concatenate([key_block, value_block], axis=0).T
    query_grad = dot_general(lat_own, query_sum.astype(BF16), 0, 0) * scaling
    pair_lat = dot_general(lat_own, pair_sum.astype(BF16), 0, 0)
    pair_all = pair_ctx + pair_lat
    wq_own = own(w_query, 0)
    pair_own = own(w_pair, 0)
    gain_ctx_part = jnp.sum(pair_own.astype(F32) * pair_ctx, axis=1) / own(gain_ctx, 0)
    gain_lat_part = (
        jnp.sum(wq_own.astype(F32) * query_grad, axis=1)
        + jnp.sum(pair_own.astype(F32) * pair_lat, axis=1)
    ) / own(gain_lat, 0)
    d_lat_part = dot_general(
        (query_sum * scaling).astype(BF16), wq_own, 1, 1
    ) + dot_general(pair_sum.astype(BF16), pair_own, 1, 1)
    lat_dot_part = (
        jnp.sum(query_sum * query_f32, axis=1)
        + jnp.sum(pair_sum[:, :key_width] * lat_key_f32, axis=1)
        + jnp.sum(pair_sum[:, key_width:] * lat_value_f32, axis=1)
    )
    small = jnp.concatenate(
        [
            d_lat_part,
            jnp.broadcast_to(lat_dot_part[:, None], (latent_rows, own_width)),
            jnp.broadcast_to(gain_ctx_part[None, :], (8, own_width)),
            jnp.broadcast_to(gain_lat_part[None, :], (8, own_width)),
        ],
        axis=0,
    )
    small = small + swap_cores(small)
    share = own_width // mp_count
    small = lax.dynamic_slice_in_dim(small, mp_index * share, share, 1)
    d_lat_in = small[:latent_rows]
    lat_dot = small[latent_rows : 2 * latent_rows] / width

    def mine_of(array, axis):
        return lax.dynamic_slice_in_dim(
            array, dp_index * own_width + mp_index * share, share, axis
        )

    grad_latents = resid_sum + lat_inv * (
        mine_of(gain_lat, 0) * d_lat_in - mine_of(lat_hat, 1) * lat_dot
    )
    return (
        routed,
        ctx_grad,
        query_grad,
        pair_all[:, :key_width],
        pair_all[:, key_width:],
        grad_w_out,
        grad_latents,
        small[2 * latent_rows],
        small[2 * latent_rows + 8],
        mine_of(gain_out_full, 0),
    )


def solution(mesh):
    placed = (
        P("dp", None),
        P("dp", None),
        P("dp", None),
        P(None, "mp"),
        P(None, "mp"),
        P(None, "mp"),
        P("mp", None),
        P(),
        P(),
        P(),
        P(),
        P("dp", "mp"),
    )
    return jax.shard_map(
        local if mesh.shape["dp"] == 16 else local_general,
        mesh=mesh,
        in_specs=placed,
        out_specs=(
            P("dp", "mp"),
            P("dp", "mp"),
            P("dp", "mp"),
            P("dp", "mp"),
            P("dp", "mp"),
            P("mp", "dp"),
            P(None, ("dp", "mp")),
            P(("dp", "mp")),
            P(("dp", "mp")),
            P(("dp", "mp")),
        ),
        check_vma=False,
    )
```
